32 devices in a mesh: dp: 2 (over x), row: 4 (over z), col: 4 (over y, core).
Axes of the slice: x: 2, y: 2, z: 4, core: 2. Of those that a mesh axis runs over, the one named last changes fastest.
Arguments:
- tokens: bfloat16 [16, 768, 1024], P(('dp', 'row'), 'col'), may hold values from -6 to 6
- memory: bfloat16 [16, 20, 768], P(('dp', 'row'), None, 'col'), may hold values from -6 to 6
- block_ids: int32 [16, 1024], P(('dp', 'row')), may hold values from 0 to 7, never falling along the last dimension, each value on 1 to 256 neighbouring positions
- valid: int32 [16], replicated, may hold values from 512 to 1024
- teacher: bfloat16 [16, 768, 1024], P(('dp', 'row'), 'col'), may hold values from -6 to 6
- w_qkv: bfloat16 [12, 147456], P('row', 'col'), may hold values from -0.21875 to 0.21875
- bias_qv: float32 [12, 128], P('row'), may hold values from -3 to 3
- w_out: bfloat16 [768, 768], P('row', 'col'), may hold values from -0.875 to 0.875
- bias_out: float32 [768], P('col'), may hold values from -2 to 2
- ln1_gain: float32 [768], P('col'), may hold values from 0.1 to 1.9
- ln1_bias: float32 [768], P('col'), may hold values from -2 to 2
- w_up: bfloat16 [768, 3072], P('col', 'row'), may hold values from -0.21875 to 0.21875
- bias_up: float32 [3072], P('row'), may hold values from -3 to 3
- w_down: bfloat16 [768, 3072], P('col', 'row'), may hold values from -0.109375 to 0.109375
- bias_down: float32 [768], P('col'), may hold values from -2 to 2
- ln2_gain: float32 [768], P('col'), may hold values from 0.1 to 1.9
- ln2_bias: float32 [768], P('col'), may hold values from -2 to 2
Outputs:
- layer_out: bfloat16 [16, 1044, 768], P(('dp', 'row'), None, 'col')
- grad_tokens: float32 [16, 1024, 768], P(('dp', 'row'), None, 'col')
- grad_memory: float32 [16, 20, 768], P(('dp', 'row'), None, 'col')
- grad_w_qkv: float32 [12, 147456], P('row', 'col')
- grad_bias_qv: float32 [12, 128], P('row')
- grad_w_out: float32 [768, 768], P('row', 'col')
- grad_bias_out: float32 [768], P('col')
- grad_ln1_gain: float32 [768], P('col')
- grad_ln1_bias: float32 [768], P('col')
- grad_w_up: float32 [768, 3072], P('col', 'row')
- grad_bias_up: float32 [3072], P('row')
- grad_w_down: float32 [768, 3072], P('col', 'row')
- grad_bias_down: float32 [768], P('col')
- grad_ln2_gain: float32 [768], P('col')
- grad_ln2_bias: float32 [768], P('col')
The draws below stay inside these ranges and needn't reach their ends.
Inputs may be any that keep to these rules, and one draw needn't show every extreme that they name: `block_ids`: along each sequence the numbers never fall; each of the 8 numbers covers 1 to 256 consecutive tokens.
All inputs are finite; a program needn't handle non-finite values.
Results may differ from the reference program's by a relative error of at most 0.015.
Values may be sent and summed in bfloat16 or wider, within the bound.
A program may use at most 192 MiB of HBM per device.

```python
import math
import jax
import jax.numpy as jnp
import numpy as np
from jax import lax

D = 768
HEADS = 12
HEAD = 64
FF = 3072
LEN = 1024
MEM = 10
BLOCK = 256
NBLOCKS = 8
SEQS = 16


def set_ends(array, key, smallest, high):
    index_at = [jax.random.randint(jax.random.fold_in(key, axis), (), 0, length) for axis, length in enumerate(array.shape)]
    main_axis = array.shape.index(max(array.shape))
    beside = index_at[:main_axis] + [(index_at[main_axis] + 1) % array.shape[main_axis]] + index_at[main_axis + 1:]
    return array.at[tuple(index_at)].set(smallest).at[tuple(beside)].set(high)


def steps_of(stream_key, shape, pieces, least, top_value):
    factor_of = 1.0
    for axis_at, parts in pieces:
        steps = jax.random.uniform(jax.random.fold_in(jax.random.fold_in(stream_key, 6), axis_at), (parts,), jnp.float32, least / len(pieces), top_value / len(pieces))
        factor_of = factor_of * jnp.repeat(jnp.exp(steps), shape[axis_at] // parts).reshape((-1,) + (1,) * (len(shape) - 1 - axis_at))
    return factor_of


def split_up(count, total, most, slope):
    weights = [(1 << 20) // math.isqrt(standing ** slope) + 1 for standing in range(2, count + 1)]
    surplus, given = total - most - (count - 1), [1] * (count - 1)
    while surplus > 0:
        free = [i for i in range(count - 1) if given[i] < most]
        whole, remaining = sum([weights[i] for i in free]), surplus
        for i in free:
            addition = min(most - given[i], max(1, remaining * weights[i] // whole), surplus)
            given[i] = given[i] + addition
            surplus = surplus - addition
    return np.array([most] + given)


def ragged(stream_key, count, total, limit, skew):
    if count == 2:
        one = jax.random.randint(stream_key, (), max(1, total - limit), min(limit, total - 1) + 1)
        return jnp.stack([one, total - one])
    tallies = jnp.asarray(split_up(count, total, limit, skew), jnp.int32)
    twos = (count - 1) // 2
    donor, receiver = tallies[1:1 + 2 * twos:2], tallies[2:2 + 2 * twos:2]
    slack = jnp.minimum(donor - 1, limit - receiver)
    moved = jax.random.randint(jax.random.fold_in(stream_key, 1), (twos,), 0, 1 << 20) % (slack + 1)
    tallies = tallies.at[1:1 + 2 * twos:2].set(donor - moved).at[2:2 + 2 * twos:2].set(receiver + moved)
    return tallies[jax.random.permutation(jax.random.fold_in(stream_key, 2), count)]


def bell_draw(key, shape, deviation, bound, shards=(), held_as=jnp.bfloat16):
    values = jax.random.normal(key, shape, jnp.float32) * deviation
    if len(shards) > 0:
        values = steps_of(key, shape, shards, -0.22, 0.18) * values
    return jnp.clip(values, min=-bound, max=bound).astype(held_as)


def setup_inputs(seed: int = 0) -> dict:
    key_list = jax.random.split(jax.random.key(seed), 18)
    return {
        "tokens": bell_draw(key_list[0], (SEQS, D, LEN), 1.0, 6.0, ((0, 8), (1, 4))),
        "memory": bell_draw(key_list[1], (SEQS, 2 * MEM, D), 1.0, 6.0, ((0, 8), (2, 4))),
        "block_ids": jax.vmap(lambda own: jnp.searchsorted(jnp.cumsum(ragged(own, NBLOCKS, LEN, BLOCK, 1)), jnp.arange(LEN), side="right"))(jax.random.split(key_list[2], SEQS)).reshape((SEQS, LEN)).astype(jnp.int32),
        "valid": set_ends(jax.random.randint(key_list[3], (SEQS,), LEN // 2, LEN + 1), jax.random.fold_in(key_list[3], 1), LEN // 2, LEN).astype(jnp.int32),
        "teacher": bell_draw(key_list[4], (SEQS, D, LEN), 1.0, 6.0, ((0, 8), (1, 4))),
        "w_qkv": bell_draw(key_list[5], (HEADS, D * 3 * HEAD), D ** -0.5, 0.21875, ((0, 4), (1, 4))),
        "bias_qv": bell_draw(key_list[6], (HEADS, 2 * HEAD), 0.5, 3.0, ((0, 4),), jnp.float32),
        "w_out": bell_draw(key_list[7], (D, D), (D // 16) ** -0.5, 0.875, ((0, 4), (1, 4))),
        "bias_out": bell_draw(key_list[8], (D,), 0.3, 2.0, ((0, 4),), jnp.float32),
        "ln1_gain": jnp.clip(1.0 + 0.18 * jax.random.normal(key_list[9], (D,), jnp.float32), 0.1, 1.9),
        "ln1_bias": bell_draw(key_list[10], (D,), 0.3, 2.0, ((0, 4),), jnp.float32),
        "w_up": bell_draw(key_list[11], (D, FF), D ** -0.5, 0.21875, ((0, 4), (1, 4))),
        "bias_up": bell_draw(key_list[12], (FF,), 0.5, 3.0, ((0, 4),), jnp.float32),
        "w_down": bell_draw(key_list[13], (D, FF), FF ** -0.5, 0.109375, ((0, 4), (1, 4))),
        "bias_down": bell_draw(key_list[14], (D,), 0.3, 2.0, ((0, 4),), jnp.float32),
        "ln2_gain": jnp.clip(1.0 + 0.18 * jax.random.normal(key_list[15], (D,), jnp.float32), 0.1, 1.9),
        "ln2_bias": bell_draw(key_list[16], (D,), 0.3, 2.0, ((0, 4),), jnp.float32),
    }


EPSILON = 1e-12
NEGATIVE = -1e+30

@jax.custom_vjp
def low(v):
    return lax.optimization_barrier(v.astype(jnp.bfloat16)).astype(jnp.float32)

@jax.custom_vjp
def low_back(v):
    return v

def low_keep(v):
    return (low(v), None)

def low_pass(kept, grad):
    return (grad,)

def back_keep(v):
    return (v, None)

def back_low(kept, grad):
    return (low(grad),)
low.defvjp(low_keep, low_pass)
low_back.defvjp(back_keep, back_low)

def round_both(value):
    return low_back(low(value))

def matmul_high(left_side, right_side):
    return jnp.dot(left_side, right_side, precision=lax.Precision.HIGHEST)

def layer_norm(summed, gain, shift):
    average = lax.optimization_barrier(jnp.mean(summed, axis=-1, keepdims=True))
    squares = lax.optimization_barrier(jnp.mean(summed * summed, axis=-1, keepdims=True))
    inverse = lax.rsqrt(squares - average * average + EPSILON)
    return (summed - average) * inverse * gain + shift

def encoder_layer(params, layer_in, row_ids):
    w_qkv, bias_qv, w_out, bias_out, gain_one, shift_one, w_up, bias_up, w_down, bias_down, gain_two, shift_two = params
    row_count = layer_in.shape[0]
    flat_qkv = jnp.transpose(w_qkv.reshape(HEADS, D, 3 * HEAD), (1, 0, 2)).reshape(D, HEADS * 3 * HEAD)
    projected = matmul_high(layer_in, flat_qkv).reshape(row_count, HEADS, 3 * HEAD)
    queries = round_both(projected[:, :, :HEAD] + bias_qv[:, :HEAD])
    key_rows = round_both(projected[:, :, HEAD:2 * HEAD])
    values = round_both(projected[:, :, 2 * HEAD:] + bias_qv[:, HEAD:])
    inv_root = 1.0 / math.sqrt(HEAD)
    scores = low_back(jnp.einsum('qhe,khe->hqk', queries, key_rows, precision=lax.Precision.HIGHEST) * inv_root)
    visible = row_ids[None, :] <= row_ids[:, None]
    masked = jnp.where(visible[None], scores, NEGATIVE)
    highest = lax.optimization_barrier(jnp.max(masked, axis=-1, keepdims=True))
    exponent = jnp.exp(masked - highest)
    attn_weights = low(exponent / lax.optimization_barrier(jnp.sum(exponent, axis=-1, keepdims=True)))
    mixed_out = jnp.einsum('hqk,khe->qhe', attn_weights, values, precision=lax.Precision.HIGHEST)
    mixed_out = round_both(mixed_out.reshape(row_count, D))
    attn_out = low_back(matmul_high(mixed_out, w_out) + bias_out)
    norm_one = layer_norm(layer_in + attn_out, gain_one, shift_one)
    gate_pre = low_back(matmul_high(low(norm_one), w_up) + bias_up)
    hidden = low(jax.nn.gelu(gate_pre, approximate=False))
    branch = low_back(matmul_high(hidden, jnp.transpose(w_down)) + bias_down)
    return layer_norm(norm_one + branch, gain_two, shift_two)

def reference(tokens, memory, block_ids, valid, teacher, w_qkv, bias_qv, w_out, bias_out, ln1_gain, ln1_bias, w_up, bias_up, w_down, bias_down, ln2_gain, ln2_bias):
    params = (w_qkv.astype(jnp.float32), bias_qv, w_out.astype(jnp.float32), bias_out, ln1_gain, ln1_bias, w_up.astype(jnp.float32), bias_up, w_down.astype(jnp.float32), bias_down, ln2_gain, ln2_bias)
    token_rows = jnp.swapaxes(tokens, 1, 2)
    teacher_rows = jnp.swapaxes(teacher, 1, 2)
    rows_in = jnp.concatenate([memory[:, :MEM], token_rows, memory[:, MEM:]], axis=1).astype(jnp.float32)
    loss_scale = SEQS * LEN / jnp.sum(valid).astype(jnp.float32)
    places = jnp.arange(LEN, dtype=jnp.int32)

    def seq_step(grad_total, packed):
        layer_in, token_ids, target, amount = packed
        row_ids = jnp.concatenate([jnp.full((MEM,), -1, jnp.int32), token_ids.astype(jnp.int32), jnp.full((MEM,), LEN, jnp.int32)])
        kept_rows = (places < amount)[:, None]

        def loss_fn(layer_params, layer_rows):
            output_rows = encoder_layer(layer_params, layer_rows, row_ids)
            mismatch = output_rows[MEM:MEM + LEN] - target.astype(jnp.float32)
            loss_sum = 0.5 * loss_scale * jnp.sum(jnp.where(kept_rows, mismatch * mismatch, 0.0))
            return (loss_sum, output_rows)
        loss_sum, pullback, output_rows = jax.vjp(loss_fn, params, layer_in, has_aux=True)
        grads, grad_rows = pullback(jnp.ones_like(loss_sum))
        grad_total = jax.tree.map(jnp.add, grad_total, grads)
        return (grad_total, (output_rows.astype(jnp.bfloat16), grad_rows))
    zeros_like = jax.tree.map(jnp.zeros_like, params)
    grad_total, (layer_out, grad_rows) = lax.scan(seq_step, zeros_like, (rows_in, block_ids, teacher_rows, valid))
    grad_tokens = grad_rows[:, MEM:MEM + LEN]
    grad_memory = jnp.concatenate([grad_rows[:, :MEM], grad_rows[:, MEM + LEN:]], axis=1)
    return (layer_out, grad_tokens, grad_memory, grad_total[0], grad_total[1], grad_total[2], grad_total[3], grad_total[4], grad_total[5], grad_total[6], grad_total[7], grad_total[8], grad_total[9], grad_total[10], grad_total[11])
```

```python
import jax
import jax.numpy as jnp
from jax import lax
from jax.experimental import pallas as pl
from jax.experimental.pallas import tpu as pltpu
from jax.sharding import PartitionSpec as P
BF=jnp.bfloat16; F32=jnp.float32
EPSILON=1e-12
CH=48

def nn(a,b): return lax.dot_general(a,b,(((1,),(0,)),((),())),preferred_element_type=F32)
def nt(a,b): return lax.dot_general(a,b,(((1,),(1,)),((),())),preferred_element_type=F32)

def gelu_pair(v):
    t = pl.reciprocal(1.0 + (0.3275911 * 0.7071067811865476) * jnp.abs(v))
    poly = t * (0.5*0.254829592 + t * (-0.5*0.284496736 + t * (0.5*1.421413741 + t * (-0.5*1.453152027 + t * (0.5*1.061405429)))))
    e = jnp.exp(-0.5 * v * v)
    half = poly * e
    cdf = jnp.where(v >= 0.0, 1.0 - half, half)
    return v * cdf, cdf + v * (e * 0.3989422804014327)

def group_sum(v):
    rows = v.shape[0]
    return jnp.sum(v.reshape(rows // 8, 8, v.shape[1]), axis=0)

def mlp_kernel(half_ref, valid_ref, mixed, x, teach, vec, bup, wa_hbm, wu_hbm, wd_hbm,
               out, g_one, g_attn, vgrad, bupgrad, gu_hbm, gd_hbm,
               tr, wraw, wt, wu, wd, h1, h2, rs1, low, lowt, brt, br, hid, dgl, gg, gu, gd, sem):
    rows, feats = x.shape
    zs = wu.shape[0]
    nb = feats // 256
    copies_a = [pltpu.make_async_copy(wa_hbm.at[z, :, pl.ds(512, 256)], wraw.at[z], sem.at[z]) for z in range(zs)]
    copies_u = [pltpu.make_async_copy(wu_hbm.at[z], wu.at[z], sem.at[zs + z]) for z in range(zs)]
    copies_d = [pltpu.make_async_copy(wd_hbm.at[z], wd.at[z], sem.at[2 * zs + z]) for z in range(zs)]
    for c in copies_a + copies_u + copies_d:
        c.start()
    for c in copies_a:
        c.wait()
    main = teach.shape[1]
    for i in range(main // 128):
        tr[pl.ds(128 * i, 128), :] = teach[:, pl.ds(128 * i, 128)].T
    tr[pl.ds(main, rows - main), :] = jnp.zeros((rows - main, feats), BF)
    low_lane = lax.broadcasted_iota(jnp.int32, (feats, 128), 1) < 64
    for k in range(zs // 2):
        z0, z1 = 2 * k, 2 * k + 1
        wt[:, pl.ds(384 * k, 128)] = wraw[z0, :, pl.ds(128, 128)]
        wt[:, pl.ds(384 * k + 128, 128)] = wraw[z1, :, pl.ds(128, 128)]
        t0 = pltpu.roll(wraw[z0, :, pl.ds(0, 128)].astype(F32), 64, 1)
        t1 = wraw[z1, :, pl.ds(0, 128)].astype(F32)
        wt[:, pl.ds(384 * k + 256, 128)] = jnp.where(low_lane, t0, t1).astype(BF)
    for n in range(nb):
        f = pl.ds(256 * n, 256)
        h1[:, f] = nt(mixed[...], wt[f, :]) + x[:, f].astype(F32) + vec[0:1, f]
    inv = 1.0 / feats

    vgrad[...] = jnp.zeros_like(vgrad)
    bupgrad[...] = jnp.zeros_like(bupgrad)

    def norm1(i, _):
        r = pl.ds(pl.multiple_of(i * CH, 16), CH)
        h = h1[r, :]
        m = jnp.sum(h, axis=1, keepdims=True) * inv
        s = jnp.sum(h * h, axis=1, keepdims=True) * inv
        rstd = lax.rsqrt(s - m * m + EPSILON)
        xhat = (h - m) * rstd
        h1[r, :] = xhat
        rs1[r, :] = jnp.broadcast_to(rstd, (CH, 128))
        low[r, :] = (xhat * vec[1:2, :] + vec[2:3, :]).astype(BF)
        return 0
    lax.fori_loop(0, rows // CH, norm1, 0)
    lowt[...] = low[...].T
    for c in copies_u:
        c.wait()

    def gate(i, _):
        z = i // nb
        f = pl.ds(pl.multiple_of((i % nb) * 256, 256), 256)
        v = nn(low[...], wu[z, :, f]) + bup[z, :, f]
        a, b = gelu_pair(v)
        hid[z, :, f] = a.astype(BF)
        dgl[z, :, f] = b
        return 0
    lax.fori_loop(0, zs * nb, gate, 0)
    for c in copies_d:
        c.wait()

    def down(n, _):
        f = pl.ds(pl.multiple_of(n * 256, 256), 256)
        acc = nt(hid[0], wd[0, f, :])
        for z in range(1, zs):
            acc = acc + nt(hid[z], wd[z, f, :])
        h2[:, f] = acc
        return 0
    lax.fori_loop(0, nb, down, 0)
    scale = vec[6:7, 0:1]
    first = half_ref[0] * main

    def norm2(i, _):
        r = pl.ds(pl.multiple_of(i * CH, 16), CH)
        h = h2[r, :] + (h1[r, :] * vec[1:2, :] + vec[2:3, :]) + vec[3:4, :]
        m = jnp.sum(h, axis=1, keepdims=True) * inv
        s = jnp.sum(h * h, axis=1, keepdims=True) * inv
        rstd = lax.rsqrt(s - m * m + EPSILON)
        xhat = (h - m) * rstd
        o = xhat * vec[4:5, :] + vec[5:6, :]
        out[r, :] = o.astype(BF)
        place = lax.broadcasted_iota(jnp.int32, (CH, 1), 0) + i * CH
        place = jnp.where(place < main, place + first, valid_ref[0])
        go = jnp.where(place < valid_ref[0], scale * (o - tr[r, :].astype(F32)), 0.0)
        a = go * vec[4:5, :]
        m1 = jnp.sum(a, axis=1, keepdims=True) * inv
        m2 = jnp.sum(a * xhat, axis=1, keepdims=True) * inv
        g2 = rstd * (a - m1 - xhat * m2)
        h2[r, :] = g2
        b = g2.astype(BF)
        br[r, :] = b
        vgrad[0] += group_sum(go * xhat)
        vgrad[1] += group_sum(go)
        vgrad[2] += group_sum(b.astype(F32))
        return 0
    lax.fori_loop(0, rows // CH, norm2, 0)
    brt[...] = br[...].T

    def back(i, _):
        z = i // nb
        f = pl.ds(pl.multiple_of((i % nb) * 256, 256), 256)
        gh = nn(br[...], wd[z, :, f])
        g = (gh * dgl[z, :, f]).astype(BF)
        gg[z, :, f] = g
        bupgrad[z, :, f] += group_sum(g.astype(F32))
        gd[z, :, f] = nn(brt[...], hid[z, :, f]).astype(BF)
        gu[z, :, f] = nn(lowt[...], g).astype(BF)
        return 0
    lax.fori_loop(0, zs * nb, back, 0)
    outs = [pltpu.make_async_copy(gd, gd_hbm, sem.at[0]), pltpu.make_async_copy(gu, gu_hbm, sem.at[1])]
    for c in outs:
        c.start()

    def first_grad(n, _):
        f = pl.ds(pl.multiple_of(n * 256, 256), 256)
        acc = h2[:, f]
        for z in range(zs):
            acc = acc + nt(gg[z], wu[z, f, :])
        h2[:, f] = acc
        return 0
    lax.fori_loop(0, nb, first_grad, 0)

    def norm1_back(i, _):
        r = pl.ds(pl.multiple_of(i * CH, 16), CH)
        g = h2[r, :]
        xhat = h1[r, :]
        a = g * vec[1:2, :]
        m1 = jnp.sum(a, axis=1, keepdims=True) * inv
        m2 = jnp.sum(a * xhat, axis=1, keepdims=True) * inv
        g1 = rs1[r, 0:1] * (a - m1 - xhat * m2)
        g_one[r, :] = g1
        b = g1.astype(BF)
        g_attn[r, :] = b
        vgrad[3] += group_sum(g * xhat)
        vgrad[4] += group_sum(g)
        vgrad[5] += group_sum(b.astype(F32))
        return 0
    lax.fori_loop(0, rows // CH, norm1_back, 0)
    for c in outs:
        c.wait()

def mlp(half, valid, mixed, x, teach, vec, bup, wa, wu, wd):
    rows, feats = x.shape; zs = wu.shape[0]
    V = lambda *s, d=BF: pltpu.VMEM(s, d)
    vm = pl.BlockSpec(memory_space=pltpu.VMEM); sm = pl.BlockSpec(memory_space=pltpu.SMEM); an = pl.BlockSpec(memory_space=pl.ANY)
    S = jax.ShapeDtypeStruct
    return pl.pallas_call(mlp_kernel,
        out_shape=(S((rows,feats),BF),S((rows,feats),F32),S((rows,feats),BF),S((6,8,feats),F32),S((zs,8,feats),F32),S(wu.shape,BF),S(wd.shape,BF)),
        in_specs=[sm,sm,vm,vm,vm,vm,vm,an,an,an],
        out_specs=(vm,vm,vm,vm,vm,an,an),
        scratch_shapes=[V(rows,feats),V(zs,feats,256),V(feats,feats),V(*wu.shape),V(*wd.shape),V(rows,feats,d=F32),V(rows,feats,d=F32),V(rows,128,d=F32),V(rows,feats),
            V(feats,rows),V(feats,rows),V(rows,feats),V(zs,rows,feats),V(zs,rows,feats,d=F32),V(zs,rows,feats),V(*wu.shape),V(*wd.shape),pltpu.SemaphoreType.DMA((3*zs,))],
        compiler_params=pltpu.CompilerParams(vmem_limit_bytes=63*2**20),
    )(half,valid,mixed,x,teach,vec,bup,wa,wu,wd)
NEG=-1e30
def tn_lanes(): return lax.broadcasted_iota(jnp.int32,(1,128),1)

def assemble_pairs(w, wp, feats):
    lo = lax.broadcasted_iota(jnp.int32, (feats, 128), 1) < 64
    wp[0] = w[0, :, pl.ds(0, 384)]
    wp[1] = w[1, :, pl.ds(0, 384)]
    a0, a1 = w[0, :, pl.ds(384, 128)].astype(F32), w[1, :, pl.ds(384, 128)].astype(F32)
    wp[2, :, pl.ds(0, 128)] = jnp.where(lo, a0, pltpu.roll(a1, 64, 1)).astype(BF)
    wp[2, :, pl.ds(128, 128)] = jnp.where(lo, pltpu.roll(a0, 64, 1), a1).astype(BF)
    b0, b1 = w[0, :, pl.ds(512, 128)].astype(F32), w[1, :, pl.ds(512, 128)].astype(F32)
    wp[2, :, pl.ds(256, 128)] = jnp.where(lo, b0, pltpu.roll(b1, 64, 1)).astype(BF)

def tiles(rows, length):
    mem = (length, rows - length, True)
    out = []
    for a in range(0, length, 256):
        spans = []
        if a:
            spans.append((0, a, False))
        spans.append((a, min(512, length - a), True))
        out.append((a, 256, spans + [mem]))
    out.append((length, rows - length, [(0, length, True), mem]))
    return out

def scores_of(kt, qm, idk, idq, p, spans):
    out = []
    for k0, kn, masked in spans:
        s = nt(kt[p, pl.ds(k0, kn), :], qm)
        if masked:
            s = jnp.where(idk[pl.ds(k0, kn), 0:1] <= idq, s, NEG)
        out.append(s)
    return out

def attn_fwd_kernel(xt, wa_hbm, bias, idk, idq, x, qt, kt, vt, mixed, lse, w, wp, vtt, ot, sem):
    feats = xt.shape[0]; rows = x.shape[0]; length = xt.shape[1] - 128
    c = pltpu.make_async_copy(wa_hbm, w, sem); c.start()
    for i in range(length // 128):
        x[pl.ds(128 * i, 128), :] = xt[:, pl.ds(128 * i, 128)].T
    x[pl.ds(length, rows - length), :] = xt[:, pl.ds(length, 128)].T[: rows - length, :]
    c.wait()
    assemble_pairs(w, wp, feats)
    rc = rows // 3

    def project(i, _):
        p = i // 3
        r = pl.ds(pl.multiple_of((i % 3) * rc, 16), rc)
        v = nn(x[r, :], wp[p]) + bias[p]
        qt[p, r, :] = (v[:, :128].astype(BF).astype(F32) * 0.125).astype(BF)
        kt[p, r, :] = v[:, 128:256].astype(BF)
        vt[p, r, :] = v[:, 256:].astype(BF)
        return 0
    lax.fori_loop(0, 9, project, 0)

    def pair(p, _):
        vtt[...] = vt[p].T
        for e in range(2):
            lanes = (tn_lanes() < 64) if e == 0 else (tn_lanes() >= 64)
            for q0, qn, spans in tiles(rows, length):
                q = qt[p, pl.ds(q0, qn), :]
                qm = jnp.where(lanes, q, jnp.zeros_like(q))
                ss = scores_of(kt, qm, idk, idq[0:1, pl.ds(q0, qn)], p, spans)
                m = jnp.max(ss[0], axis=0, keepdims=True)
                for s in ss[1:]:
                    m = jnp.maximum(m, jnp.max(s, axis=0, keepdims=True))
                tot, acc = None, None
                for s, (k0, kn, _) in zip(ss, spans):
                    ex = jnp.exp(s - m)
                    t = jnp.sum(ex, axis=0, keepdims=True)
                    o = nn(vtt[pl.ds(64 * e, 64), pl.ds(k0, kn)], ex.astype(BF))
                    tot = t if tot is None else tot + t
                    acc = o if acc is None else acc + o
                ot[pl.ds(64 * e, 64), pl.ds(q0, qn)] = acc / tot
                lse[p, e, :, pl.ds(q0, qn)] = m + jnp.log(tot)
        mixed[p] = ot[...].T.astype(BF)
        return 0
    lax.fori_loop(0, 3, pair, 0)

def attn_fwd(xt, wa, bias, idk, idq, rows):
    feats = xt.shape[0]
    V = lambda *s, d=BF: pltpu.VMEM(s, d)
    vm = pl.BlockSpec(memory_space=pltpu.VMEM); an = pl.BlockSpec(memory_space=pl.ANY)
    S = jax.ShapeDtypeStruct
    t3 = S((3, rows, 128), BF)
    return pl.pallas_call(attn_fwd_kernel,
        out_shape=(S((rows, feats), BF), t3, t3, t3, t3, S((3, 2, 1, rows), F32)),
        in_specs=[vm, an, vm, vm, vm], out_specs=(vm,) * 6,
        scratch_shapes=[V(*wa.shape), V(3, feats, 384), V(128, rows), V(128, rows, d=F32), pltpu.SemaphoreType.DMA],
        compiler_params=pltpu.CompilerParams(vmem_limit_bytes=63*2**20))(xt, wa, bias, idk, idq)

def attn_bwd_kernel(ga, mixed, xt, qt, kt, vt, lse, idk, idq, wa_hbm, gpart, bgrad, gown_hbm, w, wp, wt, gat, gm, gp, dv, dk, dqt, ktt, dd, ro, gown, sem):
    feats = xt.shape[0]; rows = ga.shape[0]; length = xt.shape[1] - 128
    c = pltpu.make_async_copy(wa_hbm, w, sem); c.start()
    gat[...] = ga[...].T
    c.wait()
    assemble_pairs(w, wp, feats)
    wt[:, pl.ds(0, 128)] = w[0, :, pl.ds(640, 128)]
    wt[:, pl.ds(128, 128)] = w[1, :, pl.ds(640, 128)]
    lo = lax.broadcasted_iota(jnp.int32, (feats, 128), 1) < 64
    wt[:, pl.ds(256, 128)] = jnp.where(lo, pltpu.roll(w[0, :, pl.ds(512, 128)].astype(F32), 64, 1), w[1, :, pl.ds(512, 128)].astype(F32)).astype(BF)
    for p in range(3):
        gm[p] = nn(ga[...], wt[:, pl.ds(128 * p, 128)]).astype(BF)

    def pair(p, _):
        ktt[...] = kt[p].T
        prod = (gm[p].astype(F32) * mixed[p].astype(F32)).T
        dd[0:1, :] = jnp.sum(prod[:64, :], axis=0, keepdims=True)
        dd[1:2, :] = jnp.sum(prod[64:, :], axis=0, keepdims=True)
        dv[...] = jnp.zeros_like(dv)
        dk[...] = jnp.zeros_like(dk)
        for e in range(2):
            lanes = (tn_lanes() < 64) if e == 0 else (tn_lanes() >= 64)
            for q0, qn, spans in tiles(rows, length):
                q = qt[p, pl.ds(q0, qn), :]
                qm = jnp.where(lanes, q, jnp.zeros_like(q))
                g = gm[p, pl.ds(q0, qn), :]
                gmm = jnp.where(lanes, g, jnp.zeros_like(g))
                ss = scores_of(kt, qm, idk, idq[0:1, pl.ds(q0, qn)], p, spans)
                l = lse[p, e, :, pl.ds(q0, qn)]
                d = dd[pl.ds(e, 1), pl.ds(q0, qn)]
                acc = None
                for s, (k0, kn, _) in zip(ss, spans):
                    pr = jnp.exp(s - l)
                    dp = nt(vt[p, pl.ds(k0, kn), :], gmm)
                    ds = (pr * (dp - d)).astype(BF)
                    dv[pl.ds(k0, kn), :] += nn(pr.astype(BF), gmm)
                    dk[pl.ds(k0, kn), :] += nn(ds, qm)
                    o = nn(ktt[pl.ds(64 * e, 64), pl.ds(k0, kn)], ds)
                    acc = o if acc is None else acc + o
                dqt[pl.ds(64 * e, 64), pl.ds(q0, qn)] = acc * 0.125
        gp[p, :, pl.ds(0, 128)] = dqt[...].T.astype(BF)
        gp[p, :, pl.ds(128, 128)] = dk[...].astype(BF)
        gp[p, :, pl.ds(256, 128)] = dv[...].astype(BF)
        return 0
    lax.fori_loop(0, 3, pair, 0)
    for p in range(3):
        bgrad[p] = group_sum(gp[p].astype(F32))
    r3 = rows // 3

    def rowsgrad(i, _):
        r = pl.ds(pl.multiple_of(i * r3, 16), r3)
        gpart[r, :] = nt(gp[0, r, :], wp[0]) + nt(gp[1, r, :], wp[1]) + nt(gp[2, r, :], wp[2])
        return 0
    lax.fori_loop(0, 3, rowsgrad, 0)
    fc = 256
    for f0 in range(0, feats, fc):
        f = pl.ds(f0, fc)
        xf = xt[f, pl.ds(0, rows)]
        af = gat[f, :]
        r0 = nn(xf, gp[0]); r1 = nn(xf, gp[1]); r2 = nn(xf, gp[2])
        o = [nn(af, mixed[p]) for p in range(3)]
        lo = lax.broadcasted_iota(jnp.int32, (fc, 128), 1) < 64
        rq, rk, rv = r2[:, :128], r2[:, 128:256], r2[:, 256:]
        sw = lambda a: pltpu.roll(a, 64, 1)
        gown[0, f, pl.ds(0, 384)] = r0.astype(BF)
        gown[1, f, pl.ds(0, 384)] = r1.astype(BF)
        gown[0, f, pl.ds(384, 128)] = jnp.where(lo, rq, sw(rk)).astype(BF)
        gown[1, f, pl.ds(384, 128)] = jnp.where(lo, sw(rq), rk).astype(BF)
        gown[0, f, pl.ds(512, 128)] = jnp.where(lo, rv, sw(o[2])).astype(BF)
        gown[1, f, pl.ds(512, 128)] = jnp.where(lo, sw(rv), o[2]).astype(BF)
        gown[0, f, pl.ds(640, 128)] = o[0].astype(BF)
        gown[1, f, pl.ds(640, 128)] = o[1].astype(BF)
    c = pltpu.make_async_copy(gown, gown_hbm, sem); c.start(); c.wait()

def attn_bwd(ga, mixed, xt, qt, kt, vt, lse, idk, idq, wa):
    feats = xt.shape[0]; rows = ga.shape[0]
    V = lambda *s, d=BF: pltpu.VMEM(s, d)
    vm = pl.BlockSpec(memory_space=pltpu.VMEM); an = pl.BlockSpec(memory_space=pl.ANY)
    S = jax.ShapeDtypeStruct
    return pl.pallas_call(attn_bwd_kernel,
        out_shape=(S((rows, feats), F32), S((3, 8, 384), F32), S(wa.shape, BF)),
        in_specs=[vm] * 9 + [an], out_specs=(vm, vm, an),
        scratch_shapes=[V(*wa.shape), V(3, feats, 384), V(feats, 384), V(feats, rows), V(3, rows, 128), V(3, rows, 384), V(rows, 128, d=F32), V(rows, 128, d=F32),
            V(128, rows, d=F32), V(128, rows), V(8, rows, d=F32), V(8, 128), V(*wa.shape), pltpu.SemaphoreType.DMA],
        compiler_params=pltpu.CompilerParams(vmem_limit_bytes=63*2**20))(ga, mixed, xt, qt, kt, vt, lse, idk, idq, wa)
MESH = pl.DeviceIdType.MESH

class Net:
    def __init__(self, send_sems, recv_sems, local_sems):
        self.ss, self.rs, self.ls = send_sems, recv_sems, local_sems
        self.count, self.locals, self.sent = 0, 0, []
        self.d, self.z, self.c = (lax.axis_index(a) for a in ("dp", "row", "col"))
        self.nd, self.nz = lax.axis_size("dp"), lax.axis_size("row")
        self.y, self.k = self.c // 2, self.c % 2
        self.x = self.d % 2
        self.xp = (self.d + 1 - 2 * self.x, self.z, self.c)
        self.yp = (self.d, self.z, lax.rem(self.c + 2, 4))
        self.kp = (self.d, self.z, self.c + 1 - 2 * self.k)
        self.ykp = (self.d, self.z, 3 - self.c)
        self.zs = [lax.rem(self.z + i, self.nz) for i in range(self.nz)]
        self.zp = [(self.d, zz, self.c) for zz in self.zs]
        self.others = [(lax.rem(self.d + 2 * i, self.nd), self.z, self.c) for i in range(1, self.nd // 2)]

    def barrier(self, peers):
        b = pltpu.get_barrier_semaphore()
        for p in peers:
            pl.semaphore_signal(b, inc=1, device_id=p, device_id_type=MESH)
        pl.semaphore_wait(b, len(peers))

    def send(self, src, dst, dev):
        i = self.count
        self.count += 1
        c = pltpu.make_async_remote_copy(src_ref=src, dst_ref=dst, send_sem=self.ss.at[i], recv_sem=self.rs.at[i], device_id=dev, device_id_type=MESH)
        c.start()
        self.sent.append(c)
        return c

    def local(self, src, dst):
        c = pltpu.make_async_copy(src, dst, self.ls.at[self.locals])
        self.locals += 1
        c.start()
        return c

    def finish(self):
        for c in self.sent:
            c.wait_send()

def gather_kernel(tok, mem, tch, la, lu, ld, ls, xt, tt, wa, wu, wd, sm, ss, rs, lsem):
    n = Net(ss, rs, lsem)
    n.barrier(n.zp[1:] + [n.yp, n.ykp, n.kp, n.xp])
    nz, y, k, c, z = n.nz, n.y, n.k, n.c, n.z
    b = la.shape[0]; hb = b // 2
    length = tok.shape[2]
    oc = lax.rem(c + 2, 4)
    half = n.x * hb
    row = lambda cc, off=0, num=b: pl.ds(pl.multiple_of(cc * b + off, 16), num)
    seq = lambda r: r

    def blk(w, zz, cc):
        return w.at[zz, row(cc)]
    def hlf(w, zz, cc, h):
        return w.at[zz, row(cc, h * hb, hb)]
    mine, theirs = n.x, 1 - n.x
    local = [n.local(tok.at[y], xt.at[row(c), pl.ds(0, length)]), n.local(mem.at[y], xt.at[row(c), pl.ds(length, 128)])]
    t_y = n.send(tok.at[1 - y], xt.at[row(c), pl.ds(0, length)], n.yp)
    m_y = n.send(mem.at[1 - y], xt.at[row(c), pl.ds(length, 128)], n.yp)
    s_z = [n.send(ls, sm.at[z, c], n.zp[i]) for i in range(1, nz)]
    s_y = [n.send(ls, sm.at[z, c], n.yp)]
    s_k = [n.send(ls, sm.at[z, c], n.kp)]
    ha = la.at[pl.ds(pl.multiple_of(half, 16), hb)]
    hu = lu.at[pl.ds(pl.multiple_of(half, 16), hb)]
    a_z = [n.send(ha, hlf(wa, z, c, mine), n.zp[i]) for i in range(1, nz)]
    a_y = [n.send(ha, hlf(wa, z, c, mine), n.yp)]
    t_k = [n.send(tok.at[y], xt.at[row(c), pl.ds(0, length)], n.kp), n.send(mem.at[y], xt.at[row(c), pl.ds(length, 128)], n.kp)]
    a_k = [n.send(la, blk(wa, z, c), n.kp)]
    for w, l in ((wa, la), (wu, lu), (wd, ld)):
        local.append(n.local(l, blk(w, z, c)))
    local.append(n.local(ls, sm.at[z, c]))
    a_x = []
    zz = lambda i: n.zs[(nz - i) % nz]
    def fwd(src, dst_list):
        return [n.send(src, src, d) for d in dst_list]
    for i in range(1, nz):
        a_z[i - 1].wait_recv()
        u = hlf(wa, zz(i), c, mine)
        a_y.append(n.send(u, u, n.yp)); a_x.append(n.send(u, u, n.xp)); a_k.append(n.send(u, u, n.kp))
        s_z[i - 1].wait_recv()
        u = sm.at[zz(i), c]
        s_y.append(n.send(u, u, n.yp)); s_k.append(n.send(u, u, n.kp))
    u_y = n.send(hu, hlf(wu, z, c, mine), n.yp)
    u_z = [n.send(hu, hlf(wu, z, c, mine), n.zp[i]) for i in range(1, nz)]
    u_k = [n.send(lu, blk(wu, z, c), n.kp)]
    d_z = [n.send(ld, blk(wd, z, c), n.zp[i]) for i in range(1, nz)]
    d_y = [n.send(ld, blk(wd, z, c), n.yp)]
    d_k = [n.send(ld, blk(wd, z, c), n.kp)]
    hw = length // 2
    tsl = lambda s, kk: tch.at[s, :, pl.ds(pl.multiple_of(kk * hw, 128), hw)]
    h_y = [n.send(tsl(1 - y, k), tt.at[row(c)], n.yp), n.send(tsl(1 - y, 1 - k), tt.at[row(c)], n.ykp), n.send(tsl(y, 1 - k), tt.at[row(c)], n.kp)]
    local.append(n.local(tsl(y, k), tt.at[row(c)]))
    t_y.wait_recv(); m_y.wait_recv()
    for w_ in (pl.ds(0, length), pl.ds(length, 128)):
        u = xt.at[row(oc), w_]
        t_k.append(n.send(u, u, n.kp))
    for i in range(nz):
        a_y[i].wait_recv()
        u = hlf(wa, zz(i), oc, mine)
        a_x.append(n.send(u, u, n.xp)); a_k.append(n.send(u, u, n.kp))
        s_y[i].wait_recv()
        u = sm.at[zz(i), oc]
        s_k.append(n.send(u, u, n.kp))
    u_x = []
    u_y.wait_recv()
    u = hlf(wu, z, oc, mine)
    u_z2 = [n.send(u, u, n.zp[i]) for i in range(1, nz)]
    u_x.append(n.send(u, u, n.xp)); u_k.append(n.send(u, u, n.kp))
    order = [(i, c) for i in range(1, nz)] + [(i, oc) for i in range(nz)]
    for cp, (i, cc) in zip(a_x, order):
        cp.wait_recv()
        u = hlf(wa, zz(i), cc, theirs)
        a_k.append(n.send(u, u, n.kp))
    for i in range(1, nz):
        u_z[i - 1].wait_recv()
        u = hlf(wu, zz(i), c, mine)
        u_x.append(n.send(u, u, n.xp)); u_k.append(n.send(u, u, n.kp))
    for i in range(1, nz):
        d_z[i - 1].wait_recv()
        u = blk(wd, zz(i), c)
        d_y.append(n.send(u, u, n.yp)); d_k.append(n.send(u, u, n.kp))
    for i in range(1, nz):
        u_z2[i - 1].wait_recv()
        u = hlf(wu, zz(i), oc, mine)
        u_x.append(n.send(u, u, n.xp)); u_k.append(n.send(u, u, n.kp))
    for i in range(nz):
        d_y[i].wait_recv()
        u = blk(wd, zz(i), oc)
        d_k.append(n.send(u, u, n.kp))
    order = [(0, oc)] + [(i, c) for i in range(1, nz)] + [(i, oc) for i in range(1, nz)]
    for cp, (i, cc) in zip(u_x, order):
        cp.wait_recv()
        u = hlf(wu, zz(i), cc, theirs)
        u_k.append(n.send(u, u, n.kp))
    for cp in h_y + t_k + a_k + s_k + u_k + d_k:
        cp.wait_recv()
    for cp in local:
        cp.wait()
    n.finish()

def gather(tok, mem, tch, la, lu, ld, ls, nz):
    b, width = lu.shape
    feats = 4 * b; length = tok.shape[2]
    vm = pl.BlockSpec(memory_space=pltpu.VMEM); an = pl.BlockSpec(memory_space=pl.ANY)
    S = jax.ShapeDtypeStruct
    w = S((nz, feats, width), BF)
    return pl.pallas_call(gather_kernel,
        out_shape=(S((feats, length + 128), BF), S((feats, length // 2), BF), w, w, w, S((nz, 4) + ls.shape, F32)),
        in_specs=[vm] * 7, out_specs=(an,) * 6,
        scratch_shapes=[pltpu.SemaphoreType.DMA((128,)), pltpu.SemaphoreType.DMA((128,)), pltpu.SemaphoreType.DMA((16,))],
        compiler_params=pltpu.CompilerParams(collective_id=1, has_side_effects=True, vmem_limit_bytes=40*2**20))(tok, mem, tch, la, lu, ld, ls)

def add_to(dst, src):
    dst[...] = (dst[...].astype(F32) + src[...].astype(F32)).astype(BF)

def sum_refs(refs):
    acc = refs[0][...].astype(F32)
    for r in refs[1:]:
        acc = acc + r[...].astype(F32)
    return acc

def reduce_kernel(gu, gd, ga, lo, gpart, g1, sv, out4, grad4, fa, fu, fd, svo,
                  hu, hd, ha, ru, rd, ux, ax, uz, uy, ut, dy, dz, dx, df, ay, az, o4, g4, gs, gr, svk, svy, svx, svz, svt, ss, rs, lsem):
    n = Net(ss, rs, lsem)
    n.barrier(n.zp[1:] + [n.yp, n.ykp, n.kp, n.xp] + n.others)
    nz, y, k, c, z, x = n.nz, n.y, n.k, n.c, n.z, n.x
    b = fu.shape[0]; hb = b // 2
    feats = gu.shape[1]
    row = lambda cc: pl.ds(pl.multiple_of(cc * b, 16), b)
    mine = pl.ds(pl.multiple_of(x * hb, 16), hb)
    theirs = pl.ds(pl.multiple_of((1 - x) * hb, 16), hb)
    d_k = [n.send(gd.at[:, row(2 * yy + 1 - k)], rd.at[yy], n.kp) for yy in range(2)]
    u_k = [n.send(gu.at[:, row(2 * yy + 1 - k)], ru.at[yy], n.kp) for yy in range(2)]
    l_d = [n.local(gd.at[:, row(2 * yy + k)], hd.at[yy]) for yy in range(2)]
    l_u = [n.local(gu.at[:, row(2 * yy + k)], hu.at[yy]) for yy in range(2)]
    oz = pl.ds(2 * k, 2)
    a_k = [n.send(ga.at[:, row(2 * yy + 1 - k)], ha.at[yy, oz], n.kp) for yy in range(2)]
    l_a = [n.local(ga.at[:, row(2 * yy + k)], ha.at[yy, oz]) for yy in range(2)]
    s_k = n.send(sv, svk, n.kp)
    rows = lo.shape[0]; main = rows - 16
    gs[pl.ds(0, main), :] = gpart[pl.ds(pl.multiple_of((1 - k) * main, 16), main), :].astype(BF)
    gs[pl.ds(main, 16), :] = gpart[pl.ds(pl.multiple_of(2 * main + (1 - k) * 16, 16), 16), :].astype(BF)
    g_k = n.send(gs, gr, n.kp)

    def split(get, dst):
        def step(i, _):
            r = pl.ds(pl.multiple_of(i * CH, 16), CH)
            v = get(r)
            for cc in range(4):
                dst[cc, r, :] = v[:, cc * b:(cc + 1) * b].astype(BF)
            return 0
        lax.fori_loop(0, rows // CH, step, 0)
    def spread(src, dst):
        l = n.local(src.at[c], dst.at[y, k])
        return l, [n.send(src.at[lax.rem(c + 2, 4)], dst.at[y, k], n.yp), n.send(src.at[3 - c], dst.at[y, k], n.ykp), n.send(src.at[c + 1 - 2 * k], dst.at[y, k], n.kp)]

    for cp in d_k:
        cp.wait_recv()
    for cp in l_d:
        cp.wait()
    zz = lambda i: n.zs[(nz - i) % nz]
    d_y = []
    for i in list(range(1, nz)) + [0]:
        add_to(hd.at[1 - y, n.zs[i]], rd.at[1 - y, n.zs[i]])
        d_y.append(n.send(hd.at[1 - y, n.zs[i]], dy.at[n.zs[i]], n.yp))
    for i in range(nz):
        add_to(hd.at[y, i], rd.at[y, i])
    for cp in u_k:
        cp.wait_recv()
    for cp in l_u:
        cp.wait()
    u_x = []
    for i in list(range(1, nz)) + [0]:
        for yy in range(2):
            add_to(hu.at[yy, n.zs[i]], ru.at[yy, n.zs[i]])
            u_x.append(n.send(hu.at[yy, n.zs[i], theirs], ux.at[yy, n.zs[i]], n.xp))
    l_o = []
    split(lambda r: lo[r, :].astype(F32), o4)
    l, o_s = spread(o4, out4)
    l_o.append(l)
    g_k.wait_recv()

    def total(r):
        return gr[r, :].astype(F32) + g1[r, :]
    def own(i, _):
        r = pl.ds(pl.multiple_of(i * 16, 16), 16)
        src = jnp.where(i < main // 16, k * main + i * 16, 2 * main + k * 16)
        v = gpart[pl.ds(pl.multiple_of(src, 16), 16), :] + gr[r, :].astype(F32) + g1[r, :]
        for cc in range(4):
            g4[cc, r, :] = v[:, cc * b:(cc + 1) * b].astype(BF)
        return 0
    lax.fori_loop(0, rows // 16, own, 0)
    l, g_s = spread(g4, grad4)
    l_o.append(l)
    for cp in a_k:
        cp.wait_recv()
    for cp in l_a:
        cp.wait()
    a_x = []
    for yy in (0, 1):
        for i in list(range(1, nz)) + [0]:
            yv = 1 - y if yy == 0 else y
            a_x.append(n.send(ha.at[yv, n.zs[i], theirs], ax.at[yv, n.zs[i]], n.xp))
    s_k.wait_recv()
    svt[...] = sv[...] + svk[...]
    s_y = n.send(svt, svy, n.yp)
    d_z = []
    for j, i in enumerate(list(range(1, nz)) + [0]):
        d_y[j].wait_recv()
        add_to(hd.at[y, n.zs[i]], dy.at[n.zs[i]])
        if i:
            d_z.append(n.send(hd.at[y, n.zs[i]], dz.at[i], n.zp[i]))
    s_y.wait_recv()
    svo[...] = svt[...] + svy[...]
    s_x = n.send(svo, svx, n.xp)
    u_z = []
    for j, i in enumerate(list(range(1, nz)) + [0]):
        for yy in range(2):
            u_x[2 * j + yy].wait_recv()
            add_to(hu.at[yy, n.zs[i], mine], ux.at[yy, n.zs[i]])
            if i:
                u_z.append(n.send(hu.at[yy, n.zs[i], mine], uz.at[i, yy], n.zp[i]))
    a_y = []
    for j, i in enumerate(list(range(1, nz)) + [0]):
        a_x[j].wait_recv()
        add_to(ha.at[1 - y, n.zs[i], mine], ax.at[1 - y, n.zs[i]])
        a_y.append(n.send(ha.at[1 - y, n.zs[i], mine], ay.at[n.zs[i]], n.yp))
    for j, i in enumerate(list(range(1, nz)) + [0]):
        a_x[nz + j].wait_recv()
        add_to(ha.at[y, n.zs[i], mine], ax.at[y, n.zs[i]])
    for cp in d_z:
        cp.wait_recv()
    df[...] = sum_refs([hd.at[y, z]] + [dz.at[i] for i in range(1, nz)]).astype(BF)
    me = n.d
    d_d = [n.send(df, dx.at[n.d], (lax.rem(n.d + i, n.nd), n.z, n.c)) for i in range(1, n.nd)]
    l_f = n.local(df, dx.at[n.d])
    s_x.wait_recv()
    svt2 = svo[...] + svx[...]
    svz[z] = svt2
    s_z = [n.send(svz.at[z], svz.at[z], n.zp[i]) for i in range(1, nz)]
    for cp in u_z:
        cp.wait_recv()
    for yy in range(2):
        ut[yy] = sum_refs([hu.at[yy, z, mine]] + [uz.at[i, yy] for i in range(1, nz)]).astype(BF)
    u_y = n.send(ut.at[1 - y], uy, n.yp)
    a_z = []
    for j, i in enumerate(list(range(1, nz)) + [0]):
        a_y[j].wait_recv()
        add_to(ha.at[y, n.zs[i], mine], ay.at[n.zs[i]])
        if i:
            a_z.append(n.send(ha.at[y, n.zs[i], mine], az.at[i], n.zp[i]))
    u_y.wait_recv()
    fu[mine, :] = sum_refs([ut.at[y], uy]).astype(BF)
    u_f = n.send(fu.at[mine], fu.at[mine], n.xp)
    for cp in a_z:
        cp.wait_recv()
    fa[mine, :] = sum_refs([ha.at[y, z, mine]] + [az.at[i] for i in range(1, nz)]).astype(BF)
    a_f = n.send(fa.at[mine], fa.at[mine], n.xp)
    l_f.wait()
    for cp in d_d + s_z:
        cp.wait_recv()
    fd[...] = sum_refs([dx.at[i] for i in range(n.nd)])
    acc = svz[0]
    for i in range(1, nz):
        acc = acc + svz[i]
    n.finish()
    svo[...] = acc
    for cp in o_s + g_s + [u_f, a_f]:
        cp.wait_recv()
    for cp in l_o:
        cp.wait()

def reduce(gu, gd, ga, lo, gpart, g1, sv, nz, nd):
    feats, width = gu.shape[1:]
    b = feats // 4; hb = b // 2; rows = lo.shape[0]
    V = lambda *s, d=BF: pltpu.VMEM(s, d)
    vm = pl.BlockSpec(memory_space=pltpu.VMEM); an = pl.BlockSpec(memory_space=pl.ANY)
    S = jax.ShapeDtypeStruct
    o = S((2, 2, rows, b), BF)
    w = S((b, width), BF)
    sm = lambda: V(*sv.shape, d=F32)
    return pl.pallas_call(reduce_kernel,
        out_shape=(o, o, w, w, S((b, width), F32), S(sv.shape, F32)),
        in_specs=[an, an, an, vm, vm, vm, vm], out_specs=(vm,) * 6,
        scratch_shapes=[V(2, nz, b, width)] * 5 + [V(2, nz, hb, width)] * 2 + [V(nz, 2, hb, width), V(hb, width), V(2, hb, width),
            V(nz, b, width), V(nz, b, width), V(nd, b, width), V(b, width), V(nz, hb, width), V(nz, hb, width),
            V(4, rows, b), V(4, rows, b), V(rows, feats), V(rows, feats), sm(), sm(), sm(), V(nz, *sv.shape, d=F32), sm(),
            pltpu.SemaphoreType.DMA((96 + nd,)), pltpu.SemaphoreType.DMA((96 + nd,)), pltpu.SemaphoreType.DMA((16,))],
        compiler_params=pltpu.CompilerParams(collective_id=2, has_side_effects=True, vmem_limit_bytes=63*2**20))(gu, gd, ga, lo, gpart, g1, sv)

def per_device(tokens, memory, block_ids, valid, teacher, w_qkv, bias_qv, w_out, bias_out, ln1_gain, ln1_bias, w_up, bias_up, w_down, bias_down, ln2_gain, ln2_bias):
    _, b, length = tokens.shape
    nd, nz = lax.axis_size("dp"), lax.axis_size("row")
    d, z, c = (lax.axis_index(a) for a in ("dp", "row", "col"))
    y, k = c // 2, c % 2
    feats = 4 * b
    half = memory.shape[1] // 2
    main = length // 2
    rows = length + 32
    wq = w_qkv.reshape(3, b, 192)
    wo = jnp.transpose(w_out)
    la = jnp.concatenate([wq[0, :, :64], wq[1, :, :64], wq[0, :, 64:128], wq[1, :, 64:128], wq[0, :, 128:], wq[1, :, 128:], wq[2], wo[:, 128:], wo[:, :128]], axis=1)
    mem = jnp.pad(jnp.swapaxes(memory, 1, 2), ((0, 0), (0, 0), (0, 128 - 2 * half)))
    ls = jnp.concatenate([jnp.concatenate([bias_out, ln1_gain, ln1_bias, bias_down, ln2_gain, ln2_bias, bias_up]).reshape(-1, 128), bias_qv, jnp.zeros((6, 128), F32)])
    xt, tt, wa, wu, wd, sm = gather(tokens, mem, teacher, la, w_up, w_down, ls, nz)
    fv = 6 * b // 128
    vecs = jnp.swapaxes(sm[0, :, :fv].reshape(4, 6, b), 0, 1).reshape(6, feats)
    scale = (valid.shape[0] * length) / jnp.sum(valid).astype(F32)
    vec = jnp.concatenate([vecs, jnp.full((2, feats), scale, F32)])
    bup = sm[:, 0, fv:fv + 6].reshape(nz, 1, 6 * 128)
    bq = lax.dynamic_slice_in_dim(sm[:, 0, fv + 6:fv + 9], 2 * k, 2, 0)
    zero = jnp.zeros((128,), F32)
    def pair_bias(h0, h1):
        return jnp.concatenate([h0[:64], h1[:64], zero, h0[64:], h1[64:]])
    bias = jnp.stack([pair_bias(bq[0, 0], bq[0, 1]), pair_bias(bq[1, 0], bq[1, 1]), pair_bias(bq[0, 2], bq[1, 2])])[:, None]
    ids = lax.dynamic_index_in_dim(block_ids, y, 0, keepdims=False)
    ids = jnp.concatenate([ids, jnp.full((half,), -1, jnp.int32), jnp.full((half,), length, jnp.int32), jnp.full((32 - 2 * half,), 2 * length, jnp.int32)])
    idk = jnp.broadcast_to(ids[:, None], (rows, 128))
    wown = lax.dynamic_slice_in_dim(wa, 2 * k, 2, 0)
    x, qt, kt, vt, mixed, lse = attn_fwd(xt, wown, bias, idk, ids[None], rows)
    def rows_of(a, kk, axis=0):
        return jnp.concatenate([lax.dynamic_slice_in_dim(a, kk * main, main, axis), lax.dynamic_slice_in_dim(a, length + kk * 16, 16, axis)], axis)
    swap = [(0, 1), (1, 0), (2, 3), (3, 2)]
    got = lax.ppermute(rows_of(mixed, 1 - k, 1), "col", swap)
    own = rows_of(mixed, k, 1)
    first = jnp.where(k == 0, own, got)
    second = jnp.where(k == 0, got, own)
    mixed_rows = jnp.concatenate([first[0], first[1], first[2], second[0], second[1], second[2]], axis=1)
    count = lax.dynamic_index_in_dim(valid, (d * nz + z) * 2 + y, 0)
    out, g_one, g_attn, vgrad, bupgrad, gu, gd = mlp(k[None], count, mixed_rows, rows_of(x, k), tt, vec, bup, wa, wu, wd)
    other = lax.ppermute(g_attn, "col", swap)
    first = jnp.where(k == 0, g_attn, other)
    second = jnp.where(k == 0, other, g_attn)
    ga = jnp.concatenate([first[:main], second[:main], first[main:], second[main:]])
    gpart, bgrad, gown = attn_bwd(ga, mixed, xt, qt, kt, vt, lse, idk, ids[None], wown)
    bg = jnp.sum(bgrad, axis=1)[None]
    bg = jnp.where((jnp.arange(2) == k)[:, None, None], bg, 0.0).reshape(3, feats)
    sv = jnp.concatenate([jnp.sum(vgrad, axis=1), jnp.sum(bupgrad, axis=1), bg, jnp.zeros((3, feats), F32)])
    out4, grad4, fa, fu, fd, sv = reduce(gu, gd, gown, out, gpart, g_one, sv, nz, nd)
    layer_out = jnp.concatenate([out4[:, 0, main:main + half], out4[:, 0, :main], out4[:, 1, :main], out4[:, 0, main + half:], out4[:, 1, main:main + 2 * half - 16]], axis=1)
    grad_tokens = grad4[:, :, :main].reshape(2, length, b).astype(F32)
    grad_memory = jnp.concatenate([grad4[:, 0, main:], grad4[:, 1, main:main + 2 * half - 16]], axis=1).astype(F32)
    fa = fa.astype(F32)
    g0 = jnp.concatenate([fa[:, 0:64], fa[:, 128:192], fa[:, 256:320]], axis=1)
    g1 = jnp.concatenate([fa[:, 64:128], fa[:, 192:256], fa[:, 320:384]], axis=1)
    grad_w_qkv = jnp.stack([g0, g1, fa[:, 384:576]]).reshape(3, b * 192)
    grad_w_out = jnp.transpose(jnp.concatenate([fa[:, 640:768], fa[:, 576:640]], axis=1))
    hb = sv[10:13].reshape(2, 3, 384)
    hb = lax.dynamic_index_in_dim(hb, z // 2, 0, keepdims=False)
    zl = z % 2
    two = lax.dynamic_index_in_dim(hb, zl, 0, keepdims=False)
    last = hb[2]
    pick = lambda r, e: jnp.concatenate([r[64 * e:64 * e + 64], r[256 + 64 * e:320 + 64 * e]])
    grad_bias_qv = jnp.stack([pick(two, 0), pick(two, 1), jnp.where(zl == 0, pick(last, 0), pick(last, 1))])
    fvec = lax.dynamic_slice_in_dim(sv[:6], c * b, b, 1)
    grad_bias_up = lax.dynamic_index_in_dim(sv[6:10], z, 0, keepdims=False)
    return (layer_out, grad_tokens, grad_memory, grad_w_qkv, grad_bias_qv, grad_w_out, fvec[5], fvec[3], fvec[4], fu.astype(F32), grad_bias_up, fd, fvec[2], fvec[0], fvec[1])

def solution(mesh):
    rows, feat = ("dp", "row"), "col"
    in_specs = (P(rows, feat, None), P(rows, None, feat), P(rows, None), P(), P(rows, feat, None), P("row", feat), P("row", None), P("row", feat), P(feat), P(feat), P(feat), P(feat, "row"), P("row"), P(feat, "row"), P(feat), P(feat), P(feat))
    out_specs = (P(rows, None, feat), P(rows, None, feat), P(rows, None, feat), P("row", feat), P("row", None), P("row", feat), P(feat), P(feat), P(feat), P(feat, "row"), P("row"), P(feat, "row"), P(feat), P(feat), P(feat))
    return jax.shard_map(per_device, mesh=mesh, in_specs=in_specs, out_specs=out_specs, check_vma=False)
```

```python
import jax
import jax.numpy as jnp
from jax import lax
from jax.experimental import pallas as pl
from jax.experimental.pallas import tpu as pltpu
from jax.sharding import PartitionSpec as P
BF=jnp.bfloat16; F32=jnp.float32
EPSILON=1e-12
CH=48

def nn(a,b): return lax.dot_general(a,b,(((1,),(0,)),((),())),preferred_element_type=F32)
def nt(a,b): return lax.dot_general(a,b,(((1,),(1,)),((),())),preferred_element_type=F32)

def gelu_pair(v):
    t = pl.reciprocal(1.0 + (0.3275911 * 0.7071067811865476) * jnp.abs(v))
    poly = t * (0.5*0.254829592 + t * (-0.5*0.284496736 + t * (0.5*1.421413741 + t * (-0.5*1.453152027 + t * (0.5*1.061405429)))))
    e = jnp.exp(-0.5 * v * v)
    half = poly * e
    cdf = jnp.where(v >= 0.0, 1.0 - half, half)
    return v * cdf, cdf + v * (e * 0.3989422804014327)

def group_sum(v):
    rows = v.shape[0]
    return jnp.sum(v.reshape(rows // 8, 8, v.shape[1]), axis=0)

def mlp_kernel(half_ref, valid_ref, mixed, x, teach, vec, bup, wa_hbm, wu_hbm, wd_hbm,
               out, g_one, g_attn, vgrad, bupgrad, gu_hbm, gd_hbm,
               tr, wraw, wt, wu, wd, h1, h2, rs1, low, lowt, brt, br, hid, dgl, gg, gu, gd, sem):
    rows, feats = x.shape
    zs = wu.shape[0]
    nb = feats // 256
    copies_a = [pltpu.make_async_copy(wa_hbm.at[z, :, pl.ds(512, 256)], wraw.at[z], sem.at[z]) for z in range(zs)]
    copies_u = [pltpu.make_async_copy(wu_hbm.at[z], wu.at[z], sem.at[zs + z]) for z in range(zs)]
    copies_d = [pltpu.make_async_copy(wd_hbm.at[z], wd.at[z], sem.at[2 * zs + z]) for z in range(zs)]
    for c in copies_a + copies_u + copies_d:
        c.start()
    for c in copies_a:
        c.wait()
    main = teach.shape[1]
    for i in range(main // 128):
        tr[pl.ds(128 * i, 128), :] = teach[:, pl.ds(128 * i, 128)].T
    tr[pl.ds(main, rows - main), :] = jnp.zeros((rows - main, feats), BF)
    low_lane = lax.broadcasted_iota(jnp.int32, (feats, 128), 1) < 64
    for k in range(zs // 2):
        z0, z1 = 2 * k, 2 * k + 1
        wt[:, pl.ds(384 * k, 128)] = wraw[z0, :, pl.ds(128, 128)]
        wt[:, pl.ds(384 * k + 128, 128)] = wraw[z1, :, pl.ds(128, 128)]
        t0 = pltpu.roll(wraw[z0, :, pl.ds(0, 128)].astype(F32), 64, 1)
        t1 = wraw[z1, :, pl.ds(0, 128)].astype(F32)
        wt[:, pl.ds(384 * k + 256, 128)] = jnp.where(low_lane, t0, t1).astype(BF)
    for n in range(nb):
        f = pl.ds(256 * n, 256)
        h1[:, f] = nt(mixed[...], wt[f, :]) + x[:, f].astype(F32) + vec[0:1, f]
    inv = 1.0 / feats

    vgrad[...] = jnp.zeros_like(vgrad)
    bupgrad[...] = jnp.zeros_like(bupgrad)

    def norm1(i, _):
        r = pl.ds(pl.multiple_of(i * CH, 16), CH)
        h = h1[r, :]
        m = jnp.sum(h, axis=1, keepdims=True) * inv
        s = jnp.sum(h * h, axis=1, keepdims=True) * inv
        rstd = lax.rsqrt(s - m * m + EPSILON)
        xhat = (h - m) * rstd
        h1[r, :] = xhat
        rs1[r, :] = jnp.broadcast_to(rstd, (CH, 128))
        low[r, :] = (xhat * vec[1:2, :] + vec[2:3, :]).astype(BF)
        return 0
    lax.fori_loop(0, rows // CH, norm1, 0)
    lowt[...] = low[...].T
    for c in copies_u:
        c.wait()

    def gate(i, _):
        z = i // nb
        f = pl.ds(pl.multiple_of((i % nb) * 256, 256), 256)
        v = nn(low[...], wu[z, :, f]) + bup[z, :, f]
        a, b = gelu_pair(v)
        hid[z, :, f] = a.astype(BF)
        dgl[z, :, f] = b
        return 0
    lax.fori_loop(0, zs * nb, gate, 0)
    for c in copies_d:
        c.wait()

    def down(n, _):
        f = pl.ds(pl.multiple_of(n * 256, 256), 256)
        acc = nt(hid[0], wd[0, f, :])
        for z in range(1, zs):
            acc = acc + nt(hid[z], wd[z, f, :])
        h2[:, f] = acc
        return 0
    lax.fori_loop(0, nb, down, 0)
    scale = vec[6:7, 0:1]
    first = half_ref[0] * main

    def norm2(i, _):
        r = pl.ds(pl.multiple_of(i * CH, 16), CH)
        h = h2[r, :] + (h1[r, :] * vec[1:2, :] + vec[2:3, :]) + vec[3:4, :]
        m = jnp.sum(h, axis=1, keepdims=True) * inv
        s = jnp.sum(h * h, axis=1, keepdims=True) * inv
        rstd = lax.rsqrt(s - m * m + EPSILON)
        xhat = (h - m) * rstd
        o = xhat * vec[4:5, :] + vec[5:6, :]
        out[r, :] = o.astype(BF)
        place = lax.broadcasted_iota(jnp.int32, (CH, 1), 0) + i * CH
        place = jnp.where(place < main, place + first, valid_ref[0])
        go = jnp.where(place < valid_ref[0], scale * (o - tr[r, :].astype(F32)), 0.0)
        a = go * vec[4:5, :]
        m1 = jnp.sum(a, axis=1, keepdims=True) * inv
        m2 = jnp.sum(a * xhat, axis=1, keepdims=True) * inv
        g2 = rstd * (a - m1 - xhat * m2)
        h2[r, :] = g2
        b = g2.astype(BF)
        br[r, :] = b
        vgrad[0] += group_sum(go * xhat)
        vgrad[1] += group_sum(go)
        vgrad[2] += group_sum(b.astype(F32))
        return 0
    lax.fori_loop(0, rows // CH, norm2, 0)
    brt[...] = br[...].T

    def back(i, _):
        z = i // nb
        f = pl.ds(pl.multiple_of((i % nb) * 256, 256), 256)
        gh = nn(br[...], wd[z, :, f])
        g = (gh * dgl[z, :, f]).astype(BF)
        gg[z, :, f] = g
        bupgrad[z, :, f] += group_sum(g.astype(F32))
        gd[z, :, f] = nn(brt[...], hid[z, :, f]).astype(BF)
        gu[z, :, f] = nn(lowt[...], g).astype(BF)
        return 0
    lax.fori_loop(0, zs * nb, back, 0)
    outs = [pltpu.make_async_copy(gd, gd_hbm, sem.at[0]), pltpu.make_async_copy(gu, gu_hbm, sem.at[1])]
    for c in outs:
        c.start()

    def first_grad(n, _):
        f = pl.ds(pl.multiple_of(n * 256, 256), 256)
        acc = h2[:, f]
        for z in range(zs):
            acc = acc + nt(gg[z], wu[z, f, :])
        h2[:, f] = acc
        return 0
    lax.fori_loop(0, nb, first_grad, 0)

    def norm1_back(i, _):
        r = pl.ds(pl.multiple_of(i * CH, 16), CH)
        g = h2[r, :]
        xhat = h1[r, :]
        a = g * vec[1:2, :]
        m1 = jnp.sum(a, axis=1, keepdims=True) * inv
        m2 = jnp.sum(a * xhat, axis=1, keepdims=True) * inv
        g1 = rs1[r, 0:1] * (a - m1 - xhat * m2)
        g_one[r, :] = g1
        b = g1.astype(BF)
        g_attn[r, :] = b
        vgrad[3] += group_sum(g * xhat)
        vgrad[4] += group_sum(g)
        vgrad[5] += group_sum(b.astype(F32))
        return 0
    lax.fori_loop(0, rows // CH, norm1_back, 0)
    for c in outs:
        c.wait()

def mlp(half, valid, mixed, x, teach, vec, bup, wa, wu, wd):
    rows, feats = x.shape; zs = wu.shape[0]
    V = lambda *s, d=BF: pltpu.VMEM(s, d)
    vm = pl.BlockSpec(memory_space=pltpu.VMEM); sm = pl.BlockSpec(memory_space=pltpu.SMEM); an = pl.BlockSpec(memory_space=pl.ANY)
    S = jax.ShapeDtypeStruct
    return pl.pallas_call(mlp_kernel,
        out_shape=(S((rows,feats),BF),S((rows,feats),F32),S((rows,feats),BF),S((6,8,feats),F32),S((zs,8,feats),F32),S(wu.shape,BF),S(wd.shape,BF)),
        in_specs=[sm,sm,vm,vm,vm,vm,vm,an,an,an],
        out_specs=(vm,vm,vm,vm,vm,an,an),
        scratch_shapes=[V(rows,feats),V(zs,feats,256),V(feats,feats),V(*wu.shape),V(*wd.shape),V(rows,feats,d=F32),V(rows,feats,d=F32),V(rows,128,d=F32),V(rows,feats),
            V(feats,rows),V(feats,rows),V(rows,feats),V(zs,rows,feats),V(zs,rows,feats,d=F32),V(zs,rows,feats),V(*wu.shape),V(*wd.shape),pltpu.SemaphoreType.DMA((3*zs,))],
        compiler_params=pltpu.CompilerParams(vmem_limit_bytes=63*2**20),
    )(half,valid,mixed,x,teach,vec,bup,wa,wu,wd)
NEG=-1e30
def tn_lanes(): return lax.broadcasted_iota(jnp.int32,(1,128),1)

def assemble_pairs(w, wp, feats):
    lo = lax.broadcasted_iota(jnp.int32, (feats, 128), 1) < 64
    wp[0] = w[0, :, pl.ds(0, 384)]
    wp[1] = w[1, :, pl.ds(0, 384)]
    a0, a1 = w[0, :, pl.ds(384, 128)].astype(F32), w[1, :, pl.ds(384, 128)].astype(F32)
    wp[2, :, pl.ds(0, 128)] = jnp.where(lo, a0, pltpu.roll(a1, 64, 1)).astype(BF)
    wp[2, :, pl.ds(128, 128)] = jnp.where(lo, pltpu.roll(a0, 64, 1), a1).astype(BF)
    b0, b1 = w[0, :, pl.ds(512, 128)].astype(F32), w[1, :, pl.ds(512, 128)].astype(F32)
    wp[2, :, pl.ds(256, 128)] = jnp.where(lo, b0, pltpu.roll(b1, 64, 1)).astype(BF)

def tiles(rows, length):
    mem = (length, rows - length, True)
    out = []
    for a in range(0, length, 256):
        spans = []
        if a:
            spans.append((0, a, False))
        spans.append((a, min(512, length - a), True))
        out.append((a, 256, spans + [mem]))
    out.append((length, rows - length, [(0, length, True), mem]))
    return out

def scores_of(kt, qm, idk, idq, p, spans):
    out = []
    for k0, kn, masked in spans:
        s = nt(kt[p, pl.ds(k0, kn), :], qm)
        if masked:
            s = jnp.where(idk[pl.ds(k0, kn), 0:1] <= idq, s, NEG)
        out.append(s)
    return out

def attn_fwd_kernel(xt, wa_hbm, bias, idk, idq, x, qt, kt, vt, mixed, lse, w, wp, vtt, ot, sem):
    feats = xt.shape[0]; rows = x.shape[0]; length = xt.shape[1] - 128
    c = pltpu.make_async_copy(wa_hbm, w, sem); c.start()
    for i in range(length // 128):
        x[pl.ds(128 * i, 128), :] = xt[:, pl.ds(128 * i, 128)].T
    x[pl.ds(length, rows - length), :] = xt[:, pl.ds(length, 128)].T[: rows - length, :]
    c.wait()
    assemble_pairs(w, wp, feats)
    rc = rows // 3

    def project(i, _):
        p = i // 3
        r = pl.ds(pl.multiple_of((i % 3) * rc, 16), rc)
        v = nn(x[r, :], wp[p]) + bias[p]
        qt[p, r, :] = (v[:, :128].astype(BF).astype(F32) * 0.125).astype(BF)
        kt[p, r, :] = v[:, 128:256].astype(BF)
        vt[p, r, :] = v[:, 256:].astype(BF)
        return 0
    lax.fori_loop(0, 9, project, 0)

    def pair(p, _):
        vtt[...] = vt[p].T
        for e in range(2):
            lanes = (tn_lanes() < 64) if e == 0 else (tn_lanes() >= 64)
            for q0, qn, spans in tiles(rows, length):
                q = qt[p, pl.ds(q0, qn), :]
                qm = jnp.where(lanes, q, jnp.zeros_like(q))
                ss = scores_of(kt, qm, idk, idq[0:1, pl.ds(q0, qn)], p, spans)
                m = jnp.max(ss[0], axis=0, keepdims=True)
                for s in ss[1:]:
                    m = jnp.maximum(m, jnp.max(s, axis=0, keepdims=True))
                tot, acc = None, None
                for s, (k0, kn, _) in zip(ss, spans):
                    ex = jnp.exp(s - m)
                    t = jnp.sum(ex, axis=0, keepdims=True)
                    o = nn(vtt[pl.ds(64 * e, 64), pl.ds(k0, kn)], ex.astype(BF))
                    tot = t if tot is None else tot + t
                    acc = o if acc is None else acc + o
                ot[pl.ds(64 * e, 64), pl.ds(q0, qn)] = acc / tot
                lse[p, e, :, pl.ds(q0, qn)] = m + jnp.log(tot)
        mixed[p] = ot[...].T.astype(BF)
        return 0
    lax.fori_loop(0, 3, pair, 0)

def attn_fwd(xt, wa, bias, idk, idq, rows):
    feats = xt.shape[0]
    V = lambda *s, d=BF: pltpu.VMEM(s, d)
    vm = pl.BlockSpec(memory_space=pltpu.VMEM); an = pl.BlockSpec(memory_space=pl.ANY)
    S = jax.ShapeDtypeStruct
    t3 = S((3, rows, 128), BF)
    return pl.pallas_call(attn_fwd_kernel,
        out_shape=(S((rows, feats), BF), t3, t3, t3, t3, S((3, 2, 1, rows), F32)),
        in_specs=[vm, an, vm, vm, vm], out_specs=(vm,) * 6,
        scratch_shapes=[V(*wa.shape), V(3, feats, 384), V(128, rows), V(128, rows, d=F32), pltpu.SemaphoreType.DMA],
        compiler_params=pltpu.CompilerParams(vmem_limit_bytes=63*2**20))(xt, wa, bias, idk, idq)

def attn_bwd_kernel(ga, mixed, xt, qt, kt, vt, lse, idk, idq, wa_hbm, gpart, bgrad, gown_hbm, w, wp, wt, gat, gm, gp, dv, dk, dqt, ktt, dd, ro, gown, sem):
    feats = xt.shape[0]; rows = ga.shape[0]; length = xt.shape[1] - 128
    c = pltpu.make_async_copy(wa_hbm, w, sem); c.start()
    gat[...] = ga[...].T
    c.wait()
    assemble_pairs(w, wp, feats)
    wt[:, pl.ds(0, 128)] = w[0, :, pl.ds(640, 128)]
    wt[:, pl.ds(128, 128)] = w[1, :, pl.ds(640, 128)]
    lo = lax.broadcasted_iota(jnp.int32, (feats, 128), 1) < 64
    wt[:, pl.ds(256, 128)] = jnp.where(lo, pltpu.roll(w[0, :, pl.ds(512, 128)].astype(F32), 64, 1), w[1, :, pl.ds(512, 128)].astype(F32)).astype(BF)
    for p in range(3):
        gm[p] = nn(ga[...], wt[:, pl.ds(128 * p, 128)]).astype(BF)

    def pair(p, _):
        ktt[...] = kt[p].T
        prod = (gm[p].astype(F32) * mixed[p].astype(F32)).T
        dd[0:1, :] = jnp.sum(prod[:64, :], axis=0, keepdims=True)
        dd[1:2, :] = jnp.sum(prod[64:, :], axis=0, keepdims=True)
        dv[...] = jnp.zeros_like(dv)
        dk[...] = jnp.zeros_like(dk)
        for e in range(2):
            lanes = (tn_lanes() < 64) if e == 0 else (tn_lanes() >= 64)
            for q0, qn, spans in tiles(rows, length):
                q = qt[p, pl.ds(q0, qn), :]
                qm = jnp.where(lanes, q, jnp.zeros_like(q))
                g = gm[p, pl.ds(q0, qn), :]
                gmm = jnp.where(lanes, g, jnp.zeros_like(g))
                ss = scores_of(kt, qm, idk, idq[0:1, pl.ds(q0, qn)], p, spans)
                l = lse[p, e, :, pl.ds(q0, qn)]
                d = dd[pl.ds(e, 1), pl.ds(q0, qn)]
                acc = None
                for s, (k0, kn, _) in zip(ss, spans):
                    pr = jnp.exp(s - l)
                    dp = nt(vt[p, pl.ds(k0, kn), :], gmm)
                    ds = (pr * (dp - d)).astype(BF)
                    dv[pl.ds(k0, kn), :] += nn(pr.astype(BF), gmm)
                    dk[pl.ds(k0, kn), :] += nn(ds, qm)
                    o = nn(ktt[pl.ds(64 * e, 64), pl.ds(k0, kn)], ds)
                    acc = o if acc is None else acc + o
                dqt[pl.ds(64 * e, 64), pl.ds(q0, qn)] = acc * 0.125
        gp[p, :, pl.ds(0, 128)] = dqt[...].T.astype(BF)
        gp[p, :, pl.ds(128, 128)] = dk[...].astype(BF)
        gp[p, :, pl.ds(256, 128)] = dv[...].astype(BF)
        return 0
    lax.fori_loop(0, 3, pair, 0)
    for p in range(3):
        bgrad[p] = group_sum(gp[p].astype(F32))
    r3 = rows // 3

    def rowsgrad(i, _):
        r = pl.ds(pl.multiple_of(i * r3, 16), r3)
        gpart[r, :] = nt(gp[0, r, :], wp[0]) + nt(gp[1, r, :], wp[1]) + nt(gp[2, r, :], wp[2])
        return 0
    lax.fori_loop(0, 3, rowsgrad, 0)
    fc = 256
    for f0 in range(0, feats, fc):
        f = pl.ds(f0, fc)
        xf = xt[f, pl.ds(0, rows)]
        af = gat[f, :]
        r0 = nn(xf, gp[0]); r1 = nn(xf, gp[1]); r2 = nn(xf, gp[2])
        o = [nn(af, mixed[p]) for p in range(3)]
        lo = lax.broadcasted_iota(jnp.int32, (fc, 128), 1) < 64
        rq, rk, rv = r2[:, :128], r2[:, 128:256], r2[:, 256:]
        sw = lambda a: pltpu.roll(a, 64, 1)
        gown[0, f, pl.ds(0, 384)] = r0.astype(BF)
        gown[1, f, pl.ds(0, 384)] = r1.astype(BF)
        gown[0, f, pl.ds(384, 128)] = jnp.where(lo, rq, sw(rk)).astype(BF)
        gown[1, f, pl.ds(384, 128)] = jnp.where(lo, sw(rq), rk).astype(BF)
        gown[0, f, pl.ds(512, 128)] = jnp.where(lo, rv, sw(o[2])).astype(BF)
        gown[1, f, pl.ds(512, 128)] = jnp.where(lo, sw(rv), o[2]).astype(BF)
        gown[0, f, pl.ds(640, 128)] = o[0].astype(BF)
        gown[1, f, pl.ds(640, 128)] = o[1].astype(BF)
    c = pltpu.make_async_copy(gown, gown_hbm, sem); c.start(); c.wait()

def attn_bwd(ga, mixed, xt, qt, kt, vt, lse, idk, idq, wa):
    feats = xt.shape[0]; rows = ga.shape[0]
    V = lambda *s, d=BF: pltpu.VMEM(s, d)
    vm = pl.BlockSpec(memory_space=pltpu.VMEM); an = pl.BlockSpec(memory_space=pl.ANY)
    S = jax.ShapeDtypeStruct
    return pl.pallas_call(attn_bwd_kernel,
        out_shape=(S((rows, feats), F32), S((3, 8, 384), F32), S(wa.shape, BF)),
        in_specs=[vm] * 9 + [an], out_specs=(vm, vm, an),
        scratch_shapes=[V(*wa.shape), V(3, feats, 384), V(feats, 384), V(feats, rows), V(3, rows, 128), V(3, rows, 384), V(rows, 128, d=F32), V(rows, 128, d=F32),
            V(128, rows, d=F32), V(128, rows), V(8, rows, d=F32), V(8, 128), V(*wa.shape), pltpu.SemaphoreType.DMA],
        compiler_params=pltpu.CompilerParams(vmem_limit_bytes=63*2**20))(ga, mixed, xt, qt, kt, vt, lse, idk, idq, wa)
MESH = pl.DeviceIdType.MESH

class Move:
    def __init__(self, net, src, dst, dev, index):
        self.net, self.src, self.dst, self.dev, self.index = net, src, dst, dev, index
    def make(self):
        return pltpu.make_async_remote_copy(src_ref=self.src(), dst_ref=self.dst(), send_sem=self.net.ss.at[self.index],
                                            recv_sem=self.net.rs.at[self.index], device_id=self.dev, device_id_type=MESH)
    def start(self):
        self.make().start()
    def wait_recv(self):
        self.make().wait_recv()
    def wait_send(self):
        self.make().wait_send()

class Copy:
    def __init__(self, net, src, dst, index):
        self.net, self.src, self.dst, self.index = net, src, dst, index
    def make(self):
        return pltpu.make_async_copy(self.src(), self.dst(), self.net.ls.at[self.index])
    def start(self):
        self.make().start()
    def wait(self):
        self.make().wait()

class Net:
    def __init__(self, send_sems, recv_sems, local_sems):
        self.ss, self.rs, self.ls = send_sems, recv_sems, local_sems
        self.count, self.locals, self.moves, self.copies = 0, 0, [], []
        self.d, self.z, self.c = (lax.axis_index(a) for a in ("dp", "row", "col"))
        self.nd, self.nz = lax.axis_size("dp"), lax.axis_size("row")
        self.y, self.k = self.c // 2, self.c % 2
        self.x = self.d % 2
        self.oc = lax.rem(self.c + 2, 4)
        self.xp = (self.d + 1 - 2 * self.x, self.z, self.c)
        self.yp = (self.d, self.z, self.oc)
        self.kp = (self.d, self.z, self.c + 1 - 2 * self.k)
        self.ykp = (self.d, self.z, 3 - self.c)
        self.zs = [lax.rem(self.z + i, self.nz) for i in range(self.nz)]
        self.zp = [(self.d, zz, self.c) for zz in self.zs]
        self.others = [(lax.rem(self.d + 2 * i, self.nd), self.z, self.c) for i in range(1, self.nd // 2)]
    def from_row(self, i):
        return self.zs[(self.nz - i) % self.nz]
    def barrier(self, peers):
        b = pltpu.get_barrier_semaphore()
        for p in peers:
            pl.semaphore_signal(b, inc=1, device_id=p, device_id_type=MESH)
        pl.semaphore_wait(b, len(peers))
    def move(self, src, dst, dev):
        m = Move(self, src, dst, dev, self.count)
        self.count += 1
        self.moves.append(m)
        return m
    def send(self, src, dst, dev):
        m = self.move(src, dst, dev)
        m.start()
        return m
    def copy(self, src, dst):
        m = Copy(self, src, dst, self.locals)
        self.locals += 1
        self.copies.append(m)
        return m
    def local(self, src, dst):
        m = self.copy(src, dst)
        m.start()
        return m
    def finish(self):
        for m in self.moves:
            m.wait_send()

def at(i, table):
    for j, events in table.items():
        if events:
            @pl.when(i == j)
            def _(events=events):
                for e in events:
                    e()

def spread_events(events, steps):
    table = {}
    for n, e in enumerate(events):
        table.setdefault(n * steps // len(events), []).append(e)
    return table

def join192(t, dst):
    lo = lax.broadcasted_iota(jnp.int32, t[0][0].shape, 1) < 64
    sw = lambda a: pltpu.roll(a, 64, 1)
    for h in range(2):
        a, b = t[2 * h], t[2 * h + 1]
        dst[:, pl.ds(384 * h, 128)] = a[0]
        dst[:, pl.ds(384 * h + 128, 128)] = jnp.where(lo, a[1], sw(b[0]))
        dst[:, pl.ds(384 * h + 256, 128)] = jnp.where(lo, sw(b[0]), sw(b[1]))

def forward_kernel(valid_ref, tok, mem, tch, la, lu, ld, ls, idk, idq,
                   xt_o, q_o, k_o, v_o, mixed_o, wa_o, ga_o, hu_o, hd_o, lse, g_one, vgrad, bupgrad, out4,
                   xt, x, wa, wu, wd, sm, tt, tr, wp, qt, kt, vt, vtt, ot, mixed, mrows, bias, vec, wt,
                   h1, h2, rs1, low, lowt, br, brt, hid, dgl, gdz, guz, hu, hd, ru, rd, ga, o4, ss, rs, lsem, zsem, zrem):
    n = Net(ss, rs, lsem)
    n.barrier(n.zp[1:] + [n.yp, n.ykp, n.kp, n.xp])
    nz, y, k, c, z, oc = n.nz, n.y, n.k, n.c, n.z, n.oc
    b = la.shape[0]; hb = b // 2
    feats = x.shape[1]; rows = x.shape[0]; length = tok.shape[2]; main = length // 2
    own_rows = main + 16
    row = lambda cc, off=0, num=b: pl.ds(pl.multiple_of(cc * b + off, 16), num)
    blk = lambda w, zz, cc: (lambda: w.at[zz, row(cc)])
    hlf = lambda w, zz, cc, h: (lambda: w.at[zz, row(cc, h * hb, hb)])
    mine, theirs = n.x, 1 - n.x
    part = lambda w: (lambda: w.at[pl.ds(pl.multiple_of(n.x * hb, 16), hb)])
    all_of = lambda r: (lambda: r)
    tail = pl.ds(length, 128); body = pl.ds(0, length)
    fz = n.from_row
    R = range(1, nz)
    local = [n.local(lambda: tok.at[y], lambda: xt.at[row(c), body]), n.local(lambda: mem.at[y], lambda: xt.at[row(c), tail])]
    s_blk = lambda zz, cc: (lambda: sm.at[zz, cc])
    a_z = [n.send(part(la), hlf(wa, z, c, mine), n.zp[i]) for i in R]
    s_z = [n.send(all_of(ls), s_blk(z, c), n.zp[i]) for i in R]
    a_y = [n.send(part(la), hlf(wa, z, c, mine), n.yp)]
    t_y = [n.send(lambda: tok.at[1 - y], lambda: xt.at[row(c), body], n.yp), n.send(lambda: mem.at[1 - y], lambda: xt.at[row(c), tail], n.yp)]
    s_y = [n.send(all_of(ls), s_blk(z, c), n.yp)]
    u_y = n.send(part(lu), hlf(wu, z, c, mine), n.yp)
    s_k = [n.send(all_of(ls), s_blk(z, c), n.kp)]
    t_k = [n.send(lambda: tok.at[y], lambda: xt.at[row(c), body], n.kp), n.send(lambda: mem.at[y], lambda: xt.at[row(c), tail], n.kp)]
    a_k = [n.send(all_of(la), blk(wa, z, c), n.kp)]
    for w, l in ((wa, la), (wu, lu), (wd, ld)):
        local.append(n.local(all_of(l), blk(w, z, c)))
    local.append(n.local(all_of(ls), s_blk(z, c)))
    fwd = lambda u, dev: n.move(u, u, dev)
    a_x = []
    for i in R:
        a_z[i - 1].wait_recv()
        u = hlf(wa, fz(i), c, mine)
        for lst, dev in ((a_y, n.yp), (a_x, n.xp), (a_k, n.kp)):
            lst.append(fwd(u, dev)); lst[-1].start()
        s_z[i - 1].wait_recv()
        u = s_blk(fz(i), c)
        for lst, dev in ((s_y, n.yp), (s_k, n.kp)):
            lst.append(fwd(u, dev)); lst[-1].start()
    u_z = [n.send(part(lu), hlf(wu, z, c, mine), n.zp[i]) for i in R]
    u_k = [n.send(all_of(lu), blk(wu, z, c), n.kp)]
    u_y.wait_recv()
    uo = hlf(wu, z, oc, mine)
    u_z2 = [fwd(uo, n.zp[i]) for i in R]
    for m in u_z2:
        m.start()
    u_x = [fwd(uo, n.xp)]
    u_k.append(fwd(uo, n.kp)); u_k[-1].start()
    for m, w_ in zip(t_y, (body, tail)):
        m.wait_recv()
        t_k.append(fwd((lambda w_=w_: xt.at[row(oc), w_]), n.kp)); t_k[-1].start()
    for i in range(nz):
        a_y[i].wait_recv()
        u = hlf(wa, fz(i), oc, mine)
        for lst, dev in ((a_x, n.xp), (a_k, n.kp)):
            lst.append(fwd(u, dev)); lst[-1].start()
        s_y[i].wait_recv()
        u = s_blk(fz(i), oc)
        s_k.append(fwd(u, n.kp)); s_k[-1].start()
    u_x[0].start()
    d_z = [n.send(all_of(ld), blk(wd, z, c), n.zp[i]) for i in R]
    d_y = [n.send(all_of(ld), blk(wd, z, c), n.yp)]
    d_k = [n.send(all_of(ld), blk(wd, z, c), n.kp)]
    tsl = lambda s, kk: (lambda: tch.at[s, :, pl.ds(pl.multiple_of(kk * main, 128), main)])
    th = lambda: tt.at[row(c)]
    h_y = [n.send(tsl(y, 1 - k), th, n.kp)]
    local.append(n.local(tsl(y, k), th))
    local[0].wait(); local[1].wait()
    for m in t_k:
        m.wait_recv()
    def turn(i, _):
        f = pl.ds(pl.multiple_of(128 * i, 128), 128)
        x[f, :] = xt[:, f].T
        return 0
    lax.fori_loop(0, length // 128, turn, 0)
    x[pl.ds(length, rows - length), :] = xt[:, tail].T[: rows - length, :]
    o_x = n.local(all_of(xt), all_of(xt_o))
    order = [(i, c) for i in R] + [(i, oc) for i in range(nz)]
    for m, (i, cc) in zip(a_x, order):
        m.wait_recv()
        a_k.append(fwd(hlf(wa, fz(i), cc, theirs), n.kp)); a_k[-1].start()
    h_y += [n.send(tsl(1 - y, k), th, n.yp), n.send(tsl(1 - y, 1 - k), th, n.ykp)]
    events = []
    def relay(wait, u, pairs):
        ms = []
        for lst, dev in pairs:
            m = fwd(u, dev)
            lst.append(m)
            ms.append(m)
        def run():
            wait()
            for m in ms:
                m.start()
        events.append(run)
    for i in R:
        relay(u_z[i - 1].wait_recv, hlf(wu, fz(i), c, mine), ((u_x, n.xp), (u_k, n.kp)))
    for i in R:
        relay(u_z2[i - 1].wait_recv, hlf(wu, fz(i), oc, mine), ((u_x, n.xp), (u_k, n.kp)))
    u_order = [(0, oc)] + [(i, c) for i in R] + [(i, oc) for i in R]
    u_units = list(zip(u_x, u_order))
    for i in R:
        relay(d_z[i - 1].wait_recv, blk(wd, fz(i), c), ((d_y, n.yp), (d_k, n.kp)))
    for m, (i, cc) in u_units:
        relay(m.wait_recv, hlf(wu, fz(i), cc, theirs), ((u_k, n.kp),))
    u_events, d_events = events, []
    events = []
    for i in range(nz):
        relay(d_y[i].wait_recv, blk(wd, fz(i), oc), ((d_k, n.kp),))
    d_events = events
    for m in s_k:
        m.wait_recv()
    for m in local[2:6]:
        m.wait()
    join192([[sm[0, cc, pl.ds(0, 8), pl.ds(0, 128)], sm[0, cc, pl.ds(0, 8), pl.ds(128, 128)]] for cc in range(4)], vec)
    lo1 = lax.broadcasted_iota(jnp.int32, (1, 128), 1) < 64
    sw = lambda a: pltpu.roll(a, 64, 1)
    bias[...] = jnp.zeros_like(bias)
    hv = [[sm[2 * k + j, 0, 11:12, pl.ds(0, 128)], sm[2 * k + j, 0, 11:12, pl.ds(128, 128)], sm[2 * k + j, 0, 12:13, pl.ds(0, 128)]] for j in range(2)]
    for p, (e0, e1) in enumerate(((hv[0][0], hv[0][1]), (hv[1][0], hv[1][1]), (hv[0][2], hv[1][2]))):
        w8 = lambda a: jnp.broadcast_to(a, (8, 128))
        lo8 = lax.broadcasted_iota(jnp.int32, (8, 128), 1) < 64
        bias[p, :, pl.ds(0, 128)] = jnp.where(lo8, w8(e0), sw(w8(e1)))
        bias[p, :, pl.ds(256, 128)] = jnp.where(lo8, sw(w8(e0)), w8(e1))
    for m in a_k:
        m.wait_recv()
    own = pl.ds(2 * k, 2)
    o_w = n.local(lambda: wa.at[own], all_of(wa_o))
    w = wa.at[own]
    assemble_pairs(w, wp, feats)
    rc = rows // 3
    ev = spread_events(u_events[:6], 9)

    def project(i, _):
        p = i // 3
        r = pl.ds(pl.multiple_of((i % 3) * rc, 16), rc)
        v = nn(x[r, :], wp[p]) + bias[p, 0:1, :]
        qt[p, r, :] = (v[:, :128].astype(BF).astype(F32) * 0.125).astype(BF)
        kt[p, r, :] = v[:, 128:256].astype(BF)
        vt[p, r, :] = v[:, 256:].astype(BF)
        at(i, ev)
        return 0
    lax.fori_loop(0, 9, project, 0)
    o_q = [n.local(all_of(a), all_of(o)) for a, o in ((qt, q_o), (kt, k_o), (vt, v_o))]
    m_k = [(n.move((lambda p=p: mixed.at[p, pl.ds(pl.multiple_of((1 - k) * main, 16), main)]), (lambda p=p: mrows.at[k * 3 + p, pl.ds(0, main)]), n.kp),
            n.move((lambda p=p: mixed.at[p, pl.ds(pl.multiple_of(length + (1 - k) * 16, 16), 16)]), (lambda p=p: mrows.at[k * 3 + p, pl.ds(main, 16)]), n.kp)) for p in range(3)]
    m_l = [(n.copy((lambda p=p: mixed.at[p, pl.ds(pl.multiple_of(k * main, 16), main)]), (lambda p=p: mrows.at[k * 3 + p, pl.ds(0, main)])),
            n.copy((lambda p=p: mixed.at[p, pl.ds(pl.multiple_of(length + k * 16, 16), 16)]), (lambda p=p: mrows.at[k * 3 + p, pl.ds(main, 16)]))) for p in range(3)]
    ev = spread_events(u_events[6:], 6)

    def head(i, _):
        p = i // 2
        e = i % 2
        he = pl.ds(pl.multiple_of(64 * e, 64), 64)

        @pl.when(e == 0)
        def _():
            vtt[...] = vt[p].T
        lanes = (lax.broadcasted_iota(jnp.int32, (1, 128), 1) // 64) == e
        for q0, qn, spans in tiles(rows, length):
            q = qt[p, pl.ds(q0, qn), :]
            qm = jnp.where(lanes, q, jnp.zeros_like(q))
            sc = scores_of(kt, qm, idk, idq[0:1, pl.ds(q0, qn)], p, spans)
            m = jnp.max(sc[0], axis=0, keepdims=True)
            for s in sc[1:]:
                m = jnp.maximum(m, jnp.max(s, axis=0, keepdims=True))
            tot, acc = None, None
            for s, (k0, kn, _) in zip(sc, spans):
                ex = jnp.exp(s - m)
                t = jnp.sum(ex, axis=0, keepdims=True)
                o = nn(vtt[he, pl.ds(k0, kn)], ex.astype(BF))
                tot = t if tot is None else tot + t
                acc = o if acc is None else acc + o
            ot[he, pl.ds(q0, qn)] = acc / tot
            lse[i, :, pl.ds(q0, qn)] = m + jnp.log(tot)

        @pl.when(e == 1)
        def _():
            mixed[p] = ot[...].T.astype(BF)
        at(i, ev)
        at(i, {2 * p + 1: [m.start for m in m_k[p] + m_l[p]] for p in range(3)})
        return 0
    lax.fori_loop(0, 6, head, 0)
    o_m = n.local(all_of(mixed), all_of(mixed_o))
    lo = lax.broadcasted_iota(jnp.int32, (feats, 128), 1) < 64
    for kk in range(2):
        z0, z1 = 2 * kk, 2 * kk + 1
        wt[:, pl.ds(384 * kk, 128)] = wa[z0, :, pl.ds(640, 128)]
        wt[:, pl.ds(384 * kk + 128, 128)] = wa[z1, :, pl.ds(640, 128)]
        t0 = pltpu.roll(wa[z0, :, pl.ds(512, 128)].astype(F32), 64, 1)
        wt[:, pl.ds(384 * kk + 256, 128)] = jnp.where(lo, t0, wa[z1, :, pl.ds(512, 128)].astype(F32)).astype(BF)
    for pair_ in m_k:
        for m in pair_:
            m.wait_recv()
    for pair_ in m_l:
        for m in pair_:
            m.wait()
    nb = feats // 256
    CHS = own_rows // CH
    for e in d_events[:0]:
        e()

    def own_slice(i, num):
        start = jnp.where(i < main, k * main + i, length + k * 16)
        return pl.ds(pl.multiple_of(start, 16), num)

    for f0 in range(0, feats, 256):
        f = pl.ds(f0, 256)
        acc = nt(mrows[0], wt[f, pl.ds(0, 128)])
        for j in range(1, 6):
            acc = acc + nt(mrows[j], wt[f, pl.ds(128 * j, 128)])
        h1[:, f] = acc + vec[0:1, f]
    inv = 1.0 / feats
    vgrad[...] = jnp.zeros_like(vgrad)
    bupgrad[...] = jnp.zeros_like(bupgrad)

    def norm1(i, _):
        r = pl.ds(pl.multiple_of(i * 16, 16), 16)
        h = h1[r, :] + x[own_slice(i * 16, 16), :].astype(F32)
        m = jnp.sum(h, axis=1, keepdims=True) * inv
        s = jnp.sum(h * h, axis=1, keepdims=True) * inv
        rstd = lax.rsqrt(s - m * m + EPSILON)
        xhat = (h - m) * rstd
        h1[r, :] = xhat
        rs1[r, :] = jnp.broadcast_to(rstd, (16, 128))
        low[r, :] = (xhat * vec[1:2, :] + vec[2:3, :]).astype(BF)
        return 0
    lax.fori_loop(0, own_rows // 16, norm1, 0, unroll=3)
    lowt[...] = low[...].T
    for m in u_k:
        m.wait_recv()
    ev = spread_events(d_events, 12)

    def gate(i, _):
        zz = i // nb
        j = i % nb
        f = pl.ds(pl.multiple_of(j * 256, 256), 256)
        v = nn(low[...], wu[zz, :, f]) + sm[zz, 0, pl.ds(8 + j, 1), :]
        a, g = gelu_pair(v)
        hid[zz, :, f] = a.astype(BF)
        dgl[zz, :, f] = g.astype(BF)
        at(i, ev)
        return 0
    lax.fori_loop(0, nz * nb, gate, 0)
    for m in h_y:
        m.wait_recv()
    local[6].wait()
    def turn_t(i, _):
        f = pl.ds(pl.multiple_of(128 * i, 128), 128)
        tr[f, :] = tt[:, f].T
        return 0
    lax.fori_loop(0, main // 128, turn_t, 0)
    tr[pl.ds(main, 16), :] = jnp.zeros((16, feats), BF)
    for m in d_k:
        m.wait_recv()

    def down(j, _):
        f = pl.ds(pl.multiple_of(j * 256, 256), 256)
        acc = nt(hid[0], wd[0, f, :])
        for zz in range(1, nz):
            acc = acc + nt(hid[zz], wd[zz, f, :])
        h2[:, f] = acc
        return 0
    lax.fori_loop(0, nb, down, 0)
    scale = vec[6:7, 0:1]

    def norm2(i, _):
        r = pl.ds(pl.multiple_of(i * CH, 16), CH)
        h = h2[r, :] + (h1[r, :] * vec[1:2, :] + vec[2:3, :]) + vec[3:4, :]
        m = jnp.sum(h, axis=1, keepdims=True) * inv
        s = jnp.sum(h * h, axis=1, keepdims=True) * inv
        rstd = lax.rsqrt(s - m * m + EPSILON)
        xhat = (h - m) * rstd
        o = xhat * vec[4:5, :] + vec[5:6, :]
        for cc in range(4):
            o4[cc, r, :] = o[:, cc * b:(cc + 1) * b].astype(BF)
        place = lax.broadcasted_iota(jnp.int32, (CH, 1), 0) + i * CH
        place = jnp.where(place < main, place + k * main, valid_ref[0])
        go = jnp.where(place < valid_ref[0], scale * (o - tr[r, :].astype(F32)), 0.0)
        a = go * vec[4:5, :]
        m1 = jnp.sum(a, axis=1, keepdims=True) * inv
        m2 = jnp.sum(a * xhat, axis=1, keepdims=True) * inv
        g2 = rstd * (a - m1 - xhat * m2)
        h2[r, :] = g2
        g2b = g2.astype(BF)
        br[r, :] = g2b
        vgrad[0] += group_sum(go * xhat)
        vgrad[1] += group_sum(go)
        vgrad[2] += group_sum(g2b.astype(F32))
        return 0
    lax.fori_loop(0, CHS, norm2, 0)
    o_dst = lambda: out4.at[y, k]
    o_s = [n.send(lambda: o4.at[oc], o_dst, n.yp), n.send(lambda: o4.at[3 - c], o_dst, n.ykp), n.send(lambda: o4.at[c + 1 - 2 * k], o_dst, n.kp)]
    o_l = n.local(lambda: o4.at[c], o_dst)
    brt[...] = br[...].T
    def gmove(which, src, dst, zz, slot, yy):
        return pltpu.make_async_remote_copy(src_ref=src.at[slot, 2 * yy + 1 - k], dst_ref=dst.at[yy, zz], send_sem=zsem.at[which, yy, zz],
                                            recv_sem=zrem.at[which, yy, zz], device_id=n.kp, device_id_type=MESH)
    def each(fn, zz, slot):
        for which, src, dst in ((0, gdz, rd), (1, guz, ru)):
            for yy in range(2):
                fn(gmove(which, src, dst, zz, slot, yy))
    def fold(zz):
        each(lambda m: m.wait_recv(), zz, 0)
        for yy in range(2):
            add_to(hd.at[yy, zz], rd.at[yy, zz])
            add_to(hu.at[yy, zz], ru.at[yy, zz])

    def back(zz, _):
        slot = zz % 2

        @pl.when(zz >= 2)
        def _():
            each(lambda m: m.wait_send(), zz - 2, slot)

        def chunk(j, _):
            f = pl.ds(pl.multiple_of(j * 256, 256), 256)
            gh = nn(br[...], wd[zz, :, f])
            g = (gh * dgl[zz, :, f].astype(F32)).astype(BF)
            bupgrad[zz, :, f] += group_sum(g.astype(F32))
            gdc = nn(brt[...], hid[zz, :, f])
            guc = nn(lowt[...], g)
            hid[zz, :, f] = g
            for cc in range(4):
                gdz[slot, cc, :, f] = gdc[cc * b:(cc + 1) * b, :].astype(BF)
                guz[slot, cc, :, f] = guc[cc * b:(cc + 1) * b, :].astype(BF)
            return 0
        lax.fori_loop(0, nb, chunk, 0)
        each(lambda m: m.start(), zz, slot)
        for yy in range(2):
            hd[yy, zz] = gdz[slot, 2 * yy + k]
            hu[yy, zz] = guz[slot, 2 * yy + k]

        @pl.when(zz >= 1)
        def _():
            fold(zz - 1)
        return 0
    lax.fori_loop(0, nz, back, 0)

    def first_grad(j, _):
        f = pl.ds(pl.multiple_of(j * 256, 256), 256)
        acc = h2[:, f]
        for zz in range(nz):
            acc = acc + nt(hid[zz], wu[zz, f, :])
        h2[:, f] = acc
        return 0
    lax.fori_loop(0, nb, first_grad, 0)
    fold(nz - 1)
    o_h = [n.local(all_of(hd), all_of(hd_o)), n.local(all_of(hu), all_of(hu_o))]

    def norm1_back(i, _):
        r = pl.ds(pl.multiple_of(i * 16, 16), 16)
        g = h2[r, :]
        xhat = h1[r, :]
        a = g * vec[1:2, :]
        m1 = jnp.sum(a, axis=1, keepdims=True) * inv
        m2 = jnp.sum(a * xhat, axis=1, keepdims=True) * inv
        g1 = rs1[r, 0:1] * (a - m1 - xhat * m2)
        g_one[r, :] = g1
        gb = g1.astype(BF)
        ga[own_slice(i * 16, 16), :] = gb
        vgrad[3] += group_sum(g * xhat)
        vgrad[4] += group_sum(g)
        vgrad[5] += group_sum(gb.astype(F32))
        return 0
    lax.fori_loop(0, own_rows // 16, norm1_back, 0, unroll=3)
    g_main = lambda: ga.at[pl.ds(pl.multiple_of(k * main, 16), main)]
    g_tail = lambda: ga.at[pl.ds(pl.multiple_of(length + k * 16, 16), 16)]
    g_k = [n.send(g_main, g_main, n.kp), n.send(g_tail, g_tail, n.kp)]
    for m in g_k:
        m.wait_recv()
    o_g = n.local(all_of(ga), all_of(ga_o))
    for m in o_s:
        m.wait_recv()
    for m in [o_x, o_w, o_m, o_l, o_g] + o_q + o_h:
        m.wait()
    for zz in range(nz - 2, nz):
        each(lambda m: m.wait_send(), zz, zz % 2)
    n.finish()

def add_to(dst, src):
    dst[...] = (dst[...].astype(F32) + src[...].astype(F32)).astype(BF)

def forward(valid, tok, mem, tch, la, lu, ld, ls, idk, idq, nz):
    b, width = lu.shape
    feats = 4 * b; length = tok.shape[2]; rows = idk.shape[0]; main = length // 2; own = main + 16
    V = lambda *s, d=BF: pltpu.VMEM(s, d)
    vm = pl.BlockSpec(memory_space=pltpu.VMEM); sm = pl.BlockSpec(memory_space=pltpu.SMEM); an = pl.BlockSpec(memory_space=pl.ANY)
    S = jax.ShapeDtypeStruct
    t3 = S((3, rows, 128), BF); h = S((2, nz, b, width), BF)
    outs = [(S((feats, length + 128), BF), an), (t3, an), (t3, an), (t3, an), (t3, an), (S((2, feats, width), BF), an), (S((rows, feats), BF), an), (h, an), (h, an),
            (S((6, 1, rows), F32), vm), (S((own, feats), F32), vm), (S((6, 8, feats), F32), vm), (S((nz, 8, width), F32), vm), (S((2, 2, own, b), BF), vm)]
    w = V(nz, feats, width)
    scratch = [V(feats, length + 128), V(rows, feats), w, w, w, V(nz, 4, *ls.shape, d=F32), V(feats, main), V(own, feats), V(3, feats, 384),
               V(3, rows, 128), V(3, rows, 128), V(3, rows, 128), V(128, rows), V(128, rows, d=F32), V(3, rows, 128), V(6, own, 128), V(3, 8, 384, d=F32), V(8, feats, d=F32), V(feats, feats),
               V(own, feats, d=F32), V(own, feats, d=F32), V(own, 128, d=F32), V(own, feats), V(feats, own), V(own, feats), V(feats, own),
               V(nz, own, width), V(nz, own, width), V(2, 4, b, width), V(2, 4, b, width)] + [V(2, nz, b, width)] * 4 + [V(rows, feats), V(4, own, b),
               pltpu.SemaphoreType.DMA((136,)), pltpu.SemaphoreType.DMA((136,)), pltpu.SemaphoreType.DMA((32,)),
               pltpu.SemaphoreType.DMA((2, 2, nz)), pltpu.SemaphoreType.DMA((2, 2, nz))]
    return pl.pallas_call(forward_kernel, out_shape=[o for o, _ in outs], out_specs=[s for _, s in outs],
        in_specs=[sm, an, an, an, an, an, an, an, vm, vm], scratch_shapes=scratch,
        compiler_params=pltpu.CompilerParams(collective_id=1, has_side_effects=True, vmem_limit_bytes=67043328))(valid, tok, mem, tch, la, lu, ld, ls, idk, idq)
class OldNet:
    def __init__(self, send_sems, recv_sems, local_sems):
        self.ss, self.rs, self.ls = send_sems, recv_sems, local_sems
        self.count, self.locals, self.sent = 0, 0, []
        self.d, self.z, self.c = (lax.axis_index(a) for a in ("dp", "row", "col"))
        self.nd, self.nz = lax.axis_size("dp"), lax.axis_size("row")
        self.y, self.k = self.c // 2, self.c % 2
        self.x = self.d % 2
        self.xp = (self.d + 1 - 2 * self.x, self.z, self.c)
        self.yp = (self.d, self.z, lax.rem(self.c + 2, 4))
        self.kp = (self.d, self.z, self.c + 1 - 2 * self.k)
        self.ykp = (self.d, self.z, 3 - self.c)
        self.zs = [lax.rem(self.z + i, self.nz) for i in range(self.nz)]
        self.zp = [(self.d, zz, self.c) for zz in self.zs]
        self.others = [(lax.rem(self.d + 2 * i, self.nd), self.z, self.c) for i in range(1, self.nd // 2)]

    def barrier(self, peers):
        b = pltpu.get_barrier_semaphore()
        for p in peers:
            pl.semaphore_signal(b, inc=1, device_id=p, device_id_type=MESH)
        pl.semaphore_wait(b, len(peers))

    def send(self, src, dst, dev):
        i = self.count
        self.count += 1
        c = pltpu.make_async_remote_copy(src_ref=src, dst_ref=dst, send_sem=self.ss.at[i], recv_sem=self.rs.at[i], device_id=dev, device_id_type=MESH)
        c.start()
        self.sent.append(c)
        return c

    def local(self, src, dst):
        c = pltpu.make_async_copy(src, dst, self.ls.at[self.locals])
        self.locals += 1
        c.start()
        return c

    def finish(self):
        for c in self.sent:
            c.wait_send()


def sum_refs(refs):
    acc = refs[0][...].astype(F32)
    for r in refs[1:]:
        acc = acc + r[...].astype(F32)
    return acc

def reduce_kernel(gu, gd, ga, gpart, g1, sv, grad4, fa, fu, fd, svo,
                  hu, hd, ha, ux, ax, uz, uy, ut, dy, dz, dx, df, ay, az, g4, gs, gr, svk, svy, svx, svz, svt, ss, rs, lsem):
    n = OldNet(ss, rs, lsem)
    n.barrier(n.zp[1:] + [n.yp, n.ykp, n.kp, n.xp] + n.others)
    nz, y, k, c, z, x = n.nz, n.y, n.k, n.c, n.z, n.x
    b = fu.shape[0]; hb = b // 2
    row = lambda cc: pl.ds(pl.multiple_of(cc * b, 16), b)
    mine = pl.ds(pl.multiple_of(x * hb, 16), hb)
    theirs = pl.ds(pl.multiple_of((1 - x) * hb, 16), hb)
    l_d = [n.local(gd, hd)]
    l_u = [n.local(gu, hu)]
    oz = pl.ds(2 * k, 2)
    a_k = [n.send(ga.at[:, row(2 * yy + 1 - k)], ha.at[yy, oz], n.kp) for yy in range(2)]
    l_a = [n.local(ga.at[:, row(2 * yy + k)], ha.at[yy, oz]) for yy in range(2)]
    s_k = n.send(sv, svk, n.kp)
    rows = g1.shape[0]; main = rows - 16
    gs[pl.ds(0, main), :] = gpart[pl.ds(pl.multiple_of((1 - k) * main, 16), main), :].astype(BF)
    gs[pl.ds(main, 16), :] = gpart[pl.ds(pl.multiple_of(2 * main + (1 - k) * 16, 16), 16), :].astype(BF)
    g_k = n.send(gs, gr, n.kp)

    def spread(src, dst):
        l = n.local(src.at[c], dst.at[y, k])
        return l, [n.send(src.at[lax.rem(c + 2, 4)], dst.at[y, k], n.yp), n.send(src.at[3 - c], dst.at[y, k], n.ykp), n.send(src.at[c + 1 - 2 * k], dst.at[y, k], n.kp)]

    for cp in l_d + l_u:
        cp.wait()
    zz = lambda i: n.zs[(nz - i) % nz]
    d_y = []
    for i in list(range(1, nz)) + [0]:
        d_y.append(n.send(hd.at[1 - y, n.zs[i]], dy.at[n.zs[i]], n.yp))
    u_x = []
    for i in list(range(1, nz)) + [0]:
        for yy in range(2):
            u_x.append(n.send(hu.at[yy, n.zs[i], theirs], ux.at[yy, n.zs[i]], n.xp))
    l_o = []
    g_k.wait_recv()

    def total(r):
        return gr[r, :].astype(F32) + g1[r, :]
    def own(i, _):
        r = pl.ds(pl.multiple_of(i * 16, 16), 16)
        src = jnp.where(i < main // 16, k * main + i * 16, 2 * main + k * 16)
        v = gpart[pl.ds(pl.multiple_of(src, 16), 16), :] + gr[r, :].astype(F32) + g1[r, :]
        for cc in range(4):
            g4[cc, r, :] = v[:, cc * b:(cc + 1) * b].astype(BF)
        return 0
    lax.fori_loop(0, rows // 16, own, 0)
    l, g_s = spread(g4, grad4)
    l_o.append(l)
    for cp in a_k:
        cp.wait_recv()
    for cp in l_a:
        cp.wait()
    a_x = []
    for yy in (0, 1):
        for i in list(range(1, nz)) + [0]:
            yv = 1 - y if yy == 0 else y
            a_x.append(n.send(ha.at[yv, n.zs[i], theirs], ax.at[yv, n.zs[i]], n.xp))
    s_k.wait_recv()
    svt[...] = sv[...] + svk[...]
    s_y = n.send(svt, svy, n.yp)
    d_z = []
    for j, i in enumerate(list(range(1, nz)) + [0]):
        d_y[j].wait_recv()
        add_to(hd.at[y, n.zs[i]], dy.at[n.zs[i]])
        if i:
            d_z.append(n.send(hd.at[y, n.zs[i]], dz.at[i], n.zp[i]))
    s_y.wait_recv()
    svo[...] = svt[...] + svy[...]
    s_x = n.send(svo, svx, n.xp)
    u_z = []
    for j, i in enumerate(list(range(1, nz)) + [0]):
        for yy in range(2):
            u_x[2 * j + yy].wait_recv()
            add_to(hu.at[yy, n.zs[i], mine], ux.at[yy, n.zs[i]])
            if i:
                u_z.append(n.send(hu.at[yy, n.zs[i], mine], uz.at[i, yy], n.zp[i]))
    a_y = []
    for j, i in enumerate(list(range(1, nz)) + [0]):
        a_x[j].wait_recv()
        add_to(ha.at[1 - y, n.zs[i], mine], ax.at[1 - y, n.zs[i]])
        a_y.append(n.send(ha.at[1 - y, n.zs[i], mine], ay.at[n.zs[i]], n.yp))
    for j, i in enumerate(list(range(1, nz)) + [0]):
        a_x[nz + j].wait_recv()
        add_to(ha.at[y, n.zs[i], mine], ax.at[y, n.zs[i]])
    for cp in d_z:
        cp.wait_recv()
    df[...] = sum_refs([hd.at[y, z]] + [dz.at[i] for i in range(1, nz)]).astype(BF)
    me = n.d
    d_d = [n.send(df, dx.at[n.d], (lax.rem(n.d + i, n.nd), n.z, n.c)) for i in range(1, n.nd)]
    l_f = n.local(df, dx.at[n.d])
    s_x.wait_recv()
    svt2 = svo[...] + svx[...]
    svz[z] = svt2
    s_z = [n.send(svz.at[z], svz.at[z], n.zp[i]) for i in range(1, nz)]
    for cp in u_z:
        cp.wait_recv()
    for yy in range(2):
        ut[yy] = sum_refs([hu.at[yy, z, mine]] + [uz.at[i, yy] for i in range(1, nz)]).astype(BF)
    u_y = n.send(ut.at[1 - y], uy, n.yp)
    a_z = []
    for j, i in enumerate(list(range(1, nz)) + [0]):
        a_y[j].wait_recv()
        add_to(ha.at[y, n.zs[i], mine], ay.at[n.zs[i]])
        if i:
            a_z.append(n.send(ha.at[y, n.zs[i], mine], az.at[i], n.zp[i]))
    u_y.wait_recv()
    fu[mine, :] = sum_refs([ut.at[y], uy]).astype(BF)
    u_f = n.send(fu.at[mine], fu.at[mine], n.xp)
    for cp in a_z:
        cp.wait_recv()
    fa[mine, :] = sum_refs([ha.at[y, z, mine]] + [az.at[i] for i in range(1, nz)]).astype(BF)
    a_f = n.send(fa.at[mine], fa.at[mine], n.xp)
    l_f.wait()
    for cp in d_d + s_z:
        cp.wait_recv()
    fd[...] = sum_refs([dx.at[i] for i in range(n.nd)])
    acc = svz[0]
    for i in range(1, nz):
        acc = acc + svz[i]
    n.finish()
    svo[...] = acc
    for cp in g_s + [u_f, a_f]:
        cp.wait_recv()
    for cp in l_o:
        cp.wait()

def reduce(gu, gd, ga, gpart, g1, sv, nz, nd):
    b, width = gu.shape[2:]
    feats = 4 * b; hb = b // 2; rows = g1.shape[0]
    V = lambda *s, d=BF: pltpu.VMEM(s, d)
    vm = pl.BlockSpec(memory_space=pltpu.VMEM); an = pl.BlockSpec(memory_space=pl.ANY)
    S = jax.ShapeDtypeStruct
    o = S((2, 2, rows, b), BF)
    w = S((b, width), BF)
    sm = lambda: V(*sv.shape, d=F32)
    return pl.pallas_call(reduce_kernel,
        out_shape=(o, w, w, S((b, width), F32), S(sv.shape, F32)),
        in_specs=[an, an, an, vm, vm, vm], out_specs=(vm,) * 5,
        scratch_shapes=[V(2, nz, b, width)] * 3 + [V(2, nz, hb, width)] * 2 + [V(nz, 2, hb, width), V(hb, width), V(2, hb, width),
            V(nz, b, width), V(nz, b, width), V(nd, b, width), V(b, width), V(nz, hb, width), V(nz, hb, width),
            V(4, rows, b), V(rows, feats), V(rows, feats), sm(), sm(), sm(), V(nz, *sv.shape, d=F32), sm(),
            pltpu.SemaphoreType.DMA((96 + nd,)), pltpu.SemaphoreType.DMA((96 + nd,)), pltpu.SemaphoreType.DMA((16,))],
        compiler_params=pltpu.CompilerParams(collective_id=2, has_side_effects=True, vmem_limit_bytes=63*2**20))(gu, gd, ga, gpart, g1, sv)

def per_device(tokens, memory, block_ids, valid, teacher, w_qkv, bias_qv, w_out, bias_out, ln1_gain, ln1_bias, w_up, bias_up, w_down, bias_down, ln2_gain, ln2_bias):
    _, b, length = tokens.shape
    nd, nz = lax.axis_size("dp"), lax.axis_size("row")
    d, z, c = (lax.axis_index(a) for a in ("dp", "row", "col"))
    y, k = c // 2, c % 2
    feats = 4 * b
    half = memory.shape[1] // 2
    main = length // 2
    rows = length + 32
    wq = w_qkv.reshape(3, b, 192)
    wo = jnp.transpose(w_out)
    la = jnp.concatenate([wq[0, :, :64], wq[1, :, :64], wq[0, :, 64:128], wq[1, :, 64:128], wq[0, :, 128:], wq[1, :, 128:], wq[2], wo[:, 128:], wo[:, :128]], axis=1)
    mem = jnp.pad(jnp.swapaxes(memory, 1, 2), ((0, 0), (0, 0), (0, 128 - 2 * half)))
    scale = (valid.shape[0] * length) / jnp.sum(valid).astype(F32)
    fv = jnp.stack([bias_out, ln1_gain, ln1_bias, bias_down, ln2_gain, ln2_bias, jnp.full((b,), scale, F32), jnp.zeros((b,), F32)])
    ls = jnp.concatenate([jnp.pad(fv, ((0, 0), (0, 256 - b))), bias_up.reshape(3, 256), jnp.pad(bias_qv.reshape(1, 384), ((0, 0), (0, 128))).reshape(2, 256), jnp.zeros((3, 256), F32)])
    ids = lax.dynamic_index_in_dim(block_ids, y, 0, keepdims=False)
    ids = jnp.concatenate([ids, jnp.full((half,), -1, jnp.int32), jnp.full((half,), length, jnp.int32), jnp.full((32 - 2 * half,), 2 * length, jnp.int32)])
    idk = jnp.broadcast_to(ids[:, None], (rows, 128))
    count = lax.dynamic_index_in_dim(valid, (d * nz + z) * 2 + y, 0)
    xt, qt, kt, vt, mixed, wown, ga, hu, hd, lse, g_one, vgrad, bupgrad, out4 = forward(count, tokens, mem, teacher, la, w_up, w_down, ls, idk, ids[None], nz)
    gpart, bgrad, gown = attn_bwd(ga, mixed, xt, qt, kt, vt, lse.reshape(3, 2, 1, rows), idk, ids[None], wown)
    bg = jnp.sum(bgrad, axis=1)[None]
    bg = jnp.where((jnp.arange(2) == k)[:, None, None], bg, 0.0).reshape(3, feats)
    sv = jnp.concatenate([jnp.sum(vgrad, axis=1), jnp.sum(bupgrad, axis=1), bg, jnp.zeros((3, feats), F32)])
    grad4, fa, fu, fd, sv = reduce(hu, hd, gown, gpart, g_one, sv, nz, nd)
    layer_out = jnp.concatenate([out4[:, 0, main:main + half], out4[:, 0, :main], out4[:, 1, :main], out4[:, 0, main + half:], out4[:, 1, main:main + 2 * half - 16]], axis=1)
    grad_tokens = grad4[:, :, :main].reshape(2, length, b).astype(F32)
    grad_memory = jnp.concatenate([grad4[:, 0, main:], grad4[:, 1, main:main + 2 * half - 16]], axis=1).astype(F32)
    fa = fa.astype(F32)
    g0 = jnp.concatenate([fa[:, 0:64], fa[:, 128:192], fa[:, 256:320]], axis=1)
    g1 = jnp.concatenate([fa[:, 64:128], fa[:, 192:256], fa[:, 320:384]], axis=1)
    grad_w_qkv = jnp.stack([g0, g1, fa[:, 384:576]]).reshape(3, b * 192)
    grad_w_out = jnp.transpose(jnp.concatenate([fa[:, 640:768], fa[:, 576:640]], axis=1))
    hb = sv[10:13].reshape(2, 3, 384)
    hb = lax.dynamic_index_in_dim(hb, z // 2, 0, keepdims=False)
    zl = z % 2
    two = lax.dynamic_index_in_dim(hb, zl, 0, keepdims=False)
    last = hb[2]
    pick = lambda r, e: jnp.concatenate([r[64 * e:64 * e + 64], r[256 + 64 * e:320 + 64 * e]])
    grad_bias_qv = jnp.stack([pick(two, 0), pick(two, 1), jnp.where(zl == 0, pick(last, 0), pick(last, 1))])
    fvec = lax.dynamic_slice_in_dim(sv[:6], c * b, b, 1)
    grad_bias_up = lax.dynamic_index_in_dim(sv[6:10], z, 0, keepdims=False)
    return (layer_out, grad_tokens, grad_memory, grad_w_qkv, grad_bias_qv, grad_w_out, fvec[5], fvec[3], fvec[4], fu.astype(F32), grad_bias_up, fd, fvec[2], fvec[0], fvec[1])

def solution(mesh):
    rows, feat = ("dp", "row"), "col"
    in_specs = (P(rows, feat, None), P(rows, None, feat), P(rows, None), P(), P(rows, feat, None), P("row", feat), P("row", None), P("row", feat), P(feat), P(feat), P(feat), P(feat, "row"), P("row"), P(feat, "row"), P(feat), P(feat), P(feat))
    out_specs = (P(rows, None, feat), P(rows, None, feat), P(rows, None, feat), P("row", feat), P("row", None), P("row", feat), P(feat), P(feat), P(feat), P(feat, "row"), P("row"), P(feat, "row"), P(feat), P(feat), P(feat))
    return jax.shard_map(per_device, mesh=mesh, in_specs=in_specs, out_specs=out_specs, check_vma=False)
```

```python
import jax
import jax.numpy as jnp
from jax import lax
from jax.experimental import pallas as pl
from jax.experimental.pallas import tpu as pltpu
from jax.sharding import PartitionSpec as P
BF=jnp.bfloat16; F32=jnp.float32
EPSILON=1e-12
CH=48

def nn(a,b): return lax.dot_general(a,b,(((1,),(0,)),((),())),preferred_element_type=F32)
def nt(a,b): return lax.dot_general(a,b,(((1,),(1,)),((),())),preferred_element_type=F32)

def gelu_pair(v):
    t = pl.reciprocal(1.0 + (0.3275911 * 0.7071067811865476) * jnp.abs(v))
    poly = t * (0.5*0.254829592 + t * (-0.5*0.284496736 + t * (0.5*1.421413741 + t * (-0.5*1.453152027 + t * (0.5*1.061405429)))))
    e = jnp.exp(-0.5 * v * v)
    half = poly * e
    cdf = jnp.where(v >= 0.0, 1.0 - half, half)
    return v * cdf, cdf + v * (e * 0.3989422804014327)

def group_sum(v):
    rows = v.shape[0]
    return jnp.sum(v.reshape(rows // 8, 8, v.shape[1]), axis=0)

def mlp_kernel(half_ref, valid_ref, mixed, x, teach, vec, bup, wa_hbm, wu_hbm, wd_hbm,
               out, g_one, g_attn, vgrad, bupgrad, gu_hbm, gd_hbm,
               tr, wraw, wt, wu, wd, h1, h2, rs1, low, lowt, brt, br, hid, dgl, gg, gu, gd, sem):
    rows, feats = x.shape
    zs = wu.shape[0]
    nb = feats // 256
    copies_a = [pltpu.make_async_copy(wa_hbm.at[z, :, pl.ds(512, 256)], wraw.at[z], sem.at[z]) for z in range(zs)]
    copies_u = [pltpu.make_async_copy(wu_hbm.at[z], wu.at[z], sem.at[zs + z]) for z in range(zs)]
    copies_d = [pltpu.make_async_copy(wd_hbm.at[z], wd.at[z], sem.at[2 * zs + z]) for z in range(zs)]
    for c in copies_a + copies_u + copies_d:
        c.start()
    for c in copies_a:
        c.wait()
    main = teach.shape[1]
    for i in range(main // 128):
        tr[pl.ds(128 * i, 128), :] = teach[:, pl.ds(128 * i, 128)].T
    tr[pl.ds(main, rows - main), :] = jnp.zeros((rows - main, feats), BF)
    low_lane = lax.broadcasted_iota(jnp.int32, (feats, 128), 1) < 64
    for k in range(zs // 2):
        z0, z1 = 2 * k, 2 * k + 1
        wt[:, pl.ds(384 * k, 128)] = wraw[z0, :, pl.ds(128, 128)]
        wt[:, pl.ds(384 * k + 128, 128)] = wraw[z1, :, pl.ds(128, 128)]
        t0 = pltpu.roll(wraw[z0, :, pl.ds(0, 128)].astype(F32), 64, 1)
        t1 = wraw[z1, :, pl.ds(0, 128)].astype(F32)
        wt[:, pl.ds(384 * k + 256, 128)] = jnp.where(low_lane, t0, t1).astype(BF)
    for n in range(nb):
        f = pl.ds(256 * n, 256)
        h1[:, f] = nt(mixed[...], wt[f, :]) + x[:, f].astype(F32) + vec[0:1, f]
    inv = 1.0 / feats

    vgrad[...] = jnp.zeros_like(vgrad)
    bupgrad[...] = jnp.zeros_like(bupgrad)

    def norm1(i, _):
        r = pl.ds(pl.multiple_of(i * CH, 16), CH)
        h = h1[r, :]
        m = jnp.sum(h, axis=1, keepdims=True) * inv
        s = jnp.sum(h * h, axis=1, keepdims=True) * inv
        rstd = lax.rsqrt(s - m * m + EPSILON)
        xhat = (h - m) * rstd
        h1[r, :] = xhat
        rs1[r, :] = jnp.broadcast_to(rstd, (CH, 128))
        low[r, :] = (xhat * vec[1:2, :] + vec[2:3, :]).astype(BF)
        return 0
    lax.fori_loop(0, rows // CH, norm1, 0)
    lowt[...] = low[...].T
    for c in copies_u:
        c.wait()

    def gate(i, _):
        z = i // nb
        f = pl.ds(pl.multiple_of((i % nb) * 256, 256), 256)
        v = nn(low[...], wu[z, :, f]) + bup[z, :, f]
        a, b = gelu_pair(v)
        hid[z, :, f] = a.astype(BF)
        dgl[z, :, f] = b
        return 0
    lax.fori_loop(0, zs * nb, gate, 0)
    for c in copies_d:
        c.wait()

    def down(n, _):
        f = pl.ds(pl.multiple_of(n * 256, 256), 256)
        acc = nt(hid[0], wd[0, f, :])
        for z in range(1, zs):
            acc = acc + nt(hid[z], wd[z, f, :])
        h2[:, f] = acc
        return 0
    lax.fori_loop(0, nb, down, 0)
    scale = vec[6:7, 0:1]
    first = half_ref[0] * main

    def norm2(i, _):
        r = pl.ds(pl.multiple_of(i * CH, 16), CH)
        h = h2[r, :] + (h1[r, :] * vec[1:2, :] + vec[2:3, :]) + vec[3:4, :]
        m = jnp.sum(h, axis=1, keepdims=True) * inv
        s = jnp.sum(h * h, axis=1, keepdims=True) * inv
        rstd = lax.rsqrt(s - m * m + EPSILON)
        xhat = (h - m) * rstd
        o = xhat * vec[4:5, :] + vec[5:6, :]
        out[r, :] = o.astype(BF)
        place = lax.broadcasted_iota(jnp.int32, (CH, 1), 0) + i * CH
        place = jnp.where(place < main, place + first, valid_ref[0])
        go = jnp.where(place < valid_ref[0], scale * (o - tr[r, :].astype(F32)), 0.0)
        a = go * vec[4:5, :]
        m1 = jnp.sum(a, axis=1, keepdims=True) * inv
        m2 = jnp.sum(a * xhat, axis=1, keepdims=True) * inv
        g2 = rstd * (a - m1 - xhat * m2)
        h2[r, :] = g2
        b = g2.astype(BF)
        br[r, :] = b
        vgrad[0] += group_sum(go * xhat)
        vgrad[1] += group_sum(go)
        vgrad[2] += group_sum(b.astype(F32))
        return 0
    lax.fori_loop(0, rows // CH, norm2, 0)
    brt[...] = br[...].T

    def back(i, _):
        z = i // nb
        f = pl.ds(pl.multiple_of((i % nb) * 256, 256), 256)
        gh = nn(br[...], wd[z, :, f])
        g = (gh * dgl[z, :, f]).astype(BF)
        gg[z, :, f] = g
        bupgrad[z, :, f] += group_sum(g.astype(F32))
        gd[z, :, f] = nn(brt[...], hid[z, :, f]).astype(BF)
        gu[z, :, f] = nn(lowt[...], g).astype(BF)
        return 0
    lax.fori_loop(0, zs * nb, back, 0)
    outs = [pltpu.make_async_copy(gd, gd_hbm, sem.at[0]), pltpu.make_async_copy(gu, gu_hbm, sem.at[1])]
    for c in outs:
        c.start()

    def first_grad(n, _):
        f = pl.ds(pl.multiple_of(n * 256, 256), 256)
        acc = h2[:, f]
        for z in range(zs):
            acc = acc + nt(gg[z], wu[z, f, :])
        h2[:, f] = acc
        return 0
    lax.fori_loop(0, nb, first_grad, 0)

    def norm1_back(i, _):
        r = pl.ds(pl.multiple_of(i * CH, 16), CH)
        g = h2[r, :]
        xhat = h1[r, :]
        a = g * vec[1:2, :]
        m1 = jnp.sum(a, axis=1, keepdims=True) * inv
        m2 = jnp.sum(a * xhat, axis=1, keepdims=True) * inv
        g1 = rs1[r, 0:1] * (a - m1 - xhat * m2)
        g_one[r, :] = g1
        b = g1.astype(BF)
        g_attn[r, :] = b
        vgrad[3] += group_sum(g * xhat)
        vgrad[4] += group_sum(g)
        vgrad[5] += group_sum(b.astype(F32))
        return 0
    lax.fori_loop(0, rows // CH, norm1_back, 0)
    for c in outs:
        c.wait()

def mlp(half, valid, mixed, x, teach, vec, bup, wa, wu, wd):
    rows, feats = x.shape; zs = wu.shape[0]
    V = lambda *s, d=BF: pltpu.VMEM(s, d)
    vm = pl.BlockSpec(memory_space=pltpu.VMEM); sm = pl.BlockSpec(memory_space=pltpu.SMEM); an = pl.BlockSpec(memory_space=pl.ANY)
    S = jax.ShapeDtypeStruct
    return pl.pallas_call(mlp_kernel,
        out_shape=(S((rows,feats),BF),S((rows,feats),F32),S((rows,feats),BF),S((6,8,feats),F32),S((zs,8,feats),F32),S(wu.shape,BF),S(wd.shape,BF)),
        in_specs=[sm,sm,vm,vm,vm,vm,vm,an,an,an],
        out_specs=(vm,vm,vm,vm,vm,an,an),
        scratch_shapes=[V(rows,feats),V(zs,feats,256),V(feats,feats),V(*wu.shape),V(*wd.shape),V(rows,feats,d=F32),V(rows,feats,d=F32),V(rows,128,d=F32),V(rows,feats),
            V(feats,rows),V(feats,rows),V(rows,feats),V(zs,rows,feats),V(zs,rows,feats,d=F32),V(zs,rows,feats),V(*wu.shape),V(*wd.shape),pltpu.SemaphoreType.DMA((3*zs,))],
        compiler_params=pltpu.CompilerParams(vmem_limit_bytes=63*2**20),
    )(half,valid,mixed,x,teach,vec,bup,wa,wu,wd)
NEG=-1e30
def tn_lanes(): return lax.broadcasted_iota(jnp.int32,(1,128),1)

def assemble_pairs(w, wp, feats):
    lo = lax.broadcasted_iota(jnp.int32, (feats, 128), 1) < 64
    wp[0] = w[0, :, pl.ds(0, 384)]
    wp[1] = w[1, :, pl.ds(0, 384)]
    a0, a1 = w[0, :, pl.ds(384, 128)].astype(F32), w[1, :, pl.ds(384, 128)].astype(F32)
    wp[2, :, pl.ds(0, 128)] = jnp.where(lo, a0, pltpu.roll(a1, 64, 1)).astype(BF)
    wp[2, :, pl.ds(128, 128)] = jnp.where(lo, pltpu.roll(a0, 64, 1), a1).astype(BF)
    b0, b1 = w[0, :, pl.ds(512, 128)].astype(F32), w[1, :, pl.ds(512, 128)].astype(F32)
    wp[2, :, pl.ds(256, 128)] = jnp.where(lo, b0, pltpu.roll(b1, 64, 1)).astype(BF)

def tiles(rows, length):
    mem = (length, rows - length, True)
    out = []
    for a in range(0, length, 256):
        spans = []
        if a:
            spans.append((0, a, False))
        spans.append((a, min(512, length - a), True))
        out.append((a, 256, spans + [mem]))
    out.append((length, rows - length, [(0, length, True), mem]))
    return out

def scores_of(kt, qm, idk, idq, p, spans):
    out = []
    for k0, kn, masked in spans:
        s = nt(kt[p, pl.ds(k0, kn), :], qm)
        if masked:
            s = jnp.where(idk[pl.ds(k0, kn), 0:1] <= idq, s, NEG)
        out.append(s)
    return out

def attn_fwd_kernel(xt, wa_hbm, bias, idk, idq, x, qt, kt, vt, mixed, lse, w, wp, vtt, ot, sem):
    feats = xt.shape[0]; rows = x.shape[0]; length = xt.shape[1] - 128
    c = pltpu.make_async_copy(wa_hbm, w, sem); c.start()
    for i in range(length // 128):
        x[pl.ds(128 * i, 128), :] = xt[:, pl.ds(128 * i, 128)].T
    x[pl.ds(length, rows - length), :] = xt[:, pl.ds(length, 128)].T[: rows - length, :]
    c.wait()
    assemble_pairs(w, wp, feats)
    rc = rows // 3

    def project(i, _):
        p = i // 3
        r = pl.ds(pl.multiple_of((i % 3) * rc, 16), rc)
        v = nn(x[r, :], wp[p]) + bias[p]
        qt[p, r, :] = (v[:, :128].astype(BF).astype(F32) * 0.125).astype(BF)
        kt[p, r, :] = v[:, 128:256].astype(BF)
        vt[p, r, :] = v[:, 256:].astype(BF)
        return 0
    lax.fori_loop(0, 9, project, 0)

    def pair(p, _):
        vtt[...] = vt[p].T
        for e in range(2):
            lanes = (tn_lanes() < 64) if e == 0 else (tn_lanes() >= 64)
            for q0, qn, spans in tiles(rows, length):
                q = qt[p, pl.ds(q0, qn), :]
                qm = jnp.where(lanes, q, jnp.zeros_like(q))
                ss = scores_of(kt, qm, idk, idq[0:1, pl.ds(q0, qn)], p, spans)
                m = jnp.max(ss[0], axis=0, keepdims=True)
                for s in ss[1:]:
                    m = jnp.maximum(m, jnp.max(s, axis=0, keepdims=True))
                tot, acc = None, None
                for s, (k0, kn, _) in zip(ss, spans):
                    ex = jnp.exp(s - m)
                    t = jnp.sum(ex, axis=0, keepdims=True)
                    o = nn(vtt[pl.ds(64 * e, 64), pl.ds(k0, kn)], ex.astype(BF))
                    tot = t if tot is None else tot + t
                    acc = o if acc is None else acc + o
                ot[pl.ds(64 * e, 64), pl.ds(q0, qn)] = acc / tot
                lse[p, e, :, pl.ds(q0, qn)] = m + jnp.log(tot)
        mixed[p] = ot[...].T.astype(BF)
        return 0
    lax.fori_loop(0, 3, pair, 0)

def attn_fwd(xt, wa, bias, idk, idq, rows):
    feats = xt.shape[0]
    V = lambda *s, d=BF: pltpu.VMEM(s, d)
    vm = pl.BlockSpec(memory_space=pltpu.VMEM); an = pl.BlockSpec(memory_space=pl.ANY)
    S = jax.ShapeDtypeStruct
    t3 = S((3, rows, 128), BF)
    return pl.pallas_call(attn_fwd_kernel,
        out_shape=(S((rows, feats), BF), t3, t3, t3, t3, S((3, 2, 1, rows), F32)),
        in_specs=[vm, an, vm, vm, vm], out_specs=(vm,) * 6,
        scratch_shapes=[V(*wa.shape), V(3, feats, 384), V(128, rows), V(128, rows, d=F32), pltpu.SemaphoreType.DMA],
        compiler_params=pltpu.CompilerParams(vmem_limit_bytes=63*2**20))(xt, wa, bias, idk, idq)

def attn_bwd_kernel(ga, mixed, xt, qt, kt, vt, lse, idk, idq, wa_hbm, gpart, bgrad, gown_hbm, w, wp, wt, gat, gm, gp, dv, dk, dqt, ktt, dd, ro, gown, sem):
    feats = xt.shape[0]; rows = ga.shape[0]; length = xt.shape[1] - 128
    c = pltpu.make_async_copy(wa_hbm, w, sem); c.start()
    gat[...] = ga[...].T
    c.wait()
    assemble_pairs(w, wp, feats)
    wt[:, pl.ds(0, 128)] = w[0, :, pl.ds(640, 128)]
    wt[:, pl.ds(128, 128)] = w[1, :, pl.ds(640, 128)]
    lo = lax.broadcasted_iota(jnp.int32, (feats, 128), 1) < 64
    wt[:, pl.ds(256, 128)] = jnp.where(lo, pltpu.roll(w[0, :, pl.ds(512, 128)].astype(F32), 64, 1), w[1, :, pl.ds(512, 128)].astype(F32)).astype(BF)
    for p in range(3):
        gm[p] = nn(ga[...], wt[:, pl.ds(128 * p, 128)]).astype(BF)

    def pair(p, _):
        ktt[...] = kt[p].T
        prod = (gm[p].astype(F32) * mixed[p].astype(F32)).T
        dd[0:1, :] = jnp.sum(prod[:64, :], axis=0, keepdims=True)
        dd[1:2, :] = jnp.sum(prod[64:, :], axis=0, keepdims=True)
        dv[...] = jnp.zeros_like(dv)
        dk[...] = jnp.zeros_like(dk)
        for e in range(2):
            lanes = (tn_lanes() < 64) if e == 0 else (tn_lanes() >= 64)
            for q0, qn, spans in tiles(rows, length):
                q = qt[p, pl.ds(q0, qn), :]
                qm = jnp.where(lanes, q, jnp.zeros_like(q))
                g = gm[p, pl.ds(q0, qn), :]
                gmm = jnp.where(lanes, g, jnp.zeros_like(g))
                ss = scores_of(kt, qm, idk, idq[0:1, pl.ds(q0, qn)], p, spans)
                l = lse[p, e, :, pl.ds(q0, qn)]
                d = dd[pl.ds(e, 1), pl.ds(q0, qn)]
                acc = None
                for s, (k0, kn, _) in zip(ss, spans):
                    pr = jnp.exp(s - l)
                    dp = nt(vt[p, pl.ds(k0, kn), :], gmm)
                    ds = (pr * (dp - d)).astype(BF)
                    dv[pl.ds(k0, kn), :] += nn(pr.astype(BF), gmm)
                    dk[pl.ds(k0, kn), :] += nn(ds, qm)
                    o = nn(ktt[pl.ds(64 * e, 64), pl.ds(k0, kn)], ds)
                    acc = o if acc is None else acc + o
                dqt[pl.ds(64 * e, 64), pl.ds(q0, qn)] = acc * 0.125
        gp[p, :, pl.ds(0, 128)] = dqt[...].T.astype(BF)
        gp[p, :, pl.ds(128, 128)] = dk[...].astype(BF)
        gp[p, :, pl.ds(256, 128)] = dv[...].astype(BF)
        return 0
    lax.fori_loop(0, 3, pair, 0)
    for p in range(3):
        bgrad[p] = group_sum(gp[p].astype(F32))
    r3 = rows // 3

    def rowsgrad(i, _):
        r = pl.ds(pl.multiple_of(i * r3, 16), r3)
        gpart[r, :] = nt(gp[0, r, :], wp[0]) + nt(gp[1, r, :], wp[1]) + nt(gp[2, r, :], wp[2])
        return 0
    lax.fori_loop(0, 3, rowsgrad, 0)
    fc = 256
    for f0 in range(0, feats, fc):
        f = pl.ds(f0, fc)
        xf = xt[f, pl.ds(0, rows)]
        af = gat[f, :]
        r0 = nn(xf, gp[0]); r1 = nn(xf, gp[1]); r2 = nn(xf, gp[2])
        o = [nn(af, mixed[p]) for p in range(3)]
        lo = lax.broadcasted_iota(jnp.int32, (fc, 128), 1) < 64
        rq, rk, rv = r2[:, :128], r2[:, 128:256], r2[:, 256:]
        sw = lambda a: pltpu.roll(a, 64, 1)
        gown[0, f, pl.ds(0, 384)] = r0.astype(BF)
        gown[1, f, pl.ds(0, 384)] = r1.astype(BF)
        gown[0, f, pl.ds(384, 128)] = jnp.where(lo, rq, sw(rk)).astype(BF)
        gown[1, f, pl.ds(384, 128)] = jnp.where(lo, sw(rq), rk).astype(BF)
        gown[0, f, pl.ds(512, 128)] = jnp.where(lo, rv, sw(o[2])).astype(BF)
        gown[1, f, pl.ds(512, 128)] = jnp.where(lo, sw(rv), o[2]).astype(BF)
        gown[0, f, pl.ds(640, 128)] = o[0].astype(BF)
        gown[1, f, pl.ds(640, 128)] = o[1].astype(BF)
    c = pltpu.make_async_copy(gown, gown_hbm, sem); c.start(); c.wait()

def attn_bwd(ga, mixed, xt, qt, kt, vt, lse, idk, idq, wa):
    feats = xt.shape[0]; rows = ga.shape[0]
    V = lambda *s, d=BF: pltpu.VMEM(s, d)
    vm = pl.BlockSpec(memory_space=pltpu.VMEM); an = pl.BlockSpec(memory_space=pl.ANY)
    S = jax.ShapeDtypeStruct
    return pl.pallas_call(attn_bwd_kernel,
        out_shape=(S((rows, feats), F32), S((3, 8, 384), F32), S(wa.shape, BF)),
        in_specs=[vm] * 9 + [an], out_specs=(vm, vm, an),
        scratch_shapes=[V(*wa.shape), V(3, feats, 384), V(feats, 384), V(feats, rows), V(3, rows, 128), V(3, rows, 384), V(rows, 128, d=F32), V(rows, 128, d=F32),
            V(128, rows, d=F32), V(128, rows), V(8, rows, d=F32), V(8, 128), V(*wa.shape), pltpu.SemaphoreType.DMA],
        compiler_params=pltpu.CompilerParams(vmem_limit_bytes=63*2**20))(ga, mixed, xt, qt, kt, vt, lse, idk, idq, wa)
MESH = pl.DeviceIdType.MESH

class Move:
    def __init__(self, net, src, dst, dev, index):
        self.net, self.src, self.dst, self.dev, self.index = net, src, dst, dev, index
    def make(self):
        return pltpu.make_async_remote_copy(src_ref=self.src(), dst_ref=self.dst(), send_sem=self.net.ss.at[self.index],
                                            recv_sem=self.net.rs.at[self.index], device_id=self.dev, device_id_type=MESH)
    def start(self):
        self.make().start()
    def wait_recv(self):
        self.make().wait_recv()
    def wait_send(self):
        self.make().wait_send()

class Copy:
    def __init__(self, net, src, dst, index):
        self.net, self.src, self.dst, self.index = net, src, dst, index
    def make(self):
        return pltpu.make_async_copy(self.src(), self.dst(), self.net.ls.at[self.index])
    def start(self):
        self.make().start()
    def wait(self):
        self.make().wait()

class Net:
    def __init__(self, send_sems, recv_sems, local_sems):
        self.ss, self.rs, self.ls = send_sems, recv_sems, local_sems
        self.count, self.locals, self.moves, self.copies = 0, 0, [], []
        self.d, self.z, self.c = (lax.axis_index(a) for a in ("dp", "row", "col"))
        self.nd, self.nz = lax.axis_size("dp"), lax.axis_size("row")
        self.y, self.k = self.c // 2, self.c % 2
        self.x = self.d % 2
        self.oc = lax.rem(self.c + 2, 4)
        self.xp = (self.d + 1 - 2 * self.x, self.z, self.c)
        self.yp = (self.d, self.z, self.oc)
        self.kp = (self.d, self.z, self.c + 1 - 2 * self.k)
        self.ykp = (self.d, self.z, 3 - self.c)
        self.zs = [lax.rem(self.z + i, self.nz) for i in range(self.nz)]
        self.zp = [(self.d, zz, self.c) for zz in self.zs]
        self.others = [(lax.rem(self.d + 2 * i, self.nd), self.z, self.c) for i in range(1, self.nd // 2)]
    def from_row(self, i):
        return self.zs[(self.nz - i) % self.nz]
    def barrier(self, peers):
        b = pltpu.get_barrier_semaphore()
        for p in peers:
            pl.semaphore_signal(b, inc=1, device_id=p, device_id_type=MESH)
        pl.semaphore_wait(b, len(peers))
    def move(self, src, dst, dev):
        m = Move(self, src, dst, dev, self.count)
        self.count += 1
        self.moves.append(m)
        return m
    def send(self, src, dst, dev):
        m = self.move(src, dst, dev)
        m.start()
        return m
    def copy(self, src, dst):
        m = Copy(self, src, dst, self.locals)
        self.locals += 1
        self.copies.append(m)
        return m
    def local(self, src, dst):
        m = self.copy(src, dst)
        m.start()
        return m
    def finish(self):
        for m in self.moves:
            m.wait_send()

def at(i, table):
    for j, events in table.items():
        if events:
            @pl.when(i == j)
            def _(events=events):
                for e in events:
                    e()

def spread_events(events, steps):
    table = {}
    for n, e in enumerate(events):
        table.setdefault(n * steps // len(events), []).append(e)
    return table

def join192(t, dst):
    lo = lax.broadcasted_iota(jnp.int32, t[0][0].shape, 1) < 64
    sw = lambda a: pltpu.roll(a, 64, 1)
    for h in range(2):
        a, b = t[2 * h], t[2 * h + 1]
        dst[:, pl.ds(384 * h, 128)] = a[0]
        dst[:, pl.ds(384 * h + 128, 128)] = jnp.where(lo, a[1], sw(b[0]))
        dst[:, pl.ds(384 * h + 256, 128)] = jnp.where(lo, sw(b[0]), sw(b[1]))

def forward_kernel(valid_ref, tok, mem, tch, la, lu, ld, ls, idk, idq,
                   xt_o, q_o, k_o, v_o, mixed_o, wa_o, ga_o, hu_o, hd_o, lse, g_one, vgrad, bupgrad, out4,
                   xt, x, wa, wu, wd, sm, tt, tr, wp, qt, kt, vt, vtt, ot, mixed, mrows, bias, vec, wt,
                   h1, h2, rs1, low, lowt, br, brt, hid, dgl, gdz, guz, hu, hd, ru, rd, ga, o4, ss, rs, lsem, zsem, zrem):
    n = Net(ss, rs, lsem)
    n.barrier(n.zp[1:] + [n.yp, n.ykp, n.kp, n.xp])
    nz, y, k, c, z, oc = n.nz, n.y, n.k, n.c, n.z, n.oc
    b = la.shape[0]; hb = b // 2
    feats = x.shape[1]; rows = x.shape[0]; length = tok.shape[2]; main = length // 2
    own_rows = main + 16
    row = lambda cc, off=0, num=b: pl.ds(pl.multiple_of(cc * b + off, 16), num)
    blk = lambda w, zz, cc: (lambda: w.at[zz, row(cc)])
    hlf = lambda w, zz, cc, h: (lambda: w.at[zz, row(cc, h * hb, hb)])
    mine, theirs = n.x, 1 - n.x
    part = lambda w: (lambda: w.at[pl.ds(pl.multiple_of(n.x * hb, 16), hb)])
    all_of = lambda r: (lambda: r)
    tail = pl.ds(length, 128); body = pl.ds(0, length)
    fz = n.from_row
    R = range(1, nz)
    local = [n.local(lambda: tok.at[y], lambda: xt.at[row(c), body]), n.local(lambda: mem.at[y], lambda: xt.at[row(c), tail])]
    s_blk = lambda zz, cc: (lambda: sm.at[zz, cc])
    a_z = [n.send(part(la), hlf(wa, z, c, mine), n.zp[i]) for i in R]
    s_z = [n.send(all_of(ls), s_blk(z, c), n.zp[i]) for i in R]
    a_y = [n.send(part(la), hlf(wa, z, c, mine), n.yp)]
    t_y = [n.send(lambda: tok.at[1 - y], lambda: xt.at[row(c), body], n.yp), n.send(lambda: mem.at[1 - y], lambda: xt.at[row(c), tail], n.yp)]
    s_y = [n.send(all_of(ls), s_blk(z, c), n.yp)]
    u_y = n.send(part(lu), hlf(wu, z, c, mine), n.yp)
    s_k = [n.send(all_of(ls), s_blk(z, c), n.kp)]
    t_k = [n.send(lambda: tok.at[y], lambda: xt.at[row(c), body], n.kp), n.send(lambda: mem.at[y], lambda: xt.at[row(c), tail], n.kp)]
    a_k = [n.send(all_of(la), blk(wa, z, c), n.kp)]
    for w, l in ((wa, la), (wu, lu), (wd, ld)):
        local.append(n.local(all_of(l), blk(w, z, c)))
    local.append(n.local(all_of(ls), s_blk(z, c)))
    fwd = lambda u, dev: n.move(u, u, dev)
    a_x = []
    for i in R:
        a_z[i - 1].wait_recv()
        u = hlf(wa, fz(i), c, mine)
        for lst, dev in ((a_y, n.yp), (a_x, n.xp), (a_k, n.kp)):
            lst.append(fwd(u, dev)); lst[-1].start()
        s_z[i - 1].wait_recv()
        u = s_blk(fz(i), c)
        for lst, dev in ((s_y, n.yp), (s_k, n.kp)):
            lst.append(fwd(u, dev)); lst[-1].start()
    u_z = [n.send(part(lu), hlf(wu, z, c, mine), n.zp[i]) for i in R]
    u_k = [n.send(all_of(lu), blk(wu, z, c), n.kp)]
    u_y.wait_recv()
    uo = hlf(wu, z, oc, mine)
    u_z2 = [fwd(uo, n.zp[i]) for i in R]
    for m in u_z2:
        m.start()
    u_x = [fwd(uo, n.xp)]
    u_k.append(fwd(uo, n.kp)); u_k[-1].start()
    for m, w_ in zip(t_y, (body, tail)):
        m.wait_recv()
        t_k.append(fwd((lambda w_=w_: xt.at[row(oc), w_]), n.kp)); t_k[-1].start()
    for i in range(nz):
        a_y[i].wait_recv()
        u = hlf(wa, fz(i), oc, mine)
        for lst, dev in ((a_x, n.xp), (a_k, n.kp)):
            lst.append(fwd(u, dev)); lst[-1].start()
        s_y[i].wait_recv()
        u = s_blk(fz(i), oc)
        s_k.append(fwd(u, n.kp)); s_k[-1].start()
    u_x[0].start()
    d_z = [n.send(all_of(ld), blk(wd, z, c), n.zp[i]) for i in R]
    d_y = [n.send(all_of(ld), blk(wd, z, c), n.yp)]
    d_k = [n.send(all_of(ld), blk(wd, z, c), n.kp)]
    tsl = lambda s, kk: (lambda: tch.at[s, :, pl.ds(pl.multiple_of(kk * main, 128), main)])
    th = lambda: tt.at[row(c)]
    h_y = [n.send(tsl(y, 1 - k), th, n.kp)]
    local.append(n.local(tsl(y, k), th))
    local[0].wait(); local[1].wait()
    for m in t_k:
        m.wait_recv()
    def turn(i, _):
        f = pl.ds(pl.multiple_of(128 * i, 128), 128)
        x[f, :] = xt[:, f].T
        return 0
    lax.fori_loop(0, length // 128, turn, 0)
    x[pl.ds(length, rows - length), :] = xt[:, tail].T[: rows - length, :]
    o_x = n.local(all_of(xt), all_of(xt_o))
    order = [(i, c) for i in R] + [(i, oc) for i in range(nz)]
    for m, (i, cc) in zip(a_x, order):
        m.wait_recv()
        a_k.append(fwd(hlf(wa, fz(i), cc, theirs), n.kp)); a_k[-1].start()
    h_y += [n.send(tsl(1 - y, k), th, n.yp), n.send(tsl(1 - y, 1 - k), th, n.ykp)]
    events = []
    def relay(wait, u, pairs):
        ms = []
        for lst, dev in pairs:
            m = fwd(u, dev)
            lst.append(m)
            ms.append(m)
        def run():
            wait()
            for m in ms:
                m.start()
        events.append(run)
    for i in R:
        relay(u_z[i - 1].wait_recv, hlf(wu, fz(i), c, mine), ((u_x, n.xp), (u_k, n.kp)))
    for i in R:
        relay(u_z2[i - 1].wait_recv, hlf(wu, fz(i), oc, mine), ((u_x, n.xp), (u_k, n.kp)))
    u_order = [(0, oc)] + [(i, c) for i in R] + [(i, oc) for i in R]
    u_units = list(zip(u_x, u_order))
    for i in R:
        relay(d_z[i - 1].wait_recv, blk(wd, fz(i), c), ((d_y, n.yp), (d_k, n.kp)))
    for m, (i, cc) in u_units:
        relay(m.wait_recv, hlf(wu, fz(i), cc, theirs), ((u_k, n.kp),))
    u_events, d_events = events, []
    events = []
    for i in range(nz):
        relay(d_y[i].wait_recv, blk(wd, fz(i), oc), ((d_k, n.kp),))
    d_events = events
    for m in s_k:
        m.wait_recv()
    for m in local[2:6]:
        m.wait()
    join192([[sm[0, cc, pl.ds(0, 8), pl.ds(0, 128)], sm[0, cc, pl.ds(0, 8), pl.ds(128, 128)]] for cc in range(4)], vec)
    lo1 = lax.broadcasted_iota(jnp.int32, (1, 128), 1) < 64
    sw = lambda a: pltpu.roll(a, 64, 1)
    bias[...] = jnp.zeros_like(bias)
    hv = [[sm[2 * k + j, 0, 11:12, pl.ds(0, 128)], sm[2 * k + j, 0, 11:12, pl.ds(128, 128)], sm[2 * k + j, 0, 12:13, pl.ds(0, 128)]] for j in range(2)]
    for p, (e0, e1) in enumerate(((hv[0][0], hv[0][1]), (hv[1][0], hv[1][1]), (hv[0][2], hv[1][2]))):
        w8 = lambda a: jnp.broadcast_to(a, (8, 128))
        lo8 = lax.broadcasted_iota(jnp.int32, (8, 128), 1) < 64
        bias[p, :, pl.ds(0, 128)] = jnp.where(lo8, w8(e0), sw(w8(e1)))
        bias[p, :, pl.ds(256, 128)] = jnp.where(lo8, sw(w8(e0)), w8(e1))
    for m in a_k:
        m.wait_recv()
    own = pl.ds(2 * k, 2)
    o_w = n.local(lambda: wa.at[own], all_of(wa_o))
    w = wa.at[own]
    assemble_pairs(w, wp, feats)
    rc = rows // 3
    ev = spread_events(u_events[:6], 9)

    def project(i, _):
        p = i // 3
        r = pl.ds(pl.multiple_of((i % 3) * rc, 16), rc)
        v = nn(x[r, :], wp[p]) + bias[p, 0:1, :]
        qt[p, r, :] = (v[:, :128].astype(BF).astype(F32) * 0.125).astype(BF)
        kt[p, r, :] = v[:, 128:256].astype(BF)
        vt[p, r, :] = v[:, 256:].astype(BF)
        at(i, ev)
        return 0
    lax.fori_loop(0, 9, project, 0)
    o_q = [n.local(all_of(a), all_of(o)) for a, o in ((qt, q_o), (kt, k_o), (vt, v_o))]
    m_k = [(n.move((lambda p=p: mixed.at[p, pl.ds(pl.multiple_of((1 - k) * main, 16), main)]), (lambda p=p: mrows.at[k * 3 + p, pl.ds(0, main)]), n.kp),
            n.move((lambda p=p: mixed.at[p, pl.ds(pl.multiple_of(length + (1 - k) * 16, 16), 16)]), (lambda p=p: mrows.at[k * 3 + p, pl.ds(main, 16)]), n.kp)) for p in range(3)]
    m_l = [(n.copy((lambda p=p: mixed.at[p, pl.ds(pl.multiple_of(k * main, 16), main)]), (lambda p=p: mrows.at[k * 3 + p, pl.ds(0, main)])),
            n.copy((lambda p=p: mixed.at[p, pl.ds(pl.multiple_of(length + k * 16, 16), 16)]), (lambda p=p: mrows.at[k * 3 + p, pl.ds(main, 16)]))) for p in range(3)]
    ev = spread_events(u_events[6:], 6)

    def head(i, _):
        p = i // 2
        e = i % 2
        he = pl.ds(pl.multiple_of(64 * e, 64), 64)

        @pl.when(e == 0)
        def _():
            vtt[...] = vt[p].T
        lanes = (lax.broadcasted_iota(jnp.int32, (1, 128), 1) // 64) == e
        for q0, qn, spans in tiles(rows, length):
            q = qt[p, pl.ds(q0, qn), :]
            qm = jnp.where(lanes, q, jnp.zeros_like(q))
            sc = scores_of(kt, qm, idk, idq[0:1, pl.ds(q0, qn)], p, spans)
            m = jnp.max(sc[0], axis=0, keepdims=True)
            for s in sc[1:]:
                m = jnp.maximum(m, jnp.max(s, axis=0, keepdims=True))
            tot, acc = None, None
            for s, (k0, kn, _) in zip(sc, spans):
                ex = jnp.exp(s - m)
                t = jnp.sum(ex, axis=0, keepdims=True)
                o = nn(vtt[he, pl.ds(k0, kn)], ex.astype(BF))
                tot = t if tot is None else tot + t
                acc = o if acc is None else acc + o
            ot[he, pl.ds(q0, qn)] = acc / tot
            lse[i, :, pl.ds(q0, qn)] = m + jnp.log(tot)

        @pl.when(e == 1)
        def _():
            mixed[p] = ot[...].T.astype(BF)
        at(i, ev)
        at(i, {2 * p + 1: [m.start for m in m_k[p] + m_l[p]] for p in range(3)})
        return 0
    lax.fori_loop(0, 6, head, 0)
    o_m = n.local(all_of(mixed), all_of(mixed_o))
    lo = lax.broadcasted_iota(jnp.int32, (feats, 128), 1) < 64
    for kk in range(2):
        z0, z1 = 2 * kk, 2 * kk + 1
        wt[:, pl.ds(384 * kk, 128)] = wa[z0, :, pl.ds(640, 128)]
        wt[:, pl.ds(384 * kk + 128, 128)] = wa[z1, :, pl.ds(640, 128)]
        t0 = pltpu.roll(wa[z0, :, pl.ds(512, 128)].astype(F32), 64, 1)
        wt[:, pl.ds(384 * kk + 256, 128)] = jnp.where(lo, t0, wa[z1, :, pl.ds(512, 128)].astype(F32)).astype(BF)
    for pair_ in m_k:
        for m in pair_:
            m.wait_recv()
    for pair_ in m_l:
        for m in pair_:
            m.wait()
    nb = feats // 256
    CHS = own_rows // CH
    for e in d_events[:0]:
        e()

    def own_slice(i, num):
        start = jnp.where(i < main, k * main + i, length + k * 16)
        return pl.ds(pl.multiple_of(start, 16), num)

    for f0 in range(0, feats, 256):
        f = pl.ds(f0, 256)
        acc = nt(mrows[0], wt[f, pl.ds(0, 128)])
        for j in range(1, 6):
            acc = acc + nt(mrows[j], wt[f, pl.ds(128 * j, 128)])
        h1[:, f] = acc + vec[0:1, f]
    inv = 1.0 / feats
    vgrad[...] = jnp.zeros_like(vgrad)
    bupgrad[...] = jnp.zeros_like(bupgrad)

    def norm1(i, _):
        r = pl.ds(pl.multiple_of(i * 16, 16), 16)
        h = h1[r, :] + x[own_slice(i * 16, 16), :].astype(F32)
        m = jnp.sum(h, axis=1, keepdims=True) * inv
        s = jnp.sum(h * h, axis=1, keepdims=True) * inv
        rstd = lax.rsqrt(s - m * m + EPSILON)
        xhat = (h - m) * rstd
        h1[r, :] = xhat
        rs1[r, :] = jnp.broadcast_to(rstd, (16, 128))
        low[r, :] = (xhat * vec[1:2, :] + vec[2:3, :]).astype(BF)
        return 0
    lax.fori_loop(0, own_rows // 16, norm1, 0, unroll=3)
    lowt[...] = low[...].T
    for m in u_k:
        m.wait_recv()
    ev = spread_events(d_events, 12)

    def gate(i, _):
        zz = i // nb
        j = i % nb
        f = pl.ds(pl.multiple_of(j * 256, 256), 256)
        v = nn(low[...], wu[zz, :, f]) + sm[zz, 0, pl.ds(8 + j, 1), :]
        a, g = gelu_pair(v)
        hid[zz, :, f] = a.astype(BF)
        dgl[zz, :, f] = g.astype(BF)
        at(i, ev)
        return 0
    lax.fori_loop(0, nz * nb, gate, 0)
    for m in h_y:
        m.wait_recv()
    local[6].wait()
    def turn_t(i, _):
        f = pl.ds(pl.multiple_of(128 * i, 128), 128)
        tr[f, :] = tt[:, f].T
        return 0
    lax.fori_loop(0, main // 128, turn_t, 0)
    tr[pl.ds(main, 16), :] = jnp.zeros((16, feats), BF)
    for m in d_k:
        m.wait_recv()

    def down(j, _):
        f = pl.ds(pl.multiple_of(j * 256, 256), 256)
        acc = nt(hid[0], wd[0, f, :])
        for zz in range(1, nz):
            acc = acc + nt(hid[zz], wd[zz, f, :])
        h2[:, f] = acc
        return 0
    lax.fori_loop(0, nb, down, 0)
    scale = vec[6:7, 0:1]

    def norm2(i, _):
        r = pl.ds(pl.multiple_of(i * CH, 16), CH)
        h = h2[r, :] + (h1[r, :] * vec[1:2, :] + vec[2:3, :]) + vec[3:4, :]
        m = jnp.sum(h, axis=1, keepdims=True) * inv
        s = jnp.sum(h * h, axis=1, keepdims=True) * inv
        rstd = lax.rsqrt(s - m * m + EPSILON)
        xhat = (h - m) * rstd
        o = xhat * vec[4:5, :] + vec[5:6, :]
        for cc in range(4):
            o4[cc, r, :] = o[:, cc * b:(cc + 1) * b].astype(BF)
        place = lax.broadcasted_iota(jnp.int32, (CH, 1), 0) + i * CH
        place = jnp.where(place < main, place + k * main, valid_ref[0])
        go = jnp.where(place < valid_ref[0], scale * (o - tr[r, :].astype(F32)), 0.0)
        a = go * vec[4:5, :]
        m1 = jnp.sum(a, axis=1, keepdims=True) * inv
        m2 = jnp.sum(a * xhat, axis=1, keepdims=True) * inv
        g2 = rstd * (a - m1 - xhat * m2)
        h2[r, :] = g2
        g2b = g2.astype(BF)
        br[r, :] = g2b
        vgrad[0] += group_sum(go * xhat)
        vgrad[1] += group_sum(go)
        vgrad[2] += group_sum(g2b.astype(F32))
        return 0
    lax.fori_loop(0, CHS, norm2, 0)
    o_dst = lambda: out4.at[y, k]
    o_s = [n.send(lambda: o4.at[oc], o_dst, n.yp), n.send(lambda: o4.at[3 - c], o_dst, n.ykp), n.send(lambda: o4.at[c + 1 - 2 * k], o_dst, n.kp)]
    o_l = n.local(lambda: o4.at[c], o_dst)
    brt[...] = br[...].T
    def gmove(which, src, dst, zz, slot, yy):
        return pltpu.make_async_remote_copy(src_ref=src.at[slot, 2 * yy + 1 - k], dst_ref=dst.at[yy, zz], send_sem=zsem.at[which, yy, zz],
                                            recv_sem=zrem.at[which, yy, zz], device_id=n.kp, device_id_type=MESH)
    def each(fn, zz, slot):
        for which, src, dst in ((0, gdz, rd), (1, guz, ru)):
            for yy in range(2):
                fn(gmove(which, src, dst, zz, slot, yy))
    def fold(zz):
        each(lambda m: m.wait_recv(), zz, 0)
        for yy in range(2):
            add_to(hd.at[yy, zz], rd.at[yy, zz])
            add_to(hu.at[yy, zz], ru.at[yy, zz])

    def back(zz, _):
        slot = zz % 2

        @pl.when(zz >= 2)
        def _():
            each(lambda m: m.wait_send(), zz - 2, slot)

        def chunk(j, _):
            f = pl.ds(pl.multiple_of(j * 256, 256), 256)
            gh = nn(br[...], wd[zz, :, f])
            g = (gh * dgl[zz, :, f].astype(F32)).astype(BF)
            bupgrad[zz, :, f] += group_sum(g.astype(F32))
            gdc = nn(brt[...], hid[zz, :, f])
            guc = nn(lowt[...], g)
            hid[zz, :, f] = g
            for cc in range(4):
                gdz[slot, cc, :, f] = gdc[cc * b:(cc + 1) * b, :].astype(BF)
                guz[slot, cc, :, f] = guc[cc * b:(cc + 1) * b, :].astype(BF)
            return 0
        lax.fori_loop(0, nb, chunk, 0)
        each(lambda m: m.start(), zz, slot)
        for yy in range(2):
            hd[yy, zz] = gdz[slot, 2 * yy + k]
            hu[yy, zz] = guz[slot, 2 * yy + k]

        @pl.when(zz >= 1)
        def _():
            fold(zz - 1)
        return 0
    lax.fori_loop(0, nz, back, 0)

    def first_grad(j, _):
        f = pl.ds(pl.multiple_of(j * 256, 256), 256)
        acc = h2[:, f]
        for zz in range(nz):
            acc = acc + nt(hid[zz], wu[zz, f, :])
        h2[:, f] = acc
        return 0
    lax.fori_loop(0, nb, first_grad, 0)
    fold(nz - 1)
    o_h = [n.local(all_of(hd), all_of(hd_o)), n.local(all_of(hu), all_of(hu_o))]

    def norm1_back(i, _):
        r = pl.ds(pl.multiple_of(i * 16, 16), 16)
        g = h2[r, :]
        xhat = h1[r, :]
        a = g * vec[1:2, :]
        m1 = jnp.sum(a, axis=1, keepdims=True) * inv
        m2 = jnp.sum(a * xhat, axis=1, keepdims=True) * inv
        g1 = rs1[r, 0:1] * (a - m1 - xhat * m2)
        g_one[r, :] = g1
        gb = g1.astype(BF)
        ga[own_slice(i * 16, 16), :] = gb
        vgrad[3] += group_sum(g * xhat)
        vgrad[4] += group_sum(g)
        vgrad[5] += group_sum(gb.astype(F32))
        return 0
    lax.fori_loop(0, own_rows // 16, norm1_back, 0, unroll=3)
    g_main = lambda: ga.at[pl.ds(pl.multiple_of(k * main, 16), main)]
    g_tail = lambda: ga.at[pl.ds(pl.multiple_of(length + k * 16, 16), 16)]
    g_k = [n.send(g_main, g_main, n.kp), n.send(g_tail, g_tail, n.kp)]
    for m in g_k:
        m.wait_recv()
    o_g = n.local(all_of(ga), all_of(ga_o))
    for m in o_s:
        m.wait_recv()
    for m in [o_x, o_w, o_m, o_l, o_g] + o_q + o_h:
        m.wait()
    for zz in range(nz - 2, nz):
        each(lambda m: m.wait_send(), zz, zz % 2)
    n.finish()

def add_to(dst, src):
    dst[...] = (dst[...].astype(F32) + src[...].astype(F32)).astype(BF)

def forward(valid, tok, mem, tch, la, lu, ld, ls, idk, idq, nz):
    b, width = lu.shape
    feats = 4 * b; length = tok.shape[2]; rows = idk.shape[0]; main = length // 2; own = main + 16
    V = lambda *s, d=BF: pltpu.VMEM(s, d)
    vm = pl.BlockSpec(memory_space=pltpu.VMEM); sm = pl.BlockSpec(memory_space=pltpu.SMEM); an = pl.BlockSpec(memory_space=pl.ANY)
    S = jax.ShapeDtypeStruct
    t3 = S((3, rows, 128), BF); h = S((2, nz, b, width), BF)
    outs = [(S((feats, length + 128), BF), an), (t3, an), (t3, an), (t3, an), (t3, an), (S((2, feats, width), BF), an), (S((rows, feats), BF), an), (h, an), (h, an),
            (S((6, 1, rows), F32), vm), (S((own, feats), F32), vm), (S((6, 8, feats), F32), vm), (S((nz, 8, width), F32), vm), (S((2, 2, own, b), BF), vm)]
    w = V(nz, feats, width)
    scratch = [V(feats, length + 128), V(rows, feats), w, w, w, V(nz, 4, *ls.shape, d=F32), V(feats, main), V(own, feats), V(3, feats, 384),
               V(3, rows, 128), V(3, rows, 128), V(3, rows, 128), V(128, rows), V(128, rows, d=F32), V(3, rows, 128), V(6, own, 128), V(3, 8, 384, d=F32), V(8, feats, d=F32), V(feats, feats),
               V(own, feats, d=F32), V(own, feats, d=F32), V(own, 128, d=F32), V(own, feats), V(feats, own), V(own, feats), V(feats, own),
               V(nz, own, width), V(nz, own, width), V(2, 4, b, width), V(2, 4, b, width)] + [V(2, nz, b, width)] * 4 + [V(rows, feats), V(4, own, b),
               pltpu.SemaphoreType.DMA((136,)), pltpu.SemaphoreType.DMA((136,)), pltpu.SemaphoreType.DMA((32,)),
               pltpu.SemaphoreType.DMA((2, 2, nz)), pltpu.SemaphoreType.DMA((2, 2, nz))]
    return pl.pallas_call(forward_kernel, out_shape=[o for o, _ in outs], out_specs=[s for _, s in outs],
        in_specs=[sm, an, an, an, an, an, an, an, vm, vm], scratch_shapes=scratch,
        compiler_params=pltpu.CompilerParams(collective_id=1, has_side_effects=True, vmem_limit_bytes=67043328))(valid, tok, mem, tch, la, lu, ld, ls, idk, idq)
def total_of(refs):
    acc = refs[0][...].astype(F32)
    for r in refs[1:]:
        acc = acc + r[...].astype(F32)
    return acc

class Piece:
    def __init__(self, n, env, col0, num, js, x_first):
        self.n, self.x_first = n, x_first
        gown, ha, ax, ay, ayf, axf, mine, theirs, order = env
        C = pl.ds(col0, num); y, k = n.y, n.k
        self.core = [n.move((lambda j=j, yy=yy: gown.at[j, 2 * yy + 1 - k, :, C]), (lambda j=j, yy=yy: ha.at[yy, 2 * k + j, :, C]), n.kp) for j in js for yy in range(2)]
        self.keep = [n.copy((lambda j=j, yy=yy: gown.at[j, 2 * yy + k, :, C]), (lambda j=j, yy=yy: ha.at[yy, 2 * k + j, :, C])) for j in js for yy in range(2)]
        zz = order if len(js) == 2 else [js[0], js[0] + 2]
        self.first, self.second, self.add1, self.add2 = [], [], [], []
        for q in zz:
            if x_first:
                self.first.append(n.move((lambda q=q: ha.at[:, q, theirs, C]), (lambda q=q: ax.at[:, q, :, C]), n.xp))
                self.add1.append(lambda q=q: [add_to(ha.at[yy, q, mine, C], ax.at[yy, q, :, C]) for yy in range(2)])
                self.second.append(n.move((lambda q=q: ha.at[1 - y, q, mine, C]), (lambda q=q: ay.at[q, :, C]), n.yp))
                self.add2.append(lambda q=q: add_to(ha.at[y, q, mine, C], ay.at[q, :, C]))
            else:
                self.first.append(n.move((lambda q=q: ha.at[1 - y, q, :, C]), (lambda q=q: ayf.at[q, :, C]), n.yp))
                self.add1.append(lambda q=q: add_to(ha.at[y, q, :, C], ayf.at[q, :, C]))
                self.second.append(n.move((lambda q=q: ha.at[y, q, theirs, C]), (lambda q=q: axf.at[q, :, C]), n.xp))
                self.add2.append(lambda q=q: add_to(ha.at[y, q, mine, C], axf.at[q, :, C]))
    def start(self):
        for m in self.core + self.keep:
            m.start()
    def ev1(self):
        for m in self.core:
            m.wait_recv()
        for m in self.keep:
            m.wait()
        for m in self.first:
            m.start()
    def ev2(self):
        for m, f, s in zip(self.first, self.add1, self.second):
            m.wait_recv(); f(); s.start()
    def ev3(self):
        for m, f in zip(self.second, self.add2):
            m.wait_recv(); f()

class Rows:
    def __init__(self, n, here, z1, z2, e, dev1, dev2, add):
        e1, e2, e3 = e
        self.a = n.move((lambda: here(e3)), (lambda: z1(1)), dev1)
        self.b = n.move((lambda: here(e1)), (lambda: z1(0)), dev1)
        self.c = n.move((lambda: here(e2)), z2, dev2)
        self.mid = lambda: add(here(e2), z1(1))
    def start(self):
        self.a.start(); self.b.start()
    def middle(self):
        self.a.wait_recv(); self.mid(); self.c.start()
    def end(self):
        self.b.wait_recv(); self.c.wait_recv()

def backward_kernel(hu_h, hd_h, ga_h, mixed_h, xt_h, q_h, k_h, v_h, w_h, o4_h, g1_h, lse, vgrad, bupgrad, idk, idq,
                    grad4, lout, gmem, g3, gwo, fu, fd, fvec, bup, bqv,
                    hu, hd, ux, uz1, uz2, ut, uy, fub, pu, dy, dz1, dz2, df, dx, pd,
                    ha, ax, ay, ayf, axf, az1, az2, fa, pa, gown,
                    ga, mixed, xt, qt, kt, vt, w, o4, g1, wp, wt, gat, gm, gp, dv, dk, dqt, ktt, dd, g4, gs, gr, lo32,
                    sv, svk, svt, svy, svo, svx, ps, svz, ss, rs, lsem):
    n = Net(ss, rs, lsem)
    nz, y, k, c, z, x, d, nd = n.nz, n.y, n.k, n.c, n.z, n.x, n.d, n.nd
    b = fu.shape[0]; hb = b // 2
    rows, feats = ga.shape
    own_rows = g1.shape[0]; main = own_rows - 16; length = 2 * main
    mine = pl.ds(pl.multiple_of(x * hb, 16), hb)
    theirs = pl.ds(pl.multiple_of((1 - x) * hb, 16), hb)
    all_of = lambda r: (lambda: r)
    l_w, l_ga, l_m = [n.local(all_of(s), all_of(t)) for s, t in ((w_h, w), (ga_h, ga), (mixed_h, mixed))]
    l_q = [n.local(all_of(s), all_of(t)) for s, t in ((k_h, kt), (q_h, qt), (v_h, vt))]
    l_x = n.local(all_of(xt_h), all_of(xt))
    l_d = n.local(lambda: hd_h.at[y], lambda: hd)
    l_u = n.local(lambda: hu_h.at[:, :, mine], lambda: hu)
    l_o = [n.local(all_of(o4_h), all_of(o4)), n.local(all_of(g1_h), all_of(g1))]
    n.barrier(n.zp[1:] + [n.yp, n.ykp, n.kp, n.xp] + n.others)
    e1 = z + 1 - 2 * lax.rem(z, 2)
    e2 = lax.rem(z + 2, nz)
    e3 = lax.rem(e1 + 2, nz)
    e = (e1, e2, e3)
    order = [e3, e1, e2, z]
    dev1, dev2 = (d, e1, c), (d, e2, c)
    d_y = [n.send((lambda q=q: hd_h.at[1 - y, q]), (lambda q=q: dy.at[q]), n.yp) for q in order]
    u_x = [n.send((lambda q=q: hu_h.at[:, q, theirs]), (lambda q=q: ux.at[:, q]), n.xp) for q in order]

    def add2(a, s):
        for yy in range(2):
            add_to(a.at[yy], s.at[yy])
    dz = Rows(n, lambda q: hd.at[q], lambda s: dz1.at[s], lambda: dz2, e, dev1, dev2, add_to)
    uz = Rows(n, lambda q: hu.at[:, q], lambda s: uz1.at[s], lambda: uz2, e, dev1, dev2, add2)
    d_x = n.move(all_of(df), all_of(dx), n.xp)
    u_y = n.move(lambda: ut.at[1 - y], all_of(uy), n.yp)
    u_f = n.move(lambda: fub.at[mine], lambda: fub.at[mine], n.xp)

    mypair = d // 2

    def pairs_sum(value, slots, view):
        if nd == 2:
            return value
        view(slots, mypair)[...] = value.astype(slots.dtype)
        ms = [n.send((lambda: view(slots, mypair)), (lambda: view(slots, mypair)), o) for o in n.others]
        for m in ms:
            m.wait_recv()
        return total_of([view(slots, i) for i in range(nd // 2)])

    def ev_dy(j):
        def run():
            d_y[j].wait_recv()
            if j == 0:
                l_d.wait()
            add_to(hd.at[order[j]], dy.at[order[j]])
            if j == 1:
                dz.start()
        return run
    def ev_ux(j):
        def run():
            u_x[j].wait_recv()
            if j == 0:
                l_u.wait()
            add2(hu.at[:, order[j]], ux.at[:, order[j]])
            if j == 1:
                uz.start()
        return run
    def ev_df():
        dz.end()
        df[...] = total_of([hd.at[z], dz1.at[0], dz2]).astype(BF)
        d_x.start()
    def ev_ut():
        uz.end()
        for yy in range(2):
            ut[yy] = total_of([hu.at[yy, z], uz1.at[0, yy], uz2.at[yy]]).astype(BF)
        u_y.start()
    def ev_uf():
        u_y.wait_recv()
        fub[mine, :] = pairs_sum(total_of([ut.at[y], uy]), pu, lambda s, i: s.at[i]).astype(BF)
        u_f.start()
    env = (gown, ha, ax, ay, ayf, axf, mine, theirs, order)
    PO = Piece(n, env, 640, 128, (0, 1), True)
    P0 = Piece(n, env, 0, 384, (0,), True)
    P1 = Piece(n, env, 0, 384, (1,), False)
    P2 = Piece(n, env, 384, 128, (0, 1), True)
    P3 = Piece(n, env, 512, 128, (0, 1), False)
    class Cols:
        def __init__(self, col0, num):
            C = pl.ds(col0, num)
            self.C = C
            self.z = Rows(n, lambda q: ha.at[y, q, mine, C], lambda s: az1.at[s, :, C], lambda: az2.at[:, C], e, dev1, dev2, add_to)
            self.f = n.move(lambda: fa.at[mine, C], lambda: fa.at[mine, C], n.xp)
        def end(self):
            self.z.end()
            C = self.C
            fa[mine, C] = pairs_sum(total_of([ha.at[y, z, mine, C], az1.at[0, :, C], az2.at[:, C]]), pa, lambda s, i: s.at[i, :, C]).astype(BF)
            self.f.start()
    ZO, Z01, Z2, Z3 = Cols(640, 128), Cols(0, 384), Cols(384, 128), Cols(512, 128)
    l_w.wait(); l_ga.wait()
    gat[...] = ga[...].T
    assemble_pairs(w, wp, feats)
    wt[:, pl.ds(0, 128)] = w[0, :, pl.ds(640, 128)]
    wt[:, pl.ds(128, 128)] = w[1, :, pl.ds(640, 128)]
    lo = lax.broadcasted_iota(jnp.int32, (feats, 128), 1) < 64
    wt[:, pl.ds(256, 128)] = jnp.where(lo, pltpu.roll(w[0, :, pl.ds(512, 128)].astype(F32), 64, 1), w[1, :, pl.ds(512, 128)].astype(F32)).astype(BF)
    r3 = rows // 3

    def mixed_grad(i, _):
        r = pl.ds(pl.multiple_of(i * r3, 16), r3)
        v = nn(ga[r, :], wt[...])
        for p in range(3):
            gm[p, r, :] = v[:, 128 * p:128 * p + 128].astype(BF)
        return 0
    lax.fori_loop(0, 3, mixed_grad, 0)
    l_m.wait()
    for cc in range(4):
        af = gat[pl.ds(b * cc, b), :]
        for j in range(2):
            gown[j, cc, :, pl.ds(640, 128)] = nn(af, mixed[j]).astype(BF)
    PO.start()
    for m in l_q:
        m.wait()
    l_x.wait()
    table = {0: [ev_dy(0), ev_ux(0)], 1: [PO.ev1], 3: [ev_dy(1), ev_ux(1)], 6: [ev_dy(2), P0.ev1], 7: [dz.middle, ev_ux(2)],
             9: [ev_dy(3)], 10: [ev_ux(3), uz.middle], 12: [P1.ev1, PO.ev2], 13: [ev_df], 14: [P0.ev2], 15: [ev_ut, PO.ev3, ZO.z.start], 16: [P1.ev2], 17: [P0.ev3, ev_uf]}
    cuts = {1: 0, 3: 1, 4: 2}

    def head(i, _):
        p = i // 2
        h = i % 2
        he = pl.ds(pl.multiple_of(64 * h, 64), 64)

        @pl.when(h == 0)
        def _():
            ktt[...] = kt[p].T
            prod = (gm[p].astype(F32) * mixed[p].astype(F32)).T
            dd[0] = jnp.sum(prod[:64, :], axis=0, keepdims=True)
            dd[1] = jnp.sum(prod[64:, :], axis=0, keepdims=True)
            dv[...] = jnp.zeros_like(dv)
            dk[...] = jnp.zeros_like(dk)
        lanes = (lax.broadcasted_iota(jnp.int32, (1, 128), 1) // 64) == h
        for t, (q0, qn, spans) in enumerate(tiles(rows, length)):
            q = qt[p, pl.ds(q0, qn), :]
            qm = jnp.where(lanes, q, jnp.zeros_like(q))
            g = gm[p, pl.ds(q0, qn), :]
            gmm = jnp.where(lanes, g, jnp.zeros_like(g))
            sc = scores_of(kt, qm, idk, idq[0:1, pl.ds(q0, qn)], p, spans)
            l = lse[i, :, pl.ds(q0, qn)]
            dl = dd[h, :, pl.ds(q0, qn)]
            acc = None
            for s, (k0, kn, _) in zip(sc, spans):
                pr = jnp.exp(s - l)
                dp = nt(vt[p, pl.ds(k0, kn), :], gmm)
                ds = (pr * (dp - dl)).astype(BF)
                dv[pl.ds(k0, kn), :] += nn(pr.astype(BF), gmm)
                dk[pl.ds(k0, kn), :] += nn(ds, qm)
                o = nn(ktt[he, pl.ds(k0, kn)], ds)
                acc = o if acc is None else acc + o
            dqt[he, pl.ds(q0, qn)] = acc * 0.125
            if t in cuts:
                at(3 * i + cuts[t], table)

        @pl.when(h == 1)
        def _():
            gp[p, :, pl.ds(0, 128)] = dqt[...].T.astype(BF)
            gp[p, :, pl.ds(128, 128)] = dk[...].astype(BF)
            gp[p, :, pl.ds(256, 128)] = dv[...].astype(BF)

        @pl.when(jnp.logical_and(h == 1, p < 2))
        def _():
            def part(cc, _):
                f = pl.ds(pl.multiple_of(b * cc, 16), b)
                gown[p, cc, :, pl.ds(0, 384)] = nn(xt[f, pl.ds(0, rows)], gp[p]).astype(BF)
                return 0
            lax.fori_loop(0, 4, part, 0)
        at(i, {1: [P0.start], 3: [P1.start]})
        return 0
    lax.fori_loop(0, 6, head, 0)
    sw = lambda a: pltpu.roll(a, 64, 1)

    def last(cc, _):
        f = pl.ds(pl.multiple_of(b * cc, 16), b)
        r2 = nn(xt[f, pl.ds(0, rows)], gp[2])
        o2 = nn(gat[f, :], mixed[2])
        lo = lax.broadcasted_iota(jnp.int32, (b, 128), 1) < 64
        rq, rk, rv = r2[:, :128], r2[:, 128:256], r2[:, 256:]
        gown[0, cc, :, pl.ds(384, 128)] = jnp.where(lo, rq, sw(rk)).astype(BF)
        gown[1, cc, :, pl.ds(384, 128)] = jnp.where(lo, sw(rq), rk).astype(BF)
        gown[0, cc, :, pl.ds(512, 128)] = jnp.where(lo, rv, sw(o2)).astype(BF)
        gown[1, cc, :, pl.ds(512, 128)] = jnp.where(lo, sw(rv), o2).astype(BF)
        return 0
    lax.fori_loop(0, 4, last, 0)
    P2.start(); P3.start()
    def rowsgrad(r):
        return nt(gp[0, r, :], wp[0]) + nt(gp[1, r, :], wp[1]) + nt(gp[2, r, :], wp[2])

    def half_rows(kk, put):
        def chunk(i, _):
            put(pl.ds(pl.multiple_of(i * 256, 16), 256), rowsgrad(pl.ds(pl.multiple_of(kk * main + i * 256, 16), 256)))
            return 0
        lax.fori_loop(0, main // 256, chunk, 0)
        put(pl.ds(main, 16), rowsgrad(pl.ds(pl.multiple_of(length + kk * 16, 16), 16)))
    def put_other(r, v):
        gs[r, :] = v.astype(BF)
    half_rows(1 - k, put_other)
    g_k = n.send(all_of(gs), all_of(gr), n.kp)
    P2.ev1(); P3.ev1()
    sv[...] = jnp.zeros_like(sv)
    for i in range(6):
        sv[pl.ds(i, 1), :] = jnp.sum(vgrad[i], axis=0, keepdims=True)
    for i in range(nz):
        sv[pl.ds(6 + i, 1), :] = jnp.sum(bupgrad[i], axis=0, keepdims=True)
    for p in range(3):
        t = jnp.sum(group_sum(gp[p].astype(F32)), axis=0, keepdims=True)
        sv[pl.ds(6 + nz + p, 1), pl.ds(0, 384)] = jnp.where(k == 0, t, 0.0)
        sv[pl.ds(6 + nz + p, 1), pl.ds(384, 384)] = jnp.where(k == 1, t, 0.0)
    s_k = n.send(all_of(sv), all_of(svk), n.kp)
    P1.ev3()
    Z01.z.start()
    ZO.z.middle()
    for m in l_o:
        m.wait()
    def put_own(r, v):
        g1[r, :] = g1[r, :] + v
    half_rows(k, put_own)
    P2.ev2(); P3.ev2()
    s_k.wait_recv()
    svt[...] = sv[...] + svk[...]
    s_y = n.send(all_of(svt), all_of(svy), n.yp)
    g_k.wait_recv()

    def own(i, _):
        r = pl.ds(pl.multiple_of(i * 48, 16), 48)
        v = g1[r, :] + gr[r, :].astype(F32)
        for cc in range(4):
            g4[cc, r, :] = v[:, cc * b:(cc + 1) * b].astype(BF)
        return 0
    lax.fori_loop(0, own_rows // 48, own, 0)
    g_l = n.local(lambda: g4.at[c], lambda: grad4.at[y, k])
    dst = lambda: grad4.at[y, k]
    g_s = [n.send(lambda: g4.at[n.oc], dst, n.yp), n.send(lambda: g4.at[3 - c], dst, n.ykp), n.send(lambda: g4.at[c + 1 - 2 * k], dst, n.kp)]
    P2.ev3(); Z2.z.start()
    P3.ev3(); Z3.z.start()
    s_y.wait_recv()
    svo[...] = svt[...] + svy[...]
    s_x = n.send(all_of(svo), all_of(svx), n.xp)
    Z01.z.middle(); ZO.end()
    half = (lout.shape[1] - length) // 2
    for s in range(2):
        lo32[pl.ds(0, half), :] = o4[s, 0, pl.ds(main, 16), :].astype(F32)[:half]
        lo32[pl.ds(half, main), :] = o4[s, 0, pl.ds(0, main), :].astype(F32)
        lo32[pl.ds(half + main, main), :] = o4[s, 1, pl.ds(0, main), :].astype(F32)
        lo32[pl.ds(half + length, 16 - half), :] = o4[s, 0, pl.ds(main, 16), :].astype(F32)[half:]
        lo32[pl.ds(length + 16, 2 * half - 16), :] = o4[s, 1, pl.ds(main, 16), :].astype(F32)[:2 * half - 16]
        lout[s] = lo32[pl.ds(0, length + 2 * half), :].astype(BF)
    Z2.z.middle(); Z3.z.middle()
    s_x.wait_recv()
    svz[z] = pairs_sum(svo[...] + svx[...], ps, lambda s, i: s.at[i])
    s_z = [n.send(lambda: svz.at[z], lambda: svz.at[z], n.zp[i]) for i in range(1, nz)]
    Z01.end()
    d_x.wait_recv()
    fd[...] = pairs_sum(total_of([df, dx]), pd, lambda s, i: s.at[i])
    u_f.wait_recv()
    fu[...] = fub[...].astype(F32)
    Z2.end(); Z3.end()
    for m in s_z:
        m.wait_recv()
    acc = svz[0]
    for i in range(1, nz):
        acc = acc + svz[i]
    pick = jnp.where(c == 0, acc[:8, 0:b], 0.0)
    for cc in range(1, 4):
        pick = pick + jnp.where(c == cc, acc[:8, cc * b:(cc + 1) * b], 0.0)
    fvec[...] = pick
    t = jnp.where(z == 0, acc[6:7], 0.0)
    for i in range(1, nz):
        t = t + jnp.where(z == i, acc[6 + i:7 + i], 0.0)
    bup[...] = t
    hbias = acc[6 + nz:9 + nz]
    hbias = jnp.where(z // 2 == 0, hbias[:, :384], hbias[:, 384:])
    odd = z % 2 == 1
    two = jnp.where(odd, hbias[1:2], hbias[0:1])
    lo1 = lax.broadcasted_iota(jnp.int32, (8, 128), 1) < 64
    w8 = lambda a: jnp.broadcast_to(a, (8, 128))
    left = lambda a, v: jnp.where(lo1, w8(a), sw(w8(v)))[0:1]
    right = lambda a, v: jnp.where(lo1, sw(w8(a)), w8(v))[0:1]
    lq, lv = hbias[2:3, :128], hbias[2:3, 256:]
    bqv[pl.ds(0, 1), :] = left(two[:, :128], two[:, 256:])
    bqv[pl.ds(1, 1), :] = right(two[:, :128], two[:, 256:])
    bqv[pl.ds(2, 1), :] = jnp.where(odd, right(lq, lv), left(lq, lv))
    for m in (ZO, Z01, Z2, Z3):
        m.f.wait_recv()
    lob = lax.broadcasted_iota(jnp.int32, (b, 128), 1) < 64
    tile = lambda i: fa[:, pl.ds(128 * i, 128)].astype(F32)
    t0, t1, t2, t3, t4, t5 = [tile(i) for i in range(6)]
    g3[0, :, pl.ds(0, 128)] = jnp.where(lob, t0, sw(t1))
    g3[0, :, pl.ds(128, 64)] = t2[:, :64]
    g3[1, :, pl.ds(0, 128)] = jnp.where(lob, sw(t0), t1)
    g3[1, :, pl.ds(128, 64)] = sw(t2)[:, :64]
    g3[2, :, pl.ds(0, 128)] = t3
    g3[2, :, pl.ds(128, 64)] = t4[:, :64]
    gwo[pl.ds(0, 128), :] = t5.T
    gwo[pl.ds(128, 64), :] = sw(t4).T[:64]
    for m in g_s:
        m.wait_recv()
    g_l.wait()
    for s in range(2):
        gmem[s, pl.ds(0, 16), :] = grad4[s, 0, pl.ds(main, 16), :].astype(F32)
        gmem[s, pl.ds(16, 2 * half - 16), :] = grad4[s, 1, pl.ds(main, 16), :].astype(F32)[:2 * half - 16]
    n.finish()

def backward(hu, hd, ga, mixed, xt, qt, kt, vt, w, o4, g1, lse, vgrad, bupgrad, idk, idq, half, nz, nd):
    b, width = hu.shape[2:]
    feats = 4 * b; hb = b // 2; rows = ga.shape[0]; own = g1.shape[0]; length = 2 * (own - 16)
    V = lambda *s, d=BF: pltpu.VMEM(s, d)
    vm = pl.BlockSpec(memory_space=pltpu.VMEM); an = pl.BlockSpec(memory_space=pl.ANY)
    S = jax.ShapeDtypeStruct
    np_ = max(1, nd // 2) if nd > 2 else 1
    pw = (hb, width) if nd > 2 else (16, 128)
    t3 = V(3, rows, 128); f3 = lambda *s: V(*s, d=F32)
    sm = f3(16, feats)
    outs = (S((2, 2, own, b), BF), S((2, length + 2 * half, b), BF), S((2, 2 * half, b), F32), S((3, b, b), F32), S((b, b), F32), S((b, width), F32), S((b, width), F32), S((8, b), F32), S((1, feats), F32), S((3, 128), F32))
    scratch = [V(2, nz, hb, width), V(nz, b, width), V(2, nz, hb, width), V(2, 2, hb, width), V(2, hb, width), V(2, hb, width), V(hb, width), V(b, width), V(np_, *pw),
               V(nz, b, width), V(2, b, width), V(b, width), V(b, width), V(b, width), V(np_, b, width) if nd > 2 else V(1, 16, 128),
               V(2, nz, b, width), V(2, nz, hb, width), V(nz, hb, width), V(nz, b, width), V(nz, hb, width), V(2, hb, width), V(hb, width), V(b, width), V(np_, *pw), V(2, 4, b, width),
               V(rows, feats), t3, V(*xt.shape), t3, t3, t3, V(*w.shape), V(*o4.shape), f3(*g1.shape), V(3, feats, 384), V(feats, 384), V(feats, rows), t3, V(3, rows, 384),
               f3(rows, 128), f3(rows, 128), f3(128, rows), V(128, rows), f3(2, 1, rows), V(4, own, b), V(own, feats), V(own, feats), f3(rows, b),
               sm, sm, sm, sm, sm, sm, f3(np_, 16, feats), f3(nz, 16, feats),
               pltpu.SemaphoreType.DMA((128 + 5 * nd,)), pltpu.SemaphoreType.DMA((128 + 5 * nd,)), pltpu.SemaphoreType.DMA((40,))]
    return pl.pallas_call(backward_kernel, out_shape=outs, in_specs=[an] * 11 + [vm] * 5, out_specs=(vm,) * len(outs), scratch_shapes=scratch,
        compiler_params=pltpu.CompilerParams(collective_id=2, has_side_effects=True, vmem_limit_bytes=67043328))(hu, hd, ga, mixed, xt, qt, kt, vt, w, o4, g1, lse, vgrad, bupgrad, idk, idq)

def per_device(tokens, memory, block_ids, valid, teacher, w_qkv, bias_qv, w_out, bias_out, ln1_gain, ln1_bias, w_up, bias_up, w_down, bias_down, ln2_gain, ln2_bias):
    _, b, length = tokens.shape
    nd, nz = lax.axis_size("dp"), lax.axis_size("row")
    d, z, c = (lax.axis_index(a) for a in ("dp", "row", "col"))
    y, k = c // 2, c % 2
    feats = 4 * b
    half = memory.shape[1] // 2
    main = length // 2
    rows = length + 32
    wq = w_qkv.reshape(3, b, 192)
    wo = jnp.transpose(w_out)
    la = jnp.concatenate([wq[0, :, :64], wq[1, :, :64], wq[0, :, 64:128], wq[1, :, 64:128], wq[0, :, 128:], wq[1, :, 128:], wq[2], wo[:, 128:], wo[:, :128]], axis=1)
    mem = jnp.pad(jnp.swapaxes(memory, 1, 2), ((0, 0), (0, 0), (0, 128 - 2 * half)))
    scale = (valid.shape[0] * length) / jnp.sum(valid).astype(F32)
    fv = jnp.stack([bias_out, ln1_gain, ln1_bias, bias_down, ln2_gain, ln2_bias, jnp.full((b,), scale, F32), jnp.zeros((b,), F32)])
    ls = jnp.concatenate([jnp.pad(fv, ((0, 0), (0, 256 - b))), bias_up.reshape(3, 256), jnp.pad(bias_qv.reshape(1, 384), ((0, 0), (0, 128))).reshape(2, 256), jnp.zeros((3, 256), F32)])
    ids = lax.dynamic_index_in_dim(block_ids, y, 0, keepdims=False)
    ids = jnp.concatenate([ids, jnp.full((half,), -1, jnp.int32), jnp.full((half,), length, jnp.int32), jnp.full((32 - 2 * half,), 2 * length, jnp.int32)])
    idk = jnp.broadcast_to(ids[:, None], (rows, 128))
    count = lax.dynamic_index_in_dim(valid, (d * nz + z) * 2 + y, 0)
    xt, qt, kt, vt, mixed, wown, ga, hu, hd, lse, g_one, vgrad, bupgrad, out4 = forward(count, tokens, mem, teacher, la, w_up, w_down, ls, idk, ids[None], nz)
    grad4, lout, gmem, g3, gwo, fu, fd, fvec, bup, bqv = backward(hu, hd, ga, mixed, xt, qt, kt, vt, wown, out4, g_one, lse, vgrad, bupgrad, idk, ids[None], half, nz, nd)
    grad_tokens = grad4[:, :, :main].reshape(2, length, b).astype(F32)
    return (lout, grad_tokens, gmem, g3.reshape(3, b * b), bqv, gwo, fvec[5], fvec[3], fvec[4], fu, bup[0], fd, fvec[2], fvec[0], fvec[1])

def solution(mesh):
    rows, feat = ("dp", "row"), "col"
    in_specs = (P(rows, feat, None), P(rows, None, feat), P(rows, None), P(), P(rows, feat, None), P("row", feat), P("row", None), P("row", feat), P(feat), P(feat), P(feat), P(feat, "row"), P("row"), P(feat, "row"), P(feat), P(feat), P(feat))
    out_specs = (P(rows, None, feat), P(rows, None, feat), P(rows, None, feat), P("row", feat), P("row", None), P("row", feat), P(feat), P(feat), P(feat), P(feat, "row"), P("row"), P(feat, "row"), P(feat), P(feat), P(feat))
    return jax.shard_map(per_device, mesh=mesh, in_specs=in_specs, out_specs=out_specs, check_vma=False)
```

```python
import jax
import jax.numpy as jnp
from jax import lax
from jax.experimental import pallas as pl
from jax.experimental.pallas import tpu as pltpu
from jax.sharding import PartitionSpec as P
BF=jnp.bfloat16; F32=jnp.float32
EPSILON=1e-12
CH=48

def nn(a,b): return lax.dot_general(a,b,(((1,),(0,)),((),())),preferred_element_type=F32)
def nt(a,b): return lax.dot_general(a,b,(((1,),(1,)),((),())),preferred_element_type=F32)

def gelu_pair(v):
    t = pl.reciprocal(1.0 + (0.3275911 * 0.7071067811865476) * jnp.abs(v))
    poly = t * (0.5*0.254829592 + t * (-0.5*0.284496736 + t * (0.5*1.421413741 + t * (-0.5*1.453152027 + t * (0.5*1.061405429)))))
    e = jnp.exp(-0.5 * v * v)
    half = poly * e
    cdf = jnp.where(v >= 0.0, 1.0 - half, half)
    return v * cdf, cdf + v * (e * 0.3989422804014327)

def group_sum(v):
    rows = v.shape[0]
    return jnp.sum(v.reshape(rows // 8, 8, v.shape[1]), axis=0)

def mlp_kernel(half_ref, valid_ref, mixed, x, teach, vec, bup, wa_hbm, wu_hbm, wd_hbm,
               out, g_one, g_attn, vgrad, bupgrad, gu_hbm, gd_hbm,
               tr, wraw, wt, wu, wd, h1, h2, rs1, low, lowt, brt, br, hid, dgl, gg, gu, gd, sem):
    rows, feats = x.shape
    zs = wu.shape[0]
    nb = feats // 256
    copies_a = [pltpu.make_async_copy(wa_hbm.at[z, :, pl.ds(512, 256)], wraw.at[z], sem.at[z]) for z in range(zs)]
    copies_u = [pltpu.make_async_copy(wu_hbm.at[z], wu.at[z], sem.at[zs + z]) for z in range(zs)]
    copies_d = [pltpu.make_async_copy(wd_hbm.at[z], wd.at[z], sem.at[2 * zs + z]) for z in range(zs)]
    for c in copies_a + copies_u + copies_d:
        c.start()
    for c in copies_a:
        c.wait()
    main = teach.shape[1]
    for i in range(main // 128):
        tr[pl.ds(128 * i, 128), :] = teach[:, pl.ds(128 * i, 128)].T
    tr[pl.ds(main, rows - main), :] = jnp.zeros((rows - main, feats), BF)
    low_lane = lax.broadcasted_iota(jnp.int32, (feats, 128), 1) < 64
    for k in range(zs // 2):
        z0, z1 = 2 * k, 2 * k + 1
        wt[:, pl.ds(384 * k, 128)] = wraw[z0, :, pl.ds(128, 128)]
        wt[:, pl.ds(384 * k + 128, 128)] = wraw[z1, :, pl.ds(128, 128)]
        t0 = pltpu.roll(wraw[z0, :, pl.ds(0, 128)].astype(F32), 64, 1)
        t1 = wraw[z1, :, pl.ds(0, 128)].astype(F32)
        wt[:, pl.ds(384 * k + 256, 128)] = jnp.where(low_lane, t0, t1).astype(BF)
    for n in range(nb):
        f = pl.ds(256 * n, 256)
        h1[:, f] = nt(mixed[...], wt[f, :]) + x[:, f].astype(F32) + vec[0:1, f]
    inv = 1.0 / feats

    vgrad[...] = jnp.zeros_like(vgrad)
    bupgrad[...] = jnp.zeros_like(bupgrad)

    def norm1(i, _):
        r = pl.ds(pl.multiple_of(i * CH, 16), CH)
        h = h1[r, :]
        m = jnp.sum(h, axis=1, keepdims=True) * inv
        s = jnp.sum(h * h, axis=1, keepdims=True) * inv
        rstd = lax.rsqrt(s - m * m + EPSILON)
        xhat = (h - m) * rstd
        h1[r, :] = xhat
        rs1[r, :] = jnp.broadcast_to(rstd, (CH, 128))
        low[r, :] = (xhat * vec[1:2, :] + vec[2:3, :]).astype(BF)
        return 0
    lax.fori_loop(0, rows // CH, norm1, 0)
    lowt[...] = low[...].T
    for c in copies_u:
        c.wait()

    def gate(i, _):
        z = i // nb
        f = pl.ds(pl.multiple_of((i % nb) * 256, 256), 256)
        v = nn(low[...], wu[z, :, f]) + bup[z, :, f]
        a, b = gelu_pair(v)
        hid[z, :, f] = a.astype(BF)
        dgl[z, :, f] = b
        return 0
    lax.fori_loop(0, zs * nb, gate, 0)
    for c in copies_d:
        c.wait()

    def down(n, _):
        f = pl.ds(pl.multiple_of(n * 256, 256), 256)
        acc = nt(hid[0], wd[0, f, :])
        for z in range(1, zs):
            acc = acc + nt(hid[z], wd[z, f, :])
        h2[:, f] = acc
        return 0
    lax.fori_loop(0, nb, down, 0)
    scale = vec[6:7, 0:1]
    first = half_ref[0] * main

    def norm2(i, _):
        r = pl.ds(pl.multiple_of(i * CH, 16), CH)
        h = h2[r, :] + (h1[r, :] * vec[1:2, :] + vec[2:3, :]) + vec[3:4, :]
        m = jnp.sum(h, axis=1, keepdims=True) * inv
        s = jnp.sum(h * h, axis=1, keepdims=True) * inv
        rstd = lax.rsqrt(s - m * m + EPSILON)
        xhat = (h - m) * rstd
        o = xhat * vec[4:5, :] + vec[5:6, :]
        out[r, :] = o.astype(BF)
        place = lax.broadcasted_iota(jnp.int32, (CH, 1), 0) + i * CH
        place = jnp.where(place < main, place + first, valid_ref[0])
        go = jnp.where(place < valid_ref[0], scale * (o - tr[r, :].astype(F32)), 0.0)
        a = go * vec[4:5, :]
        m1 = jnp.sum(a, axis=1, keepdims=True) * inv
        m2 = jnp.sum(a * xhat, axis=1, keepdims=True) * inv
        g2 = rstd * (a - m1 - xhat * m2)
        h2[r, :] = g2
        b = g2.astype(BF)
        br[r, :] = b
        vgrad[0] += group_sum(go * xhat)
        vgrad[1] += group_sum(go)
        vgrad[2] += group_sum(b.astype(F32))
        return 0
    lax.fori_loop(0, rows // CH, norm2, 0)
    brt[...] = br[...].T

    def back(i, _):
        z = i // nb
        f = pl.ds(pl.multiple_of((i % nb) * 256, 256), 256)
        gh = nn(br[...], wd[z, :, f])
        g = (gh * dgl[z, :, f]).astype(BF)
        gg[z, :, f] = g
        bupgrad[z, :, f] += group_sum(g.astype(F32))
        gd[z, :, f] = nn(brt[...], hid[z, :, f]).astype(BF)
        gu[z, :, f] = nn(lowt[...], g).astype(BF)
        return 0
    lax.fori_loop(0, zs * nb, back, 0)
    outs = [pltpu.make_async_copy(gd, gd_hbm, sem.at[0]), pltpu.make_async_copy(gu, gu_hbm, sem.at[1])]
    for c in outs:
        c.start()

    def first_grad(n, _):
        f = pl.ds(pl.multiple_of(n * 256, 256), 256)
        acc = h2[:, f]
        for z in range(zs):
            acc = acc + nt(gg[z], wu[z, f, :])
        h2[:, f] = acc
        return 0
    lax.fori_loop(0, nb, first_grad, 0)

    def norm1_back(i, _):
        r = pl.ds(pl.multiple_of(i * CH, 16), CH)
        g = h2[r, :]
        xhat = h1[r, :]
        a = g * vec[1:2, :]
        m1 = jnp.sum(a, axis=1, keepdims=True) * inv
        m2 = jnp.sum(a * xhat, axis=1, keepdims=True) * inv
        g1 = rs1[r, 0:1] * (a - m1 - xhat * m2)
        g_one[r, :] = g1
        b = g1.astype(BF)
        g_attn[r, :] = b
        vgrad[3] += group_sum(g * xhat)
        vgrad[4] += group_sum(g)
        vgrad[5] += group_sum(b.astype(F32))
        return 0
    lax.fori_loop(0, rows // CH, norm1_back, 0)
    for c in outs:
        c.wait()

def mlp(half, valid, mixed, x, teach, vec, bup, wa, wu, wd):
    rows, feats = x.shape; zs = wu.shape[0]
    V = lambda *s, d=BF: pltpu.VMEM(s, d)
    vm = pl.BlockSpec(memory_space=pltpu.VMEM); sm = pl.BlockSpec(memory_space=pltpu.SMEM); an = pl.BlockSpec(memory_space=pl.ANY)
    S = jax.ShapeDtypeStruct
    return pl.pallas_call(mlp_kernel,
        out_shape=(S((rows,feats),BF),S((rows,feats),F32),S((rows,feats),BF),S((6,8,feats),F32),S((zs,8,feats),F32),S(wu.shape,BF),S(wd.shape,BF)),
        in_specs=[sm,sm,vm,vm,vm,vm,vm,an,an,an],
        out_specs=(vm,vm,vm,vm,vm,an,an),
        scratch_shapes=[V(rows,feats),V(zs,feats,256),V(feats,feats),V(*wu.shape),V(*wd.shape),V(rows,feats,d=F32),V(rows,feats,d=F32),V(rows,128,d=F32),V(rows,feats),
            V(feats,rows),V(feats,rows),V(rows,feats),V(zs,rows,feats),V(zs,rows,feats,d=F32),V(zs,rows,feats),V(*wu.shape),V(*wd.shape),pltpu.SemaphoreType.DMA((3*zs,))],
        compiler_params=pltpu.CompilerParams(vmem_limit_bytes=63*2**20),
    )(half,valid,mixed,x,teach,vec,bup,wa,wu,wd)
NEG=-1e30
def tn_lanes(): return lax.broadcasted_iota(jnp.int32,(1,128),1)

def assemble_pairs(w, wp, feats):
    lo = lax.broadcasted_iota(jnp.int32, (feats, 128), 1) < 64
    wp[0] = w[0, :, pl.ds(0, 384)]
    wp[1] = w[1, :, pl.ds(0, 384)]
    a0, a1 = w[0, :, pl.ds(384, 128)].astype(F32), w[1, :, pl.ds(384, 128)].astype(F32)
    wp[2, :, pl.ds(0, 128)] = jnp.where(lo, a0, pltpu.roll(a1, 64, 1)).astype(BF)
    wp[2, :, pl.ds(128, 128)] = jnp.where(lo, pltpu.roll(a0, 64, 1), a1).astype(BF)
    b0, b1 = w[0, :, pl.ds(512, 128)].astype(F32), w[1, :, pl.ds(512, 128)].astype(F32)
    wp[2, :, pl.ds(256, 128)] = jnp.where(lo, b0, pltpu.roll(b1, 64, 1)).astype(BF)

def tiles(rows, length):
    mem = (length, rows - length, True)
    out = []
    for a in range(0, length, 256):
        spans = []
        if a:
            spans.append((0, a, False))
        spans.append((a, min(512, length - a), True))
        out.append((a, 256, spans + [mem]))
    out.append((length, rows - length, [(0, length, True), mem]))
    return out

def scores_of(kt, qm, idk, idq, p, spans):
    out = []
    for k0, kn, masked in spans:
        s = nt(kt[p, pl.ds(k0, kn), :], qm)
        if masked:
            s = jnp.where(idk[pl.ds(k0, kn), 0:1] <= idq, s, NEG)
        out.append(s)
    return out

def attn_fwd_kernel(xt, wa_hbm, bias, idk, idq, x, qt, kt, vt, mixed, lse, w, wp, vtt, ot, sem):
    feats = xt.shape[0]; rows = x.shape[0]; length = xt.shape[1] - 128
    c = pltpu.make_async_copy(wa_hbm, w, sem); c.start()
    for i in range(length // 128):
        x[pl.ds(128 * i, 128), :] = xt[:, pl.ds(128 * i, 128)].T
    x[pl.ds(length, rows - length), :] = xt[:, pl.ds(length, 128)].T[: rows - length, :]
    c.wait()
    assemble_pairs(w, wp, feats)
    rc = rows // 3

    def project(i, _):
        p = i // 3
        r = pl.ds(pl.multiple_of((i % 3) * rc, 16), rc)
        v = nn(x[r, :], wp[p]) + bias[p]
        qt[p, r, :] = (v[:, :128].astype(BF).astype(F32) * 0.125).astype(BF)
        kt[p, r, :] = v[:, 128:256].astype(BF)
        vt[p, r, :] = v[:, 256:].astype(BF)
        return 0
    lax.fori_loop(0, 9, project, 0)

    def pair(p, _):
        vtt[...] = vt[p].T
        for e in range(2):
            lanes = (tn_lanes() < 64) if e == 0 else (tn_lanes() >= 64)
            for q0, qn, spans in tiles(rows, length):
                q = qt[p, pl.ds(q0, qn), :]
                qm = jnp.where(lanes, q, jnp.zeros_like(q))
                ss = scores_of(kt, qm, idk, idq[0:1, pl.ds(q0, qn)], p, spans)
                m = jnp.max(ss[0], axis=0, keepdims=True)
                for s in ss[1:]:
                    m = jnp.maximum(m, jnp.max(s, axis=0, keepdims=True))
                tot, acc = None, None
                for s, (k0, kn, _) in zip(ss, spans):
                    ex = jnp.exp(s - m)
                    t = jnp.sum(ex, axis=0, keepdims=True)
                    o = nn(vtt[pl.ds(64 * e, 64), pl.ds(k0, kn)], ex.astype(BF))
                    tot = t if tot is None else tot + t
                    acc = o if acc is None else acc + o
                ot[pl.ds(64 * e, 64), pl.ds(q0, qn)] = acc / tot
                lse[p, e, :, pl.ds(q0, qn)] = m + jnp.log(tot)
        mixed[p] = ot[...].T.astype(BF)
        return 0
    lax.fori_loop(0, 3, pair, 0)

def attn_fwd(xt, wa, bias, idk, idq, rows):
    feats = xt.shape[0]
    V = lambda *s, d=BF: pltpu.VMEM(s, d)
    vm = pl.BlockSpec(memory_space=pltpu.VMEM); an = pl.BlockSpec(memory_space=pl.ANY)
    S = jax.ShapeDtypeStruct
    t3 = S((3, rows, 128), BF)
    return pl.pallas_call(attn_fwd_kernel,
        out_shape=(S((rows, feats), BF), t3, t3, t3, t3, S((3, 2, 1, rows), F32)),
        in_specs=[vm, an, vm, vm, vm], out_specs=(vm,) * 6,
        scratch_shapes=[V(*wa.shape), V(3, feats, 384), V(128, rows), V(128, rows, d=F32), pltpu.SemaphoreType.DMA],
        compiler_params=pltpu.CompilerParams(vmem_limit_bytes=63*2**20))(xt, wa, bias, idk, idq)

def attn_bwd_kernel(ga, mixed, xt, qt, kt, vt, lse, idk, idq, wa_hbm, gpart, bgrad, gown_hbm, w, wp, wt, gat, gm, gp, dv, dk, dqt, ktt, dd, ro, gown, sem):
    feats = xt.shape[0]; rows = ga.shape[0]; length = xt.shape[1] - 128
    c = pltpu.make_async_copy(wa_hbm, w, sem); c.start()
    gat[...] = ga[...].T
    c.wait()
    assemble_pairs(w, wp, feats)
    wt[:, pl.ds(0, 128)] = w[0, :, pl.ds(640, 128)]
    wt[:, pl.ds(128, 128)] = w[1, :, pl.ds(640, 128)]
    lo = lax.broadcasted_iota(jnp.int32, (feats, 128), 1) < 64
    wt[:, pl.ds(256, 128)] = jnp.where(lo, pltpu.roll(w[0, :, pl.ds(512, 128)].astype(F32), 64, 1), w[1, :, pl.ds(512, 128)].astype(F32)).astype(BF)
    for p in range(3):
        gm[p] = nn(ga[...], wt[:, pl.ds(128 * p, 128)]).astype(BF)

    def pair(p, _):
        ktt[...] = kt[p].T
        prod = (gm[p].astype(F32) * mixed[p].astype(F32)).T
        dd[0:1, :] = jnp.sum(prod[:64, :], axis=0, keepdims=True)
        dd[1:2, :] = jnp.sum(prod[64:, :], axis=0, keepdims=True)
        dv[...] = jnp.zeros_like(dv)
        dk[...] = jnp.zeros_like(dk)
        for e in range(2):
            lanes = (tn_lanes() < 64) if e == 0 else (tn_lanes() >= 64)
            for q0, qn, spans in tiles(rows, length):
                q = qt[p, pl.ds(q0, qn), :]
                qm = jnp.where(lanes, q, jnp.zeros_like(q))
                g = gm[p, pl.ds(q0, qn), :]
                gmm = jnp.where(lanes, g, jnp.zeros_like(g))
                ss = scores_of(kt, qm, idk, idq[0:1, pl.ds(q0, qn)], p, spans)
                l = lse[p, e, :, pl.ds(q0, qn)]
                d = dd[pl.ds(e, 1), pl.ds(q0, qn)]
                acc = None
                for s, (k0, kn, _) in zip(ss, spans):
                    pr = jnp.exp(s - l)
                    dp = nt(vt[p, pl.ds(k0, kn), :], gmm)
                    ds = (pr * (dp - d)).astype(BF)
                    dv[pl.ds(k0, kn), :] += nn(pr.astype(BF), gmm)
                    dk[pl.ds(k0, kn), :] += nn(ds, qm)
                    o = nn(ktt[pl.ds(64 * e, 64), pl.ds(k0, kn)], ds)
                    acc = o if acc is None else acc + o
                dqt[pl.ds(64 * e, 64), pl.ds(q0, qn)] = acc * 0.125
        gp[p, :, pl.ds(0, 128)] = dqt[...].T.astype(BF)
        gp[p, :, pl.ds(128, 128)] = dk[...].astype(BF)
        gp[p, :, pl.ds(256, 128)] = dv[...].astype(BF)
        return 0
    lax.fori_loop(0, 3, pair, 0)
    for p in range(3):
        bgrad[p] = group_sum(gp[p].astype(F32))
    r3 = rows // 3

    def rowsgrad(i, _):
        r = pl.ds(pl.multiple_of(i * r3, 16), r3)
        gpart[r, :] = nt(gp[0, r, :], wp[0]) + nt(gp[1, r, :], wp[1]) + nt(gp[2, r, :], wp[2])
        return 0
    lax.fori_loop(0, 3, rowsgrad, 0)
    fc = 256
    for f0 in range(0, feats, fc):
        f = pl.ds(f0, fc)
        xf = xt[f, pl.ds(0, rows)]
        af = gat[f, :]
        r0 = nn(xf, gp[0]); r1 = nn(xf, gp[1]); r2 = nn(xf, gp[2])
        o = [nn(af, mixed[p]) for p in range(3)]
        lo = lax.broadcasted_iota(jnp.int32, (fc, 128), 1) < 64
        rq, rk, rv = r2[:, :128], r2[:, 128:256], r2[:, 256:]
        sw = lambda a: pltpu.roll(a, 64, 1)
        gown[0, f, pl.ds(0, 384)] = r0.astype(BF)
        gown[1, f, pl.ds(0, 384)] = r1.astype(BF)
        gown[0, f, pl.ds(384, 128)] = jnp.where(lo, rq, sw(rk)).astype(BF)
        gown[1, f, pl.ds(384, 128)] = jnp.where(lo, sw(rq), rk).astype(BF)
        gown[0, f, pl.ds(512, 128)] = jnp.where(lo, rv, sw(o[2])).astype(BF)
        gown[1, f, pl.ds(512, 128)] = jnp.where(lo, sw(rv), o[2]).astype(BF)
        gown[0, f, pl.ds(640, 128)] = o[0].astype(BF)
        gown[1, f, pl.ds(640, 128)] = o[1].astype(BF)
    c = pltpu.make_async_copy(gown, gown_hbm, sem); c.start(); c.wait()

def attn_bwd(ga, mixed, xt, qt, kt, vt, lse, idk, idq, wa):
    feats = xt.shape[0]; rows = ga.shape[0]
    V = lambda *s, d=BF: pltpu.VMEM(s, d)
    vm = pl.BlockSpec(memory_space=pltpu.VMEM); an = pl.BlockSpec(memory_space=pl.ANY)
    S = jax.ShapeDtypeStruct
    return pl.pallas_call(attn_bwd_kernel,
        out_shape=(S((rows, feats), F32), S((3, 8, 384), F32), S(wa.shape, BF)),
        in_specs=[vm] * 9 + [an], out_specs=(vm, vm, an),
        scratch_shapes=[V(*wa.shape), V(3, feats, 384), V(feats, 384), V(feats, rows), V(3, rows, 128), V(3, rows, 384), V(rows, 128, d=F32), V(rows, 128, d=F32),
            V(128, rows, d=F32), V(128, rows), V(8, rows, d=F32), V(8, 128), V(*wa.shape), pltpu.SemaphoreType.DMA],
        compiler_params=pltpu.CompilerParams(vmem_limit_bytes=63*2**20))(ga, mixed, xt, qt, kt, vt, lse, idk, idq, wa)
MESH = pl.DeviceIdType.MESH

class Move:
    def __init__(self, net, src, dst, dev, index):
        self.net, self.src, self.dst, self.dev, self.index = net, src, dst, dev, index
    def make(self):
        return pltpu.make_async_remote_copy(src_ref=self.src(), dst_ref=self.dst(), send_sem=self.net.ss.at[self.index],
                                            recv_sem=self.net.rs.at[self.index], device_id=self.dev, device_id_type=MESH)
    def start(self):
        self.make().start()
    def wait_recv(self):
        self.make().wait_recv()
    def wait_send(self):
        self.make().wait_send()

class Copy:
    def __init__(self, net, src, dst, index):
        self.net, self.src, self.dst, self.index = net, src, dst, index
    def make(self):
        return pltpu.make_async_copy(self.src(), self.dst(), self.net.ls.at[self.index])
    def start(self):
        self.make().start()
    def wait(self):
        self.make().wait()

class Net:
    def __init__(self, send_sems, recv_sems, local_sems):
        self.ss, self.rs, self.ls = send_sems, recv_sems, local_sems
        self.count, self.locals, self.moves, self.copies = 0, 0, [], []
        self.d, self.z, self.c = (lax.axis_index(a) for a in ("dp", "row", "col"))
        self.nd, self.nz = lax.axis_size("dp"), lax.axis_size("row")
        self.y, self.k = self.c // 2, self.c % 2
        self.x = self.d % 2
        self.oc = lax.rem(self.c + 2, 4)
        self.xp = (self.d + 1 - 2 * self.x, self.z, self.c)
        self.yp = (self.d, self.z, self.oc)
        self.kp = (self.d, self.z, self.c + 1 - 2 * self.k)
        self.ykp = (self.d, self.z, 3 - self.c)
        self.zs = [lax.rem(self.z + i, self.nz) for i in range(self.nz)]
        self.zp = [(self.d, zz, self.c) for zz in self.zs]
        self.others = [(lax.rem(self.d + 2 * i, self.nd), self.z, self.c) for i in range(1, self.nd // 2)]
    def from_row(self, i):
        return self.zs[(self.nz - i) % self.nz]
    def barrier(self, peers):
        b = pltpu.get_barrier_semaphore()
        for p in peers:
            pl.semaphore_signal(b, inc=1, device_id=p, device_id_type=MESH)
        pl.semaphore_wait(b, len(peers))
    def move(self, src, dst, dev):
        m = Move(self, src, dst, dev, self.count)
        self.count += 1
        self.moves.append(m)
        return m
    def send(self, src, dst, dev):
        m = self.move(src, dst, dev)
        m.start()
        return m
    def copy(self, src, dst):
        m = Copy(self, src, dst, self.locals)
        self.locals += 1
        self.copies.append(m)
        return m
    def local(self, src, dst):
        m = self.copy(src, dst)
        m.start()
        return m
    def finish(self):
        for m in self.moves:
            m.wait_send()

def at(i, table):
    for j, events in table.items():
        if events:
            @pl.when(i == j)
            def _(events=events):
                for e in events:
                    e()

def spread_events(events, steps):
    table = {}
    for n, e in enumerate(events):
        table.setdefault(n * steps // len(events), []).append(e)
    return table

def join192(t, dst):
    lo = lax.broadcasted_iota(jnp.int32, t[0][0].shape, 1) < 64
    sw = lambda a: pltpu.roll(a, 64, 1)
    for h in range(2):
        a, b = t[2 * h], t[2 * h + 1]
        dst[:, pl.ds(384 * h, 128)] = a[0]
        dst[:, pl.ds(384 * h + 128, 128)] = jnp.where(lo, a[1], sw(b[0]))
        dst[:, pl.ds(384 * h + 256, 128)] = jnp.where(lo, sw(b[0]), sw(b[1]))

def row_ids(ids, y, half, idk, idq):
    length = ids.shape[1]
    idq[:, pl.ds(0, length)] = ids[pl.ds(y, 1), :].astype(F32)
    i = lax.broadcasted_iota(jnp.int32, (1, 128), 1)
    idq[:, pl.ds(length, 128)] = jnp.where(i < half, -1.0, jnp.where(i < 2 * half, 1.0 * length, 2.0 * length))
    for j in range(length // 128 + 1):
        idk[pl.ds(128 * j, 128), :] = jnp.broadcast_to(idq[:, pl.ds(128 * j, 128)], (128, 128)).T

def pack_inputs(w3, wo, la, vecs, bias_up, bias_qv, scale, ls, memory, mtmp, mem):
    b = w3.shape[1]
    f = lambda r: r.astype(F32)
    lo = lax.broadcasted_iota(jnp.int32, (b, 128), 1) < 64
    t0, t1 = f(w3[0, :, pl.ds(0, 128)]), f(w3[1, :, pl.ds(0, 128)])
    la[:, pl.ds(0, 128)] = jnp.where(lo, t0, pltpu.roll(t1, 64, 1)).astype(BF)
    la[:, pl.ds(128, 128)] = jnp.where(lo, pltpu.roll(t0, 64, 1), t1).astype(BF)
    v = [f(w3[j, :, pl.ds(128, 64)]) for j in range(3)]
    la[:, pl.ds(256, 128)] = jnp.concatenate([v[0], v[1]], axis=1).astype(BF)
    la[:, pl.ds(384, 128)] = w3[2, :, pl.ds(0, 128)]
    wot = f(wo[...]).T
    la[:, pl.ds(512, 128)] = jnp.concatenate([v[2], wot[:, 128:]], axis=1).astype(BF)
    la[:, pl.ds(640, 128)] = wot[:, :128].astype(BF)
    ls[...] = jnp.zeros_like(ls)
    for j, r in enumerate(vecs):
        ls[pl.ds(j, 1), pl.ds(0, b)] = r[...]
    ls[pl.ds(6, 1), :] = scale
    for j in range(3):
        ls[pl.ds(8 + j, 1), :] = bias_up[:, pl.ds(256 * j, 256)]
    ls[pl.ds(11, 1), pl.ds(0, 128)] = bias_qv[0:1, :]
    ls[pl.ds(11, 1), pl.ds(128, 128)] = bias_qv[1:2, :]
    ls[pl.ds(12, 1), pl.ds(0, 128)] = bias_qv[2:3, :]
    mtmp[...] = jnp.zeros_like(mtmp)
    for s in range(2):
        mtmp[pl.ds(0, memory.shape[1]), :] = f(memory[s])
        mem[s] = mtmp[...].T.astype(BF)

def forward_kernel(valid_ref, tok, memory, tch, w3, wo, lu, ld, v0, v1, v2, v3, v4, v5, bias_up, bias_qv, ids,
                   xt_o, q_o, k_o, v_o, mixed_o, wa_o, ga_o, hu_o, hd_o, lse, g_one, vgrad, bupgrad, out4,
                   xt, x, wa, wu, wd, sm, tt, tr, wp, qt, kt, vt, vtt, ot, mixed, mrows, bias, vec, wt,
                   h1, h2, rs1, low, lowt, br, brt, hid, dgl, gdz, guz, hu, hd, ru, rd, ga, o4, la, ls, mem, mtmp, idk, idq, ss, rs, lsem, zsem, zrem):
    n = Net(ss, rs, lsem)
    total = lax.fori_loop(0, valid_ref.shape[0], lambda i, t: t + valid_ref[i], jnp.int32(0))
    count = valid_ref[(n.d * n.nz + n.z) * 2 + n.y]
    scale_row = (valid_ref.shape[0] * tok.shape[2]) / jnp.full((1, 256), total, jnp.int32).astype(F32)
    pack_inputs(w3, wo, la, (v0, v1, v2, v3, v4, v5), bias_up, bias_qv, scale_row, ls, memory, mtmp, mem)
    n.barrier(n.zp[1:] + [n.yp, n.ykp, n.kp, n.xp])
    nz, y, k, c, z, oc = n.nz, n.y, n.k, n.c, n.z, n.oc
    b = la.shape[0]; hb = b // 2
    feats = x.shape[1]; rows = x.shape[0]; length = tok.shape[2]; main = length // 2
    own_rows = main + 16
    row = lambda cc, off=0, num=b: pl.ds(pl.multiple_of(cc * b + off, 16), num)
    blk = lambda w, zz, cc: (lambda: w.at[zz, row(cc)])
    hlf = lambda w, zz, cc, h: (lambda: w.at[zz, row(cc, h * hb, hb)])
    mine, theirs = n.x, 1 - n.x
    part = lambda w: (lambda: w.at[pl.ds(pl.multiple_of(n.x * hb, 16), hb)])
    all_of = lambda r: (lambda: r)
    tail = pl.ds(length, 128); body = pl.ds(0, length)
    fz = n.from_row
    R = range(1, nz)
    e1 = z + 1 - 2 * lax.rem(z, 2)
    e2 = lax.rem(z + 2, nz)
    e3 = lax.rem(e1 + 2, nz)
    dev1, dev2 = (n.d, e1, c), (n.d, e2, c)
    order = [z, e2, e1, e3]
    s_blk = lambda zz, cc: (lambda: sm.at[zz, cc])
    fwd = lambda u, dev: n.move(u, u, dev)
    local = [n.local(lambda: tok.at[y], lambda: xt.at[row(c), body]), n.local(lambda: mem.at[y], lambda: xt.at[row(c), tail])]
    au = lambda zz, cc: hlf(wa, zz, cc, mine)
    a2 = n.send(part(la), au(z, c), dev2)
    a1 = n.send(part(la), au(z, c), dev1)
    a_y = [n.send(part(la), au(z, c), n.yp)]
    a_k = [n.send(all_of(la), blk(wa, z, c), n.kp)]
    s_z = [n.send(all_of(ls), s_blk(z, c), n.zp[i]) for i in R]
    s_y = [n.send(all_of(ls), s_blk(z, c), n.yp)]
    s_k = [n.send(all_of(ls), s_blk(z, c), n.kp)]
    t_k = [n.send(lambda: tok.at[y], lambda: xt.at[row(c), body], n.kp), n.send(lambda: mem.at[y], lambda: xt.at[row(c), tail], n.kp)]
    for w, l in ((wa, la), (wu, lu), (wd, ld)):
        local.append(n.local(all_of(l), blk(w, z, c)))
    local.append(n.local(all_of(ls), s_blk(z, c)))
    a_x, a_xu = [], []
    def pass_on(u, lists):
        for lst, dev in lists:
            lst.append(fwd(u, dev)); lst[-1].start()
    def a_own(zz):
        a_xu.append((zz, c))
        pass_on(au(zz, c), ((a_x, n.xp), (a_y, n.yp), (a_k, n.kp)))
    def a_far(i):
        a_y[i].wait_recv()
        a_xu.append((order[i], oc))
        pass_on(au(order[i], oc), ((a_x, n.xp), (a_k, n.kp)))
    def a_home(i):
        a_x[i].wait_recv()
        pass_on(hlf(wa, *a_xu[i], theirs), ((a_k, n.kp),))
    a_far(0)
    a2.wait_recv()
    a3 = fwd(au(e2, c), dev1); a3.start()
    a_own(e2)
    t_y = [n.send(lambda: tok.at[1 - y], lambda: xt.at[row(c), body], n.yp), n.send(lambda: mem.at[1 - y], lambda: xt.at[row(c), tail], n.yp)]
    a1.wait_recv()
    a_own(e1)
    a_far(1)
    for i in R:
        s_z[i - 1].wait_recv()
        pass_on(s_blk(fz(i), c), ((s_y, n.yp), (s_k, n.kp)))
    a3.wait_recv()
    a_own(e3)
    uu = lambda zz, cc: blk(wu, zz, cc)
    du = lambda zz, cc: hlf(wd, zz, cc, mine)
    u2 = n.send(all_of(lu), uu(z, c), dev2)
    u1 = n.send(all_of(lu), uu(z, c), dev1)
    d_y = n.send(part(ld), du(z, c), n.yp)
    u_y = [n.send(all_of(lu), uu(z, c), n.yp)]
    u_k = {0: n.send(all_of(lu), uu(z, c), n.kp)}
    d_k = [n.send(all_of(ld), blk(wd, z, c), n.kp)]
    tsl = lambda s, kk: (lambda: tch.at[s, :, pl.ds(pl.multiple_of(kk * main, 128), main)])
    th = lambda: tt.at[row(c)]
    h_y = [n.send(tsl(y, 1 - k), th, n.kp)]
    local.append(n.local(tsl(y, k), th))
    row_ids(ids, y, memory.shape[1] // 2, idk, idq)
    for m, w_ in zip(t_y, (body, tail)):
        m.wait_recv()
        t_k.append(fwd((lambda w_=w_: xt.at[row(oc), w_]), n.kp)); t_k[-1].start()
    for i in range(3):
        a_home(i)
    local[0].wait(); local[1].wait()
    for m in t_k:
        m.wait_recv()
    def turn(i, _):
        f = pl.ds(pl.multiple_of(128 * i, 128), 128)
        x[f, :] = xt[:, f].T
        return 0
    lax.fori_loop(0, length // 128, turn, 0)
    x[pl.ds(length, rows - length), :] = xt[:, tail].T[: rows - length, :]
    o_x = n.local(all_of(xt), all_of(xt_o))
    for i in range(nz):
        s_y[i].wait_recv()
        pass_on(s_blk(fz(i), oc), ((s_k, n.kp),))
    a_far(2)
    a_far(3)
    for i in range(3, 5):
        a_home(i)
    u2.wait_recv()
    u3 = fwd(uu(e2, c), dev1); u3.start()
    d2 = n.send(part(ld), du(z, c), dev2)
    d1 = n.send(part(ld), du(z, c), dev1)
    def u_put(i, cc, y_too=True):
        m = fwd(uu(order[i], cc), n.kp)
        u_k[(i, cc is oc)] = m
        if y_too:
            u_y.append(fwd(uu(order[i], cc), n.yp))
            u_y[-1].start()
        m.start()
    u_put(1, c)
    d_y.wait_recv()
    d_x, d_xu = [], []
    def d_put(zz, cc):
        d_xu.append((zz, cc))
        d_x.append(fwd(du(zz, cc), n.xp)); d_k.append(fwd(du(zz, cc), n.kp))
        return [d_x[-1], d_k[-1]]
    for m in d_put(z, oc):
        m.start()
    for i in range(5, 7):
        a_home(i)
    def step(wait, moves):
        def run():
            wait.wait_recv()
            for m in moves:
                m.start()
        return run
    def u_step(wait, i):
        u_y.append(fwd(uu(order[i], c), n.yp))
        u_w.append(fwd(uu(order[i], c), n.kp))
        return step(wait, [u_y[-1], u_w[-1]])
    u_w = list(u_k.values())
    def u_far(i):
        u_w.append(fwd(uu(order[i], oc), n.kp))
        return step(u_y[i], [u_w[-1]])
    d3, d2o, d1o, d3o = fwd(du(e2, c), dev1), fwd(du(z, oc), dev2), fwd(du(z, oc), dev1), fwd(du(e2, oc), dev1)
    E_u1 = u_step(u1, 2)
    E_u3 = u_step(u3, 3)
    h_m = [n.move(tsl(1 - y, k), th, n.yp), n.move(tsl(1 - y, 1 - k), th, n.ykp)]
    def E_h():
        for m in h_m:
            m.start()
    h_y += h_m
    E_uy = [u_far(i) for i in range(4)]
    E_d2 = step(d2, [d3] + d_put(e2, c))
    def E_do():
        d2o.start(); d1o.start()
    E_d1 = step(d1, d_put(e1, c))
    E_d3 = step(d3, d_put(e3, c))
    E_d2o = step(d2o, [d3o] + d_put(e2, oc))
    E_d1o = step(d1o, d_put(e1, oc))
    E_d3o = step(d3o, d_put(e3, oc))
    E_dx = []
    for m, (zz, cc) in zip(d_x, d_xu):
        d_k.append(fwd(hlf(wd, zz, cc, theirs), n.kp))
        E_dx.append(step(m, [d_k[-1]]))
    proj_events = {1: [E_u1], 8: [E_u3, E_h]}
    head_events = {2: [E_do, E_dx[0]], 4: [E_uy[0]], 6: [E_d2], 8: [E_d1], 10: [E_d3, E_uy[1]], 12: [E_dx[1], E_dx[2]], 14: [E_d2o, E_uy[2]], 16: [E_d1o, E_dx[3]]}
    out_events = [E_d3o]
    gate_events = {0: [], 3: [], 6: [E_dx[4], E_dx[5]], 9: [E_dx[6]]}
    for m in s_k:
        m.wait_recv()
    for m in local[2:6]:
        m.wait()
    join192([[sm[0, cc, pl.ds(0, 8), pl.ds(0, 128)], sm[0, cc, pl.ds(0, 8), pl.ds(128, 128)]] for cc in range(4)], vec)
    lo1 = lax.broadcasted_iota(jnp.int32, (1, 128), 1) < 64
    sw = lambda a: pltpu.roll(a, 64, 1)
    bias[...] = jnp.zeros_like(bias)
    hv = [[sm[2 * k + j, 0, 11:12, pl.ds(0, 128)], sm[2 * k + j, 0, 11:12, pl.ds(128, 128)], sm[2 * k + j, 0, 12:13, pl.ds(0, 128)]] for j in range(2)]
    for p, (ea, eb) in enumerate(((hv[0][0], hv[0][1]), (hv[1][0], hv[1][1]), (hv[0][2], hv[1][2]))):
        w8 = lambda a: jnp.broadcast_to(a, (8, 128))
        lo8 = lax.broadcasted_iota(jnp.int32, (8, 128), 1) < 64
        bias[p, :, pl.ds(0, 128)] = jnp.where(lo8, w8(ea), sw(w8(eb)))
        bias[p, :, pl.ds(256, 128)] = jnp.where(lo8, sw(w8(ea)), w8(eb))
    for m in a_k:
        m.wait_recv()
    own = pl.ds(2 * k, 2)
    o_w = n.local(lambda: wa.at[own], all_of(wa_o))
    w = wa.at[own]
    assemble_pairs(w, wp, feats)
    rc = rows // 3

    def project(i, _):
        p = i // 3
        r = pl.ds(pl.multiple_of((i % 3) * rc, 16), rc)
        v = nn(x[r, :], wp[p]) + bias[p, 0:1, :]
        qt[p, r, :] = (v[:, :128].astype(BF).astype(F32) * 0.125).astype(BF)
        kt[p, r, :] = v[:, 128:256].astype(BF)
        vt[p, r, :] = v[:, 256:].astype(BF)
        at(i, proj_events)
        return 0
    lax.fori_loop(0, 9, project, 0)
    o_q = [n.local(all_of(a), all_of(o)) for a, o in ((qt, q_o), (kt, k_o), (vt, v_o))]
    m_k = [(n.move((lambda p=p: mixed.at[p, pl.ds(pl.multiple_of((1 - k) * main, 16), main)]), (lambda p=p: mrows.at[k * 3 + p, pl.ds(0, main)]), n.kp),
            n.move((lambda p=p: mixed.at[p, pl.ds(pl.multiple_of(length + (1 - k) * 16, 16), 16)]), (lambda p=p: mrows.at[k * 3 + p, pl.ds(main, 16)]), n.kp)) for p in range(3)]
    m_l = [(n.copy((lambda p=p: mixed.at[p, pl.ds(pl.multiple_of(k * main, 16), main)]), (lambda p=p: mrows.at[k * 3 + p, pl.ds(0, main)])),
            n.copy((lambda p=p: mixed.at[p, pl.ds(pl.multiple_of(length + k * 16, 16), 16)]), (lambda p=p: mrows.at[k * 3 + p, pl.ds(main, 16)]))) for p in range(3)]
    cuts = {1: 0, 3: 1, 4: 2}

    def head(i, _):
        p = i // 2
        e = i % 2
        he = pl.ds(pl.multiple_of(64 * e, 64), 64)

        @pl.when(e == 0)
        def _():
            vtt[...] = vt[p].T
        lanes = (lax.broadcasted_iota(jnp.int32, (1, 128), 1) // 64) == e
        for t_, (q0, qn, spans) in enumerate(tiles(rows, length)):
            q = qt[p, pl.ds(q0, qn), :]
            qm = jnp.where(lanes, q, jnp.zeros_like(q))
            sc = scores_of(kt, qm, idk, idq[0:1, pl.ds(q0, qn)], p, spans)
            m = jnp.max(sc[0], axis=0, keepdims=True)
            for s in sc[1:]:
                m = jnp.maximum(m, jnp.max(s, axis=0, keepdims=True))
            tot, acc = None, None
            for s, (k0, kn, _) in zip(sc, spans):
                ex = jnp.exp(s - m)
                t = jnp.sum(ex, axis=0, keepdims=True)
                o = nn(vtt[he, pl.ds(k0, kn)], ex.astype(BF))
                tot = t if tot is None else tot + t
                acc = o if acc is None else acc + o
            ot[he, pl.ds(q0, qn)] = acc / tot
            lse[i, :, pl.ds(q0, qn)] = m + jnp.log(tot)
            if t_ in cuts:
                at(3 * i + cuts[t_], head_events)

        @pl.when(e == 1)
        def _():
            mixed[p] = ot[...].T.astype(BF)
        at(i, {2 * p + 1: [m.start for m in m_k[p] + m_l[p]] for p in range(3)})
        return 0
    lax.fori_loop(0, 6, head, 0)
    o_m = n.local(all_of(mixed), all_of(mixed_o))
    lo = lax.broadcasted_iota(jnp.int32, (feats, 128), 1) < 64
    for kk in range(2):
        z0, z1 = 2 * kk, 2 * kk + 1
        wt[:, pl.ds(384 * kk, 128)] = wa[z0, :, pl.ds(640, 128)]
        wt[:, pl.ds(384 * kk + 128, 128)] = wa[z1, :, pl.ds(640, 128)]
        t0 = pltpu.roll(wa[z0, :, pl.ds(512, 128)].astype(F32), 64, 1)
        wt[:, pl.ds(384 * kk + 256, 128)] = jnp.where(lo, t0, wa[z1, :, pl.ds(512, 128)].astype(F32)).astype(BF)
    for pair_ in m_k:
        for m in pair_:
            m.wait_recv()
    for pair_ in m_l:
        for m in pair_:
            m.wait()
    nb = feats // 256
    CHS = own_rows // CH

    def own_slice(i, num):
        start = jnp.where(i < main, k * main + i, length + k * 16)
        return pl.ds(pl.multiple_of(start, 16), num)

    for f0 in range(0, feats, 256):
        f = pl.ds(f0, 256)
        acc = nt(mrows[0], wt[f, pl.ds(0, 128)])
        for j in range(1, 6):
            acc = acc + nt(mrows[j], wt[f, pl.ds(128 * j, 128)])
        h1[:, f] = acc + vec[0:1, f]
    for e in out_events:
        e()
    inv = 1.0 / feats
    vgrad[...] = jnp.zeros_like(vgrad)
    bupgrad[...] = jnp.zeros_like(bupgrad)

    def norm1(i, _):
        r = pl.ds(pl.multiple_of(i * 16, 16), 16)
        h = h1[r, :] + x[own_slice(i * 16, 16), :].astype(F32)
        m = jnp.sum(h, axis=1, keepdims=True) * inv
        s = jnp.sum(h * h, axis=1, keepdims=True) * inv
        rstd = lax.rsqrt(s - m * m + EPSILON)
        xhat = (h - m) * rstd
        h1[r, :] = xhat
        rs1[r, :] = jnp.broadcast_to(rstd, (16, 128))
        low[r, :] = (xhat * vec[1:2, :] + vec[2:3, :]).astype(BF)
        return 0
    lax.fori_loop(0, own_rows // 16, norm1, 0, unroll=3)
    lowt[...] = low[...].T
    E_uy[3]()
    for m in u_w:
        m.wait_recv()

    def gate(i, _):
        at(i, gate_events)
        zz = i // nb
        j = i % nb
        f = pl.ds(pl.multiple_of(j * 256, 256), 256)
        v = nn(low[...], wu[zz, :, f]) + sm[zz, 0, pl.ds(8 + j, 1), :]
        a, g = gelu_pair(v)
        hid[zz, :, f] = a.astype(BF)
        dgl[zz, :, f] = g.astype(BF)
        return 0
    lax.fori_loop(0, nz * nb, gate, 0)
    for m in h_y:
        m.wait_recv()
    local[6].wait()
    def turn_t(i, _):
        f = pl.ds(pl.multiple_of(128 * i, 128), 128)
        tr[f, :] = tt[:, f].T
        return 0
    lax.fori_loop(0, main // 128, turn_t, 0)
    tr[pl.ds(main, 16), :] = jnp.zeros((16, feats), BF)
    for m in d_k:
        m.wait_recv()

    def down(j, _):
        f = pl.ds(pl.multiple_of(j * 256, 256), 256)
        acc = nt(hid[0], wd[0, f, :])
        for zz in range(1, nz):
            acc = acc + nt(hid[zz], wd[zz, f, :])
        h2[:, f] = acc
        return 0
    lax.fori_loop(0, nb, down, 0)
    scale = vec[6:7, 0:1]
    o4[:, :, pl.ds(b, o4.shape[2] - b)] = jnp.zeros((4, own_rows, o4.shape[2] - b), BF)

    def norm2(i, _):
        r = pl.ds(pl.multiple_of(i * CH, 16), CH)
        h = h2[r, :] + (h1[r, :] * vec[1:2, :] + vec[2:3, :]) + vec[3:4, :]
        m = jnp.sum(h, axis=1, keepdims=True) * inv
        s = jnp.sum(h * h, axis=1, keepdims=True) * inv
        rstd = lax.rsqrt(s - m * m + EPSILON)
        xhat = (h - m) * rstd
        o = xhat * vec[4:5, :] + vec[5:6, :]
        for cc in range(4):
            o4[cc, r, pl.ds(0, b)] = o[:, cc * b:(cc + 1) * b].astype(BF)
        place = lax.broadcasted_iota(jnp.int32, (CH, 1), 0) + i * CH
        place = jnp.where(place < main, place + k * main, count)
        go = jnp.where(place < count, scale * (o - tr[r, :].astype(F32)), 0.0)
        a = go * vec[4:5, :]
        m1 = jnp.sum(a, axis=1, keepdims=True) * inv
        m2 = jnp.sum(a * xhat, axis=1, keepdims=True) * inv
        g2 = rstd * (a - m1 - xhat * m2)
        h2[r, :] = g2
        g2b = g2.astype(BF)
        br[r, :] = g2b
        vgrad[0] += group_sum(go * xhat)
        vgrad[1] += group_sum(go)
        vgrad[2] += group_sum(g2b.astype(F32))
        return 0
    lax.fori_loop(0, CHS, norm2, 0)
    o_dst = lambda: out4.at[y, k]
    o_s = [n.send(lambda: o4.at[oc], o_dst, n.yp), n.send(lambda: o4.at[3 - c], o_dst, n.ykp), n.send(lambda: o4.at[c + 1 - 2 * k], o_dst, n.kp)]
    o_l = n.local(lambda: o4.at[c], o_dst)
    brt[...] = br[...].T
    def gmove(which, src, dst, zz, slot, yy):
        return pltpu.make_async_remote_copy(src_ref=src.at[slot, 2 * yy + 1 - k], dst_ref=dst.at[yy, zz], send_sem=zsem.at[which, yy, zz],
                                            recv_sem=zrem.at[which, yy, zz], device_id=n.kp, device_id_type=MESH)
    def each(fn, zz, slot):
        for which, src, dst in ((0, gdz, rd), (1, guz, ru)):
            for yy in range(2):
                fn(gmove(which, src, dst, zz, slot, yy))
    def fold(zz):
        each(lambda m: m.wait_recv(), zz, 0)
        for yy in range(2):
            add_to(hd.at[yy, zz], rd.at[yy, zz])
            add_to(hu.at[yy, zz], ru.at[yy, zz])

    def back(zz, _):
        slot = zz % 2

        @pl.when(zz >= 2)
        def _():
            each(lambda m: m.wait_send(), zz - 2, slot)

        def chunk(j, _):
            f = pl.ds(pl.multiple_of(j * 256, 256), 256)
            gh = nn(br[...], wd[zz, :, f])
            g = (gh * dgl[zz, :, f].astype(F32)).astype(BF)
            bupgrad[zz, :, f] += group_sum(g.astype(F32))
            gdc = nn(brt[...], hid[zz, :, f])
            guc = nn(lowt[...], g)
            hid[zz, :, f] = g
            for cc in range(4):
                gdz[slot, cc, :, f] = gdc[cc * b:(cc + 1) * b, :].astype(BF)
                guz[slot, cc, :, f] = guc[cc * b:(cc + 1) * b, :].astype(BF)
            return 0
        lax.fori_loop(0, nb, chunk, 0)
        each(lambda m: m.start(), zz, slot)
        for yy in range(2):
            hd[yy, zz] = gdz[slot, 2 * yy + k]
            hu[yy, zz] = guz[slot, 2 * yy + k]

        @pl.when(zz >= 1)
        def _():
            fold(zz - 1)
        return 0
    lax.fori_loop(0, nz, back, 0)

    def first_grad(j, _):
        f = pl.ds(pl.multiple_of(j * 256, 256), 256)
        acc = h2[:, f]
        for zz in range(nz):
            acc = acc + nt(hid[zz], wu[zz, f, :])
        h2[:, f] = acc
        return 0
    lax.fori_loop(0, nb, first_grad, 0)
    fold(nz - 1)
    o_h = [n.local(all_of(hd), all_of(hd_o)), n.local(all_of(hu), all_of(hu_o))]

    def norm1_back(i, _):
        r = pl.ds(pl.multiple_of(i * 16, 16), 16)
        g = h2[r, :]
        xhat = h1[r, :]
        a = g * vec[1:2, :]
        m1 = jnp.sum(a, axis=1, keepdims=True) * inv
        m2 = jnp.sum(a * xhat, axis=1, keepdims=True) * inv
        g1 = rs1[r, 0:1] * (a - m1 - xhat * m2)
        g_one[r, :] = g1
        gb = g1.astype(BF)
        ga[own_slice(i * 16, 16), :] = gb
        vgrad[3] += group_sum(g * xhat)
        vgrad[4] += group_sum(g)
        vgrad[5] += group_sum(gb.astype(F32))
        return 0
    lax.fori_loop(0, own_rows // 16, norm1_back, 0, unroll=3)
    g_main = lambda: ga.at[pl.ds(pl.multiple_of(k * main, 16), main)]
    g_tail = lambda: ga.at[pl.ds(pl.multiple_of(length + k * 16, 16), 16)]
    g_k = [n.send(g_main, g_main, n.kp), n.send(g_tail, g_tail, n.kp)]
    for m in g_k:
        m.wait_recv()
    o_g = n.local(all_of(ga), all_of(ga_o))
    for m in o_s:
        m.wait_recv()
    for m in [o_x, o_w, o_m, o_l, o_g] + o_q + o_h:
        m.wait()
    for zz in range(nz - 2, nz):
        each(lambda m: m.wait_send(), zz, zz % 2)
    n.finish()

def add_to(dst, src):
    dst[...] = (dst[...].astype(F32) + src[...].astype(F32)).astype(BF)

def forward(valid, tok, memory, tch, w3, wo, lu, ld, vecs, bias_up, bias_qv, ids, nz):
    b, width = lu.shape
    feats = 4 * b; length = tok.shape[2]; rows = length + 32; main = length // 2; own = main + 16
    V = lambda *s, d=BF: pltpu.VMEM(s, d)
    vm = pl.BlockSpec(memory_space=pltpu.VMEM); sm = pl.BlockSpec(memory_space=pltpu.SMEM); an = pl.BlockSpec(memory_space=pl.ANY)
    S = jax.ShapeDtypeStruct
    t3 = S((3, rows, 128), BF); h = S((2, nz, b, width), BF)
    outs = [(S((feats, length + 128), BF), an), (t3, an), (t3, an), (t3, an), (t3, an), (S((2, feats, width), BF), an), (S((rows, feats), BF), an), (h, an), (h, an),
            (S((6, 1, rows), F32), vm), (S((own, feats), F32), vm), (S((6, 8, feats), F32), vm), (S((nz, 8, width), F32), vm), (S((2, 2, own, 256), BF), vm)]
    w = V(nz, feats, width)
    scratch = [V(feats, length + 128), V(rows, feats), w, w, w, V(nz, 4, 16, 256, d=F32), V(feats, main), V(own, feats), V(3, feats, 384),
               V(3, rows, 128), V(3, rows, 128), V(3, rows, 128), V(128, rows), V(128, rows, d=F32), V(3, rows, 128), V(6, own, 128), V(3, 8, 384, d=F32), V(8, feats, d=F32), V(feats, feats),
               V(own, feats, d=F32), V(own, feats, d=F32), V(own, 128, d=F32), V(own, feats), V(feats, own), V(own, feats), V(feats, own),
               V(nz, own, width), V(nz, own, width), V(2, 4, b, width), V(2, 4, b, width)] + [V(2, nz, b, width)] * 4 + [V(rows, feats), V(4, own, 256), V(b, width), V(16, 256, d=F32), V(2, b, 128), V(128, b, d=F32), V(length + 128, 128, d=F32), V(1, length + 128, d=F32),
               pltpu.SemaphoreType.DMA((136,)), pltpu.SemaphoreType.DMA((136,)), pltpu.SemaphoreType.DMA((32,)),
               pltpu.SemaphoreType.DMA((2, 2, nz)), pltpu.SemaphoreType.DMA((2, 2, nz))]
    return pl.pallas_call(forward_kernel, out_shape=[o for o, _ in outs], out_specs=[s for _, s in outs],
        in_specs=[sm, an, vm, an, vm, vm, an, an] + [vm] * 9, scratch_shapes=scratch,
        compiler_params=pltpu.CompilerParams(collective_id=1, has_side_effects=True, vmem_limit_bytes=67043328))(valid, tok, memory, tch, w3, wo, lu, ld, *vecs, bias_up, bias_qv, ids)
def total_of(refs):
    acc = refs[0][...].astype(F32)
    for r in refs[1:]:
        acc = acc + r[...].astype(F32)
    return acc

class Piece:
    def __init__(self, n, env, col0, num, js, x_first):
        self.n, self.x_first = n, x_first
        gown, ha, ax, ay, ayf, axf, mine, theirs, order = env
        C = pl.ds(col0, num); y, k = n.y, n.k
        self.core = [n.move((lambda j=j, yy=yy: gown.at[j, 2 * yy + 1 - k, :, C]), (lambda j=j, yy=yy: ha.at[yy, 2 * k + j, :, C]), n.kp) for j in js for yy in range(2)]
        self.keep = [n.copy((lambda j=j, yy=yy: gown.at[j, 2 * yy + k, :, C]), (lambda j=j, yy=yy: ha.at[yy, 2 * k + j, :, C])) for j in js for yy in range(2)]
        zz = order if len(js) == 2 else [js[0], js[0] + 2]
        self.first, self.second, self.add1, self.add2 = [], [], [], []
        for q in zz:
            if x_first:
                self.first.append(n.move((lambda q=q: ha.at[:, q, theirs, C]), (lambda q=q: ax.at[:, q, :, C]), n.xp))
                self.add1.append(lambda q=q: [add_to(ha.at[yy, q, mine, C], ax.at[yy, q, :, C]) for yy in range(2)])
                self.second.append(n.move((lambda q=q: ha.at[1 - y, q, mine, C]), (lambda q=q: ay.at[q, :, C]), n.yp))
                self.add2.append(lambda q=q: add_to(ha.at[y, q, mine, C], ay.at[q, :, C]))
            else:
                self.first.append(n.move((lambda q=q: ha.at[1 - y, q, :, C]), (lambda q=q: ayf.at[q, :, C]), n.yp))
                self.add1.append(lambda q=q: add_to(ha.at[y, q, :, C], ayf.at[q, :, C]))
                self.second.append(n.move((lambda q=q: ha.at[y, q, theirs, C]), (lambda q=q: axf.at[q, :, C]), n.xp))
                self.add2.append(lambda q=q: add_to(ha.at[y, q, mine, C], axf.at[q, :, C]))
    def start(self):
        for m in self.core + self.keep:
            m.start()
    def ev1(self):
        for m in self.core:
            m.wait_recv()
        for m in self.keep:
            m.wait()
        for m in self.first:
            m.start()
    def ev2(self):
        for m, f, s in zip(self.first, self.add1, self.second):
            m.wait_recv(); f(); s.start()
    def ev3(self):
        for m, f in zip(self.second, self.add2):
            m.wait_recv(); f()

class Rows:
    def __init__(self, n, here, z1, z2, e, dev1, dev2, add):
        e1, e2, e3 = e
        self.a = n.move((lambda: here(e3)), (lambda: z1(1)), dev1)
        self.b = n.move((lambda: here(e1)), (lambda: z1(0)), dev1)
        self.c = n.move((lambda: here(e2)), z2, dev2)
        self.mid = lambda: add(here(e2), z1(1))
    def start(self):
        self.a.start(); self.b.start()
    def middle(self):
        self.a.wait_recv(); self.mid(); self.c.start()
    def end(self):
        self.b.wait_recv(); self.c.wait_recv()

def backward_kernel(hu_h, hd_h, ga_h, mixed_h, xt_h, q_h, k_h, v_h, w_h, o4_h, g1_h, lse, vgrad, bupgrad, ids,
                    grad4, lout, gmem, g3, gwo, fu, fd, fvec, bup, bqv,
                    hu, hd, ux, uz1, uz2, ut, uy, fub, pu, dy, dz1, dz2, df, dx, pd,
                    ha, ax, ay, ayf, axf, az1, az2, fa, pa, gown,
                    ga, mixed, xt, qt, kt, vt, w, o4, g1, wp, wt, gat, gm, gp, dv, dk, dqt, ktt, dd, g4, gs, gr, lo32,
                    sv, svk, svt, svy, svo, svx, ps, svz, idk, idq, ss, rs, lsem):
    n = Net(ss, rs, lsem)
    nz, y, k, c, z, x, d, nd = n.nz, n.y, n.k, n.c, n.z, n.x, n.d, n.nd
    b = fu.shape[0]; hb = b // 2
    rows, feats = ga.shape
    fb = pl.ds(0, b)
    own_rows = g1.shape[0]; main = own_rows - 16; length = 2 * main
    mine = pl.ds(pl.multiple_of(x * hb, 16), hb)
    theirs = pl.ds(pl.multiple_of((1 - x) * hb, 16), hb)
    all_of = lambda r: (lambda: r)
    l_w, l_ga, l_m = [n.local(all_of(s), all_of(t)) for s, t in ((w_h, w), (ga_h, ga), (mixed_h, mixed))]
    l_q = [n.local(all_of(s), all_of(t)) for s, t in ((k_h, kt), (q_h, qt), (v_h, vt))]
    l_x = n.local(all_of(xt_h), all_of(xt))
    l_d = n.local(lambda: hd_h.at[y], lambda: hd)
    l_u = n.local(lambda: hu_h.at[:, :, mine], lambda: hu)
    l_o = [n.local(all_of(o4_h), all_of(o4)), n.local(all_of(g1_h), all_of(g1))]
    n.barrier(n.zp[1:] + [n.yp, n.ykp, n.kp, n.xp] + n.others)
    e1 = z + 1 - 2 * lax.rem(z, 2)
    e2 = lax.rem(z + 2, nz)
    e3 = lax.rem(e1 + 2, nz)
    e = (e1, e2, e3)
    order = [e3, e2, e1, z]
    dev1, dev2 = (d, e1, c), (d, e2, c)
    d_y = [n.send((lambda q=q: hd_h.at[1 - y, q]), (lambda q=q: dy.at[q]), n.yp) for q in order]
    u_x = [n.send((lambda q=q: hu_h.at[:, q, theirs]), (lambda q=q: ux.at[:, q]), n.xp) for q in order]

    def add2(a, s):
        for yy in range(2):
            add_to(a.at[yy], s.at[yy])
    dz = Rows(n, lambda q: hd.at[q], lambda s: dz1.at[s], lambda: dz2, e, dev1, dev2, add_to)
    uz = Rows(n, lambda q: hu.at[:, q], lambda s: uz1.at[s], lambda: uz2, e, dev1, dev2, add2)
    d_x = n.move(all_of(df), all_of(dx), n.xp)
    u_y = n.move(lambda: ut.at[1 - y], all_of(uy), n.yp)
    u_f = n.move(lambda: fub.at[mine], lambda: fub.at[mine], n.xp)

    mypair = d // 2

    def pairs_sum(value, slots, view):
        if nd == 2:
            return value
        view(slots, mypair)[...] = value.astype(slots.dtype)
        ms = [n.send((lambda: view(slots, mypair)), (lambda: view(slots, mypair)), o) for o in n.others]
        for m in ms:
            m.wait_recv()
        return total_of([view(slots, i) for i in range(nd // 2)])

    def ev_dy(j):
        def run():
            d_y[j].wait_recv()
            if j == 0:
                l_d.wait()
            add_to(hd.at[order[j]], dy.at[order[j]])
            if j == 0:
                dz.a.start()
        return run
    def ev_ux(j):
        def run():
            u_x[j].wait_recv()
            if j == 0:
                l_u.wait()
            add2(hu.at[:, order[j]], ux.at[:, order[j]])
            if j == 0:
                uz.a.start()
        return run
    def ev_df():
        dz.end()
        df[...] = total_of([hd.at[z], dz1.at[0], dz2]).astype(BF)
        d_x.start()
    def ev_ut():
        uz.end()
        for yy in range(2):
            ut[yy] = total_of([hu.at[yy, z], uz1.at[0, yy], uz2.at[yy]]).astype(BF)
        u_y.start()
    def ev_uf():
        u_y.wait_recv()
        fub[mine, :] = pairs_sum(total_of([ut.at[y], uy]), pu, lambda s, i: s.at[i]).astype(BF)
        u_f.start()
    env = (gown, ha, ax, ay, ayf, axf, mine, theirs, order)
    PO = Piece(n, env, 640, 128, (0, 1), True)
    P0 = Piece(n, env, 0, 384, (0,), True)
    P1 = Piece(n, env, 0, 384, (1,), False)
    P2 = Piece(n, env, 384, 128, (0, 1), True)
    P3 = Piece(n, env, 512, 128, (0, 1), False)
    class Cols:
        def __init__(self, col0, num):
            C = pl.ds(col0, num)
            self.C = C
            self.z = Rows(n, lambda q: ha.at[y, q, mine, C], lambda s: az1.at[s, :, C], lambda: az2.at[:, C], e, dev1, dev2, add_to)
            self.f = n.move(lambda: fa.at[mine, C], lambda: fa.at[mine, C], n.xp)
        def end(self):
            self.z.end()
            C = self.C
            fa[mine, C] = pairs_sum(total_of([ha.at[y, z, mine, C], az1.at[0, :, C], az2.at[:, C]]), pa, lambda s, i: s.at[i, :, C]).astype(BF)
            self.f.start()
    ZO, Z01, Z2, Z3 = Cols(640, 128), Cols(0, 384), Cols(384, 128), Cols(512, 128)
    row_ids(ids, y, gmem.shape[1] // 2, idk, idq)
    l_w.wait(); l_ga.wait()
    gat[...] = ga[...].T
    assemble_pairs(w, wp, feats)
    wt[:, pl.ds(0, 128)] = w[0, :, pl.ds(640, 128)]
    wt[:, pl.ds(128, 128)] = w[1, :, pl.ds(640, 128)]
    lo = lax.broadcasted_iota(jnp.int32, (feats, 128), 1) < 64
    wt[:, pl.ds(256, 128)] = jnp.where(lo, pltpu.roll(w[0, :, pl.ds(512, 128)].astype(F32), 64, 1), w[1, :, pl.ds(512, 128)].astype(F32)).astype(BF)
    r3 = rows // 3

    def mixed_grad(i, _):
        r = pl.ds(pl.multiple_of(i * r3, 16), r3)
        v = nn(ga[r, :], wt[...])
        for p in range(3):
            gm[p, r, :] = v[:, 128 * p:128 * p + 128].astype(BF)
        return 0
    lax.fori_loop(0, 3, mixed_grad, 0)
    l_m.wait()
    for cc in range(4):
        af = gat[pl.ds(b * cc, b), :]
        for j in range(2):
            gown[j, cc, :, pl.ds(640, 128)] = nn(af, mixed[j]).astype(BF)
    PO.start()
    for m in l_q:
        m.wait()
    l_x.wait()
    def ev_b():
        dz.b.start(); uz.b.start()
    table = {0: [ev_dy(0), ev_ux(0)], 1: [PO.ev1], 4: [ev_dy(1), ev_ux(1), dz.middle], 7: [ev_dy(2), ev_ux(2), P0.ev1], 8: [uz.middle], 9: [ev_b],
             11: [ev_dy(3), ev_ux(3)], 13: [PO.ev2, P1.ev1], 16: [PO.ev3, ZO.z.start, P0.ev2]}
    cuts = {1: 0, 3: 1, 4: 2}

    def head(i, _):
        p = i // 2
        h = i % 2
        he = pl.ds(pl.multiple_of(64 * h, 64), 64)

        @pl.when(h == 0)
        def _():
            ktt[...] = kt[p].T
            prod = (gm[p].astype(F32) * mixed[p].astype(F32)).T
            dd[0] = jnp.sum(prod[:64, :], axis=0, keepdims=True)
            dd[1] = jnp.sum(prod[64:, :], axis=0, keepdims=True)
            dv[...] = jnp.zeros_like(dv)
            dk[...] = jnp.zeros_like(dk)
        lanes = (lax.broadcasted_iota(jnp.int32, (1, 128), 1) // 64) == h
        for t, (q0, qn, spans) in enumerate(tiles(rows, length)):
            q = qt[p, pl.ds(q0, qn), :]
            qm = jnp.where(lanes, q, jnp.zeros_like(q))
            g = gm[p, pl.ds(q0, qn), :]
            gmm = jnp.where(lanes, g, jnp.zeros_like(g))
            sc = scores_of(kt, qm, idk, idq[0:1, pl.ds(q0, qn)], p, spans)
            l = lse[i, :, pl.ds(q0, qn)]
            dl = dd[h, :, pl.ds(q0, qn)]
            acc = None
            for s, (k0, kn, _) in zip(sc, spans):
                pr = jnp.exp(s - l)
                dp = nt(vt[p, pl.ds(k0, kn), :], gmm)
                ds = (pr * (dp - dl)).astype(BF)
                dv[pl.ds(k0, kn), :] += nn(pr.astype(BF), gmm)
                dk[pl.ds(k0, kn), :] += nn(ds, qm)
                o = nn(ktt[he, pl.ds(k0, kn)], ds)
                acc = o if acc is None else acc + o
            dqt[he, pl.ds(q0, qn)] = acc * 0.125
            if t in cuts:
                at(3 * i + cuts[t], table)

        @pl.when(h == 1)
        def _():
            gp[p, :, pl.ds(0, 128)] = dqt[...].T.astype(BF)
            gp[p, :, pl.ds(128, 128)] = dk[...].astype(BF)
            gp[p, :, pl.ds(256, 128)] = dv[...].astype(BF)

        @pl.when(jnp.logical_and(h == 1, p < 2))
        def _():
            def part(cc, _):
                f = pl.ds(pl.multiple_of(b * cc, 16), b)
                gown[p, cc, :, pl.ds(0, 384)] = nn(xt[f, pl.ds(0, rows)], gp[p]).astype(BF)
                return 0
            lax.fori_loop(0, 4, part, 0)
        at(i, {1: [P0.start], 3: [P1.start]})
        return 0
    lax.fori_loop(0, 6, head, 0)
    sv[...] = jnp.zeros_like(sv)
    for i in range(6):
        sv[pl.ds(i, 1), :] = jnp.sum(vgrad[i], axis=0, keepdims=True)
    for i in range(nz):
        sv[pl.ds(6 + i, 1), :] = jnp.sum(bupgrad[i], axis=0, keepdims=True)
    for p in range(3):
        t = jnp.sum(group_sum(gp[p].astype(F32)), axis=0, keepdims=True)
        sv[pl.ds(6 + nz + p, 1), pl.ds(0, 384)] = jnp.where(k == 0, t, 0.0)
        sv[pl.ds(6 + nz + p, 1), pl.ds(384, 384)] = jnp.where(k == 1, t, 0.0)
    s_k = n.send(all_of(sv), all_of(svk), n.kp)
    sw = lambda a: pltpu.roll(a, 64, 1)

    def last(cc, _):
        f = pl.ds(pl.multiple_of(b * cc, 16), b)
        r2 = nn(xt[f, pl.ds(0, rows)], gp[2])
        o2 = nn(gat[f, :], mixed[2])
        lo = lax.broadcasted_iota(jnp.int32, (b, 128), 1) < 64
        rq, rk, rv = r2[:, :128], r2[:, 128:256], r2[:, 256:]
        gown[0, cc, :, pl.ds(384, 128)] = jnp.where(lo, rq, sw(rk)).astype(BF)
        gown[1, cc, :, pl.ds(384, 128)] = jnp.where(lo, sw(rq), rk).astype(BF)
        gown[0, cc, :, pl.ds(512, 128)] = jnp.where(lo, rv, sw(o2)).astype(BF)
        gown[1, cc, :, pl.ds(512, 128)] = jnp.where(lo, sw(rv), o2).astype(BF)
        return 0
    lax.fori_loop(0, 4, last, 0)
    P2.start(); P3.start()
    def rowsgrad(r):
        return nt(gp[0, r, :], wp[0]) + nt(gp[1, r, :], wp[1]) + nt(gp[2, r, :], wp[2])

    def half_rows(kk, put):
        def chunk(i, _):
            put(pl.ds(pl.multiple_of(i * 256, 16), 256), rowsgrad(pl.ds(pl.multiple_of(kk * main + i * 256, 16), 256)))
            return 0
        lax.fori_loop(0, main // 256, chunk, 0)
        put(pl.ds(main, 16), rowsgrad(pl.ds(pl.multiple_of(length + kk * 16, 16), 16)))
    def put_other(r, v):
        gs[r, :] = v.astype(BF)
    half_rows(1 - k, put_other)
    g_k = n.send(all_of(gs), all_of(gr), n.kp)
    s_k.wait_recv()
    svt[...] = sv[...] + svk[...]
    s_y = n.send(all_of(svt), all_of(svy), n.yp)
    P2.ev1(); P3.ev1()
    P1.ev2(); P0.ev3()
    ev_ut()
    ev_df()
    for m in l_o:
        m.wait()
    g4[:, :, pl.ds(b, g4.shape[2] - b)] = jnp.zeros((4, own_rows, g4.shape[2] - b), BF)
    def put_own(r, v):
        g1[r, :] = g1[r, :] + v
    half_rows(k, put_own)
    s_y.wait_recv()
    svo[...] = svt[...] + svy[...]
    s_x = n.send(all_of(svo), all_of(svx), n.xp)
    P1.ev3(); Z01.z.start(); ZO.z.middle()
    P2.ev2()
    g_k.wait_recv()

    def own(i, _):
        r = pl.ds(pl.multiple_of(i * 48, 16), 48)
        v = g1[r, :] + gr[r, :].astype(F32)
        for cc in range(4):
            g4[cc, r, fb] = v[:, cc * b:(cc + 1) * b].astype(BF)
        return 0
    lax.fori_loop(0, own_rows // 48, own, 0)
    g_l = n.local(lambda: g4.at[c], lambda: grad4.at[y, k])
    dst = lambda: grad4.at[y, k]
    g_s = [n.send(lambda: g4.at[n.oc], dst, n.yp), n.send(lambda: g4.at[3 - c], dst, n.ykp), n.send(lambda: g4.at[c + 1 - 2 * k], dst, n.kp)]
    P3.ev2()
    s_x.wait_recv()
    svz[z] = pairs_sum(svo[...] + svx[...], ps, lambda s, i: s.at[i])
    s_z = [n.send(lambda: svz.at[z], lambda: svz.at[z], n.zp[i]) for i in range(1, nz)]
    P2.ev3(); Z2.z.start()
    ev_uf()
    Z01.z.middle(); ZO.end()
    P3.ev3(); Z3.z.start()
    half = (lout.shape[1] - length) // 2
    for s in range(2):
        lo32[pl.ds(0, half), :] = o4[s, 0, pl.ds(main, 16), fb].astype(F32)[:half]
        lo32[pl.ds(half, main), :] = o4[s, 0, pl.ds(0, main), fb].astype(F32)
        lo32[pl.ds(half + main, main), :] = o4[s, 1, pl.ds(0, main), fb].astype(F32)
        lo32[pl.ds(half + length, 16 - half), :] = o4[s, 0, pl.ds(main, 16), fb].astype(F32)[half:]
        lo32[pl.ds(length + 16, 2 * half - 16), :] = o4[s, 1, pl.ds(main, 16), fb].astype(F32)[:2 * half - 16]
        lout[s] = lo32[pl.ds(0, length + 2 * half), :].astype(BF)
    Z2.z.middle(); Z01.end(); Z3.z.middle()
    d_x.wait_recv()
    fd[...] = pairs_sum(total_of([df, dx]), pd, lambda s, i: s.at[i])
    u_f.wait_recv()
    fu[...] = fub[...].astype(F32)
    Z2.end(); Z3.end()
    for m in s_z:
        m.wait_recv()
    acc = svz[0]
    for i in range(1, nz):
        acc = acc + svz[i]
    pick = jnp.where(c == 0, acc[:8, 0:b], 0.0)
    for cc in range(1, 4):
        pick = pick + jnp.where(c == cc, acc[:8, cc * b:(cc + 1) * b], 0.0)
    fvec[...] = pick
    t = jnp.where(z == 0, acc[6:7], 0.0)
    for i in range(1, nz):
        t = t + jnp.where(z == i, acc[6 + i:7 + i], 0.0)
    bup[...] = t
    hbias = acc[6 + nz:9 + nz]
    hbias = jnp.where(z // 2 == 0, hbias[:, :384], hbias[:, 384:])
    odd = z % 2 == 1
    two = jnp.where(odd, hbias[1:2], hbias[0:1])
    lo1 = lax.broadcasted_iota(jnp.int32, (8, 128), 1) < 64
    w8 = lambda a: jnp.broadcast_to(a, (8, 128))
    left = lambda a, v: jnp.where(lo1, w8(a), sw(w8(v)))[0:1]
    right = lambda a, v: jnp.where(lo1, sw(w8(a)), w8(v))[0:1]
    lq, lv = hbias[2:3, :128], hbias[2:3, 256:]
    bqv[pl.ds(0, 1), :] = left(two[:, :128], two[:, 256:])
    bqv[pl.ds(1, 1), :] = right(two[:, :128], two[:, 256:])
    bqv[pl.ds(2, 1), :] = jnp.where(odd, right(lq, lv), left(lq, lv))
    for m in (ZO, Z01, Z2, Z3):
        m.f.wait_recv()
    lob = lax.broadcasted_iota(jnp.int32, (b, 128), 1) < 64
    tile = lambda i: fa[:, pl.ds(128 * i, 128)].astype(F32)
    t0, t1, t2, t3, t4, t5 = [tile(i) for i in range(6)]
    g3[0, :, pl.ds(0, 128)] = jnp.where(lob, t0, sw(t1))
    g3[0, :, pl.ds(128, 64)] = t2[:, :64]
    g3[1, :, pl.ds(0, 128)] = jnp.where(lob, sw(t0), t1)
    g3[1, :, pl.ds(128, 64)] = sw(t2)[:, :64]
    g3[2, :, pl.ds(0, 128)] = t3
    g3[2, :, pl.ds(128, 64)] = t4[:, :64]
    gwo[pl.ds(0, 128), :] = t5.T
    gwo[pl.ds(128, 64), :] = sw(t4).T[:64]
    for m in g_s:
        m.wait_recv()
    g_l.wait()
    for s in range(2):
        gmem[s, pl.ds(0, 16), :] = grad4[s, 0, pl.ds(main, 16), fb].astype(F32)
        gmem[s, pl.ds(16, 2 * half - 16), :] = grad4[s, 1, pl.ds(main, 16), fb].astype(F32)[:2 * half - 16]
    n.finish()

def backward(hu, hd, ga, mixed, xt, qt, kt, vt, w, o4, g1, lse, vgrad, bupgrad, ids, half, nz, nd):
    b, width = hu.shape[2:]
    feats = 4 * b; hb = b // 2; rows = ga.shape[0]; own = g1.shape[0]; length = 2 * (own - 16)
    V = lambda *s, d=BF: pltpu.VMEM(s, d)
    vm = pl.BlockSpec(memory_space=pltpu.VMEM); an = pl.BlockSpec(memory_space=pl.ANY)
    S = jax.ShapeDtypeStruct
    np_ = max(1, nd // 2) if nd > 2 else 1
    pw = (hb, width) if nd > 2 else (16, 128)
    t3 = V(3, rows, 128); f3 = lambda *s: V(*s, d=F32)
    sm = f3(16, feats)
    outs = (S((2, 2, own, 256), BF), S((2, length + 2 * half, b), BF), S((2, 2 * half, b), F32), S((3, b, b), F32), S((b, b), F32), S((b, width), F32), S((b, width), F32), S((8, b), F32), S((1, feats), F32), S((3, 128), F32))
    scratch = [V(2, nz, hb, width), V(nz, b, width), V(2, nz, hb, width), V(2, 2, hb, width), V(2, hb, width), V(2, hb, width), V(hb, width), V(b, width), V(np_, *pw),
               V(nz, b, width), V(2, b, width), V(b, width), V(b, width), V(b, width), V(np_, b, width) if nd > 2 else V(1, 16, 128),
               V(2, nz, b, width), V(2, nz, hb, width), V(nz, hb, width), V(nz, b, width), V(nz, hb, width), V(2, hb, width), V(hb, width), V(b, width), V(np_, *pw), V(2, 4, b, width),
               V(rows, feats), t3, V(*xt.shape), t3, t3, t3, V(*w.shape), V(*o4.shape), f3(*g1.shape), V(3, feats, 384), V(feats, 384), V(feats, rows), t3, V(3, rows, 384),
               f3(rows, 128), f3(rows, 128), f3(128, rows), V(128, rows), f3(2, 1, rows), V(4, own, 256), V(own, feats), V(own, feats), f3(rows, b),
               sm, sm, sm, sm, sm, sm, f3(np_, 16, feats), f3(nz, 16, feats), f3(length + 128, 128), f3(1, length + 128),
               pltpu.SemaphoreType.DMA((128 + 5 * nd,)), pltpu.SemaphoreType.DMA((128 + 5 * nd,)), pltpu.SemaphoreType.DMA((40,))]
    return pl.pallas_call(backward_kernel, out_shape=outs, in_specs=[an] * 11 + [vm] * 4, out_specs=(vm,) * len(outs), scratch_shapes=scratch,
        compiler_params=pltpu.CompilerParams(collective_id=2, has_side_effects=True, vmem_limit_bytes=67043328))(hu, hd, ga, mixed, xt, qt, kt, vt, w, o4, g1, lse, vgrad, bupgrad, ids)

def per_device(tokens, memory, block_ids, valid, teacher, w_qkv, bias_qv, w_out, bias_out, ln1_gain, ln1_bias, w_up, bias_up, w_down, bias_down, ln2_gain, ln2_bias):
    _, b, length = tokens.shape
    nd, nz = lax.axis_size("dp"), lax.axis_size("row")
    d, z, c = (lax.axis_index(a) for a in ("dp", "row", "col"))
    y, k = c // 2, c % 2
    feats = 4 * b
    half = memory.shape[1] // 2
    main = length // 2
    rows = length + 32
    one = lambda a: a.reshape(1, -1)
    xt, qt, kt, vt, mixed, wown, ga, hu, hd, lse, g_one, vgrad, bupgrad, out4 = forward(valid, tokens, memory, teacher, w_qkv.reshape(3, b, 192), w_out, w_up, w_down, [one(a) for a in (bias_out, ln1_gain, ln1_bias, bias_down, ln2_gain, ln2_bias)], one(bias_up), bias_qv, block_ids, nz)
    grad4, lout, gmem, g3, gwo, fu, fd, fvec, bup, bqv = backward(hu, hd, ga, mixed, xt, qt, kt, vt, wown, out4, g_one, lse, vgrad, bupgrad, block_ids, half, nz, nd)
    grad_tokens = grad4[:, :, :main, :b].reshape(2, length, b).astype(F32)
    return (lout, grad_tokens, gmem, g3.reshape(3, b * b), bqv, gwo, fvec[5], fvec[3], fvec[4], fu, bup[0], fd, fvec[2], fvec[0], fvec[1])

def solution(mesh):
    rows, feat = ("dp", "row"), "col"
    in_specs = (P(rows, feat, None), P(rows, None, feat), P(rows, None), P(), P(rows, feat, None), P("row", feat), P("row", None), P("row", feat), P(feat), P(feat), P(feat), P(feat, "row"), P("row"), P(feat, "row"), P(feat), P(feat), P(feat))
    out_specs = (P(rows, None, feat), P(rows, None, feat), P(rows, None, feat), P("row", feat), P("row", None), P("row", feat), P(feat), P(feat), P(feat), P(feat, "row"), P("row"), P(feat, "row"), P(feat), P(feat), P(feat))
    return jax.shard_map(per_device, mesh=mesh, in_specs=in_specs, out_specs=out_specs, check_vma=False)
```

```python
import jax
import jax.numpy as jnp
from jax import lax
from jax.experimental import pallas as pl
from jax.experimental.pallas import tpu as pltpu
from jax.sharding import PartitionSpec as P
BF=jnp.bfloat16; F32=jnp.float32
EPSILON=1e-12
CH=48

def nn(a,b): return lax.dot_general(a,b,(((1,),(0,)),((),())),preferred_element_type=F32)
def nt(a,b): return lax.dot_general(a,b,(((1,),(1,)),((),())),preferred_element_type=F32)

def gelu_pair(v):
    t = pl.reciprocal(1.0 + (0.3275911 * 0.7071067811865476) * jnp.abs(v))
    poly = t * (0.5*0.254829592 + t * (-0.5*0.284496736 + t * (0.5*1.421413741 + t * (-0.5*1.453152027 + t * (0.5*1.061405429)))))
    e = jnp.exp(-0.5 * v * v)
    half = poly * e
    cdf = jnp.where(v >= 0.0, 1.0 - half, half)
    return v * cdf, cdf + v * (e * 0.3989422804014327)

def group_sum(v):
    rows = v.shape[0]
    return jnp.sum(v.reshape(rows // 8, 8, v.shape[1]), axis=0)

def mlp_kernel(half_ref, valid_ref, mixed, x, teach, vec, bup, wa_hbm, wu_hbm, wd_hbm,
               out, g_one, g_attn, vgrad, bupgrad, gu_hbm, gd_hbm,
               tr, wraw, wt, wu, wd, h1, h2, rs1, low, lowt, brt, br, hid, dgl, gg, gu, gd, sem):
    rows, feats = x.shape
    zs = wu.shape[0]
    nb = feats // 256
    copies_a = [pltpu.make_async_copy(wa_hbm.at[z, :, pl.ds(512, 256)], wraw.at[z], sem.at[z]) for z in range(zs)]
    copies_u = [pltpu.make_async_copy(wu_hbm.at[z], wu.at[z], sem.at[zs + z]) for z in range(zs)]
    copies_d = [pltpu.make_async_copy(wd_hbm.at[z], wd.at[z], sem.at[2 * zs + z]) for z in range(zs)]
    for c in copies_a + copies_u + copies_d:
        c.start()
    for c in copies_a:
        c.wait()
    main = teach.shape[1]
    for i in range(main // 128):
        tr[pl.ds(128 * i, 128), :] = teach[:, pl.ds(128 * i, 128)].T
    tr[pl.ds(main, rows - main), :] = jnp.zeros((rows - main, feats), BF)
    low_lane = lax.broadcasted_iota(jnp.int32, (feats, 128), 1) < 64
    for k in range(zs // 2):
        z0, z1 = 2 * k, 2 * k + 1
        wt[:, pl.ds(384 * k, 128)] = wraw[z0, :, pl.ds(128, 128)]
        wt[:, pl.ds(384 * k + 128, 128)] = wraw[z1, :, pl.ds(128, 128)]
        t0 = pltpu.roll(wraw[z0, :, pl.ds(0, 128)].astype(F32), 64, 1)
        t1 = wraw[z1, :, pl.ds(0, 128)].astype(F32)
        wt[:, pl.ds(384 * k + 256, 128)] = jnp.where(low_lane, t0, t1).astype(BF)
    for n in range(nb):
        f = pl.ds(256 * n, 256)
        h1[:, f] = nt(mixed[...], wt[f, :]) + x[:, f].astype(F32) + vec[0:1, f]
    inv = 1.0 / feats

    vgrad[...] = jnp.zeros_like(vgrad)
    bupgrad[...] = jnp.zeros_like(bupgrad)

    def norm1(i, _):
        r = pl.ds(pl.multiple_of(i * CH, 16), CH)
        h = h1[r, :]
        m = jnp.sum(h, axis=1, keepdims=True) * inv
        s = jnp.sum(h * h, axis=1, keepdims=True) * inv
        rstd = lax.rsqrt(s - m * m + EPSILON)
        xhat = (h - m) * rstd
        h1[r, :] = xhat
        rs1[r, :] = jnp.broadcast_to(rstd, (CH, 128))
        low[r, :] = (xhat * vec[1:2, :] + vec[2:3, :]).astype(BF)
        return 0
    lax.fori_loop(0, rows // CH, norm1, 0)
    lowt[...] = low[...].T
    for c in copies_u:
        c.wait()

    def gate(i, _):
        z = i // nb
        f = pl.ds(pl.multiple_of((i % nb) * 256, 256), 256)
        v = nn(low[...], wu[z, :, f]) + bup[z, :, f]
        a, b = gelu_pair(v)
        hid[z, :, f] = a.astype(BF)
        dgl[z, :, f] = b
        return 0
    lax.fori_loop(0, zs * nb, gate, 0)
    for c in copies_d:
        c.wait()

    def down(n, _):
        f = pl.ds(pl.multiple_of(n * 256, 256), 256)
        acc = nt(hid[0], wd[0, f, :])
        for z in range(1, zs):
            acc = acc + nt(hid[z], wd[z, f, :])
        h2[:, f] = acc
        return 0
    lax.fori_loop(0, nb, down, 0)
    scale = vec[6:7, 0:1]
    first = half_ref[0] * main

    def norm2(i, _):
        r = pl.ds(pl.multiple_of(i * CH, 16), CH)
        h = h2[r, :] + (h1[r, :] * vec[1:2, :] + vec[2:3, :]) + vec[3:4, :]
        m = jnp.sum(h, axis=1, keepdims=True) * inv
        s = jnp.sum(h * h, axis=1, keepdims=True) * inv
        rstd = lax.rsqrt(s - m * m + EPSILON)
        xhat = (h - m) * rstd
        o = xhat * vec[4:5, :] + vec[5:6, :]
        out[r, :] = o.astype(BF)
        place = lax.broadcasted_iota(jnp.int32, (CH, 1), 0) + i * CH
        place = jnp.where(place < main, place + first, valid_ref[0])
        go = jnp.where(place < valid_ref[0], scale * (o - tr[r, :].astype(F32)), 0.0)
        a = go * vec[4:5, :]
        m1 = jnp.sum(a, axis=1, keepdims=True) * inv
        m2 = jnp.sum(a * xhat, axis=1, keepdims=True) * inv
        g2 = rstd * (a - m1 - xhat * m2)
        h2[r, :] = g2
        b = g2.astype(BF)
        br[r, :] = b
        vgrad[0] += group_sum(go * xhat)
        vgrad[1] += group_sum(go)
        vgrad[2] += group_sum(b.astype(F32))
        return 0
    lax.fori_loop(0, rows // CH, norm2, 0)
    brt[...] = br[...].T

    def back(i, _):
        z = i // nb
        f = pl.ds(pl.multiple_of((i % nb) * 256, 256), 256)
        gh = nn(br[...], wd[z, :, f])
        g = (gh * dgl[z, :, f]).astype(BF)
        gg[z, :, f] = g
        bupgrad[z, :, f] += group_sum(g.astype(F32))
        gd[z, :, f] = nn(brt[...], hid[z, :, f]).astype(BF)
        gu[z, :, f] = nn(lowt[...], g).astype(BF)
        return 0
    lax.fori_loop(0, zs * nb, back, 0)
    outs = [pltpu.make_async_copy(gd, gd_hbm, sem.at[0]), pltpu.make_async_copy(gu, gu_hbm, sem.at[1])]
    for c in outs:
        c.start()

    def first_grad(n, _):
        f = pl.ds(pl.multiple_of(n * 256, 256), 256)
        acc = h2[:, f]
        for z in range(zs):
            acc = acc + nt(gg[z], wu[z, f, :])
        h2[:, f] = acc
        return 0
    lax.fori_loop(0, nb, first_grad, 0)

    def norm1_back(i, _):
        r = pl.ds(pl.multiple_of(i * CH, 16), CH)
        g = h2[r, :]
        xhat = h1[r, :]
        a = g * vec[1:2, :]
        m1 = jnp.sum(a, axis=1, keepdims=True) * inv
        m2 = jnp.sum(a * xhat, axis=1, keepdims=True) * inv
        g1 = rs1[r, 0:1] * (a - m1 - xhat * m2)
        g_one[r, :] = g1
        b = g1.astype(BF)
        g_attn[r, :] = b
        vgrad[3] += group_sum(g * xhat)
        vgrad[4] += group_sum(g)
        vgrad[5] += group_sum(b.astype(F32))
        return 0
    lax.fori_loop(0, rows // CH, norm1_back, 0)
    for c in outs:
        c.wait()

def mlp(half, valid, mixed, x, teach, vec, bup, wa, wu, wd):
    rows, feats = x.shape; zs = wu.shape[0]
    V = lambda *s, d=BF: pltpu.VMEM(s, d)
    vm = pl.BlockSpec(memory_space=pltpu.VMEM); sm = pl.BlockSpec(memory_space=pltpu.SMEM); an = pl.BlockSpec(memory_space=pl.ANY)
    S = jax.ShapeDtypeStruct
    return pl.pallas_call(mlp_kernel,
        out_shape=(S((rows,feats),BF),S((rows,feats),F32),S((rows,feats),BF),S((6,8,feats),F32),S((zs,8,feats),F32),S(wu.shape,BF),S(wd.shape,BF)),
        in_specs=[sm,sm,vm,vm,vm,vm,vm,an,an,an],
        out_specs=(vm,vm,vm,vm,vm,an,an),
        scratch_shapes=[V(rows,feats),V(zs,feats,256),V(feats,feats),V(*wu.shape),V(*wd.shape),V(rows,feats,d=F32),V(rows,feats,d=F32),V(rows,128,d=F32),V(rows,feats),
            V(feats,rows),V(feats,rows),V(rows,feats),V(zs,rows,feats),V(zs,rows,feats,d=F32),V(zs,rows,feats),V(*wu.shape),V(*wd.shape),pltpu.SemaphoreType.DMA((3*zs,))],
        compiler_params=pltpu.CompilerParams(vmem_limit_bytes=63*2**20),
    )(half,valid,mixed,x,teach,vec,bup,wa,wu,wd)
NEG=-1e30
def tn_lanes(): return lax.broadcasted_iota(jnp.int32,(1,128),1)

def assemble_pairs(w, wp, feats):
    lo = lax.broadcasted_iota(jnp.int32, (feats, 128), 1) < 64
    wp[0] = w[0, :, pl.ds(0, 384)]
    wp[1] = w[1, :, pl.ds(0, 384)]
    a0, a1 = w[0, :, pl.ds(384, 128)].astype(F32), w[1, :, pl.ds(384, 128)].astype(F32)
    wp[2, :, pl.ds(0, 128)] = jnp.where(lo, a0, pltpu.roll(a1, 64, 1)).astype(BF)
    wp[2, :, pl.ds(128, 128)] = jnp.where(lo, pltpu.roll(a0, 64, 1), a1).astype(BF)
    b0, b1 = w[0, :, pl.ds(512, 128)].astype(F32), w[1, :, pl.ds(512, 128)].astype(F32)
    wp[2, :, pl.ds(256, 128)] = jnp.where(lo, b0, pltpu.roll(b1, 64, 1)).astype(BF)

def tiles(rows, length):
    mem = (length, rows - length, True)
    out = []
    for a in range(0, length, 256):
        spans = []
        if a:
            spans.append((0, a, False))
        spans.append((a, min(512, length - a), True))
        out.append((a, 256, spans + [mem]))
    out.append((length, rows - length, [(0, length, True), mem]))
    return out

def scores_of(kt, qm, idk, idq, p, spans):
    out = []
    for k0, kn, masked in spans:
        s = nt(kt[p, pl.ds(k0, kn), :], qm)
        if masked:
            s = jnp.where(idk[pl.ds(k0, kn), 0:1] <= idq, s, NEG)
        out.append(s)
    return out

def attn_fwd_kernel(xt, wa_hbm, bias, idk, idq, x, qt, kt, vt, mixed, lse, w, wp, vtt, ot, sem):
    feats = xt.shape[0]; rows = x.shape[0]; length = xt.shape[1] - 128
    c = pltpu.make_async_copy(wa_hbm, w, sem); c.start()
    for i in range(length // 128):
        x[pl.ds(128 * i, 128), :] = xt[:, pl.ds(128 * i, 128)].T
    x[pl.ds(length, rows - length), :] = xt[:, pl.ds(length, 128)].T[: rows - length, :]
    c.wait()
    assemble_pairs(w, wp, feats)
    rc = rows // 3

    def project(i, _):
        p = i // 3
        r = pl.ds(pl.multiple_of((i % 3) * rc, 16), rc)
        v = nn(x[r, :], wp[p]) + bias[p]
        qt[p, r, :] = (v[:, :128].astype(BF).astype(F32) * 0.125).astype(BF)
        kt[p, r, :] = v[:, 128:256].astype(BF)
        vt[p, r, :] = v[:, 256:].astype(BF)
        return 0
    lax.fori_loop(0, 9, project, 0)

    def pair(p, _):
        vtt[...] = vt[p].T
        for e in range(2):
            lanes = (tn_lanes() < 64) if e == 0 else (tn_lanes() >= 64)
            for q0, qn, spans in tiles(rows, length):
                q = qt[p, pl.ds(q0, qn), :]
                qm = jnp.where(lanes, q, jnp.zeros_like(q))
                ss = scores_of(kt, qm, idk, idq[0:1, pl.ds(q0, qn)], p, spans)
                m = jnp.max(ss[0], axis=0, keepdims=True)
                for s in ss[1:]:
                    m = jnp.maximum(m, jnp.max(s, axis=0, keepdims=True))
                tot, acc = None, None
                for s, (k0, kn, _) in zip(ss, spans):
                    ex = jnp.exp(s - m)
                    t = jnp.sum(ex, axis=0, keepdims=True)
                    o = nn(vtt[pl.ds(64 * e, 64), pl.ds(k0, kn)], ex.astype(BF))
                    tot = t if tot is None else tot + t
                    acc = o if acc is None else acc + o
                ot[pl.ds(64 * e, 64), pl.ds(q0, qn)] = acc / tot
                lse[p, e, :, pl.ds(q0, qn)] = m + jnp.log(tot)
        mixed[p] = ot[...].T.astype(BF)
        return 0
    lax.fori_loop(0, 3, pair, 0)

def attn_fwd(xt, wa, bias, idk, idq, rows):
    feats = xt.shape[0]
    V = lambda *s, d=BF: pltpu.VMEM(s, d)
    vm = pl.BlockSpec(memory_space=pltpu.VMEM); an = pl.BlockSpec(memory_space=pl.ANY)
    S = jax.ShapeDtypeStruct
    t3 = S((3, rows, 128), BF)
    return pl.pallas_call(attn_fwd_kernel,
        out_shape=(S((rows, feats), BF), t3, t3, t3, t3, S((3, 2, 1, rows), F32)),
        in_specs=[vm, an, vm, vm, vm], out_specs=(vm,) * 6,
        scratch_shapes=[V(*wa.shape), V(3, feats, 384), V(128, rows), V(128, rows, d=F32), pltpu.SemaphoreType.DMA],
        compiler_params=pltpu.CompilerParams(vmem_limit_bytes=63*2**20))(xt, wa, bias, idk, idq)

def attn_bwd_kernel(ga, mixed, xt, qt, kt, vt, lse, idk, idq, wa_hbm, gpart, bgrad, gown_hbm, w, wp, wt, gat, gm, gp, dv, dk, dqt, ktt, dd, ro, gown, sem):
    feats = xt.shape[0]; rows = ga.shape[0]; length = xt.shape[1] - 128
    c = pltpu.make_async_copy(wa_hbm, w, sem); c.start()
    gat[...] = ga[...].T
    c.wait()
    assemble_pairs(w, wp, feats)
    wt[:, pl.ds(0, 128)] = w[0, :, pl.ds(640, 128)]
    wt[:, pl.ds(128, 128)] = w[1, :, pl.ds(640, 128)]
    lo = lax.broadcasted_iota(jnp.int32, (feats, 128), 1) < 64
    wt[:, pl.ds(256, 128)] = jnp.where(lo, pltpu.roll(w[0, :, pl.ds(512, 128)].astype(F32), 64, 1), w[1, :, pl.ds(512, 128)].astype(F32)).astype(BF)
    for p in range(3):
        gm[p] = nn(ga[...], wt[:, pl.ds(128 * p, 128)]).astype(BF)

    def pair(p, _):
        ktt[...] = kt[p].T
        prod = (gm[p].astype(F32) * mixed[p].astype(F32)).T
        dd[0:1, :] = jnp.sum(prod[:64, :], axis=0, keepdims=True)
        dd[1:2, :] = jnp.sum(prod[64:, :], axis=0, keepdims=True)
        dv[...] = jnp.zeros_like(dv)
        dk[...] = jnp.zeros_like(dk)
        for e in range(2):
            lanes = (tn_lanes() < 64) if e == 0 else (tn_lanes() >= 64)
            for q0, qn, spans in tiles(rows, length):
                q = qt[p, pl.ds(q0, qn), :]
                qm = jnp.where(lanes, q, jnp.zeros_like(q))
                g = gm[p, pl.ds(q0, qn), :]
                gmm = jnp.where(lanes, g, jnp.zeros_like(g))
                ss = scores_of(kt, qm, idk, idq[0:1, pl.ds(q0, qn)], p, spans)
                l = lse[p, e, :, pl.ds(q0, qn)]
                d = dd[pl.ds(e, 1), pl.ds(q0, qn)]
                acc = None
                for s, (k0, kn, _) in zip(ss, spans):
                    pr = jnp.exp(s - l)
                    dp = nt(vt[p, pl.ds(k0, kn), :], gmm)
                    ds = (pr * (dp - d)).astype(BF)
                    dv[pl.ds(k0, kn), :] += nn(pr.astype(BF), gmm)
                    dk[pl.ds(k0, kn), :] += nn(ds, qm)
                    o = nn(ktt[pl.ds(64 * e, 64), pl.ds(k0, kn)], ds)
                    acc = o if acc is None else acc + o
                dqt[pl.ds(64 * e, 64), pl.ds(q0, qn)] = acc * 0.125
        gp[p, :, pl.ds(0, 128)] = dqt[...].T.astype(BF)
        gp[p, :, pl.ds(128, 128)] = dk[...].astype(BF)
        gp[p, :, pl.ds(256, 128)] = dv[...].astype(BF)
        return 0
    lax.fori_loop(0, 3, pair, 0)
    for p in range(3):
        bgrad[p] = group_sum(gp[p].astype(F32))
    r3 = rows // 3

    def rowsgrad(i, _):
        r = pl.ds(pl.multiple_of(i * r3, 16), r3)
        gpart[r, :] = nt(gp[0, r, :], wp[0]) + nt(gp[1, r, :], wp[1]) + nt(gp[2, r, :], wp[2])
        return 0
    lax.fori_loop(0, 3, rowsgrad, 0)
    fc = 256
    for f0 in range(0, feats, fc):
        f = pl.ds(f0, fc)
        xf = xt[f, pl.ds(0, rows)]
        af = gat[f, :]
        r0 = nn(xf, gp[0]); r1 = nn(xf, gp[1]); r2 = nn(xf, gp[2])
        o = [nn(af, mixed[p]) for p in range(3)]
        lo = lax.broadcasted_iota(jnp.int32, (fc, 128), 1) < 64
        rq, rk, rv = r2[:, :128], r2[:, 128:256], r2[:, 256:]
        sw = lambda a: pltpu.roll(a, 64, 1)
        gown[0, f, pl.ds(0, 384)] = r0.astype(BF)
        gown[1, f, pl.ds(0, 384)] = r1.astype(BF)
        gown[0, f, pl.ds(384, 128)] = jnp.where(lo, rq, sw(rk)).astype(BF)
        gown[1, f, pl.ds(384, 128)] = jnp.where(lo, sw(rq), rk).astype(BF)
        gown[0, f, pl.ds(512, 128)] = jnp.where(lo, rv, sw(o[2])).astype(BF)
        gown[1, f, pl.ds(512, 128)] = jnp.where(lo, sw(rv), o[2]).astype(BF)
        gown[0, f, pl.ds(640, 128)] = o[0].astype(BF)
        gown[1, f, pl.ds(640, 128)] = o[1].astype(BF)
    c = pltpu.make_async_copy(gown, gown_hbm, sem); c.start(); c.wait()

def attn_bwd(ga, mixed, xt, qt, kt, vt, lse, idk, idq, wa):
    feats = xt.shape[0]; rows = ga.shape[0]
    V = lambda *s, d=BF: pltpu.VMEM(s, d)
    vm = pl.BlockSpec(memory_space=pltpu.VMEM); an = pl.BlockSpec(memory_space=pl.ANY)
    S = jax.ShapeDtypeStruct
    return pl.pallas_call(attn_bwd_kernel,
        out_shape=(S((rows, feats), F32), S((3, 8, 384), F32), S(wa.shape, BF)),
        in_specs=[vm] * 9 + [an], out_specs=(vm, vm, an),
        scratch_shapes=[V(*wa.shape), V(3, feats, 384), V(feats, 384), V(feats, rows), V(3, rows, 128), V(3, rows, 384), V(rows, 128, d=F32), V(rows, 128, d=F32),
            V(128, rows, d=F32), V(128, rows), V(8, rows, d=F32), V(8, 128), V(*wa.shape), pltpu.SemaphoreType.DMA],
        compiler_params=pltpu.CompilerParams(vmem_limit_bytes=63*2**20))(ga, mixed, xt, qt, kt, vt, lse, idk, idq, wa)
MESH = pl.DeviceIdType.MESH

class Move:
    def __init__(self, net, src, dst, dev, index):
        self.net, self.src, self.dst, self.dev, self.index = net, src, dst, dev, index
    def make(self):
        return pltpu.make_async_remote_copy(src_ref=self.src(), dst_ref=self.dst(), send_sem=self.net.ss.at[self.index],
                                            recv_sem=self.net.rs.at[self.index], device_id=self.dev, device_id_type=MESH)
    def start(self):
        self.make().start()
    def wait_recv(self):
        self.make().wait_recv()
    def wait_send(self):
        self.make().wait_send()

class Copy:
    def __init__(self, net, src, dst, index):
        self.net, self.src, self.dst, self.index = net, src, dst, index
    def make(self):
        return pltpu.make_async_copy(self.src(), self.dst(), self.net.ls.at[self.index])
    def start(self):
        self.make().start()
    def wait(self):
        self.make().wait()

class Net:
    def __init__(self, send_sems, recv_sems, local_sems):
        self.ss, self.rs, self.ls = send_sems, recv_sems, local_sems
        self.count, self.locals, self.moves, self.copies = 0, 0, [], []
        self.d, self.z, self.c = (lax.axis_index(a) for a in ("dp", "row", "col"))
        self.nd, self.nz = lax.axis_size("dp"), lax.axis_size("row")
        self.y, self.k = self.c // 2, self.c % 2
        self.x = self.d % 2
        self.oc = lax.rem(self.c + 2, 4)
        self.xp = (self.d + 1 - 2 * self.x, self.z, self.c)
        self.yp = (self.d, self.z, self.oc)
        self.kp = (self.d, self.z, self.c + 1 - 2 * self.k)
        self.ykp = (self.d, self.z, 3 - self.c)
        self.zs = [lax.rem(self.z + i, self.nz) for i in range(self.nz)]
        self.zp = [(self.d, zz, self.c) for zz in self.zs]
        self.others = [(lax.rem(self.d + 2 * i, self.nd), self.z, self.c) for i in range(1, self.nd // 2)]
    def from_row(self, i):
        return self.zs[(self.nz - i) % self.nz]
    def hello(self, peers):
        b = pltpu.get_barrier_semaphore()
        for p in peers:
            pl.semaphore_signal(b, inc=1, device_id=p, device_id_type=MESH)
    def await_hello(self, peers):
        pl.semaphore_wait(pltpu.get_barrier_semaphore(), len(peers))
    def barrier(self, peers):
        self.hello(peers)
        self.await_hello(peers)
    def move(self, src, dst, dev):
        m = Move(self, src, dst, dev, self.count)
        self.count += 1
        self.moves.append(m)
        return m
    def send(self, src, dst, dev):
        m = self.move(src, dst, dev)
        m.start()
        return m
    def copy(self, src, dst):
        m = Copy(self, src, dst, self.locals)
        self.locals += 1
        self.copies.append(m)
        return m
    def local(self, src, dst):
        m = self.copy(src, dst)
        m.start()
        return m
    def finish(self):
        for m in self.moves:
            m.wait_send()

def at(i, table):
    for j, events in table.items():
        if events:
            @pl.when(i == j)
            def _(events=events):
                for e in events:
                    e()

def spread_events(events, steps):
    table = {}
    for n, e in enumerate(events):
        table.setdefault(n * steps // len(events), []).append(e)
    return table

def join192(t, dst):
    lo = lax.broadcasted_iota(jnp.int32, t[0][0].shape, 1) < 64
    sw = lambda a: pltpu.roll(a, 64, 1)
    for h in range(2):
        a, b = t[2 * h], t[2 * h + 1]
        dst[:, pl.ds(384 * h, 128)] = a[0]
        dst[:, pl.ds(384 * h + 128, 128)] = jnp.where(lo, a[1], sw(b[0]))
        dst[:, pl.ds(384 * h + 256, 128)] = jnp.where(lo, sw(b[0]), sw(b[1]))

def row_ids(ids, y, half, idk, idq):
    length = ids.shape[1]
    idq[:, pl.ds(0, length)] = ids[pl.ds(y, 1), :].astype(F32)
    i = lax.broadcasted_iota(jnp.int32, (1, 128), 1)
    idq[:, pl.ds(length, 128)] = jnp.where(i < half, -1.0, jnp.where(i < 2 * half, 1.0 * length, 2.0 * length))
    for j in range(length // 128 + 1):
        idk[pl.ds(128 * j, 128), :] = jnp.broadcast_to(idq[:, pl.ds(128 * j, 128)], (128, 128)).T

def pack_inputs(w3, wo, la, vecs, bias_up, bias_qv, scale, ls, memory, mtmp, mem):
    b = w3.shape[1]
    f = lambda r: r.astype(F32)
    lo = lax.broadcasted_iota(jnp.int32, (b, 128), 1) < 64
    t0, t1 = f(w3[0, :, pl.ds(0, 128)]), f(w3[1, :, pl.ds(0, 128)])
    la[:, pl.ds(0, 128)] = jnp.where(lo, t0, pltpu.roll(t1, 64, 1)).astype(BF)
    la[:, pl.ds(128, 128)] = jnp.where(lo, pltpu.roll(t0, 64, 1), t1).astype(BF)
    v = [f(w3[j, :, pl.ds(128, 64)]) for j in range(3)]
    la[:, pl.ds(256, 128)] = jnp.concatenate([v[0], v[1]], axis=1).astype(BF)
    la[:, pl.ds(384, 128)] = w3[2, :, pl.ds(0, 128)]
    wot = f(wo[...]).T
    la[:, pl.ds(512, 128)] = jnp.concatenate([v[2], wot[:, 128:]], axis=1).astype(BF)
    la[:, pl.ds(640, 128)] = wot[:, :128].astype(BF)
    ls[...] = jnp.zeros_like(ls)
    for j, r in enumerate(vecs):
        ls[pl.ds(j, 1), pl.ds(0, b)] = r[...]
    ls[pl.ds(6, 1), :] = scale
    for j in range(3):
        ls[pl.ds(8 + j, 1), :] = bias_up[:, pl.ds(256 * j, 256)]
    ls[pl.ds(11, 1), pl.ds(0, 128)] = bias_qv[0:1, :]
    ls[pl.ds(11, 1), pl.ds(128, 128)] = bias_qv[1:2, :]
    ls[pl.ds(12, 1), pl.ds(0, 128)] = bias_qv[2:3, :]
    mtmp[...] = jnp.zeros_like(mtmp)
    for s in range(2):
        mtmp[pl.ds(0, memory.shape[1]), :] = f(memory[s])
        mem[s] = mtmp[...].T.astype(BF)

def forward_kernel(valid_ref, tok, memory, tch, w3, wo, lu, ld, v0, v1, v2, v3, v4, v5, bias_up, bias_qv, ids,
                   xt_o, q_o, k_o, v_o, mixed_o, wa_o, ga_o, hu_o, hd_o, lse, g_one, vgrad, bupgrad, out4,
                   xt, x, wa, wu, wd, sm, tt, tr, wp, qt, kt, vt, vtt, ot, mixed, mrows, bias, vec, wt,
                   h1, h2, rs1, low, lowt, br, brt, hid, dgl, gdz, guz, hu, hd, ru, rd, ga, o4, la, ls, mem, mtmp, idk, idq, ss, rs, lsem, zsem, zrem):
    n = Net(ss, rs, lsem)
    peers = n.zp[1:] + [n.yp, n.ykp, n.kp, n.xp]
    n.hello(peers)
    total = lax.fori_loop(0, valid_ref.shape[0], lambda i, t: t + valid_ref[i], jnp.int32(0))
    count = valid_ref[(n.d * n.nz + n.z) * 2 + n.y]
    scale_row = (valid_ref.shape[0] * tok.shape[2]) / jnp.full((1, 256), total, jnp.int32).astype(F32)
    pack_inputs(w3, wo, la, (v0, v1, v2, v3, v4, v5), bias_up, bias_qv, scale_row, ls, memory, mtmp, mem)
    n.await_hello(peers)
    nz, y, k, c, z, oc = n.nz, n.y, n.k, n.c, n.z, n.oc
    b = la.shape[0]; hb = b // 2
    feats = x.shape[1]; rows = x.shape[0]; length = tok.shape[2]; main = length // 2
    own_rows = main + 16
    row = lambda cc, off=0, num=b: pl.ds(pl.multiple_of(cc * b + off, 16), num)
    blk = lambda w, zz, cc: (lambda: w.at[zz, row(cc)])
    hlf = lambda w, zz, cc, h: (lambda: w.at[zz, row(cc, h * hb, hb)])
    mine, theirs = n.x, 1 - n.x
    part = lambda w: (lambda: w.at[pl.ds(pl.multiple_of(n.x * hb, 16), hb)])
    all_of = lambda r: (lambda: r)
    tail = pl.ds(length, 128); body = pl.ds(0, length)
    fz = n.from_row
    R = range(1, nz)
    e1 = z + 1 - 2 * lax.rem(z, 2)
    e2 = lax.rem(z + 2, nz)
    e3 = lax.rem(e1 + 2, nz)
    dev1, dev2 = (n.d, e1, c), (n.d, e2, c)
    order = [z, e2, e1, e3]
    s_blk = lambda zz, cc: (lambda: sm.at[zz, cc])
    fwd = lambda u, dev: n.move(u, u, dev)
    local = [n.local(lambda: tok.at[y], lambda: xt.at[row(c), body]), n.local(lambda: mem.at[y], lambda: xt.at[row(c), tail])]
    au = lambda zz, cc: hlf(wa, zz, cc, mine)
    a2 = n.send(part(la), au(z, c), dev2)
    a1 = n.send(part(la), au(z, c), dev1)
    a_y = [n.send(part(la), au(z, c), n.yp)]
    a_k = [n.send(all_of(la), blk(wa, z, c), n.kp)]
    s_z = [n.send(all_of(ls), s_blk(z, c), n.zp[i]) for i in R]
    s_y = [n.send(all_of(ls), s_blk(z, c), n.yp)]
    s_k = [n.send(all_of(ls), s_blk(z, c), n.kp)]
    t_k = [n.send(lambda: tok.at[y], lambda: xt.at[row(c), body], n.kp), n.send(lambda: mem.at[y], lambda: xt.at[row(c), tail], n.kp)]
    for w, l in ((wa, la), (wu, lu), (wd, ld)):
        local.append(n.local(all_of(l), blk(w, z, c)))
    local.append(n.local(all_of(ls), s_blk(z, c)))
    a_x, a_xu = [], []
    def pass_on(u, lists):
        for lst, dev in lists:
            lst.append(fwd(u, dev)); lst[-1].start()
    def a_own(zz):
        a_xu.append((zz, c))
        pass_on(au(zz, c), ((a_x, n.xp), (a_y, n.yp), (a_k, n.kp)))
    def a_far(i):
        a_y[i].wait_recv()
        a_xu.append((order[i], oc))
        pass_on(au(order[i], oc), ((a_x, n.xp), (a_k, n.kp)))
    def a_home(i):
        a_x[i].wait_recv()
        pass_on(hlf(wa, *a_xu[i], theirs), ((a_k, n.kp),))
    a_far(0)
    a2.wait_recv()
    a3 = fwd(au(e2, c), dev1); a3.start()
    a_own(e2)
    a1.wait_recv()
    a_own(e1)
    a_far(1)
    for i in R:
        s_z[i - 1].wait_recv()
        pass_on(s_blk(fz(i), c), ((s_y, n.yp), (s_k, n.kp)))
    a3.wait_recv()
    a_own(e3)
    t_y = [n.send(lambda: tok.at[1 - y], lambda: xt.at[row(c), body], n.yp), n.send(lambda: mem.at[1 - y], lambda: xt.at[row(c), tail], n.yp)]
    uu = lambda zz, cc: blk(wu, zz, cc)
    du = lambda zz, cc: hlf(wd, zz, cc, mine)
    u2 = n.send(all_of(lu), uu(z, c), dev2)
    u1 = n.send(all_of(lu), uu(z, c), dev1)
    d_y = n.send(part(ld), du(z, c), n.yp)
    u_y = [n.send(all_of(lu), uu(z, c), n.yp)]
    u_k = {0: n.send(all_of(lu), uu(z, c), n.kp)}
    d_k = [n.send(all_of(ld), blk(wd, z, c), n.kp)]
    tsl = lambda s, kk: (lambda: tch.at[s, :, pl.ds(pl.multiple_of(kk * main, 128), main)])
    th = lambda: tt.at[row(c)]
    h_y = [n.send(tsl(y, 1 - k), th, n.kp)]
    local.append(n.local(tsl(y, k), th))
    a_far(2)
    a_far(3)
    row_ids(ids, y, memory.shape[1] // 2, idk, idq)
    for i in range(3):
        a_home(i)
    for i in range(nz):
        s_y[i].wait_recv()
        pass_on(s_blk(fz(i), oc), ((s_k, n.kp),))
    local[0].wait(); local[1].wait()
    a_home(3)
    for m, w_ in zip(t_y, (body, tail)):
        m.wait_recv()
        t_k.append(fwd((lambda w_=w_: xt.at[row(oc), w_]), n.kp)); t_k[-1].start()
    a_home(4)
    for m in t_k:
        m.wait_recv()
    def turn(i, _):
        f = pl.ds(pl.multiple_of(128 * i, 128), 128)
        x[f, :] = xt[:, f].T
        return 0
    lax.fori_loop(0, length // 128, turn, 0)
    x[pl.ds(length, rows - length), :] = xt[:, tail].T[: rows - length, :]
    o_x = n.local(all_of(xt), all_of(xt_o))
    u2.wait_recv()
    u3 = fwd(uu(e2, c), dev1); u3.start()
    d2 = n.send(part(ld), du(z, c), dev2)
    d1 = n.send(part(ld), du(z, c), dev1)
    def u_put(i, cc, y_too=True):
        m = fwd(uu(order[i], cc), n.kp)
        u_k[(i, cc is oc)] = m
        if y_too:
            u_y.append(fwd(uu(order[i], cc), n.yp))
            u_y[-1].start()
        m.start()
    u_put(1, c)
    d_x, d_xu = [], []
    def d_put(zz, cc):
        d_xu.append((zz, cc))
        d_x.append(fwd(du(zz, cc), n.xp)); d_k.append(fwd(du(zz, cc), n.kp))
        return [d_x[-1], d_k[-1]]
    d_own = d_put(z, oc)
    for i in range(5, 7):
        a_home(i)
    def step(wait, moves):
        def run():
            wait.wait_recv()
            for m in moves:
                m.start()
        return run
    def u_step(wait, i):
        u_y.append(fwd(uu(order[i], c), n.yp))
        u_w.append(fwd(uu(order[i], c), n.kp))
        return step(wait, [u_y[-1], u_w[-1]])
    u_w = list(u_k.values())
    def u_far(i):
        u_w.append(fwd(uu(order[i], oc), n.kp))
        return step(u_y[i], [u_w[-1]])
    E_dy = step(d_y, d_own)
    d3, d2o, d1o, d3o = fwd(du(e2, c), dev1), fwd(du(z, oc), dev2), fwd(du(z, oc), dev1), fwd(du(e2, oc), dev1)
    E_u1 = u_step(u1, 2)
    E_u3 = u_step(u3, 3)
    h_m = [n.move(tsl(1 - y, k), th, n.yp), n.move(tsl(1 - y, 1 - k), th, n.ykp)]
    def E_h():
        for m in h_m:
            m.start()
    h_y += h_m
    E_uy = [u_far(i) for i in range(4)]
    E_d2 = step(d2, [d3] + d_put(e2, c))
    def E_do():
        d2o.start(); d1o.start()
    E_d1 = step(d1, d_put(e1, c))
    E_d3 = step(d3, d_put(e3, c))
    E_d2o = step(d2o, [d3o] + d_put(e2, oc))
    E_d1o = step(d1o, d_put(e1, oc))
    E_d3o = step(d3o, d_put(e3, oc))
    E_dx = []
    for m, (zz, cc) in zip(d_x, d_xu):
        d_k.append(fwd(hlf(wd, zz, cc, theirs), n.kp))
        E_dx.append(step(m, [d_k[-1]]))
    proj_events = {0: [E_dy], 1: [E_u1]}
    head_events = {2: [E_do, E_dx[0]], 4: [E_uy[0], E_u3, E_h], 6: [E_d2], 8: [E_d1], 10: [E_uy[1]], 12: [E_dx[1], E_dx[2]], 13: [E_d3], 14: [E_d2o], 15: [E_uy[2]], 17: [E_d1o, E_dx[3]]}
    out_events = [E_d3o]
    gate_events = {0: [], 3: [], 6: [E_dx[4], E_dx[5]], 9: [E_dx[6]]}
    for m in s_k:
        m.wait_recv()
    for m in local[2:6]:
        m.wait()
    join192([[sm[0, cc, pl.ds(0, 8), pl.ds(0, 128)], sm[0, cc, pl.ds(0, 8), pl.ds(128, 128)]] for cc in range(4)], vec)
    lo1 = lax.broadcasted_iota(jnp.int32, (1, 128), 1) < 64
    sw = lambda a: pltpu.roll(a, 64, 1)
    bias[...] = jnp.zeros_like(bias)
    hv = [[sm[2 * k + j, 0, 11:12, pl.ds(0, 128)], sm[2 * k + j, 0, 11:12, pl.ds(128, 128)], sm[2 * k + j, 0, 12:13, pl.ds(0, 128)]] for j in range(2)]
    for p, (ea, eb) in enumerate(((hv[0][0], hv[0][1]), (hv[1][0], hv[1][1]), (hv[0][2], hv[1][2]))):
        w8 = lambda a: jnp.broadcast_to(a, (8, 128))
        lo8 = lax.broadcasted_iota(jnp.int32, (8, 128), 1) < 64
        bias[p, :, pl.ds(0, 128)] = jnp.where(lo8, w8(ea), sw(w8(eb)))
        bias[p, :, pl.ds(256, 128)] = jnp.where(lo8, sw(w8(ea)), w8(eb))
    for m in a_k:
        m.wait_recv()
    own = pl.ds(2 * k, 2)
    o_w = n.local(lambda: wa.at[own], all_of(wa_o))
    w = wa.at[own]
    assemble_pairs(w, wp, feats)
    rc = rows // 3

    def project(i, _):
        p = i // 3
        r = pl.ds(pl.multiple_of((i % 3) * rc, 16), rc)
        v = nn(x[r, :], wp[p]) + bias[p, 0:1, :]
        qt[p, r, :] = (v[:, :128].astype(BF).astype(F32) * 0.125).astype(BF)
        kt[p, r, :] = v[:, 128:256].astype(BF)
        vt[p, r, :] = v[:, 256:].astype(BF)
        at(i, proj_events)
        return 0
    lax.fori_loop(0, 9, project, 0)
    o_q = [n.local(all_of(a), all_of(o)) for a, o in ((qt, q_o), (kt, k_o), (vt, v_o))]
    m_k = [(n.move((lambda p=p: mixed.at[p, pl.ds(pl.multiple_of((1 - k) * main, 16), main)]), (lambda p=p: mrows.at[k * 3 + p, pl.ds(0, main)]), n.kp),
            n.move((lambda p=p: mixed.at[p, pl.ds(pl.multiple_of(length + (1 - k) * 16, 16), 16)]), (lambda p=p: mrows.at[k * 3 + p, pl.ds(main, 16)]), n.kp)) for p in range(3)]
    m_l = [(n.copy((lambda p=p: mixed.at[p, pl.ds(pl.multiple_of(k * main, 16), main)]), (lambda p=p: mrows.at[k * 3 + p, pl.ds(0, main)])),
            n.copy((lambda p=p: mixed.at[p, pl.ds(pl.multiple_of(length + k * 16, 16), 16)]), (lambda p=p: mrows.at[k * 3 + p, pl.ds(main, 16)]))) for p in range(3)]
    cuts = {1: 0, 3: 1, 4: 2}

    def head(i, _):
        p = i // 2
        e = i % 2
        he = pl.ds(pl.multiple_of(64 * e, 64), 64)

        @pl.when(e == 0)
        def _():
            vtt[...] = vt[p].T
        lanes = (lax.broadcasted_iota(jnp.int32, (1, 128), 1) // 64) == e
        for t_, (q0, qn, spans) in enumerate(tiles(rows, length)):
            q = qt[p, pl.ds(q0, qn), :]
            qm = jnp.where(lanes, q, jnp.zeros_like(q))
            sc = scores_of(kt, qm, idk, idq[0:1, pl.ds(q0, qn)], p, spans)
            m = jnp.max(sc[0], axis=0, keepdims=True)
            for s in sc[1:]:
                m = jnp.maximum(m, jnp.max(s, axis=0, keepdims=True))
            tot, acc = None, None
            for s, (k0, kn, _) in zip(sc, spans):
                ex = jnp.exp(s - m)
                t = jnp.sum(ex, axis=0, keepdims=True)
                o = nn(vtt[he, pl.ds(k0, kn)], ex.astype(BF))
                tot = t if tot is None else tot + t
                acc = o if acc is None else acc + o
            ot[he, pl.ds(q0, qn)] = acc / tot
            lse[i, :, pl.ds(q0, qn)] = m + jnp.log(tot)
            if t_ in cuts:
                at(3 * i + cuts[t_], head_events)

        @pl.when(e == 1)
        def _():
            mixed[p] = ot[...].T.astype(BF)
        at(i, {2 * p + 1: [m.start for m in m_k[p] + m_l[p]] for p in range(3)})
        return 0
    lax.fori_loop(0, 6, head, 0)
    o_m = n.local(all_of(mixed), all_of(mixed_o))
    lo = lax.broadcasted_iota(jnp.int32, (feats, 128), 1) < 64
    for kk in range(2):
        z0, z1 = 2 * kk, 2 * kk + 1
        wt[:, pl.ds(384 * kk, 128)] = wa[z0, :, pl.ds(640, 128)]
        wt[:, pl.ds(384 * kk + 128, 128)] = wa[z1, :, pl.ds(640, 128)]
        t0 = pltpu.roll(wa[z0, :, pl.ds(512, 128)].astype(F32), 64, 1)
        wt[:, pl.ds(384 * kk + 256, 128)] = jnp.where(lo, t0, wa[z1, :, pl.ds(512, 128)].astype(F32)).astype(BF)
    for pair_ in m_k:
        for m in pair_:
            m.wait_recv()
    for pair_ in m_l:
        for m in pair_:
            m.wait()
    nb = feats // 256
    CHS = own_rows // CH

    def own_slice(i, num):
        start = jnp.where(i < main, k * main + i, length + k * 16)
        return pl.ds(pl.multiple_of(start, 16), num)

    for f0 in range(0, feats, 256):
        f = pl.ds(f0, 256)
        acc = nt(mrows[0], wt[f, pl.ds(0, 128)])
        for j in range(1, 6):
            acc = acc + nt(mrows[j], wt[f, pl.ds(128 * j, 128)])
        h1[:, f] = acc + vec[0:1, f]
    for e in out_events:
        e()
    inv = 1.0 / feats
    vgrad[...] = jnp.zeros_like(vgrad)
    bupgrad[...] = jnp.zeros_like(bupgrad)

    def norm1(i, _):
        r = pl.ds(pl.multiple_of(i * 16, 16), 16)
        h = h1[r, :] + x[own_slice(i * 16, 16), :].astype(F32)
        m = jnp.sum(h, axis=1, keepdims=True) * inv
        s = jnp.sum(h * h, axis=1, keepdims=True) * inv
        rstd = lax.rsqrt(s - m * m + EPSILON)
        xhat = (h - m) * rstd
        h1[r, :] = xhat
        rs1[r, :] = jnp.broadcast_to(rstd, (16, 128))
        low[r, :] = (xhat * vec[1:2, :] + vec[2:3, :]).astype(BF)
        return 0
    lax.fori_loop(0, own_rows // 16, norm1, 0, unroll=3)
    lowt[...] = low[...].T
    E_uy[3]()
    for m in u_w:
        m.wait_recv()

    def gate(i, _):
        at(i, gate_events)
        zz = i // nb
        j = i % nb
        f = pl.ds(pl.multiple_of(j * 256, 256), 256)
        v = nn(low[...], wu[zz, :, f]) + sm[zz, 0, pl.ds(8 + j, 1), :]
        a, g = gelu_pair(v)
        hid[zz, :, f] = a.astype(BF)
        dgl[zz, :, f] = g.astype(BF)
        return 0
    lax.fori_loop(0, nz * nb, gate, 0)
    for m in h_y:
        m.wait_recv()
    local[6].wait()
    def turn_t(i, _):
        f = pl.ds(pl.multiple_of(128 * i, 128), 128)
        tr[f, :] = tt[:, f].T
        return 0
    lax.fori_loop(0, main // 128, turn_t, 0)
    tr[pl.ds(main, 16), :] = jnp.zeros((16, feats), BF)
    for m in d_k:
        m.wait_recv()

    def down(j, _):
        f = pl.ds(pl.multiple_of(j * 256, 256), 256)
        acc = nt(hid[0], wd[0, f, :])
        for zz in range(1, nz):
            acc = acc + nt(hid[zz], wd[zz, f, :])
        h2[:, f] = acc
        return 0
    lax.fori_loop(0, nb, down, 0)
    scale = vec[6:7, 0:1]
    o4[:, :, pl.ds(b, o4.shape[2] - b)] = jnp.zeros((4, own_rows, o4.shape[2] - b), BF)

    def norm2(i, _):
        r = pl.ds(pl.multiple_of(i * CH, 16), CH)
        h = h2[r, :] + (h1[r, :] * vec[1:2, :] + vec[2:3, :]) + vec[3:4, :]
        m = jnp.sum(h, axis=1, keepdims=True) * inv
        s = jnp.sum(h * h, axis=1, keepdims=True) * inv
        rstd = lax.rsqrt(s - m * m + EPSILON)
        xhat = (h - m) * rstd
        o = xhat * vec[4:5, :] + vec[5:6, :]
        for cc in range(4):
            o4[cc, r, pl.ds(0, b)] = o[:, cc * b:(cc + 1) * b].astype(BF)
        place = lax.broadcasted_iota(jnp.int32, (CH, 1), 0) + i * CH
        place = jnp.where(place < main, place + k * main, count)
        go = jnp.where(place < count, scale * (o - tr[r, :].astype(F32)), 0.0)
        a = go * vec[4:5, :]
        m1 = jnp.sum(a, axis=1, keepdims=True) * inv
        m2 = jnp.sum(a * xhat, axis=1, keepdims=True) * inv
        g2 = rstd * (a - m1 - xhat * m2)
        h2[r, :] = g2
        g2b = g2.astype(BF)
        br[r, :] = g2b
        vgrad[0] += group_sum(go * xhat)
        vgrad[1] += group_sum(go)
        vgrad[2] += group_sum(g2b.astype(F32))
        return 0
    lax.fori_loop(0, CHS, norm2, 0)
    o_dst = lambda: out4.at[y, k]
    o_s = [n.send(lambda: o4.at[oc], o_dst, n.yp), n.send(lambda: o4.at[3 - c], o_dst, n.ykp), n.send(lambda: o4.at[c + 1 - 2 * k], o_dst, n.kp)]
    o_l = n.local(lambda: o4.at[c], o_dst)
    brt[...] = br[...].T
    def gmove(which, src, dst, zz, slot, yy):
        return pltpu.make_async_remote_copy(src_ref=src.at[slot, 2 * yy + 1 - k], dst_ref=dst.at[yy, zz], send_sem=zsem.at[which, yy, zz],
                                            recv_sem=zrem.at[which, yy, zz], device_id=n.kp, device_id_type=MESH)
    def each(fn, zz, slot):
        for which, src, dst in ((0, gdz, rd), (1, guz, ru)):
            for yy in range(2):
                fn(gmove(which, src, dst, zz, slot, yy))
    def fold(zz):
        each(lambda m: m.wait_recv(), zz, 0)
        for yy in range(2):
            add_to(hd.at[yy, zz], rd.at[yy, zz])
            add_to(hu.at[yy, zz], ru.at[yy, zz])

    def back(zz, _):
        slot = zz % 2

        @pl.when(zz >= 2)
        def _():
            each(lambda m: m.wait_send(), zz - 2, slot)

        def chunk(j, _):
            f = pl.ds(pl.multiple_of(j * 256, 256), 256)
            gh = nn(br[...], wd[zz, :, f])
            g = (gh * dgl[zz, :, f].astype(F32)).astype(BF)
            bupgrad[zz, :, f] += group_sum(g.astype(F32))
            gdc = nn(brt[...], hid[zz, :, f])
            guc = nn(lowt[...], g)
            hid[zz, :, f] = g
            for cc in range(4):
                gdz[slot, cc, :, f] = gdc[cc * b:(cc + 1) * b, :].astype(BF)
                guz[slot, cc, :, f] = guc[cc * b:(cc + 1) * b, :].astype(BF)
            return 0
        lax.fori_loop(0, nb, chunk, 0)
        each(lambda m: m.start(), zz, slot)
        for yy in range(2):
            hd[yy, zz] = gdz[slot, 2 * yy + k]
            hu[yy, zz] = guz[slot, 2 * yy + k]

        @pl.when(zz >= 1)
        def _():
            fold(zz - 1)
        return 0
    lax.fori_loop(0, nz, back, 0)

    def first_grad(j, _):
        f = pl.ds(pl.multiple_of(j * 256, 256), 256)
        acc = h2[:, f]
        for zz in range(nz):
            acc = acc + nt(hid[zz], wu[zz, f, :])
        h2[:, f] = acc
        return 0
    lax.fori_loop(0, nb, first_grad, 0)
    fold(nz - 1)
    o_h = [n.local(all_of(hd), all_of(hd_o)), n.local(all_of(hu), all_of(hu_o))]

    def norm1_back(i, _):
        r = pl.ds(pl.multiple_of(i * 16, 16), 16)
        g = h2[r, :]
        xhat = h1[r, :]
        a = g * vec[1:2, :]
        m1 = jnp.sum(a, axis=1, keepdims=True) * inv
        m2 = jnp.sum(a * xhat, axis=1, keepdims=True) * inv
        g1 = rs1[r, 0:1] * (a - m1 - xhat * m2)
        g_one[r, :] = g1
        gb = g1.astype(BF)
        ga[own_slice(i * 16, 16), :] = gb
        vgrad[3] += group_sum(g * xhat)
        vgrad[4] += group_sum(g)
        vgrad[5] += group_sum(gb.astype(F32))
        return 0
    lax.fori_loop(0, own_rows // 16, norm1_back, 0, unroll=3)
    g_main = lambda: ga.at[pl.ds(pl.multiple_of(k * main, 16), main)]
    g_tail = lambda: ga.at[pl.ds(pl.multiple_of(length + k * 16, 16), 16)]
    g_k = [n.send(g_main, g_main, n.kp), n.send(g_tail, g_tail, n.kp)]
    for m in g_k:
        m.wait_recv()
    o_g = n.local(all_of(ga), all_of(ga_o))
    for m in o_s:
        m.wait_recv()
    for m in [o_x, o_w, o_m, o_l, o_g] + o_q + o_h:
        m.wait()
    for zz in range(nz - 2, nz):
        each(lambda m: m.wait_send(), zz, zz % 2)
    n.finish()

def add_to(dst, src):
    dst[...] = (dst[...].astype(F32) + src[...].astype(F32)).astype(BF)

def forward(valid, tok, memory, tch, w3, wo, lu, ld, vecs, bias_up, bias_qv, ids, nz):
    b, width = lu.shape
    feats = 4 * b; length = tok.shape[2]; rows = length + 32; main = length // 2; own = main + 16
    V = lambda *s, d=BF: pltpu.VMEM(s, d)
    vm = pl.BlockSpec(memory_space=pltpu.VMEM); sm = pl.BlockSpec(memory_space=pltpu.SMEM); an = pl.BlockSpec(memory_space=pl.ANY)
    S = jax.ShapeDtypeStruct
    t3 = S((3, rows, 128), BF); h = S((2, nz, b, width), BF)
    outs = [(S((feats, length + 128), BF), an), (t3, an), (t3, an), (t3, an), (t3, an), (S((2, feats, width), BF), an), (S((rows, feats), BF), an), (h, an), (h, an),
            (S((6, 1, rows), F32), vm), (S((own, feats), F32), vm), (S((6, 8, feats), F32), vm), (S((nz, 8, width), F32), vm), (S((2, 2, own, 256), BF), vm)]
    w = V(nz, feats, width)
    scratch = [V(feats, length + 128), V(rows, feats), w, w, w, V(nz, 4, 16, 256, d=F32), V(feats, main), V(own, feats), V(3, feats, 384),
               V(3, rows, 128), V(3, rows, 128), V(3, rows, 128), V(128, rows), V(128, rows, d=F32), V(3, rows, 128), V(6, own, 128), V(3, 8, 384, d=F32), V(8, feats, d=F32), V(feats, feats),
               V(own, feats, d=F32), V(own, feats, d=F32), V(own, 128, d=F32), V(own, feats), V(feats, own), V(own, feats), V(feats, own),
               V(nz, own, width), V(nz, own, width), V(2, 4, b, width), V(2, 4, b, width)] + [V(2, nz, b, width)] * 4 + [V(rows, feats), V(4, own, 256), V(b, width), V(16, 256, d=F32), V(2, b, 128), V(128, b, d=F32), V(length + 128, 128, d=F32), V(1, length + 128, d=F32),
               pltpu.SemaphoreType.DMA((136,)), pltpu.SemaphoreType.DMA((136,)), pltpu.SemaphoreType.DMA((32,)),
               pltpu.SemaphoreType.DMA((2, 2, nz)), pltpu.SemaphoreType.DMA((2, 2, nz))]
    return pl.pallas_call(forward_kernel, out_shape=[o for o, _ in outs], out_specs=[s for _, s in outs],
        in_specs=[sm, an, vm, an, vm, vm, an, an] + [vm] * 9, scratch_shapes=scratch,
        compiler_params=pltpu.CompilerParams(collective_id=1, has_side_effects=True, vmem_limit_bytes=67043328))(valid, tok, memory, tch, w3, wo, lu, ld, *vecs, bias_up, bias_qv, ids)
def total_of(refs):
    acc = refs[0][...].astype(F32)
    for r in refs[1:]:
        acc = acc + r[...].astype(F32)
    return acc

class Piece:
    def __init__(self, n, env, col0, num, js, x_first):
        self.n, self.x_first = n, x_first
        gown, ha, ax, ay, ayf, axf, mine, theirs, order = env
        C = pl.ds(col0, num); y, k = n.y, n.k
        self.core = [n.move((lambda j=j, yy=yy: gown.at[j, 2 * yy + 1 - k, :, C]), (lambda j=j, yy=yy: ha.at[yy, 2 * k + j, :, C]), n.kp) for j in js for yy in range(2)]
        self.keep = [n.copy((lambda j=j, yy=yy: gown.at[j, 2 * yy + k, :, C]), (lambda j=j, yy=yy: ha.at[yy, 2 * k + j, :, C])) for j in js for yy in range(2)]
        zz = order if len(js) == 2 else [js[0], js[0] + 2]
        self.first, self.second, self.add1, self.add2 = [], [], [], []
        for q in zz:
            if x_first:
                self.first.append(n.move((lambda q=q: ha.at[:, q, theirs, C]), (lambda q=q: ax.at[:, q, :, C]), n.xp))
                self.add1.append(lambda q=q: [add_to(ha.at[yy, q, mine, C], ax.at[yy, q, :, C]) for yy in range(2)])
                self.second.append(n.move((lambda q=q: ha.at[1 - y, q, mine, C]), (lambda q=q: ay.at[q, :, C]), n.yp))
                self.add2.append(lambda q=q: add_to(ha.at[y, q, mine, C], ay.at[q, :, C]))
            else:
                self.first.append(n.move((lambda q=q: ha.at[1 - y, q, :, C]), (lambda q=q: ayf.at[q, :, C]), n.yp))
                self.add1.append(lambda q=q: add_to(ha.at[y, q, :, C], ayf.at[q, :, C]))
                self.second.append(n.move((lambda q=q: ha.at[y, q, theirs, C]), (lambda q=q: axf.at[q, :, C]), n.xp))
                self.add2.append(lambda q=q: add_to(ha.at[y, q, mine, C], axf.at[q, :, C]))
    def start(self):
        for m in self.core + self.keep:
            m.start()
    def ev1(self):
        for m in self.core:
            m.wait_recv()
        for m in self.keep:
            m.wait()
        for m in self.first:
            m.start()
    def ev2(self):
        for m, f, s in zip(self.first, self.add1, self.second):
            m.wait_recv(); f(); s.start()
    def ev3(self):
        for m, f in zip(self.second, self.add2):
            m.wait_recv(); f()

class Rows:
    def __init__(self, n, here, z1, z2, e, dev1, dev2, add):
        e1, e2, e3 = e
        self.a = n.move((lambda: here(e3)), (lambda: z1(1)), dev1)
        self.b = n.move((lambda: here(e1)), (lambda: z1(0)), dev1)
        self.c = n.move((lambda: here(e2)), z2, dev2)
        self.mid = lambda: add(here(e2), z1(1))
    def start(self):
        self.a.start(); self.b.start()
    def middle(self):
        self.a.wait_recv(); self.mid(); self.c.start()
    def end(self):
        self.b.wait_recv(); self.c.wait_recv()

def backward_kernel(hu_h, hd_h, ga_h, mixed_h, xt_h, q_h, k_h, v_h, w_h, o4_h, g1_h, lse, vgrad, bupgrad, ids,
                    grad4, lout, gmem, g3, gwo, fu, fd, fvec, bup, bqv,
                    hu, hd, ux, uz1, uz2, ut, uy, fub, pu, dy, dz1, dz2, df, dx, pd,
                    ha, ax, ay, ayf, axf, az1, az2, fa, pa, gown,
                    ga, mixed, xt, qt, kt, vt, w, o4, g1, wp, wt, gat, gm, gp, dv, dk, dqt, ktt, dd, g4, gs, gr, lo32,
                    sv, svk, svt, svy, svo, svx, ps, svz, idk, idq, ss, rs, lsem):
    n = Net(ss, rs, lsem)
    nz, y, k, c, z, x, d, nd = n.nz, n.y, n.k, n.c, n.z, n.x, n.d, n.nd
    b = fu.shape[0]; hb = b // 2
    rows, feats = ga.shape
    fb = pl.ds(0, b)
    own_rows = g1.shape[0]; main = own_rows - 16; length = 2 * main
    mine = pl.ds(pl.multiple_of(x * hb, 16), hb)
    theirs = pl.ds(pl.multiple_of((1 - x) * hb, 16), hb)
    all_of = lambda r: (lambda: r)
    l_w, l_ga, l_m = [n.local(all_of(s), all_of(t)) for s, t in ((w_h, w), (ga_h, ga), (mixed_h, mixed))]
    l_q = [n.local(all_of(s), all_of(t)) for s, t in ((k_h, kt), (q_h, qt), (v_h, vt))]
    l_x = n.local(all_of(xt_h), all_of(xt))
    l_d = n.local(lambda: hd_h.at[y], lambda: hd)
    l_u = n.local(lambda: hu_h.at[:, :, mine], lambda: hu)
    l_o = [n.local(all_of(o4_h), all_of(o4)), n.local(all_of(g1_h), all_of(g1))]
    n.barrier(n.zp[1:] + [n.yp, n.ykp, n.kp, n.xp] + n.others)
    e1 = z + 1 - 2 * lax.rem(z, 2)
    e2 = lax.rem(z + 2, nz)
    e3 = lax.rem(e1 + 2, nz)
    e = (e1, e2, e3)
    order = [e3, e2, e1, z]
    dev1, dev2 = (d, e1, c), (d, e2, c)
    d_y = [n.send((lambda q=q: hd_h.at[1 - y, q]), (lambda q=q: dy.at[q]), n.yp) for q in order]
    u_x = [n.send((lambda q=q: hu_h.at[:, q, theirs]), (lambda q=q: ux.at[:, q]), n.xp) for q in order]

    def add2(a, s):
        for yy in range(2):
            add_to(a.at[yy], s.at[yy])
    dz = Rows(n, lambda q: hd.at[q], lambda s: dz1.at[s], lambda: dz2, e, dev1, dev2, add_to)
    uz = Rows(n, lambda q: hu.at[:, q], lambda s: uz1.at[s], lambda: uz2, e, dev1, dev2, add2)
    d_x = n.move(all_of(df), all_of(dx), n.xp)
    u_y = n.move(lambda: ut.at[1 - y], all_of(uy), n.yp)
    u_f = n.move(lambda: fub.at[mine], lambda: fub.at[mine], n.xp)

    mypair = d // 2

    def pairs_sum(value, slots, view):
        if nd == 2:
            return value
        view(slots, mypair)[...] = value.astype(slots.dtype)
        ms = [n.send((lambda: view(slots, mypair)), (lambda: view(slots, mypair)), o) for o in n.others]
        for m in ms:
            m.wait_recv()
        return total_of([view(slots, i) for i in range(nd // 2)])

    def ev_dy(j):
        def run():
            d_y[j].wait_recv()
            if j == 0:
                l_d.wait()
            add_to(hd.at[order[j]], dy.at[order[j]])
            if j == 0:
                dz.a.start()
        return run
    def ev_ux(j):
        def run():
            u_x[j].wait_recv()
            if j == 0:
                l_u.wait()
            add2(hu.at[:, order[j]], ux.at[:, order[j]])
            if j == 0:
                uz.a.start()
        return run
    def ev_df():
        dz.end()
        df[...] = total_of([hd.at[z], dz1.at[0], dz2]).astype(BF)
        d_x.start()
    def ev_ut():
        uz.end()
        for yy in range(2):
            ut[yy] = total_of([hu.at[yy, z], uz1.at[0, yy], uz2.at[yy]]).astype(BF)
        u_y.start()
    def ev_uf():
        u_y.wait_recv()
        fub[mine, :] = pairs_sum(total_of([ut.at[y], uy]), pu, lambda s, i: s.at[i]).astype(BF)
        u_f.start()
    env = (gown, ha, ax, ay, ayf, axf, mine, theirs, order)
    PO = Piece(n, env, 640, 128, (0, 1), True)
    P0 = Piece(n, env, 0, 384, (0,), True)
    P1 = Piece(n, env, 0, 384, (1,), False)
    P2 = Piece(n, env, 384, 128, (0, 1), True)
    P3 = Piece(n, env, 512, 128, (0, 1), False)
    class Cols:
        def __init__(self, col0, num):
            C = pl.ds(col0, num)
            self.C = C
            self.z = Rows(n, lambda q: ha.at[y, q, mine, C], lambda s: az1.at[s, :, C], lambda: az2.at[:, C], e, dev1, dev2, add_to)
            self.f = n.move(lambda: fa.at[mine, C], lambda: fa.at[mine, C], n.xp)
        def end(self):
            self.z.end()
            C = self.C
            fa[mine, C] = pairs_sum(total_of([ha.at[y, z, mine, C], az1.at[0, :, C], az2.at[:, C]]), pa, lambda s, i: s.at[i, :, C]).astype(BF)
            self.f.start()
    ZO, Z01, Z2, Z3 = Cols(640, 128), Cols(0, 384), Cols(384, 128), Cols(512, 128)
    row_ids(ids, y, gmem.shape[1] // 2, idk, idq)
    l_w.wait(); l_ga.wait()
    gat[...] = ga[...].T
    assemble_pairs(w, wp, feats)
    wt[:, pl.ds(0, 128)] = w[0, :, pl.ds(640, 128)]
    wt[:, pl.ds(128, 128)] = w[1, :, pl.ds(640, 128)]
    lo = lax.broadcasted_iota(jnp.int32, (feats, 128), 1) < 64
    wt[:, pl.ds(256, 128)] = jnp.where(lo, pltpu.roll(w[0, :, pl.ds(512, 128)].astype(F32), 64, 1), w[1, :, pl.ds(512, 128)].astype(F32)).astype(BF)
    r3 = rows // 3

    def mixed_grad(i, _):
        r = pl.ds(pl.multiple_of(i * r3, 16), r3)
        v = nn(ga[r, :], wt[...])
        for p in range(3):
            gm[p, r, :] = v[:, 128 * p:128 * p + 128].astype(BF)
        return 0
    lax.fori_loop(0, 3, mixed_grad, 0)
    l_m.wait()
    for cc in range(4):
        af = gat[pl.ds(b * cc, b), :]
        for j in range(2):
            gown[j, cc, :, pl.ds(640, 128)] = nn(af, mixed[j]).astype(BF)
    PO.start()
    for m in l_q:
        m.wait()
    l_x.wait()
    def ev_b():
        dz.b.start(); uz.b.start()
    table = {0: [ev_dy(0), ev_ux(0)], 1: [PO.ev1], 4: [ev_dy(1), ev_ux(1)], 6: [dz.middle], 7: [ev_dy(2), ev_ux(2), P0.ev1], 9: [uz.middle], 10: [ev_b],
             11: [ev_dy(3), ev_ux(3)], 13: [PO.ev2], 15: [P1.ev1], 16: [PO.ev3, ZO.z.start, P0.ev2]}
    cuts = {1: 0, 3: 1, 4: 2}

    def head(i, _):
        p = i // 2
        h = i % 2
        he = pl.ds(pl.multiple_of(64 * h, 64), 64)

        @pl.when(h == 0)
        def _():
            ktt[...] = kt[p].T
            prod = (gm[p].astype(F32) * mixed[p].astype(F32)).T
            dd[0] = jnp.sum(prod[:64, :], axis=0, keepdims=True)
            dd[1] = jnp.sum(prod[64:, :], axis=0, keepdims=True)
            dv[...] = jnp.zeros_like(dv)
            dk[...] = jnp.zeros_like(dk)
        lanes = (lax.broadcasted_iota(jnp.int32, (1, 128), 1) // 64) == h
        for t, (q0, qn, spans) in enumerate(tiles(rows, length)):
            q = qt[p, pl.ds(q0, qn), :]
            qm = jnp.where(lanes, q, jnp.zeros_like(q))
            g = gm[p, pl.ds(q0, qn), :]
            gmm = jnp.where(lanes, g, jnp.zeros_like(g))
            sc = scores_of(kt, qm, idk, idq[0:1, pl.ds(q0, qn)], p, spans)
            l = lse[i, :, pl.ds(q0, qn)]
            dl = dd[h, :, pl.ds(q0, qn)]
            acc = None
            for s, (k0, kn, _) in zip(sc, spans):
                pr = jnp.exp(s - l)
                dp = nt(vt[p, pl.ds(k0, kn), :], gmm)
                ds = (pr * (dp - dl)).astype(BF)
                dv[pl.ds(k0, kn), :] += nn(pr.astype(BF), gmm)
                dk[pl.ds(k0, kn), :] += nn(ds, qm)
                o = nn(ktt[he, pl.ds(k0, kn)], ds)
                acc = o if acc is None else acc + o
            dqt[he, pl.ds(q0, qn)] = acc * 0.125
            if t in cuts:
                at(3 * i + cuts[t], table)

        @pl.when(h == 1)
        def _():
            gp[p, :, pl.ds(0, 128)] = dqt[...].T.astype(BF)
            gp[p, :, pl.ds(128, 128)] = dk[...].astype(BF)
            gp[p, :, pl.ds(256, 128)] = dv[...].astype(BF)

        @pl.when(jnp.logical_and(h == 1, p < 2))
        def _():
            def part(cc, _):
                f = pl.ds(pl.multiple_of(b * cc, 16), b)
                gown[p, cc, :, pl.ds(0, 384)] = nn(xt[f, pl.ds(0, rows)], gp[p]).astype(BF)
                return 0
            lax.fori_loop(0, 4, part, 0)
        at(i, {1: [P0.start], 3: [P1.start]})
        return 0
    lax.fori_loop(0, 6, head, 0)
    sv[...] = jnp.zeros_like(sv)
    for i in range(6):
        sv[pl.ds(i, 1), :] = jnp.sum(vgrad[i], axis=0, keepdims=True)
    for i in range(nz):
        sv[pl.ds(6 + i, 1), :] = jnp.sum(bupgrad[i], axis=0, keepdims=True)
    for p in range(3):
        t = jnp.sum(group_sum(gp[p].astype(F32)), axis=0, keepdims=True)
        sv[pl.ds(6 + nz + p, 1), pl.ds(0, 384)] = jnp.where(k == 0, t, 0.0)
        sv[pl.ds(6 + nz + p, 1), pl.ds(384, 384)] = jnp.where(k == 1, t, 0.0)
    s_k = n.send(all_of(sv), all_of(svk), n.kp)
    sw = lambda a: pltpu.roll(a, 64, 1)

    def last(cc, _):
        f = pl.ds(pl.multiple_of(b * cc, 16), b)
        r2 = nn(xt[f, pl.ds(0, rows)], gp[2])
        o2 = nn(gat[f, :], mixed[2])
        lo = lax.broadcasted_iota(jnp.int32, (b, 128), 1) < 64
        rq, rk, rv = r2[:, :128], r2[:, 128:256], r2[:, 256:]
        gown[0, cc, :, pl.ds(384, 128)] = jnp.where(lo, rq, sw(rk)).astype(BF)
        gown[1, cc, :, pl.ds(384, 128)] = jnp.where(lo, sw(rq), rk).astype(BF)
        gown[0, cc, :, pl.ds(512, 128)] = jnp.where(lo, rv, sw(o2)).astype(BF)
        gown[1, cc, :, pl.ds(512, 128)] = jnp.where(lo, sw(rv), o2).astype(BF)
        return 0
    lax.fori_loop(0, 4, last, 0)
    P2.start(); P3.start()
    def rowsgrad(r):
        return nt(gp[0, r, :], wp[0]) + nt(gp[1, r, :], wp[1]) + nt(gp[2, r, :], wp[2])

    def half_rows(kk, put):
        def chunk(i, _):
            put(pl.ds(pl.multiple_of(i * 256, 16), 256), rowsgrad(pl.ds(pl.multiple_of(kk * main + i * 256, 16), 256)))
            return 0
        lax.fori_loop(0, main // 256, chunk, 0)
        put(pl.ds(main, 16), rowsgrad(pl.ds(pl.multiple_of(length + kk * 16, 16), 16)))
    def put_other(r, v):
        gs[r, :] = v.astype(BF)
    half_rows(1 - k, put_other)
    g_k = n.send(all_of(gs), all_of(gr), n.kp)
    s_k.wait_recv()
    svt[...] = sv[...] + svk[...]
    s_y = n.send(all_of(svt), all_of(svy), n.yp)
    P1.ev2(); P0.ev3()
    P2.ev1(); P3.ev1()
    ev_ut()
    for m in l_o:
        m.wait()
    g4[:, :, pl.ds(b, g4.shape[2] - b)] = jnp.zeros((4, own_rows, g4.shape[2] - b), BF)
    def put_own(r, v):
        g1[r, :] = g1[r, :] + v
    half_rows(k, put_own)
    s_y.wait_recv()
    svo[...] = svt[...] + svy[...]
    s_x = n.send(all_of(svo), all_of(svx), n.xp)
    ev_df()
    P1.ev3(); Z01.z.start(); ZO.z.middle()
    P2.ev2()
    g_k.wait_recv()

    def own(i, _):
        r = pl.ds(pl.multiple_of(i * 48, 16), 48)
        v = g1[r, :] + gr[r, :].astype(F32)
        for cc in range(4):
            g4[cc, r, fb] = v[:, cc * b:(cc + 1) * b].astype(BF)
        return 0
    lax.fori_loop(0, own_rows // 48, own, 0)
    g_l = n.local(lambda: g4.at[c], lambda: grad4.at[y, k])
    dst = lambda: grad4.at[y, k]
    g_s = [n.send(lambda: g4.at[n.oc], dst, n.yp), n.send(lambda: g4.at[3 - c], dst, n.ykp), n.send(lambda: g4.at[c + 1 - 2 * k], dst, n.kp)]
    P3.ev2()
    s_x.wait_recv()
    svz[z] = pairs_sum(svo[...] + svx[...], ps, lambda s, i: s.at[i])
    s_z = [n.send(lambda: svz.at[z], lambda: svz.at[z], n.zp[i]) for i in range(1, nz)]
    P2.ev3(); Z2.z.start()
    ev_uf()
    Z01.z.middle(); ZO.end()
    P3.ev3(); Z3.z.start()
    half = (lout.shape[1] - length) // 2
    for s in range(2):
        lo32[pl.ds(0, half), :] = o4[s, 0, pl.ds(main, 16), fb].astype(F32)[:half]
        lo32[pl.ds(half, main), :] = o4[s, 0, pl.ds(0, main), fb].astype(F32)
        lo32[pl.ds(half + main, main), :] = o4[s, 1, pl.ds(0, main), fb].astype(F32)
        lo32[pl.ds(half + length, 16 - half), :] = o4[s, 0, pl.ds(main, 16), fb].astype(F32)[half:]
        lo32[pl.ds(length + 16, 2 * half - 16), :] = o4[s, 1, pl.ds(main, 16), fb].astype(F32)[:2 * half - 16]
        lout[s] = lo32[pl.ds(0, length + 2 * half), :].astype(BF)
    Z2.z.middle(); Z01.end(); Z3.z.middle()
    d_x.wait_recv()
    fd[...] = pairs_sum(total_of([df, dx]), pd, lambda s, i: s.at[i])
    u_f.wait_recv()
    fu[...] = fub[...].astype(F32)
    Z2.end(); Z3.end()
    for m in s_z:
        m.wait_recv()
    acc = svz[0]
    for i in range(1, nz):
        acc = acc + svz[i]
    pick = jnp.where(c == 0, acc[:8, 0:b], 0.0)
    for cc in range(1, 4):
        pick = pick + jnp.where(c == cc, acc[:8, cc * b:(cc + 1) * b], 0.0)
    fvec[...] = pick
    t = jnp.where(z == 0, acc[6:7], 0.0)
    for i in range(1, nz):
        t = t + jnp.where(z == i, acc[6 + i:7 + i], 0.0)
    bup[...] = t
    hbias = acc[6 + nz:9 + nz]
    hbias = jnp.where(z // 2 == 0, hbias[:, :384], hbias[:, 384:])
    odd = z % 2 == 1
    two = jnp.where(odd, hbias[1:2], hbias[0:1])
    lo1 = lax.broadcasted_iota(jnp.int32, (8, 128), 1) < 64
    w8 = lambda a: jnp.broadcast_to(a, (8, 128))
    left = lambda a, v: jnp.where(lo1, w8(a), sw(w8(v)))[0:1]
    right = lambda a, v: jnp.where(lo1, sw(w8(a)), w8(v))[0:1]
    lq, lv = hbias[2:3, :128], hbias[2:3, 256:]
    bqv[pl.ds(0, 1), :] = left(two[:, :128], two[:, 256:])
    bqv[pl.ds(1, 1), :] = right(two[:, :128], two[:, 256:])
    bqv[pl.ds(2, 1), :] = jnp.where(odd, right(lq, lv), left(lq, lv))
    for m in (ZO, Z01, Z2, Z3):
        m.f.wait_recv()
    lob = lax.broadcasted_iota(jnp.int32, (b, 128), 1) < 64
    tile = lambda i: fa[:, pl.ds(128 * i, 128)].astype(F32)
    t0, t1, t2, t3, t4, t5 = [tile(i) for i in range(6)]
    g3[0, :, pl.ds(0, 128)] = jnp.where(lob, t0, sw(t1))
    g3[0, :, pl.ds(128, 64)] = t2[:, :64]
    g3[1, :, pl.ds(0, 128)] = jnp.where(lob, sw(t0), t1)
    g3[1, :, pl.ds(128, 64)] = sw(t2)[:, :64]
    g3[2, :, pl.ds(0, 128)] = t3
    g3[2, :, pl.ds(128, 64)] = t4[:, :64]
    gwo[pl.ds(0, 128), :] = t5.T
    gwo[pl.ds(128, 64), :] = sw(t4).T[:64]
    for m in g_s:
        m.wait_recv()
    g_l.wait()
    for s in range(2):
        gmem[s, pl.ds(0, 16), :] = grad4[s, 0, pl.ds(main, 16), fb].astype(F32)
        gmem[s, pl.ds(16, 2 * half - 16), :] = grad4[s, 1, pl.ds(main, 16), fb].astype(F32)[:2 * half - 16]
    n.finish()

def backward(hu, hd, ga, mixed, xt, qt, kt, vt, w, o4, g1, lse, vgrad, bupgrad, ids, half, nz, nd):
    b, width = hu.shape[2:]
    feats = 4 * b; hb = b // 2; rows = ga.shape[0]; own = g1.shape[0]; length = 2 * (own - 16)
    V = lambda *s, d=BF: pltpu.VMEM(s, d)
    vm = pl.BlockSpec(memory_space=pltpu.VMEM); an = pl.BlockSpec(memory_space=pl.ANY)
    S = jax.ShapeDtypeStruct
    np_ = max(1, nd // 2) if nd > 2 else 1
    pw = (hb, width) if nd > 2 else (16, 128)
    t3 = V(3, rows, 128); f3 = lambda *s: V(*s, d=F32)
    sm = f3(16, feats)
    outs = (S((2, 2, own, 256), BF), S((2, length + 2 * half, b), BF), S((2, 2 * half, b), F32), S((3, b, b), F32), S((b, b), F32), S((b, width), F32), S((b, width), F32), S((8, b), F32), S((1, feats), F32), S((3, 128), F32))
    scratch = [V(2, nz, hb, width), V(nz, b, width), V(2, nz, hb, width), V(2, 2, hb, width), V(2, hb, width), V(2, hb, width), V(hb, width), V(b, width), V(np_, *pw),
               V(nz, b, width), V(2, b, width), V(b, width), V(b, width), V(b, width), V(np_, b, width) if nd > 2 else V(1, 16, 128),
               V(2, nz, b, width), V(2, nz, hb, width), V(nz, hb, width), V(nz, b, width), V(nz, hb, width), V(2, hb, width), V(hb, width), V(b, width), V(np_, *pw), V(2, 4, b, width),
               V(rows, feats), t3, V(*xt.shape), t3, t3, t3, V(*w.shape), V(*o4.shape), f3(*g1.shape), V(3, feats, 384), V(feats, 384), V(feats, rows), t3, V(3, rows, 384),
               f3(rows, 128), f3(rows, 128), f3(128, rows), V(128, rows), f3(2, 1, rows), V(4, own, 256), V(own, feats), V(own, feats), f3(rows, b),
               sm, sm, sm, sm, sm, sm, f3(np_, 16, feats), f3(nz, 16, feats), f3(length + 128, 128), f3(1, length + 128),
               pltpu.SemaphoreType.DMA((128 + 5 * nd,)), pltpu.SemaphoreType.DMA((128 + 5 * nd,)), pltpu.SemaphoreType.DMA((40,))]
    return pl.pallas_call(backward_kernel, out_shape=outs, in_specs=[an] * 11 + [vm] * 4, out_specs=(vm,) * len(outs), scratch_shapes=scratch,
        compiler_params=pltpu.CompilerParams(collective_id=2, has_side_effects=True, vmem_limit_bytes=67043328))(hu, hd, ga, mixed, xt, qt, kt, vt, w, o4, g1, lse, vgrad, bupgrad, ids)

def per_device(tokens, memory, block_ids, valid, teacher, w_qkv, bias_qv, w_out, bias_out, ln1_gain, ln1_bias, w_up, bias_up, w_down, bias_down, ln2_gain, ln2_bias):
    _, b, length = tokens.shape
    nd, nz = lax.axis_size("dp"), lax.axis_size("row")
    d, z, c = (lax.axis_index(a) for a in ("dp", "row", "col"))
    y, k = c // 2, c % 2
    feats = 4 * b
    half = memory.shape[1] // 2
    main = length // 2
    rows = length + 32
    one = lambda a: a.reshape(1, -1)
    xt, qt, kt, vt, mixed, wown, ga, hu, hd, lse, g_one, vgrad, bupgrad, out4 = forward(valid, tokens, memory, teacher, w_qkv.reshape(3, b, 192), w_out, w_up, w_down, [one(a) for a in (bias_out, ln1_gain, ln1_bias, bias_down, ln2_gain, ln2_bias)], one(bias_up), bias_qv, block_ids, nz)
    grad4, lout, gmem, g3, gwo, fu, fd, fvec, bup, bqv = backward(hu, hd, ga, mixed, xt, qt, kt, vt, wown, out4, g_one, lse, vgrad, bupgrad, block_ids, half, nz, nd)
    grad_tokens = grad4[:, :, :main, :b].reshape(2, length, b).astype(F32)
    return (lout, grad_tokens, gmem, g3.reshape(3, b * b), bqv, gwo, fvec[5], fvec[3], fvec[4], fu, bup[0], fd, fvec[2], fvec[0], fvec[1])

def solution(mesh):
    rows, feat = ("dp", "row"), "col"
    in_specs = (P(rows, feat, None), P(rows, None, feat), P(rows, None), P(), P(rows, feat, None), P("row", feat), P("row", None), P("row", feat), P(feat), P(feat), P(feat), P(feat, "row"), P("row"), P(feat, "row"), P(feat), P(feat), P(feat))
    out_specs = (P(rows, None, feat), P(rows, None, feat), P(rows, None, feat), P("row", feat), P("row", None), P("row", feat), P(feat), P(feat), P(feat), P(feat, "row"), P("row"), P(feat, "row"), P(feat), P(feat), P(feat))
    return jax.shard_map(per_device, mesh=mesh, in_specs=in_specs, out_specs=out_specs, check_vma=False)
```

```python
import jax
import jax.numpy as jnp
from jax import lax
from jax.experimental import pallas as pl
from jax.experimental.pallas import tpu as pltpu
from jax.sharding import PartitionSpec as P
BF=jnp.bfloat16; F32=jnp.float32
EPSILON=1e-12
CH=48

def nn(a,b): return lax.dot_general(a,b,(((1,),(0,)),((),())),preferred_element_type=F32)
def nt(a,b): return lax.dot_general(a,b,(((1,),(1,)),((),())),preferred_element_type=F32)

def gelu_pair(v):
    t = pl.reciprocal(1.0 + (0.3275911 * 0.7071067811865476) * jnp.abs(v))
    poly = t * (0.5*0.254829592 + t * (-0.5*0.284496736 + t * (0.5*1.421413741 + t * (-0.5*1.453152027 + t * (0.5*1.061405429)))))
    e = jnp.exp(-0.5 * v * v)
    half = poly * e
    cdf = jnp.where(v >= 0.0, 1.0 - half, half)
    return v * cdf, cdf + v * (e * 0.3989422804014327)

def group_sum(v):
    rows = v.shape[0]
    return jnp.sum(v.reshape(rows // 8, 8, v.shape[1]), axis=0)

def mlp_kernel(half_ref, valid_ref, mixed, x, teach, vec, bup, wa_hbm, wu_hbm, wd_hbm,
               out, g_one, g_attn, vgrad, bupgrad, gu_hbm, gd_hbm,
               tr, wraw, wt, wu, wd, h1, h2, rs1, low, lowt, brt, br, hid, dgl, gg, gu, gd, sem):
    rows, feats = x.shape
    zs = wu.shape[0]
    nb = feats // 256
    copies_a = [pltpu.make_async_copy(wa_hbm.at[z, :, pl.ds(512, 256)], wraw.at[z], sem.at[z]) for z in range(zs)]
    copies_u = [pltpu.make_async_copy(wu_hbm.at[z], wu.at[z], sem.at[zs + z]) for z in range(zs)]
    copies_d = [pltpu.make_async_copy(wd_hbm.at[z], wd.at[z], sem.at[2 * zs + z]) for z in range(zs)]
    for c in copies_a + copies_u + copies_d:
        c.start()
    for c in copies_a:
        c.wait()
    main = teach.shape[1]
    for i in range(main // 128):
        tr[pl.ds(128 * i, 128), :] = teach[:, pl.ds(128 * i, 128)].T
    tr[pl.ds(main, rows - main), :] = jnp.zeros((rows - main, feats), BF)
    low_lane = lax.broadcasted_iota(jnp.int32, (feats, 128), 1) < 64
    for k in range(zs // 2):
        z0, z1 = 2 * k, 2 * k + 1
        wt[:, pl.ds(384 * k, 128)] = wraw[z0, :, pl.ds(128, 128)]
        wt[:, pl.ds(384 * k + 128, 128)] = wraw[z1, :, pl.ds(128, 128)]
        t0 = pltpu.roll(wraw[z0, :, pl.ds(0, 128)].astype(F32), 64, 1)
        t1 = wraw[z1, :, pl.ds(0, 128)].astype(F32)
        wt[:, pl.ds(384 * k + 256, 128)] = jnp.where(low_lane, t0, t1).astype(BF)
    for n in range(nb):
        f = pl.ds(256 * n, 256)
        h1[:, f] = nt(mixed[...], wt[f, :]) + x[:, f].astype(F32) + vec[0:1, f]
    inv = 1.0 / feats

    vgrad[...] = jnp.zeros_like(vgrad)
    bupgrad[...] = jnp.zeros_like(bupgrad)

    def norm1(i, _):
        r = pl.ds(pl.multiple_of(i * CH, 16), CH)
        h = h1[r, :]
        m = jnp.sum(h, axis=1, keepdims=True) * inv
        s = jnp.sum(h * h, axis=1, keepdims=True) * inv
        rstd = lax.rsqrt(s - m * m + EPSILON)
        xhat = (h - m) * rstd
        h1[r, :] = xhat
        rs1[r, :] = jnp.broadcast_to(rstd, (CH, 128))
        low[r, :] = (xhat * vec[1:2, :] + vec[2:3, :]).astype(BF)
        return 0
    lax.fori_loop(0, rows // CH, norm1, 0)
    lowt[...] = low[...].T
    for c in copies_u:
        c.wait()

    def gate(i, _):
        z = i // nb
        f = pl.ds(pl.multiple_of((i % nb) * 256, 256), 256)
        v = nn(low[...], wu[z, :, f]) + bup[z, :, f]
        a, b = gelu_pair(v)
        hid[z, :, f] = a.astype(BF)
        dgl[z, :, f] = b
        return 0
    lax.fori_loop(0, zs * nb, gate, 0)
    for c in copies_d:
        c.wait()

    def down(n, _):
        f = pl.ds(pl.multiple_of(n * 256, 256), 256)
        acc = nt(hid[0], wd[0, f, :])
        for z in range(1, zs):
            acc = acc + nt(hid[z], wd[z, f, :])
        h2[:, f] = acc
        return 0
    lax.fori_loop(0, nb, down, 0)
    scale = vec[6:7, 0:1]
    first = half_ref[0] * main

    def norm2(i, _):
        r = pl.ds(pl.multiple_of(i * CH, 16), CH)
        h = h2[r, :] + (h1[r, :] * vec[1:2, :] + vec[2:3, :]) + vec[3:4, :]
        m = jnp.sum(h, axis=1, keepdims=True) * inv
        s = jnp.sum(h * h, axis=1, keepdims=True) * inv
        rstd = lax.rsqrt(s - m * m + EPSILON)
        xhat = (h - m) * rstd
        o = xhat * vec[4:5, :] + vec[5:6, :]
        out[r, :] = o.astype(BF)
        place = lax.broadcasted_iota(jnp.int32, (CH, 1), 0) + i * CH
        place = jnp.where(place < main, place + first, valid_ref[0])
        go = jnp.where(place < valid_ref[0], scale * (o - tr[r, :].astype(F32)), 0.0)
        a = go * vec[4:5, :]
        m1 = jnp.sum(a, axis=1, keepdims=True) * inv
        m2 = jnp.sum(a * xhat, axis=1, keepdims=True) * inv
        g2 = rstd * (a - m1 - xhat * m2)
        h2[r, :] = g2
        b = g2.astype(BF)
        br[r, :] = b
        vgrad[0] += group_sum(go * xhat)
        vgrad[1] += group_sum(go)
        vgrad[2] += group_sum(b.astype(F32))
        return 0
    lax.fori_loop(0, rows // CH, norm2, 0)
    brt[...] = br[...].T

    def back(i, _):
        z = i // nb
        f = pl.ds(pl.multiple_of((i % nb) * 256, 256), 256)
        gh = nn(br[...], wd[z, :, f])
        g = (gh * dgl[z, :, f]).astype(BF)
        gg[z, :, f] = g
        bupgrad[z, :, f] += group_sum(g.astype(F32))
        gd[z, :, f] = nn(brt[...], hid[z, :, f]).astype(BF)
        gu[z, :, f] = nn(lowt[...], g).astype(BF)
        return 0
    lax.fori_loop(0, zs * nb, back, 0)
    outs = [pltpu.make_async_copy(gd, gd_hbm, sem.at[0]), pltpu.make_async_copy(gu, gu_hbm, sem.at[1])]
    for c in outs:
        c.start()

    def first_grad(n, _):
        f = pl.ds(pl.multiple_of(n * 256, 256), 256)
        acc = h2[:, f]
        for z in range(zs):
            acc = acc + nt(gg[z], wu[z, f, :])
        h2[:, f] = acc
        return 0
    lax.fori_loop(0, nb, first_grad, 0)

    def norm1_back(i, _):
        r = pl.ds(pl.multiple_of(i * CH, 16), CH)
        g = h2[r, :]
        xhat = h1[r, :]
        a = g * vec[1:2, :]
        m1 = jnp.sum(a, axis=1, keepdims=True) * inv
        m2 = jnp.sum(a * xhat, axis=1, keepdims=True) * inv
        g1 = rs1[r, 0:1] * (a - m1 - xhat * m2)
        g_one[r, :] = g1
        b = g1.astype(BF)
        g_attn[r, :] = b
        vgrad[3] += group_sum(g * xhat)
        vgrad[4] += group_sum(g)
        vgrad[5] += group_sum(b.astype(F32))
        return 0
    lax.fori_loop(0, rows // CH, norm1_back, 0)
    for c in outs:
        c.wait()

def mlp(half, valid, mixed, x, teach, vec, bup, wa, wu, wd):
    rows, feats = x.shape; zs = wu.shape[0]
    V = lambda *s, d=BF: pltpu.VMEM(s, d)
    vm = pl.BlockSpec(memory_space=pltpu.VMEM); sm = pl.BlockSpec(memory_space=pltpu.SMEM); an = pl.BlockSpec(memory_space=pl.ANY)
    S = jax.ShapeDtypeStruct
    return pl.pallas_call(mlp_kernel,
        out_shape=(S((rows,feats),BF),S((rows,feats),F32),S((rows,feats),BF),S((6,8,feats),F32),S((zs,8,feats),F32),S(wu.shape,BF),S(wd.shape,BF)),
        in_specs=[sm,sm,vm,vm,vm,vm,vm,an,an,an],
        out_specs=(vm,vm,vm,vm,vm,an,an),
        scratch_shapes=[V(rows,feats),V(zs,feats,256),V(feats,feats),V(*wu.shape),V(*wd.shape),V(rows,feats,d=F32),V(rows,feats,d=F32),V(rows,128,d=F32),V(rows,feats),
            V(feats,rows),V(feats,rows),V(rows,feats),V(zs,rows,feats),V(zs,rows,feats,d=F32),V(zs,rows,feats),V(*wu.shape),V(*wd.shape),pltpu.SemaphoreType.DMA((3*zs,))],
        compiler_params=pltpu.CompilerParams(vmem_limit_bytes=63*2**20),
    )(half,valid,mixed,x,teach,vec,bup,wa,wu,wd)
NEG=-1e30
def tn_lanes(): return lax.broadcasted_iota(jnp.int32,(1,128),1)

def assemble_pairs(w, wp, feats):
    lo = lax.broadcasted_iota(jnp.int32, (feats, 128), 1) < 64
    wp[0] = w[0, :, pl.ds(0, 384)]
    wp[1] = w[1, :, pl.ds(0, 384)]
    a0, a1 = w[0, :, pl.ds(384, 128)].astype(F32), w[1, :, pl.ds(384, 128)].astype(F32)
    wp[2, :, pl.ds(0, 128)] = jnp.where(lo, a0, pltpu.roll(a1, 64, 1)).astype(BF)
    wp[2, :, pl.ds(128, 128)] = jnp.where(lo, pltpu.roll(a0, 64, 1), a1).astype(BF)
    b0, b1 = w[0, :, pl.ds(512, 128)].astype(F32), w[1, :, pl.ds(512, 128)].astype(F32)
    wp[2, :, pl.ds(256, 128)] = jnp.where(lo, b0, pltpu.roll(b1, 64, 1)).astype(BF)

def tiles(rows, length):
    mem = (length, rows - length, True)
    out = []
    for a in range(0, length, 256):
        spans = []
        if a:
            spans.append((0, a, False))
        spans.append((a, min(512, length - a), True))
        out.append((a, 256, spans + [mem]))
    out.append((length, rows - length, [(0, length, True), mem]))
    return out

def scores_of(kt, qm, idk, idq, p, spans):
    out = []
    for k0, kn, masked in spans:
        s = nt(kt[p, pl.ds(k0, kn), :], qm)
        if masked:
            s = jnp.where(idk[pl.ds(k0, kn), 0:1] <= idq, s, NEG)
        out.append(s)
    return out

def attn_fwd_kernel(xt, wa_hbm, bias, idk, idq, x, qt, kt, vt, mixed, lse, w, wp, vtt, ot, sem):
    feats = xt.shape[0]; rows = x.shape[0]; length = xt.shape[1] - 128
    c = pltpu.make_async_copy(wa_hbm, w, sem); c.start()
    for i in range(length // 128):
        x[pl.ds(128 * i, 128), :] = xt[:, pl.ds(128 * i, 128)].T
    x[pl.ds(length, rows - length), :] = xt[:, pl.ds(length, 128)].T[: rows - length, :]
    c.wait()
    assemble_pairs(w, wp, feats)
    rc = rows // 3

    def project(i, _):
        p = i // 3
        r = pl.ds(pl.multiple_of((i % 3) * rc, 16), rc)
        v = nn(x[r, :], wp[p]) + bias[p]
        qt[p, r, :] = (v[:, :128].astype(BF).astype(F32) * 0.125).astype(BF)
        kt[p, r, :] = v[:, 128:256].astype(BF)
        vt[p, r, :] = v[:, 256:].astype(BF)
        return 0
    lax.fori_loop(0, 9, project, 0)

    def pair(p, _):
        vtt[...] = vt[p].T
        for e in range(2):
            lanes = (tn_lanes() < 64) if e == 0 else (tn_lanes() >= 64)
            for q0, qn, spans in tiles(rows, length):
                q = qt[p, pl.ds(q0, qn), :]
                qm = jnp.where(lanes, q, jnp.zeros_like(q))
                ss = scores_of(kt, qm, idk, idq[0:1, pl.ds(q0, qn)], p, spans)
                m = jnp.max(ss[0], axis=0, keepdims=True)
                for s in ss[1:]:
                    m = jnp.maximum(m, jnp.max(s, axis=0, keepdims=True))
                tot, acc = None, None
                for s, (k0, kn, _) in zip(ss, spans):
                    ex = jnp.exp(s - m)
                    t = jnp.sum(ex, axis=0, keepdims=True)
                    o = nn(vtt[pl.ds(64 * e, 64), pl.ds(k0, kn)], ex.astype(BF))
                    tot = t if tot is None else tot + t
                    acc = o if acc is None else acc + o
                ot[pl.ds(64 * e, 64), pl.ds(q0, qn)] = acc / tot
                lse[p, e, :, pl.ds(q0, qn)] = m + jnp.log(tot)
        mixed[p] = ot[...].T.astype(BF)
        return 0
    lax.fori_loop(0, 3, pair, 0)

def attn_fwd(xt, wa, bias, idk, idq, rows):
    feats = xt.shape[0]
    V = lambda *s, d=BF: pltpu.VMEM(s, d)
    vm = pl.BlockSpec(memory_space=pltpu.VMEM); an = pl.BlockSpec(memory_space=pl.ANY)
    S = jax.ShapeDtypeStruct
    t3 = S((3, rows, 128), BF)
    return pl.pallas_call(attn_fwd_kernel,
        out_shape=(S((rows, feats), BF), t3, t3, t3, t3, S((3, 2, 1, rows), F32)),
        in_specs=[vm, an, vm, vm, vm], out_specs=(vm,) * 6,
        scratch_shapes=[V(*wa.shape), V(3, feats, 384), V(128, rows), V(128, rows, d=F32), pltpu.SemaphoreType.DMA],
        compiler_params=pltpu.CompilerParams(vmem_limit_bytes=63*2**20))(xt, wa, bias, idk, idq)

def attn_bwd_kernel(ga, mixed, xt, qt, kt, vt, lse, idk, idq, wa_hbm, gpart, bgrad, gown_hbm, w, wp, wt, gat, gm, gp, dv, dk, dqt, ktt, dd, ro, gown, sem):
    feats = xt.shape[0]; rows = ga.shape[0]; length = xt.shape[1] - 128
    c = pltpu.make_async_copy(wa_hbm, w, sem); c.start()
    gat[...] = ga[...].T
    c.wait()
    assemble_pairs(w, wp, feats)
    wt[:, pl.ds(0, 128)] = w[0, :, pl.ds(640, 128)]
    wt[:, pl.ds(128, 128)] = w[1, :, pl.ds(640, 128)]
    lo = lax.broadcasted_iota(jnp.int32, (feats, 128), 1) < 64
    wt[:, pl.ds(256, 128)] = jnp.where(lo, pltpu.roll(w[0, :, pl.ds(512, 128)].astype(F32), 64, 1), w[1, :, pl.ds(512, 128)].astype(F32)).astype(BF)
    for p in range(3):
        gm[p] = nn(ga[...], wt[:, pl.ds(128 * p, 128)]).astype(BF)

    def pair(p, _):
        ktt[...] = kt[p].T
        prod = (gm[p].astype(F32) * mixed[p].astype(F32)).T
        dd[0:1, :] = jnp.sum(prod[:64, :], axis=0, keepdims=True)
        dd[1:2, :] = jnp.sum(prod[64:, :], axis=0, keepdims=True)
        dv[...] = jnp.zeros_like(dv)
        dk[...] = jnp.zeros_like(dk)
        for e in range(2):
            lanes = (tn_lanes() < 64) if e == 0 else (tn_lanes() >= 64)
            for q0, qn, spans in tiles(rows, length):
                q = qt[p, pl.ds(q0, qn), :]
                qm = jnp.where(lanes, q, jnp.zeros_like(q))
                g = gm[p, pl.ds(q0, qn), :]
                gmm = jnp.where(lanes, g, jnp.zeros_like(g))
                ss = scores_of(kt, qm, idk, idq[0:1, pl.ds(q0, qn)], p, spans)
                l = lse[p, e, :, pl.ds(q0, qn)]
                d = dd[pl.ds(e, 1), pl.ds(q0, qn)]
                acc = None
                for s, (k0, kn, _) in zip(ss, spans):
                    pr = jnp.exp(s - l)
                    dp = nt(vt[p, pl.ds(k0, kn), :], gmm)
                    ds = (pr * (dp - d)).astype(BF)
                    dv[pl.ds(k0, kn), :] += nn(pr.astype(BF), gmm)
                    dk[pl.ds(k0, kn), :] += nn(ds, qm)
                    o = nn(ktt[pl.ds(64 * e, 64), pl.ds(k0, kn)], ds)
                    acc = o if acc is None else acc + o
                dqt[pl.ds(64 * e, 64), pl.ds(q0, qn)] = acc * 0.125
        gp[p, :, pl.ds(0, 128)] = dqt[...].T.astype(BF)
        gp[p, :, pl.ds(128, 128)] = dk[...].astype(BF)
        gp[p, :, pl.ds(256, 128)] = dv[...].astype(BF)
        return 0
    lax.fori_loop(0, 3, pair, 0)
    for p in range(3):
        bgrad[p] = group_sum(gp[p].astype(F32))
    r3 = rows // 3

    def rowsgrad(i, _):
        r = pl.ds(pl.multiple_of(i * r3, 16), r3)
        gpart[r, :] = nt(gp[0, r, :], wp[0]) + nt(gp[1, r, :], wp[1]) + nt(gp[2, r, :], wp[2])
        return 0
    lax.fori_loop(0, 3, rowsgrad, 0)
    fc = 256
    for f0 in range(0, feats, fc):
        f = pl.ds(f0, fc)
        xf = xt[f, pl.ds(0, rows)]
        af = gat[f, :]
        r0 = nn(xf, gp[0]); r1 = nn(xf, gp[1]); r2 = nn(xf, gp[2])
        o = [nn(af, mixed[p]) for p in range(3)]
        lo = lax.broadcasted_iota(jnp.int32, (fc, 128), 1) < 64
        rq, rk, rv = r2[:, :128], r2[:, 128:256], r2[:, 256:]
        sw = lambda a: pltpu.roll(a, 64, 1)
        gown[0, f, pl.ds(0, 384)] = r0.astype(BF)
        gown[1, f, pl.ds(0, 384)] = r1.astype(BF)
        gown[0, f, pl.ds(384, 128)] = jnp.where(lo, rq, sw(rk)).astype(BF)
        gown[1, f, pl.ds(384, 128)] = jnp.where(lo, sw(rq), rk).astype(BF)
        gown[0, f, pl.ds(512, 128)] = jnp.where(lo, rv, sw(o[2])).astype(BF)
        gown[1, f, pl.ds(512, 128)] = jnp.where(lo, sw(rv), o[2]).astype(BF)
        gown[0, f, pl.ds(640, 128)] = o[0].astype(BF)
        gown[1, f, pl.ds(640, 128)] = o[1].astype(BF)
    c = pltpu.make_async_copy(gown, gown_hbm, sem); c.start(); c.wait()

def attn_bwd(ga, mixed, xt, qt, kt, vt, lse, idk, idq, wa):
    feats = xt.shape[0]; rows = ga.shape[0]
    V = lambda *s, d=BF: pltpu.VMEM(s, d)
    vm = pl.BlockSpec(memory_space=pltpu.VMEM); an = pl.BlockSpec(memory_space=pl.ANY)
    S = jax.ShapeDtypeStruct
    return pl.pallas_call(attn_bwd_kernel,
        out_shape=(S((rows, feats), F32), S((3, 8, 384), F32), S(wa.shape, BF)),
        in_specs=[vm] * 9 + [an], out_specs=(vm, vm, an),
        scratch_shapes=[V(*wa.shape), V(3, feats, 384), V(feats, 384), V(feats, rows), V(3, rows, 128), V(3, rows, 384), V(rows, 128, d=F32), V(rows, 128, d=F32),
            V(128, rows, d=F32), V(128, rows), V(8, rows, d=F32), V(8, 128), V(*wa.shape), pltpu.SemaphoreType.DMA],
        compiler_params=pltpu.CompilerParams(vmem_limit_bytes=63*2**20))(ga, mixed, xt, qt, kt, vt, lse, idk, idq, wa)
MESH = pl.DeviceIdType.MESH

class Move:
    def __init__(self, net, src, dst, dev, index):
        self.net, self.src, self.dst, self.dev, self.index = net, src, dst, dev, index
    def make(self):
        return pltpu.make_async_remote_copy(src_ref=self.src(), dst_ref=self.dst(), send_sem=self.net.ss.at[self.index],
                                            recv_sem=self.net.rs.at[self.index], device_id=self.dev, device_id_type=MESH)
    def start(self):
        self.make().start()
    def wait_recv(self):
        self.make().wait_recv()
    def wait_send(self):
        self.make().wait_send()

class Copy:
    def __init__(self, net, src, dst, index):
        self.net, self.src, self.dst, self.index = net, src, dst, index
    def make(self):
        return pltpu.make_async_copy(self.src(), self.dst(), self.net.ls.at[self.index])
    def start(self):
        self.make().start()
    def wait(self):
        self.make().wait()

class Net:
    def __init__(self, send_sems, recv_sems, local_sems):
        self.ss, self.rs, self.ls = send_sems, recv_sems, local_sems
        self.count, self.locals, self.moves, self.copies = 0, 0, [], []
        self.d, self.z, self.c = (lax.axis_index(a) for a in ("dp", "row", "col"))
        self.nd, self.nz = lax.axis_size("dp"), lax.axis_size("row")
        self.y, self.k = self.c // 2, self.c % 2
        self.x = self.d % 2
        self.oc = lax.rem(self.c + 2, 4)
        self.xp = (self.d + 1 - 2 * self.x, self.z, self.c)
        self.yp = (self.d, self.z, self.oc)
        self.kp = (self.d, self.z, self.c + 1 - 2 * self.k)
        self.ykp = (self.d, self.z, 3 - self.c)
        self.zs = [lax.rem(self.z + i, self.nz) for i in range(self.nz)]
        self.zp = [(self.d, zz, self.c) for zz in self.zs]
        self.others = [(lax.rem(self.d + 2 * i, self.nd), self.z, self.c) for i in range(1, self.nd // 2)]
    def from_row(self, i):
        return self.zs[(self.nz - i) % self.nz]
    def hello(self, peers):
        b = pltpu.get_barrier_semaphore()
        for p in peers:
            pl.semaphore_signal(b, inc=1, device_id=p, device_id_type=MESH)
    def await_hello(self, peers):
        pl.semaphore_wait(pltpu.get_barrier_semaphore(), len(peers))
    def barrier(self, peers):
        self.hello(peers)
        self.await_hello(peers)
    def move(self, src, dst, dev):
        m = Move(self, src, dst, dev, self.count)
        self.count += 1
        self.moves.append(m)
        return m
    def send(self, src, dst, dev):
        m = self.move(src, dst, dev)
        m.start()
        return m
    def copy(self, src, dst):
        m = Copy(self, src, dst, self.locals)
        self.locals += 1
        self.copies.append(m)
        return m
    def local(self, src, dst):
        m = self.copy(src, dst)
        m.start()
        return m
    def finish(self):
        for m in self.moves:
            m.wait_send()

def at(i, table):
    for j, events in table.items():
        if events:
            @pl.when(i == j)
            def _(events=events):
                for e in events:
                    e()

def spread_events(events, steps):
    table = {}
    for n, e in enumerate(events):
        table.setdefault(n * steps // len(events), []).append(e)
    return table

def join192(t, dst):
    lo = lax.broadcasted_iota(jnp.int32, t[0][0].shape, 1) < 64
    sw = lambda a: pltpu.roll(a, 64, 1)
    for h in range(2):
        a, b = t[2 * h], t[2 * h + 1]
        dst[:, pl.ds(384 * h, 128)] = a[0]
        dst[:, pl.ds(384 * h + 128, 128)] = jnp.where(lo, a[1], sw(b[0]))
        dst[:, pl.ds(384 * h + 256, 128)] = jnp.where(lo, sw(b[0]), sw(b[1]))

def row_ids(ids, y, half, idk, idq):
    length = ids.shape[1]
    idq[:, pl.ds(0, length)] = ids[pl.ds(y, 1), :].astype(F32)
    i = lax.broadcasted_iota(jnp.int32, (1, 128), 1)
    idq[:, pl.ds(length, 128)] = jnp.where(i < half, -1.0, jnp.where(i < 2 * half, 1.0 * length, 2.0 * length))
    for j in range(length // 128 + 1):
        idk[pl.ds(128 * j, 128), :] = jnp.broadcast_to(idq[:, pl.ds(128 * j, 128)], (128, 128)).T

def pack_inputs(w3, wo, la, vecs, bias_up, bias_qv, scale, ls, memory, mtmp, mem):
    b = w3.shape[1]
    f = lambda r: r.astype(F32)
    lo = lax.broadcasted_iota(jnp.int32, (b, 128), 1) < 64
    t0, t1 = f(w3[0, :, pl.ds(0, 128)]), f(w3[1, :, pl.ds(0, 128)])
    la[:, pl.ds(0, 128)] = jnp.where(lo, t0, pltpu.roll(t1, 64, 1)).astype(BF)
    la[:, pl.ds(128, 128)] = jnp.where(lo, pltpu.roll(t0, 64, 1), t1).astype(BF)
    v = [f(w3[j, :, pl.ds(128, 64)]) for j in range(3)]
    la[:, pl.ds(256, 128)] = jnp.concatenate([v[0], v[1]], axis=1).astype(BF)
    la[:, pl.ds(384, 128)] = w3[2, :, pl.ds(0, 128)]
    wot = f(wo[...]).T
    la[:, pl.ds(512, 128)] = jnp.concatenate([v[2], wot[:, 128:]], axis=1).astype(BF)
    la[:, pl.ds(640, 128)] = wot[:, :128].astype(BF)
    ls[...] = jnp.zeros_like(ls)
    for j, r in enumerate(vecs):
        ls[pl.ds(j, 1), pl.ds(0, b)] = r[...]
    ls[pl.ds(6, 1), :] = scale
    for j in range(3):
        ls[pl.ds(8 + j, 1), :] = bias_up[:, pl.ds(256 * j, 256)]
    ls[pl.ds(11, 1), pl.ds(0, 128)] = bias_qv[0:1, :]
    ls[pl.ds(11, 1), pl.ds(128, 128)] = bias_qv[1:2, :]
    ls[pl.ds(12, 1), pl.ds(0, 128)] = bias_qv[2:3, :]
    mtmp[...] = jnp.zeros_like(mtmp)
    for s in range(2):
        mtmp[pl.ds(0, memory.shape[1]), :] = f(memory[s])
        mem[s] = mtmp[...].T.astype(BF)

def forward_kernel(valid_ref, tok, memory, tch, w3, wo, lu, ld, v0, v1, v2, v3, v4, v5, bias_up, bias_qv, ids,
                   xt_o, q_o, k_o, v_o, mixed_o, wa_o, ga_o, hu_o, hd_o, lse, g_one, vgrad, bupgrad, out4,
                   xt, x, wa, wu, wd, sm, tt, tr, wp, qt, kt, vt, vtt, ot, mixed, mrows, bias, vec, wt,
                   h1, h2, rs1, low, lowt, br, brt, hid, dgl, gdz, guz, hu, hd, ru, rd, ga, o4, la, ls, mem, mtmp, idk, idq, ss, rs, lsem, zsem, zrem):
    n = Net(ss, rs, lsem)
    peers = n.zp[1:] + [n.yp, n.ykp, n.kp, n.xp]
    n.hello(peers)
    total = lax.fori_loop(0, valid_ref.shape[0], lambda i, t: t + valid_ref[i], jnp.int32(0))
    count = valid_ref[(n.d * n.nz + n.z) * 2 + n.y]
    scale_row = (valid_ref.shape[0] * tok.shape[2]) / jnp.full((1, 256), total, jnp.int32).astype(F32)
    pack_inputs(w3, wo, la, (v0, v1, v2, v3, v4, v5), bias_up, bias_qv, scale_row, ls, memory, mtmp, mem)
    n.await_hello(peers)
    nz, y, k, c, z, oc = n.nz, n.y, n.k, n.c, n.z, n.oc
    b = la.shape[0]; hb = b // 2
    feats = x.shape[1]; rows = x.shape[0]; length = tok.shape[2]; main = length // 2
    own_rows = main + 16
    row = lambda cc, off=0, num=b: pl.ds(pl.multiple_of(cc * b + off, 16), num)
    blk = lambda w, zz, cc: (lambda: w.at[zz, row(cc)])
    hlf = lambda w, zz, cc, h: (lambda: w.at[zz, row(cc, h * hb, hb)])
    mine, theirs = n.x, 1 - n.x
    part = lambda w: (lambda: w.at[pl.ds(pl.multiple_of(n.x * hb, 16), hb)])
    all_of = lambda r: (lambda: r)
    tail = pl.ds(length, 128); body = pl.ds(0, length)
    fz = n.from_row
    R = range(1, nz)
    e1 = z + 1 - 2 * lax.rem(z, 2)
    e2 = lax.rem(z + 2, nz)
    e3 = lax.rem(e1 + 2, nz)
    dev1, dev2 = (n.d, e1, c), (n.d, e2, c)
    order = [z, e2, e1, e3]
    s_blk = lambda zz, cc: (lambda: sm.at[zz, cc])
    fwd = lambda u, dev: n.move(u, u, dev)
    local = [n.local(lambda: tok.at[y], lambda: xt.at[row(c), body]), n.local(lambda: mem.at[y], lambda: xt.at[row(c), tail])]
    au = lambda zz, cc: hlf(wa, zz, cc, mine)
    a2 = n.send(part(la), au(z, c), dev2)
    a1 = n.send(part(la), au(z, c), dev1)
    a_y = [n.send(part(la), au(z, c), n.yp)]
    a_k = [n.send(all_of(la), blk(wa, z, c), n.kp)]
    s_z = [n.send(all_of(ls), s_blk(z, c), n.zp[i]) for i in R]
    s_y = [n.send(all_of(ls), s_blk(z, c), n.yp)]
    s_k = [n.send(all_of(ls), s_blk(z, c), n.kp)]
    t_k = [n.send(lambda: tok.at[y], lambda: xt.at[row(c), body], n.kp), n.send(lambda: mem.at[y], lambda: xt.at[row(c), tail], n.kp)]
    for w, l in ((wa, la), (wu, lu), (wd, ld)):
        local.append(n.local(all_of(l), blk(w, z, c)))
    local.append(n.local(all_of(ls), s_blk(z, c)))
    a_x, a_xu = [], []
    def pass_on(u, lists):
        for lst, dev in lists:
            lst.append(fwd(u, dev)); lst[-1].start()
    def a_own(zz):
        a_xu.append((zz, c))
        pass_on(au(zz, c), ((a_x, n.xp), (a_y, n.yp), (a_k, n.kp)))
    def a_far(i):
        a_y[i].wait_recv()
        a_xu.append((order[i], oc))
        pass_on(au(order[i], oc), ((a_x, n.xp), (a_k, n.kp)))
    def a_home(i):
        a_x[i].wait_recv()
        pass_on(hlf(wa, *a_xu[i], theirs), ((a_k, n.kp),))
    first, second = pl.ds(0, main), pl.ds(main, main)
    t_y = [n.send(lambda: tok.at[1 - y, :, first], lambda: xt.at[row(c), first], n.yp), n.send(lambda: mem.at[1 - y], lambda: xt.at[row(c), tail], n.yp)]
    def t_pass(i, w_):
        t_y[i].wait_recv()
        t_k.append(fwd(lambda: xt.at[row(oc), w_], n.kp)); t_k[-1].start()
    a_far(0)
    a2.wait_recv()
    a3 = fwd(au(e2, c), dev1); a3.start()
    a_own(e2)
    a1.wait_recv()
    a_own(e1)
    a_far(1)
    for i in R:
        s_z[i - 1].wait_recv()
        pass_on(s_blk(fz(i), c), ((s_y, n.yp), (s_k, n.kp)))
    a3.wait_recv()
    a_own(e3)
    t_y.append(n.send(lambda: tok.at[1 - y, :, second], lambda: xt.at[row(c), second], n.yp))
    t_pass(0, first)
    t_pass(1, tail)
    uu = lambda zz, cc: blk(wu, zz, cc)
    du = lambda zz, cc: hlf(wd, zz, cc, mine)
    u2 = n.send(all_of(lu), uu(z, c), dev2)
    u1 = n.send(all_of(lu), uu(z, c), dev1)
    d_y = n.send(part(ld), du(z, c), n.yp)
    u_y = [n.send(all_of(lu), uu(z, c), n.yp)]
    u_k = {0: n.send(all_of(lu), uu(z, c), n.kp)}
    d_k = [n.send(all_of(ld), blk(wd, z, c), n.kp)]
    tsl = lambda s, kk: (lambda: tch.at[s, :, pl.ds(pl.multiple_of(kk * main, 128), main)])
    th = lambda: tt.at[row(c)]
    h_y = [n.send(tsl(y, 1 - k), th, n.kp)]
    local.append(n.local(tsl(y, k), th))
    a_far(2)
    a_far(3)
    row_ids(ids, y, memory.shape[1] // 2, idk, idq)
    for i in range(3):
        a_home(i)
    for i in range(nz):
        s_y[i].wait_recv()
        pass_on(s_blk(fz(i), oc), ((s_k, n.kp),))
    local[0].wait(); local[1].wait()
    a_home(3)
    t_pass(2, second)
    a_home(4)
    for m in t_k:
        m.wait_recv()
    def turn(i, _):
        f = pl.ds(pl.multiple_of(128 * i, 128), 128)
        x[f, :] = xt[:, f].T
        return 0
    lax.fori_loop(0, length // 128, turn, 0)
    x[pl.ds(length, rows - length), :] = xt[:, tail].T[: rows - length, :]
    o_x = n.local(all_of(xt), all_of(xt_o))
    u2.wait_recv()
    u3 = fwd(uu(e2, c), dev1); u3.start()
    d2 = n.send(part(ld), du(z, c), dev2)
    d1 = n.send(part(ld), du(z, c), dev1)
    def u_put(i, cc, y_too=True):
        m = fwd(uu(order[i], cc), n.kp)
        u_k[(i, cc is oc)] = m
        if y_too:
            u_y.append(fwd(uu(order[i], cc), n.yp))
            u_y[-1].start()
        m.start()
    u_put(1, c)
    d_x, d_xu = [], []
    def d_put(zz, cc):
        d_xu.append((zz, cc))
        d_x.append(fwd(du(zz, cc), n.xp)); d_k.append(fwd(du(zz, cc), n.kp))
        return [d_x[-1], d_k[-1]]
    d_own = d_put(z, oc)
    for i in range(5, 7):
        a_home(i)
    def step(wait, moves):
        def run():
            wait.wait_recv()
            for m in moves:
                m.start()
        return run
    def u_step(wait, i):
        u_y.append(fwd(uu(order[i], c), n.yp))
        u_w.append(fwd(uu(order[i], c), n.kp))
        return step(wait, [u_y[-1], u_w[-1]])
    u_w = list(u_k.values())
    def u_far(i):
        u_w.append(fwd(uu(order[i], oc), n.kp))
        return step(u_y[i], [u_w[-1]])
    E_dy = step(d_y, d_own)
    d3, d2o, d1o, d3o = fwd(du(e2, c), dev1), fwd(du(z, oc), dev2), fwd(du(z, oc), dev1), fwd(du(e2, oc), dev1)
    E_u1 = u_step(u1, 2)
    E_u3 = u_step(u3, 3)
    h_m = [n.move(tsl(1 - y, k), th, n.yp), n.move(tsl(1 - y, 1 - k), th, n.ykp)]
    def E_h():
        for m in h_m:
            m.start()
    h_y += h_m
    E_uy = [u_far(i) for i in range(4)]
    E_d2 = step(d2, [d3] + d_put(e2, c))
    def E_do():
        d2o.start(); d1o.start()
    E_d1 = step(d1, d_put(e1, c))
    E_d3 = step(d3, d_put(e3, c))
    E_d2o = step(d2o, [d3o] + d_put(e2, oc))
    E_d1o = step(d1o, d_put(e1, oc))
    E_d3o = step(d3o, d_put(e3, oc))
    E_dx = []
    for m, (zz, cc) in zip(d_x, d_xu):
        d_k.append(fwd(hlf(wd, zz, cc, theirs), n.kp))
        E_dx.append(step(m, [d_k[-1]]))
    proj_events = {0: [E_dy], 1: [E_u1]}
    head_events = {2: [E_do, E_dx[0]], 4: [E_uy[0], E_u3, E_h], 6: [E_d2], 8: [E_d1], 10: [E_uy[1]], 14: [E_d3, E_d2o], 15: [E_uy[2], E_dx[1], E_dx[2]], 17: [E_d1o]}
    out_events = [E_d3o, E_dx[3]]
    gate_events = {0: [], 3: [], 6: [E_dx[4], E_dx[5]], 9: [E_dx[6]]}
    for m in s_k:
        m.wait_recv()
    for m in local[2:6]:
        m.wait()
    join192([[sm[0, cc, pl.ds(0, 8), pl.ds(0, 128)], sm[0, cc, pl.ds(0, 8), pl.ds(128, 128)]] for cc in range(4)], vec)
    lo1 = lax.broadcasted_iota(jnp.int32, (1, 128), 1) < 64
    sw = lambda a: pltpu.roll(a, 64, 1)
    bias[...] = jnp.zeros_like(bias)
    hv = [[sm[2 * k + j, 0, 11:12, pl.ds(0, 128)], sm[2 * k + j, 0, 11:12, pl.ds(128, 128)], sm[2 * k + j, 0, 12:13, pl.ds(0, 128)]] for j in range(2)]
    for p, (ea, eb) in enumerate(((hv[0][0], hv[0][1]), (hv[1][0], hv[1][1]), (hv[0][2], hv[1][2]))):
        w8 = lambda a: jnp.broadcast_to(a, (8, 128))
        lo8 = lax.broadcasted_iota(jnp.int32, (8, 128), 1) < 64
        bias[p, :, pl.ds(0, 128)] = jnp.where(lo8, w8(ea), sw(w8(eb)))
        bias[p, :, pl.ds(256, 128)] = jnp.where(lo8, sw(w8(ea)), w8(eb))
    for m in a_k:
        m.wait_recv()
    own = pl.ds(2 * k, 2)
    o_w = n.local(lambda: wa.at[own], all_of(wa_o))
    w = wa.at[own]
    assemble_pairs(w, wp, feats)
    rc = rows // 3

    def project(i, _):
        p = i // 3
        r = pl.ds(pl.multiple_of((i % 3) * rc, 16), rc)
        v = nn(x[r, :], wp[p]) + bias[p, 0:1, :]
        qt[p, r, :] = (v[:, :128].astype(BF).astype(F32) * 0.125).astype(BF)
        kt[p, r, :] = v[:, 128:256].astype(BF)
        vt[p, r, :] = v[:, 256:].astype(BF)
        at(i, proj_events)
        return 0
    lax.fori_loop(0, 9, project, 0)
    o_q = [n.local(all_of(a), all_of(o)) for a, o in ((qt, q_o), (kt, k_o), (vt, v_o))]
    m_k = [(n.move((lambda p=p: mixed.at[p, pl.ds(pl.multiple_of((1 - k) * main, 16), main)]), (lambda p=p: mrows.at[k * 3 + p, pl.ds(0, main)]), n.kp),
            n.move((lambda p=p: mixed.at[p, pl.ds(pl.multiple_of(length + (1 - k) * 16, 16), 16)]), (lambda p=p: mrows.at[k * 3 + p, pl.ds(main, 16)]), n.kp)) for p in range(3)]
    m_l = [(n.copy((lambda p=p: mixed.at[p, pl.ds(pl.multiple_of(k * main, 16), main)]), (lambda p=p: mrows.at[k * 3 + p, pl.ds(0, main)])),
            n.copy((lambda p=p: mixed.at[p, pl.ds(pl.multiple_of(length + k * 16, 16), 16)]), (lambda p=p: mrows.at[k * 3 + p, pl.ds(main, 16)]))) for p in range(3)]
    cuts = {1: 0, 3: 1, 4: 2}

    def head(i, _):
        p = i // 2
        e = i % 2
        he = pl.ds(pl.multiple_of(64 * e, 64), 64)

        @pl.when(e == 0)
        def _():
            vtt[...] = vt[p].T
        lanes = (lax.broadcasted_iota(jnp.int32, (1, 128), 1) // 64) == e
        for t_, (q0, qn, spans) in enumerate(tiles(rows, length)):
            q = qt[p, pl.ds(q0, qn), :]
            qm = jnp.where(lanes, q, jnp.zeros_like(q))
            sc = scores_of(kt, qm, idk, idq[0:1, pl.ds(q0, qn)], p, spans)
            m = jnp.max(sc[0], axis=0, keepdims=True)
            for s in sc[1:]:
                m = jnp.maximum(m, jnp.max(s, axis=0, keepdims=True))
            tot, acc = None, None
            for s, (k0, kn, _) in zip(sc, spans):
                ex = jnp.exp(s - m)
                t = jnp.sum(ex, axis=0, keepdims=True)
                o = nn(vtt[he, pl.ds(k0, kn)], ex.astype(BF))
                tot = t if tot is None else tot + t
                acc = o if acc is None else acc + o
            ot[he, pl.ds(q0, qn)] = acc / tot
            lse[i, :, pl.ds(q0, qn)] = m + jnp.log(tot)
            if t_ in cuts:
                at(3 * i + cuts[t_], head_events)

        @pl.when(e == 1)
        def _():
            mixed[p] = ot[...].T.astype(BF)
        at(i, {2 * p + 1: [m.start for m in m_k[p] + m_l[p]] for p in range(3)})
        return 0
    lax.fori_loop(0, 6, head, 0)
    o_m = n.local(all_of(mixed), all_of(mixed_o))
    lo = lax.broadcasted_iota(jnp.int32, (feats, 128), 1) < 64
    for kk in range(2):
        z0, z1 = 2 * kk, 2 * kk + 1
        wt[:, pl.ds(384 * kk, 128)] = wa[z0, :, pl.ds(640, 128)]
        wt[:, pl.ds(384 * kk + 128, 128)] = wa[z1, :, pl.ds(640, 128)]
        t0 = pltpu.roll(wa[z0, :, pl.ds(512, 128)].astype(F32), 64, 1)
        wt[:, pl.ds(384 * kk + 256, 128)] = jnp.where(lo, t0, wa[z1, :, pl.ds(512, 128)].astype(F32)).astype(BF)
    for pair_ in m_k:
        for m in pair_:
            m.wait_recv()
    for pair_ in m_l:
        for m in pair_:
            m.wait()
    nb = feats // 256
    CHS = own_rows // CH

    def own_slice(i, num):
        start = jnp.where(i < main, k * main + i, length + k * 16)
        return pl.ds(pl.multiple_of(start, 16), num)

    for f0 in range(0, feats, 256):
        f = pl.ds(f0, 256)
        acc = nt(mrows[0], wt[f, pl.ds(0, 128)])
        for j in range(1, 6):
            acc = acc + nt(mrows[j], wt[f, pl.ds(128 * j, 128)])
        h1[:, f] = acc + vec[0:1, f]
    for e in out_events:
        e()
    inv = 1.0 / feats
    vgrad[...] = jnp.zeros_like(vgrad)
    bupgrad[...] = jnp.zeros_like(bupgrad)

    def norm1(i, _):
        r = pl.ds(pl.multiple_of(i * 16, 16), 16)
        h = h1[r, :] + x[own_slice(i * 16, 16), :].astype(F32)
        m = jnp.sum(h, axis=1, keepdims=True) * inv
        s = jnp.sum(h * h, axis=1, keepdims=True) * inv
        rstd = lax.rsqrt(s - m * m + EPSILON)
        xhat = (h - m) * rstd
        h1[r, :] = xhat
        rs1[r, :] = jnp.broadcast_to(rstd, (16, 128))
        low[r, :] = (xhat * vec[1:2, :] + vec[2:3, :]).astype(BF)
        return 0
    lax.fori_loop(0, own_rows // 16, norm1, 0, unroll=3)
    lowt[...] = low[...].T
    E_uy[3]()
    for m in u_w:
        m.wait_recv()

    def gate(i, _):
        at(i, gate_events)
        zz = i // nb
        j = i % nb
        f = pl.ds(pl.multiple_of(j * 256, 256), 256)
        v = nn(low[...], wu[zz, :, f]) + sm[zz, 0, pl.ds(8 + j, 1), :]
        a, g = gelu_pair(v)
        hid[zz, :, f] = a.astype(BF)
        dgl[zz, :, f] = g.astype(BF)
        return 0
    lax.fori_loop(0, nz * nb, gate, 0)
    for m in h_y:
        m.wait_recv()
    local[6].wait()
    def turn_t(i, _):
        f = pl.ds(pl.multiple_of(128 * i, 128), 128)
        tr[f, :] = tt[:, f].T
        return 0
    lax.fori_loop(0, main // 128, turn_t, 0)
    tr[pl.ds(main, 16), :] = jnp.zeros((16, feats), BF)
    for m in d_k:
        m.wait_recv()

    def down(j, _):
        f = pl.ds(pl.multiple_of(j * 256, 256), 256)
        acc = nt(hid[0], wd[0, f, :])
        for zz in range(1, nz):
            acc = acc + nt(hid[zz], wd[zz, f, :])
        h2[:, f] = acc
        return 0
    lax.fori_loop(0, nb, down, 0)
    scale = vec[6:7, 0:1]
    o4[:, :, pl.ds(b, o4.shape[2] - b)] = jnp.zeros((4, own_rows, o4.shape[2] - b), BF)

    def norm2(i, _):
        r = pl.ds(pl.multiple_of(i * CH, 16), CH)
        h = h2[r, :] + (h1[r, :] * vec[1:2, :] + vec[2:3, :]) + vec[3:4, :]
        m = jnp.sum(h, axis=1, keepdims=True) * inv
        s = jnp.sum(h * h, axis=1, keepdims=True) * inv
        rstd = lax.rsqrt(s - m * m + EPSILON)
        xhat = (h - m) * rstd
        o = xhat * vec[4:5, :] + vec[5:6, :]
        for cc in range(4):
            o4[cc, r, pl.ds(0, b)] = o[:, cc * b:(cc + 1) * b].astype(BF)
        place = lax.broadcasted_iota(jnp.int32, (CH, 1), 0) + i * CH
        place = jnp.where(place < main, place + k * main, count)
        go = jnp.where(place < count, scale * (o - tr[r, :].astype(F32)), 0.0)
        a = go * vec[4:5, :]
        m1 = jnp.sum(a, axis=1, keepdims=True) * inv
        m2 = jnp.sum(a * xhat, axis=1, keepdims=True) * inv
        g2 = rstd * (a - m1 - xhat * m2)
        h2[r, :] = g2
        g2b = g2.astype(BF)
        br[r, :] = g2b
        vgrad[0] += group_sum(go * xhat)
        vgrad[1] += group_sum(go)
        vgrad[2] += group_sum(g2b.astype(F32))
        return 0
    lax.fori_loop(0, CHS, norm2, 0)
    o_dst = lambda: out4.at[y, k]
    o_s = [n.send(lambda: o4.at[oc], o_dst, n.yp), n.send(lambda: o4.at[3 - c], o_dst, n.ykp), n.send(lambda: o4.at[c + 1 - 2 * k], o_dst, n.kp)]
    o_l = n.local(lambda: o4.at[c], o_dst)
    brt[...] = br[...].T
    def gmove(which, src, dst, zz, slot, yy):
        return pltpu.make_async_remote_copy(src_ref=src.at[slot, 2 * yy + 1 - k], dst_ref=dst.at[yy, zz], send_sem=zsem.at[which, yy, zz],
                                            recv_sem=zrem.at[which, yy, zz], device_id=n.kp, device_id_type=MESH)
    def each(fn, zz, slot):
        for which, src, dst in ((0, gdz, rd), (1, guz, ru)):
            for yy in range(2):
                fn(gmove(which, src, dst, zz, slot, yy))
    def fold(zz):
        each(lambda m: m.wait_recv(), zz, 0)
        for yy in range(2):
            add_to(hd.at[yy, zz], rd.at[yy, zz])
            add_to(hu.at[yy, zz], ru.at[yy, zz])

    def back(zz, _):
        slot = zz % 2

        @pl.when(zz >= 2)
        def _():
            each(lambda m: m.wait_send(), zz - 2, slot)

        def chunk(j, _):
            f = pl.ds(pl.multiple_of(j * 256, 256), 256)
            gh = nn(br[...], wd[zz, :, f])
            g = (gh * dgl[zz, :, f].astype(F32)).astype(BF)
            bupgrad[zz, :, f] += group_sum(g.astype(F32))
            gdc = nn(brt[...], hid[zz, :, f])
            guc = nn(lowt[...], g)
            hid[zz, :, f] = g
            for cc in range(4):
                gdz[slot, cc, :, f] = gdc[cc * b:(cc + 1) * b, :].astype(BF)
                guz[slot, cc, :, f] = guc[cc * b:(cc + 1) * b, :].astype(BF)
            return 0
        lax.fori_loop(0, nb, chunk, 0)
        each(lambda m: m.start(), zz, slot)
        for yy in range(2):
            hd[yy, zz] = gdz[slot, 2 * yy + k]
            hu[yy, zz] = guz[slot, 2 * yy + k]

        @pl.when(zz >= 1)
        def _():
            fold(zz - 1)
        return 0
    lax.fori_loop(0, nz, back, 0)

    def first_grad(j, _):
        f = pl.ds(pl.multiple_of(j * 256, 256), 256)
        acc = h2[:, f]
        for zz in range(nz):
            acc = acc + nt(hid[zz], wu[zz, f, :])
        h2[:, f] = acc
        return 0
    lax.fori_loop(0, nb, first_grad, 0)
    fold(nz - 1)
    o_h = [n.local(all_of(hd), all_of(hd_o)), n.local(all_of(hu), all_of(hu_o))]

    def norm1_back(i, _):
        r = pl.ds(pl.multiple_of(i * 16, 16), 16)
        g = h2[r, :]
        xhat = h1[r, :]
        a = g * vec[1:2, :]
        m1 = jnp.sum(a, axis=1, keepdims=True) * inv
        m2 = jnp.sum(a * xhat, axis=1, keepdims=True) * inv
        g1 = rs1[r, 0:1] * (a - m1 - xhat * m2)
        g_one[r, :] = g1
        gb = g1.astype(BF)
        ga[own_slice(i * 16, 16), :] = gb
        vgrad[3] += group_sum(g * xhat)
        vgrad[4] += group_sum(g)
        vgrad[5] += group_sum(gb.astype(F32))
        return 0
    lax.fori_loop(0, own_rows // 16, norm1_back, 0, unroll=3)
    g_main = lambda: ga.at[pl.ds(pl.multiple_of(k * main, 16), main)]
    g_tail = lambda: ga.at[pl.ds(pl.multiple_of(length + k * 16, 16), 16)]
    g_k = [n.send(g_main, g_main, n.kp), n.send(g_tail, g_tail, n.kp)]
    for m in g_k:
        m.wait_recv()
    o_g = n.local(all_of(ga), all_of(ga_o))
    for m in o_s:
        m.wait_recv()
    for m in [o_x, o_w, o_m, o_l, o_g] + o_q + o_h:
        m.wait()
    for zz in range(nz - 2, nz):
        each(lambda m: m.wait_send(), zz, zz % 2)
    n.finish()

def add_to(dst, src):
    dst[...] = (dst[...].astype(F32) + src[...].astype(F32)).astype(BF)

def forward(valid, tok, memory, tch, w3, wo, lu, ld, vecs, bias_up, bias_qv, ids, nz):
    b, width = lu.shape
    feats = 4 * b; length = tok.shape[2]; rows = length + 32; main = length // 2; own = main + 16
    V = lambda *s, d=BF: pltpu.VMEM(s, d)
    vm = pl.BlockSpec(memory_space=pltpu.VMEM); sm = pl.BlockSpec(memory_space=pltpu.SMEM); an = pl.BlockSpec(memory_space=pl.ANY)
    S = jax.ShapeDtypeStruct
    t3 = S((3, rows, 128), BF); h = S((2, nz, b, width), BF)
    outs = [(S((feats, length + 128), BF), an), (t3, an), (t3, an), (t3, an), (t3, an), (S((2, feats, width), BF), an), (S((rows, feats), BF), an), (h, an), (h, an),
            (S((6, 1, rows), F32), vm), (S((own, feats), F32), vm), (S((6, 8, feats), F32), vm), (S((nz, 8, width), F32), vm), (S((2, 2, own, 256), BF), vm)]
    w = V(nz, feats, width)
    scratch = [V(feats, length + 128), V(rows, feats), w, w, w, V(nz, 4, 16, 256, d=F32), V(feats, main), V(own, feats), V(3, feats, 384),
               V(3, rows, 128), V(3, rows, 128), V(3, rows, 128), V(128, rows), V(128, rows, d=F32), V(3, rows, 128), V(6, own, 128), V(3, 8, 384, d=F32), V(8, feats, d=F32), V(feats, feats),
               V(own, feats, d=F32), V(own, feats, d=F32), V(own, 128, d=F32), V(own, feats), V(feats, own), V(own, feats), V(feats, own),
               V(nz, own, width), V(nz, own, width), V(2, 4, b, width), V(2, 4, b, width)] + [V(2, nz, b, width)] * 4 + [V(rows, feats), V(4, own, 256), V(b, width), V(16, 256, d=F32), V(2, b, 128), V(128, b, d=F32), V(length + 128, 128, d=F32), V(1, length + 128, d=F32),
               pltpu.SemaphoreType.DMA((136,)), pltpu.SemaphoreType.DMA((136,)), pltpu.SemaphoreType.DMA((32,)),
               pltpu.SemaphoreType.DMA((2, 2, nz)), pltpu.SemaphoreType.DMA((2, 2, nz))]
    return pl.pallas_call(forward_kernel, out_shape=[o for o, _ in outs], out_specs=[s for _, s in outs],
        in_specs=[sm, an, vm, an, vm, vm, an, an] + [vm] * 9, scratch_shapes=scratch,
        compiler_params=pltpu.CompilerParams(collective_id=1, has_side_effects=True, vmem_limit_bytes=67043328))(valid, tok, memory, tch, w3, wo, lu, ld, *vecs, bias_up, bias_qv, ids)
def total_of(refs):
    acc = refs[0][...].astype(F32)
    for r in refs[1:]:
        acc = acc + r[...].astype(F32)
    return acc

class Piece:
    def __init__(self, n, env, col0, num, js, x_first):
        self.n, self.x_first = n, x_first
        gown, ha, ax, ay, ayf, axf, mine, theirs, order = env
        C = pl.ds(col0, num); y, k = n.y, n.k
        self.core = [n.move((lambda j=j, yy=yy: gown.at[j, 2 * yy + 1 - k, :, C]), (lambda j=j, yy=yy: ha.at[yy, 2 * k + j, :, C]), n.kp) for j in js for yy in range(2)]
        self.keep = [n.copy((lambda j=j, yy=yy: gown.at[j, 2 * yy + k, :, C]), (lambda j=j, yy=yy: ha.at[yy, 2 * k + j, :, C])) for j in js for yy in range(2)]
        zz = order if len(js) == 2 else [js[0], js[0] + 2]
        self.first, self.second, self.add1, self.add2 = [], [], [], []
        for q in zz:
            if x_first:
                self.first.append(n.move((lambda q=q: ha.at[:, q, theirs, C]), (lambda q=q: ax.at[:, q, :, C]), n.xp))
                self.add1.append(lambda q=q: [add_to(ha.at[yy, q, mine, C], ax.at[yy, q, :, C]) for yy in range(2)])
                self.second.append(n.move((lambda q=q: ha.at[1 - y, q, mine, C]), (lambda q=q: ay.at[q, :, C]), n.yp))
                self.add2.append(lambda q=q: add_to(ha.at[y, q, mine, C], ay.at[q, :, C]))
            else:
                self.first.append(n.move((lambda q=q: ha.at[1 - y, q, :, C]), (lambda q=q: ayf.at[q, :, C]), n.yp))
                self.add1.append(lambda q=q: add_to(ha.at[y, q, :, C], ayf.at[q, :, C]))
                self.second.append(n.move((lambda q=q: ha.at[y, q, theirs, C]), (lambda q=q: axf.at[q, :, C]), n.xp))
                self.add2.append(lambda q=q: add_to(ha.at[y, q, mine, C], axf.at[q, :, C]))
    def start(self):
        for m in self.core + self.keep:
            m.start()
    def ev1(self):
        for m in self.core:
            m.wait_recv()
        for m in self.keep:
            m.wait()
        for m in self.first:
            m.start()
    def ev2(self):
        for m, f, s in zip(self.first, self.add1, self.second):
            m.wait_recv(); f(); s.start()
    def ev3(self):
        for m, f in zip(self.second, self.add2):
            m.wait_recv(); f()

class Rows:
    def __init__(self, n, here, z1, z2, e, dev1, dev2, add):
        e1, e2, e3 = e
        self.a = n.move((lambda: here(e3)), (lambda: z1(1)), dev1)
        self.b = n.move((lambda: here(e1)), (lambda: z1(0)), dev1)
        self.c = n.move((lambda: here(e2)), z2, dev2)
        self.mid = lambda: add(here(e2), z1(1))
    def start(self):
        self.a.start(); self.b.start()
    def middle(self):
        self.a.wait_recv(); self.mid(); self.c.start()
    def end(self):
        self.b.wait_recv(); self.c.wait_recv()

def backward_kernel(hu_h, hd_h, ga_h, mixed_h, xt_h, q_h, k_h, v_h, w_h, o4_h, g1_h, lse, vgrad, bupgrad, ids,
                    grad4, lout, gmem, g3, gwo, fu, fd, fvec, bup, bqv,
                    hu, hd, ux, uz1, uz2, ut, uy, fub, pu, dy, dz1, dz2, df, dx, pd,
                    ha, ax, ay, ayf, axf, az1, az2, fa, pa, gown,
                    ga, mixed, xt, qt, kt, vt, w, o4, g1, wp, wt, gat, gm, gp, dv, dk, dqt, ktt, dd, g4, gs, gr, lo32,
                    sv, svk, svt, svy, svo, svx, ps, svz, idk, idq, ss, rs, lsem):
    n = Net(ss, rs, lsem)
    nz, y, k, c, z, x, d, nd = n.nz, n.y, n.k, n.c, n.z, n.x, n.d, n.nd
    b = fu.shape[0]; hb = b // 2
    rows, feats = ga.shape
    fb = pl.ds(0, b)
    own_rows = g1.shape[0]; main = own_rows - 16; length = 2 * main
    mine = pl.ds(pl.multiple_of(x * hb, 16), hb)
    theirs = pl.ds(pl.multiple_of((1 - x) * hb, 16), hb)
    all_of = lambda r: (lambda: r)
    l_w, l_ga, l_m = [n.local(all_of(s), all_of(t)) for s, t in ((w_h, w), (ga_h, ga), (mixed_h, mixed))]
    l_q = [n.local(all_of(s), all_of(t)) for s, t in ((k_h, kt), (q_h, qt), (v_h, vt))]
    l_x = n.local(all_of(xt_h), all_of(xt))
    l_d = n.local(lambda: hd_h.at[y], lambda: hd)
    l_u = n.local(lambda: hu_h.at[:, :, mine], lambda: hu)
    l_o = [n.local(all_of(o4_h), all_of(o4)), n.local(all_of(g1_h), all_of(g1))]
    n.barrier(n.zp[1:] + [n.yp, n.ykp, n.kp, n.xp] + n.others)
    e1 = z + 1 - 2 * lax.rem(z, 2)
    e2 = lax.rem(z + 2, nz)
    e3 = lax.rem(e1 + 2, nz)
    e = (e1, e2, e3)
    order = [e3, e2, e1, z]
    dev1, dev2 = (d, e1, c), (d, e2, c)
    d_y = [n.send((lambda q=q: hd_h.at[1 - y, q]), (lambda q=q: dy.at[q]), n.yp) for q in order]
    u_x = [n.send((lambda q=q: hu_h.at[:, q, theirs]), (lambda q=q: ux.at[:, q]), n.xp) for q in order]

    def add2(a, s):
        for yy in range(2):
            add_to(a.at[yy], s.at[yy])
    dz = Rows(n, lambda q: hd.at[q], lambda s: dz1.at[s], lambda: dz2, e, dev1, dev2, add_to)
    uz = Rows(n, lambda q: hu.at[:, q], lambda s: uz1.at[s], lambda: uz2, e, dev1, dev2, add2)
    d_x = n.move(all_of(df), all_of(dx), n.xp)
    u_y = n.move(lambda: ut.at[1 - y], all_of(uy), n.yp)
    u_f = n.move(lambda: fub.at[mine], lambda: fub.at[mine], n.xp)

    mypair = d // 2

    def pairs_sum(value, slots, view):
        if nd == 2:
            return value
        view(slots, mypair)[...] = value.astype(slots.dtype)
        ms = [n.send((lambda: view(slots, mypair)), (lambda: view(slots, mypair)), o) for o in n.others]
        for m in ms:
            m.wait_recv()
        return total_of([view(slots, i) for i in range(nd // 2)])

    def ev_dy(j):
        def run():
            d_y[j].wait_recv()
            if j == 0:
                l_d.wait()
            add_to(hd.at[order[j]], dy.at[order[j]])
            if j == 0:
                dz.a.start()
        return run
    def ev_ux(j):
        def run():
            u_x[j].wait_recv()
            if j == 0:
                l_u.wait()
            add2(hu.at[:, order[j]], ux.at[:, order[j]])
            if j == 0:
                uz.a.start()
        return run
    def ev_df():
        dz.end()
        df[...] = total_of([hd.at[z], dz1.at[0], dz2]).astype(BF)
        d_x.start()
    def ev_ut():
        uz.end()
        for yy in range(2):
            ut[yy] = total_of([hu.at[yy, z], uz1.at[0, yy], uz2.at[yy]]).astype(BF)
        u_y.start()
    def ev_uf():
        u_y.wait_recv()
        fub[mine, :] = pairs_sum(total_of([ut.at[y], uy]), pu, lambda s, i: s.at[i]).astype(BF)
        u_f.start()
    env = (gown, ha, ax, ay, ayf, axf, mine, theirs, order)
    PO = Piece(n, env, 640, 128, (0, 1), True)
    P0 = Piece(n, env, 0, 384, (0,), True)
    P1 = Piece(n, env, 0, 384, (1,), False)
    P2 = Piece(n, env, 384, 128, (0, 1), True)
    P3 = Piece(n, env, 512, 128, (0, 1), False)
    class Cols:
        def __init__(self, col0, num):
            C = pl.ds(col0, num)
            self.C = C
            self.z = Rows(n, lambda q: ha.at[y, q, mine, C], lambda s: az1.at[s, :, C], lambda: az2.at[:, C], e, dev1, dev2, add_to)
            self.f = n.move(lambda: fa.at[mine, C], lambda: fa.at[mine, C], n.xp)
        def end(self):
            self.z.end()
            C = self.C
            fa[mine, C] = pairs_sum(total_of([ha.at[y, z, mine, C], az1.at[0, :, C], az2.at[:, C]]), pa, lambda s, i: s.at[i, :, C]).astype(BF)
            self.f.start()
    ZO, Z01, Z2, Z3 = Cols(640, 128), Cols(0, 384), Cols(384, 128), Cols(512, 128)
    row_ids(ids, y, gmem.shape[1] // 2, idk, idq)
    l_w.wait(); l_ga.wait()
    gat[...] = ga[...].T
    assemble_pairs(w, wp, feats)
    wt[:, pl.ds(0, 128)] = w[0, :, pl.ds(640, 128)]
    wt[:, pl.ds(128, 128)] = w[1, :, pl.ds(640, 128)]
    lo = lax.broadcasted_iota(jnp.int32, (feats, 128), 1) < 64
    wt[:, pl.ds(256, 128)] = jnp.where(lo, pltpu.roll(w[0, :, pl.ds(512, 128)].astype(F32), 64, 1), w[1, :, pl.ds(512, 128)].astype(F32)).astype(BF)
    r3 = rows // 3

    def mixed_grad(i, _):
        r = pl.ds(pl.multiple_of(i * r3, 16), r3)
        v = nn(ga[r, :], wt[...])
        for p in range(3):
            gm[p, r, :] = v[:, 128 * p:128 * p + 128].astype(BF)
        return 0
    lax.fori_loop(0, 3, mixed_grad, 0)
    l_m.wait()
    for cc in range(4):
        af = gat[pl.ds(b * cc, b), :]
        for j in range(2):
            gown[j, cc, :, pl.ds(640, 128)] = nn(af, mixed[j]).astype(BF)
    PO.start()
    for m in l_q:
        m.wait()
    l_x.wait()
    def ev_b():
        dz.b.start(); uz.b.start()
    table = {0: [ev_dy(0), ev_ux(0)], 1: [PO.ev1], 4: [ev_dy(1), ev_ux(1)], 6: [dz.middle], 7: [ev_dy(2), ev_ux(2), P0.ev1], 9: [uz.middle], 10: [ev_b],
             11: [ev_dy(3), ev_ux(3)], 13: [PO.ev2], 15: [P1.ev1], 16: [PO.ev3, ZO.z.start, P0.ev2]}
    cuts = {1: 0, 3: 1, 4: 2}

    def head(i, _):
        p = i // 2
        h = i % 2
        he = pl.ds(pl.multiple_of(64 * h, 64), 64)

        @pl.when(h == 0)
        def _():
            ktt[...] = kt[p].T
            prod = (gm[p].astype(F32) * mixed[p].astype(F32)).T
            dd[0] = jnp.sum(prod[:64, :], axis=0, keepdims=True)
            dd[1] = jnp.sum(prod[64:, :], axis=0, keepdims=True)
            dv[...] = jnp.zeros_like(dv)
            dk[...] = jnp.zeros_like(dk)
        lanes = (lax.broadcasted_iota(jnp.int32, (1, 128), 1) // 64) == h
        for t, (q0, qn, spans) in enumerate(tiles(rows, length)):
            q = qt[p, pl.ds(q0, qn), :]
            qm = jnp.where(lanes, q, jnp.zeros_like(q))
            g = gm[p, pl.ds(q0, qn), :]
            gmm = jnp.where(lanes, g, jnp.zeros_like(g))
            sc = scores_of(kt, qm, idk, idq[0:1, pl.ds(q0, qn)], p, spans)
            l = lse[i, :, pl.ds(q0, qn)]
            dl = dd[h, :, pl.ds(q0, qn)]
            acc = None
            for s, (k0, kn, _) in zip(sc, spans):
                pr = jnp.exp(s - l)
                dp = nt(vt[p, pl.ds(k0, kn), :], gmm)
                ds = (pr * (dp - dl)).astype(BF)
                dv[pl.ds(k0, kn), :] += nn(pr.astype(BF), gmm)
                dk[pl.ds(k0, kn), :] += nn(ds, qm)
                o = nn(ktt[he, pl.ds(k0, kn)], ds)
                acc = o if acc is None else acc + o
            dqt[he, pl.ds(q0, qn)] = acc * 0.125
            if t in cuts:
                at(3 * i + cuts[t], table)

        @pl.when(h == 1)
        def _():
            gp[p, :, pl.ds(0, 128)] = dqt[...].T.astype(BF)
            gp[p, :, pl.ds(128, 128)] = dk[...].astype(BF)
            gp[p, :, pl.ds(256, 128)] = dv[...].astype(BF)

        @pl.when(jnp.logical_and(h == 1, p < 2))
        def _():
            def part(cc, _):
                f = pl.ds(pl.multiple_of(b * cc, 16), b)
                gown[p, cc, :, pl.ds(0, 384)] = nn(xt[f, pl.ds(0, rows)], gp[p]).astype(BF)
                return 0
            lax.fori_loop(0, 4, part, 0)
        at(i, {1: [P0.start], 3: [P1.start]})
        return 0
    lax.fori_loop(0, 6, head, 0)
    sv[...] = jnp.zeros_like(sv)
    for i in range(6):
        sv[pl.ds(i, 1), :] = jnp.sum(vgrad[i], axis=0, keepdims=True)
    for i in range(nz):
        sv[pl.ds(6 + i, 1), :] = jnp.sum(bupgrad[i], axis=0, keepdims=True)
    for p in range(3):
        t = jnp.sum(group_sum(gp[p].astype(F32)), axis=0, keepdims=True)
        sv[pl.ds(6 + nz + p, 1), pl.ds(0, 384)] = jnp.where(k == 0, t, 0.0)
        sv[pl.ds(6 + nz + p, 1), pl.ds(384, 384)] = jnp.where(k == 1, t, 0.0)
    s_k = n.send(all_of(sv), all_of(svk), n.kp)
    sw = lambda a: pltpu.roll(a, 64, 1)

    def last(cc, _):
        f = pl.ds(pl.multiple_of(b * cc, 16), b)
        r2 = nn(xt[f, pl.ds(0, rows)], gp[2])
        o2 = nn(gat[f, :], mixed[2])
        lo = lax.broadcasted_iota(jnp.int32, (b, 128), 1) < 64
        rq, rk, rv = r2[:, :128], r2[:, 128:256], r2[:, 256:]
        gown[0, cc, :, pl.ds(384, 128)] = jnp.where(lo, rq, sw(rk)).astype(BF)
        gown[1, cc, :, pl.ds(384, 128)] = jnp.where(lo, sw(rq), rk).astype(BF)
        gown[0, cc, :, pl.ds(512, 128)] = jnp.where(lo, rv, sw(o2)).astype(BF)
        gown[1, cc, :, pl.ds(512, 128)] = jnp.where(lo, sw(rv), o2).astype(BF)
        return 0
    lax.fori_loop(0, 4, last, 0)
    P2.start(); P3.start()
    def rowsgrad(r):
        return nt(gp[0, r, :], wp[0]) + nt(gp[1, r, :], wp[1]) + nt(gp[2, r, :], wp[2])

    def half_rows(kk, put):
        def chunk(i, _):
            put(pl.ds(pl.multiple_of(i * 256, 16), 256), rowsgrad(pl.ds(pl.multiple_of(kk * main + i * 256, 16), 256)))
            return 0
        lax.fori_loop(0, main // 256, chunk, 0)
        put(pl.ds(main, 16), rowsgrad(pl.ds(pl.multiple_of(length + kk * 16, 16), 16)))
    def put_other(r, v):
        gs[r, :] = v.astype(BF)
    half_rows(1 - k, put_other)
    g_k = n.send(all_of(gs), all_of(gr), n.kp)
    s_k.wait_recv()
    svt[...] = sv[...] + svk[...]
    s_y = n.send(all_of(svt), all_of(svy), n.yp)
    P1.ev2()
    P2.ev1(); P3.ev1()
    for m in l_o:
        m.wait()
    g4[:, :, pl.ds(b, g4.shape[2] - b)] = jnp.zeros((4, own_rows, g4.shape[2] - b), BF)
    def put_own(r, v):
        g1[r, :] = g1[r, :] + v
    half_rows(k, put_own)
    s_y.wait_recv()
    svo[...] = svt[...] + svy[...]
    s_x = n.send(all_of(svo), all_of(svx), n.xp)
    ev_ut()
    P0.ev3()
    ev_df()
    P1.ev3(); Z01.z.start(); ZO.z.middle()
    P2.ev2()
    g_k.wait_recv()

    def own(i, _):
        r = pl.ds(pl.multiple_of(i * 48, 16), 48)
        v = g1[r, :] + gr[r, :].astype(F32)
        for cc in range(4):
            g4[cc, r, fb] = v[:, cc * b:(cc + 1) * b].astype(BF)
        return 0
    lax.fori_loop(0, own_rows // 48, own, 0)
    g_l = n.local(lambda: g4.at[c], lambda: grad4.at[y, k])
    dst = lambda: grad4.at[y, k]
    g_s = [n.send(lambda: g4.at[n.oc], dst, n.yp), n.send(lambda: g4.at[3 - c], dst, n.ykp), n.send(lambda: g4.at[c + 1 - 2 * k], dst, n.kp)]
    P3.ev2()
    s_x.wait_recv()
    svz[z] = pairs_sum(svo[...] + svx[...], ps, lambda s, i: s.at[i])
    s_z = [n.send(lambda: svz.at[z], lambda: svz.at[z], n.zp[i]) for i in range(1, nz)]
    P2.ev3(); Z2.z.start()
    ev_uf()
    Z01.z.middle(); ZO.end()
    P3.ev3(); Z3.z.start()
    half = (lout.shape[1] - length) // 2
    for s in range(2):
        lo32[pl.ds(0, half), :] = o4[s, 0, pl.ds(main, 16), fb].astype(F32)[:half]
        lo32[pl.ds(half, main), :] = o4[s, 0, pl.ds(0, main), fb].astype(F32)
        lo32[pl.ds(half + main, main), :] = o4[s, 1, pl.ds(0, main), fb].astype(F32)
        lo32[pl.ds(half + length, 16 - half), :] = o4[s, 0, pl.ds(main, 16), fb].astype(F32)[half:]
        lo32[pl.ds(length + 16, 2 * half - 16), :] = o4[s, 1, pl.ds(main, 16), fb].astype(F32)[:2 * half - 16]
        lout[s] = lo32[pl.ds(0, length + 2 * half), :].astype(BF)
    Z2.z.middle(); Z01.end(); Z3.z.middle()
    d_x.wait_recv()
    fd[...] = pairs_sum(total_of([df, dx]), pd, lambda s, i: s.at[i])
    u_f.wait_recv()
    fu[...] = fub[...].astype(F32)
    Z2.end(); Z3.end()
    for m in s_z:
        m.wait_recv()
    acc = svz[0]
    for i in range(1, nz):
        acc = acc + svz[i]
    pick = jnp.where(c == 0, acc[:8, 0:b], 0.0)
    for cc in range(1, 4):
        pick = pick + jnp.where(c == cc, acc[:8, cc * b:(cc + 1) * b], 0.0)
    fvec[...] = pick
    t = jnp.where(z == 0, acc[6:7], 0.0)
    for i in range(1, nz):
        t = t + jnp.where(z == i, acc[6 + i:7 + i], 0.0)
    bup[...] = t
    hbias = acc[6 + nz:9 + nz]
    hbias = jnp.where(z // 2 == 0, hbias[:, :384], hbias[:, 384:])
    odd = z % 2 == 1
    two = jnp.where(odd, hbias[1:2], hbias[0:1])
    lo1 = lax.broadcasted_iota(jnp.int32, (8, 128), 1) < 64
    w8 = lambda a: jnp.broadcast_to(a, (8, 128))
    left = lambda a, v: jnp.where(lo1, w8(a), sw(w8(v)))[0:1]
    right = lambda a, v: jnp.where(lo1, sw(w8(a)), w8(v))[0:1]
    lq, lv = hbias[2:3, :128], hbias[2:3, 256:]
    bqv[pl.ds(0, 1), :] = left(two[:, :128], two[:, 256:])
    bqv[pl.ds(1, 1), :] = right(two[:, :128], two[:, 256:])
    bqv[pl.ds(2, 1), :] = jnp.where(odd, right(lq, lv), left(lq, lv))
    for m in (ZO, Z01, Z2, Z3):
        m.f.wait_recv()
    lob = lax.broadcasted_iota(jnp.int32, (b, 128), 1) < 64
    tile = lambda i: fa[:, pl.ds(128 * i, 128)].astype(F32)
    t0, t1, t2, t3, t4, t5 = [tile(i) for i in range(6)]
    g3[0, :, pl.ds(0, 128)] = jnp.where(lob, t0, sw(t1))
    g3[0, :, pl.ds(128, 64)] = t2[:, :64]
    g3[1, :, pl.ds(0, 128)] = jnp.where(lob, sw(t0), t1)
    g3[1, :, pl.ds(128, 64)] = sw(t2)[:, :64]
    g3[2, :, pl.ds(0, 128)] = t3
    g3[2, :, pl.ds(128, 64)] = t4[:, :64]
    gwo[pl.ds(0, 128), :] = t5.T
    gwo[pl.ds(128, 64), :] = sw(t4).T[:64]
    for m in g_s:
        m.wait_recv()
    g_l.wait()
    for s in range(2):
        gmem[s, pl.ds(0, 16), :] = grad4[s, 0, pl.ds(main, 16), fb].astype(F32)
        gmem[s, pl.ds(16, 2 * half - 16), :] = grad4[s, 1, pl.ds(main, 16), fb].astype(F32)[:2 * half - 16]
    n.finish()

def backward(hu, hd, ga, mixed, xt, qt, kt, vt, w, o4, g1, lse, vgrad, bupgrad, ids, half, nz, nd):
    b, width = hu.shape[2:]
    feats = 4 * b; hb = b // 2; rows = ga.shape[0]; own = g1.shape[0]; length = 2 * (own - 16)
    V = lambda *s, d=BF: pltpu.VMEM(s, d)
    vm = pl.BlockSpec(memory_space=pltpu.VMEM); an = pl.BlockSpec(memory_space=pl.ANY)
    S = jax.ShapeDtypeStruct
    np_ = max(1, nd // 2) if nd > 2 else 1
    pw = (hb, width) if nd > 2 else (16, 128)
    t3 = V(3, rows, 128); f3 = lambda *s: V(*s, d=F32)
    sm = f3(16, feats)
    outs = (S((2, 2, own, 256), BF), S((2, length + 2 * half, b), BF), S((2, 2 * half, b), F32), S((3, b, b), F32), S((b, b), F32), S((b, width), F32), S((b, width), F32), S((8, b), F32), S((1, feats), F32), S((3, 128), F32))
    scratch = [V(2, nz, hb, width), V(nz, b, width), V(2, nz, hb, width), V(2, 2, hb, width), V(2, hb, width), V(2, hb, width), V(hb, width), V(b, width), V(np_, *pw),
               V(nz, b, width), V(2, b, width), V(b, width), V(b, width), V(b, width), V(np_, b, width) if nd > 2 else V(1, 16, 128),
               V(2, nz, b, width), V(2, nz, hb, width), V(nz, hb, width), V(nz, b, width), V(nz, hb, width), V(2, hb, width), V(hb, width), V(b, width), V(np_, *pw), V(2, 4, b, width),
               V(rows, feats), t3, V(*xt.shape), t3, t3, t3, V(*w.shape), V(*o4.shape), f3(*g1.shape), V(3, feats, 384), V(feats, 384), V(feats, rows), t3, V(3, rows, 384),
               f3(rows, 128), f3(rows, 128), f3(128, rows), V(128, rows), f3(2, 1, rows), V(4, own, 256), V(own, feats), V(own, feats), f3(rows, b),
               sm, sm, sm, sm, sm, sm, f3(np_, 16, feats), f3(nz, 16, feats), f3(length + 128, 128), f3(1, length + 128),
               pltpu.SemaphoreType.DMA((128 + 5 * nd,)), pltpu.SemaphoreType.DMA((128 + 5 * nd,)), pltpu.SemaphoreType.DMA((40,))]
    return pl.pallas_call(backward_kernel, out_shape=outs, in_specs=[an] * 11 + [vm] * 4, out_specs=(vm,) * len(outs), scratch_shapes=scratch,
        compiler_params=pltpu.CompilerParams(collective_id=2, has_side_effects=True, vmem_limit_bytes=67043328))(hu, hd, ga, mixed, xt, qt, kt, vt, w, o4, g1, lse, vgrad, bupgrad, ids)

def per_device(tokens, memory, block_ids, valid, teacher, w_qkv, bias_qv, w_out, bias_out, ln1_gain, ln1_bias, w_up, bias_up, w_down, bias_down, ln2_gain, ln2_bias):
    _, b, length = tokens.shape
    nd, nz = lax.axis_size("dp"), lax.axis_size("row")
    d, z, c = (lax.axis_index(a) for a in ("dp", "row", "col"))
    y, k = c // 2, c % 2
    feats = 4 * b
    half = memory.shape[1] // 2
    main = length // 2
    rows = length + 32
    one = lambda a: a.reshape(1, -1)
    xt, qt, kt, vt, mixed, wown, ga, hu, hd, lse, g_one, vgrad, bupgrad, out4 = forward(valid, tokens, memory, teacher, w_qkv.reshape(3, b, 192), w_out, w_up, w_down, [one(a) for a in (bias_out, ln1_gain, ln1_bias, bias_down, ln2_gain, ln2_bias)], one(bias_up), bias_qv, block_ids, nz)
    grad4, lout, gmem, g3, gwo, fu, fd, fvec, bup, bqv = backward(hu, hd, ga, mixed, xt, qt, kt, vt, wown, out4, g_one, lse, vgrad, bupgrad, block_ids, half, nz, nd)
    grad_tokens = grad4[:, :, :main, :b].reshape(2, length, b).astype(F32)
    return (lout, grad_tokens, gmem, g3.reshape(3, b * b), bqv, gwo, fvec[5], fvec[3], fvec[4], fu, bup[0], fd, fvec[2], fvec[0], fvec[1])

def solution(mesh):
    rows, feat = ("dp", "row"), "col"
    in_specs = (P(rows, feat, None), P(rows, None, feat), P(rows, None), P(), P(rows, feat, None), P("row", feat), P("row", None), P("row", feat), P(feat), P(feat), P(feat), P(feat, "row"), P("row"), P(feat, "row"), P(feat), P(feat), P(feat))
    out_specs = (P(rows, None, feat), P(rows, None, feat), P(rows, None, feat), P("row", feat), P("row", None), P("row", feat), P(feat), P(feat), P(feat), P(feat, "row"), P("row"), P(feat, "row"), P(feat), P(feat), P(feat))
    return jax.shard_map(per_device, mesh=mesh, in_specs=in_specs, out_specs=out_specs, check_vma=False)
```

```python
import jax
import jax.numpy as jnp
from jax import lax
from jax.experimental import pallas as pl
from jax.experimental.pallas import tpu as pltpu
from jax.sharding import PartitionSpec as P
BF=jnp.bfloat16; F32=jnp.float32
EPSILON=1e-12
CH=48

def nn(a,b): return lax.dot_general(a,b,(((1,),(0,)),((),())),preferred_element_type=F32)
def nt(a,b): return lax.dot_general(a,b,(((1,),(1,)),((),())),preferred_element_type=F32)

def gelu_pair(v):
    t = pl.reciprocal(1.0 + (0.3275911 * 0.7071067811865476) * jnp.abs(v))
    poly = t * (0.5*0.254829592 + t * (-0.5*0.284496736 + t * (0.5*1.421413741 + t * (-0.5*1.453152027 + t * (0.5*1.061405429)))))
    e = jnp.exp(-0.5 * v * v)
    half = poly * e
    cdf = jnp.where(v >= 0.0, 1.0 - half, half)
    return v * cdf, cdf + v * (e * 0.3989422804014327)

def group_sum(v):
    rows = v.shape[0]
    return jnp.sum(v.reshape(rows // 8, 8, v.shape[1]), axis=0)

def mlp_kernel(half_ref, valid_ref, mixed, x, teach, vec, bup, wa_hbm, wu_hbm, wd_hbm,
               out, g_one, g_attn, vgrad, bupgrad, gu_hbm, gd_hbm,
               tr, wraw, wt, wu, wd, h1, h2, rs1, low, lowt, brt, br, hid, dgl, gg, gu, gd, sem):
    rows, feats = x.shape
    zs = wu.shape[0]
    nb = feats // 256
    copies_a = [pltpu.make_async_copy(wa_hbm.at[z, :, pl.ds(512, 256)], wraw.at[z], sem.at[z]) for z in range(zs)]
    copies_u = [pltpu.make_async_copy(wu_hbm.at[z], wu.at[z], sem.at[zs + z]) for z in range(zs)]
    copies_d = [pltpu.make_async_copy(wd_hbm.at[z], wd.at[z], sem.at[2 * zs + z]) for z in range(zs)]
    for c in copies_a + copies_u + copies_d:
        c.start()
    for c in copies_a:
        c.wait()
    main = teach.shape[1]
    for i in range(main // 128):
        tr[pl.ds(128 * i, 128), :] = teach[:, pl.ds(128 * i, 128)].T
    tr[pl.ds(main, rows - main), :] = jnp.zeros((rows - main, feats), BF)
    low_lane = lax.broadcasted_iota(jnp.int32, (feats, 128), 1) < 64
    for k in range(zs // 2):
        z0, z1 = 2 * k, 2 * k + 1
        wt[:, pl.ds(384 * k, 128)] = wraw[z0, :, pl.ds(128, 128)]
        wt[:, pl.ds(384 * k + 128, 128)] = wraw[z1, :, pl.ds(128, 128)]
        t0 = pltpu.roll(wraw[z0, :, pl.ds(0, 128)].astype(F32), 64, 1)
        t1 = wraw[z1, :, pl.ds(0, 128)].astype(F32)
        wt[:, pl.ds(384 * k + 256, 128)] = jnp.where(low_lane, t0, t1).astype(BF)
    for n in range(nb):
        f = pl.ds(256 * n, 256)
        h1[:, f] = nt(mixed[...], wt[f, :]) + x[:, f].astype(F32) + vec[0:1, f]
    inv = 1.0 / feats

    vgrad[...] = jnp.zeros_like(vgrad)
    bupgrad[...] = jnp.zeros_like(bupgrad)

    def norm1(i, _):
        r = pl.ds(pl.multiple_of(i * CH, 16), CH)
        h = h1[r, :]
        m = jnp.sum(h, axis=1, keepdims=True) * inv
        s = jnp.sum(h * h, axis=1, keepdims=True) * inv
        rstd = lax.rsqrt(s - m * m + EPSILON)
        xhat = (h - m) * rstd
        h1[r, :] = xhat
        rs1[r, :] = jnp.broadcast_to(rstd, (CH, 128))
        low[r, :] = (xhat * vec[1:2, :] + vec[2:3, :]).astype(BF)
        return 0
    lax.fori_loop(0, rows // CH, norm1, 0)
    lowt[...] = low[...].T
    for c in copies_u:
        c.wait()

    def gate(i, _):
        z = i // nb
        f = pl.ds(pl.multiple_of((i % nb) * 256, 256), 256)
        v = nn(low[...], wu[z, :, f]) + bup[z, :, f]
        a, b = gelu_pair(v)
        hid[z, :, f] = a.astype(BF)
        dgl[z, :, f] = b
        return 0
    lax.fori_loop(0, zs * nb, gate, 0)
    for c in copies_d:
        c.wait()

    def down(n, _):
        f = pl.ds(pl.multiple_of(n * 256, 256), 256)
        acc = nt(hid[0], wd[0, f, :])
        for z in range(1, zs):
            acc = acc + nt(hid[z], wd[z, f, :])
        h2[:, f] = acc
        return 0
    lax.fori_loop(0, nb, down, 0)
    scale = vec[6:7, 0:1]
    first = half_ref[0] * main

    def norm2(i, _):
        r = pl.ds(pl.multiple_of(i * CH, 16), CH)
        h = h2[r, :] + (h1[r, :] * vec[1:2, :] + vec[2:3, :]) + vec[3:4, :]
        m = jnp.sum(h, axis=1, keepdims=True) * inv
        s = jnp.sum(h * h, axis=1, keepdims=True) * inv
        rstd = lax.rsqrt(s - m * m + EPSILON)
        xhat = (h - m) * rstd
        o = xhat * vec[4:5, :] + vec[5:6, :]
        out[r, :] = o.astype(BF)
        place = lax.broadcasted_iota(jnp.int32, (CH, 1), 0) + i * CH
        place = jnp.where(place < main, place + first, valid_ref[0])
        go = jnp.where(place < valid_ref[0], scale * (o - tr[r, :].astype(F32)), 0.0)
        a = go * vec[4:5, :]
        m1 = jnp.sum(a, axis=1, keepdims=True) * inv
        m2 = jnp.sum(a * xhat, axis=1, keepdims=True) * inv
        g2 = rstd * (a - m1 - xhat * m2)
        h2[r, :] = g2
        b = g2.astype(BF)
        br[r, :] = b
        vgrad[0] += group_sum(go * xhat)
        vgrad[1] += group_sum(go)
        vgrad[2] += group_sum(b.astype(F32))
        return 0
    lax.fori_loop(0, rows // CH, norm2, 0)
    brt[...] = br[...].T

    def back(i, _):
        z = i // nb
        f = pl.ds(pl.multiple_of((i % nb) * 256, 256), 256)
        gh = nn(br[...], wd[z, :, f])
        g = (gh * dgl[z, :, f]).astype(BF)
        gg[z, :, f] = g
        bupgrad[z, :, f] += group_sum(g.astype(F32))
        gd[z, :, f] = nn(brt[...], hid[z, :, f]).astype(BF)
        gu[z, :, f] = nn(lowt[...], g).astype(BF)
        return 0
    lax.fori_loop(0, zs * nb, back, 0)
    outs = [pltpu.make_async_copy(gd, gd_hbm, sem.at[0]), pltpu.make_async_copy(gu, gu_hbm, sem.at[1])]
    for c in outs:
        c.start()

    def first_grad(n, _):
        f = pl.ds(pl.multiple_of(n * 256, 256), 256)
        acc = h2[:, f]
        for z in range(zs):
            acc = acc + nt(gg[z], wu[z, f, :])
        h2[:, f] = acc
        return 0
    lax.fori_loop(0, nb, first_grad, 0)

    def norm1_back(i, _):
        r = pl.ds(pl.multiple_of(i * CH, 16), CH)
        g = h2[r, :]
        xhat = h1[r, :]
        a = g * vec[1:2, :]
        m1 = jnp.sum(a, axis=1, keepdims=True) * inv
        m2 = jnp.sum(a * xhat, axis=1, keepdims=True) * inv
        g1 = rs1[r, 0:1] * (a - m1 - xhat * m2)
        g_one[r, :] = g1
        b = g1.astype(BF)
        g_attn[r, :] = b
        vgrad[3] += group_sum(g * xhat)
        vgrad[4] += group_sum(g)
        vgrad[5] += group_sum(b.astype(F32))
        return 0
    lax.fori_loop(0, rows // CH, norm1_back, 0)
    for c in outs:
        c.wait()

def mlp(half, valid, mixed, x, teach, vec, bup, wa, wu, wd):
    rows, feats = x.shape; zs = wu.shape[0]
    V = lambda *s, d=BF: pltpu.VMEM(s, d)
    vm = pl.BlockSpec(memory_space=pltpu.VMEM); sm = pl.BlockSpec(memory_space=pltpu.SMEM); an = pl.BlockSpec(memory_space=pl.ANY)
    S = jax.ShapeDtypeStruct
    return pl.pallas_call(mlp_kernel,
        out_shape=(S((rows,feats),BF),S((rows,feats),F32),S((rows,feats),BF),S((6,8,feats),F32),S((zs,8,feats),F32),S(wu.shape,BF),S(wd.shape,BF)),
        in_specs=[sm,sm,vm,vm,vm,vm,vm,an,an,an],
        out_specs=(vm,vm,vm,vm,vm,an,an),
        scratch_shapes=[V(rows,feats),V(zs,feats,256),V(feats,feats),V(*wu.shape),V(*wd.shape),V(rows,feats,d=F32),V(rows,feats,d=F32),V(rows,128,d=F32),V(rows,feats),
            V(feats,rows),V(feats,rows),V(rows,feats),V(zs,rows,feats),V(zs,rows,feats,d=F32),V(zs,rows,feats),V(*wu.shape),V(*wd.shape),pltpu.SemaphoreType.DMA((3*zs,))],
        compiler_params=pltpu.CompilerParams(vmem_limit_bytes=63*2**20),
    )(half,valid,mixed,x,teach,vec,bup,wa,wu,wd)
NEG=-1e30
def tn_lanes(): return lax.broadcasted_iota(jnp.int32,(1,128),1)

def assemble_pairs(w, wp, feats):
    lo = lax.broadcasted_iota(jnp.int32, (feats, 128), 1) < 64
    wp[0] = w[0, :, pl.ds(0, 384)]
    wp[1] = w[1, :, pl.ds(0, 384)]
    a0, a1 = w[0, :, pl.ds(384, 128)].astype(F32), w[1, :, pl.ds(384, 128)].astype(F32)
    wp[2, :, pl.ds(0, 128)] = jnp.where(lo, a0, pltpu.roll(a1, 64, 1)).astype(BF)
    wp[2, :, pl.ds(128, 128)] = jnp.where(lo, pltpu.roll(a0, 64, 1), a1).astype(BF)
    b0, b1 = w[0, :, pl.ds(512, 128)].astype(F32), w[1, :, pl.ds(512, 128)].astype(F32)
    wp[2, :, pl.ds(256, 128)] = jnp.where(lo, b0, pltpu.roll(b1, 64, 1)).astype(BF)

def tiles(rows, length):
    mem = (length, rows - length, True)
    out = []
    for a in range(0, length, 256):
        spans = []
        if a:
            spans.append((0, a, False))
        spans.append((a, min(512, length - a), True))
        out.append((a, 256, spans + [mem]))
    out.append((length, rows - length, [(0, length, True), mem]))
    return out

def scores_of(kt, qm, idk, idq, p, spans):
    out = []
    for k0, kn, masked in spans:
        s = nt(kt[p, pl.ds(k0, kn), :], qm)
        if masked:
            s = jnp.where(idk[pl.ds(k0, kn), 0:1] <= idq, s, NEG)
        out.append(s)
    return out

def attn_fwd_kernel(xt, wa_hbm, bias, idk, idq, x, qt, kt, vt, mixed, lse, w, wp, vtt, ot, sem):
    feats = xt.shape[0]; rows = x.shape[0]; length = xt.shape[1] - 128
    c = pltpu.make_async_copy(wa_hbm, w, sem); c.start()
    for i in range(length // 128):
        x[pl.ds(128 * i, 128), :] = xt[:, pl.ds(128 * i, 128)].T
    x[pl.ds(length, rows - length), :] = xt[:, pl.ds(length, 128)].T[: rows - length, :]
    c.wait()
    assemble_pairs(w, wp, feats)
    rc = rows // 3

    def project(i, _):
        p = i // 3
        r = pl.ds(pl.multiple_of((i % 3) * rc, 16), rc)
        v = nn(x[r, :], wp[p]) + bias[p]
        qt[p, r, :] = (v[:, :128].astype(BF).astype(F32) * 0.125).astype(BF)
        kt[p, r, :] = v[:, 128:256].astype(BF)
        vt[p, r, :] = v[:, 256:].astype(BF)
        return 0
    lax.fori_loop(0, 9, project, 0)

    def pair(p, _):
        vtt[...] = vt[p].T
        for e in range(2):
            lanes = (tn_lanes() < 64) if e == 0 else (tn_lanes() >= 64)
            for q0, qn, spans in tiles(rows, length):
                q = qt[p, pl.ds(q0, qn), :]
                qm = jnp.where(lanes, q, jnp.zeros_like(q))
                ss = scores_of(kt, qm, idk, idq[0:1, pl.ds(q0, qn)], p, spans)
                m = jnp.max(ss[0], axis=0, keepdims=True)
                for s in ss[1:]:
                    m = jnp.maximum(m, jnp.max(s, axis=0, keepdims=True))
                tot, acc = None, None
                for s, (k0, kn, _) in zip(ss, spans):
                    ex = jnp.exp(s - m)
                    t = jnp.sum(ex, axis=0, keepdims=True)
                    o = nn(vtt[pl.ds(64 * e, 64), pl.ds(k0, kn)], ex.astype(BF))
                    tot = t if tot is None else tot + t
                    acc = o if acc is None else acc + o
                ot[pl.ds(64 * e, 64), pl.ds(q0, qn)] = acc / tot
                lse[p, e, :, pl.ds(q0, qn)] = m + jnp.log(tot)
        mixed[p] = ot[...].T.astype(BF)
        return 0
    lax.fori_loop(0, 3, pair, 0)

def attn_fwd(xt, wa, bias, idk, idq, rows):
    feats = xt.shape[0]
    V = lambda *s, d=BF: pltpu.VMEM(s, d)
    vm = pl.BlockSpec(memory_space=pltpu.VMEM); an = pl.BlockSpec(memory_space=pl.ANY)
    S = jax.ShapeDtypeStruct
    t3 = S((3, rows, 128), BF)
    return pl.pallas_call(attn_fwd_kernel,
        out_shape=(S((rows, feats), BF), t3, t3, t3, t3, S((3, 2, 1, rows), F32)),
        in_specs=[vm, an, vm, vm, vm], out_specs=(vm,) * 6,
        scratch_shapes=[V(*wa.shape), V(3, feats, 384), V(128, rows), V(128, rows, d=F32), pltpu.SemaphoreType.DMA],
        compiler_params=pltpu.CompilerParams(vmem_limit_bytes=63*2**20))(xt, wa, bias, idk, idq)

def attn_bwd_kernel(ga, mixed, xt, qt, kt, vt, lse, idk, idq, wa_hbm, gpart, bgrad, gown_hbm, w, wp, wt, gat, gm, gp, dv, dk, dqt, ktt, dd, ro, gown, sem):
    feats = xt.shape[0]; rows = ga.shape[0]; length = xt.shape[1] - 128
    c = pltpu.make_async_copy(wa_hbm, w, sem); c.start()
    gat[...] = ga[...].T
    c.wait()
    assemble_pairs(w, wp, feats)
    wt[:, pl.ds(0, 128)] = w[0, :, pl.ds(640, 128)]
    wt[:, pl.ds(128, 128)] = w[1, :, pl.ds(640, 128)]
    lo = lax.broadcasted_iota(jnp.int32, (feats, 128), 1) < 64
    wt[:, pl.ds(256, 128)] = jnp.where(lo, pltpu.roll(w[0, :, pl.ds(512, 128)].astype(F32), 64, 1), w[1, :, pl.ds(512, 128)].astype(F32)).astype(BF)
    for p in range(3):
        gm[p] = nn(ga[...], wt[:, pl.ds(128 * p, 128)]).astype(BF)

    def pair(p, _):
        ktt[...] = kt[p].T
        prod = (gm[p].astype(F32) * mixed[p].astype(F32)).T
        dd[0:1, :] = jnp.sum(prod[:64, :], axis=0, keepdims=True)
        dd[1:2, :] = jnp.sum(prod[64:, :], axis=0, keepdims=True)
        dv[...] = jnp.zeros_like(dv)
        dk[...] = jnp.zeros_like(dk)
        for e in range(2):
            lanes = (tn_lanes() < 64) if e == 0 else (tn_lanes() >= 64)
            for q0, qn, spans in tiles(rows, length):
                q = qt[p, pl.ds(q0, qn), :]
                qm = jnp.where(lanes, q, jnp.zeros_like(q))
                g = gm[p, pl.ds(q0, qn), :]
                gmm = jnp.where(lanes, g, jnp.zeros_like(g))
                ss = scores_of(kt, qm, idk, idq[0:1, pl.ds(q0, qn)], p, spans)
                l = lse[p, e, :, pl.ds(q0, qn)]
                d = dd[pl.ds(e, 1), pl.ds(q0, qn)]
                acc = None
                for s, (k0, kn, _) in zip(ss, spans):
                    pr = jnp.exp(s - l)
                    dp = nt(vt[p, pl.ds(k0, kn), :], gmm)
                    ds = (pr * (dp - d)).astype(BF)
                    dv[pl.ds(k0, kn), :] += nn(pr.astype(BF), gmm)
                    dk[pl.ds(k0, kn), :] += nn(ds, qm)
                    o = nn(ktt[pl.ds(64 * e, 64), pl.ds(k0, kn)], ds)
                    acc = o if acc is None else acc + o
                dqt[pl.ds(64 * e, 64), pl.ds(q0, qn)] = acc * 0.125
        gp[p, :, pl.ds(0, 128)] = dqt[...].T.astype(BF)
        gp[p, :, pl.ds(128, 128)] = dk[...].astype(BF)
        gp[p, :, pl.ds(256, 128)] = dv[...].astype(BF)
        return 0
    lax.fori_loop(0, 3, pair, 0)
    for p in range(3):
        bgrad[p] = group_sum(gp[p].astype(F32))
    r3 = rows // 3

    def rowsgrad(i, _):
        r = pl.ds(pl.multiple_of(i * r3, 16), r3)
        gpart[r, :] = nt(gp[0, r, :], wp[0]) + nt(gp[1, r, :], wp[1]) + nt(gp[2, r, :], wp[2])
        return 0
    lax.fori_loop(0, 3, rowsgrad, 0)
    fc = 256
    for f0 in range(0, feats, fc):
        f = pl.ds(f0, fc)
        xf = xt[f, pl.ds(0, rows)]
        af = gat[f, :]
        r0 = nn(xf, gp[0]); r1 = nn(xf, gp[1]); r2 = nn(xf, gp[2])
        o = [nn(af, mixed[p]) for p in range(3)]
        lo = lax.broadcasted_iota(jnp.int32, (fc, 128), 1) < 64
        rq, rk, rv = r2[:, :128], r2[:, 128:256], r2[:, 256:]
        sw = lambda a: pltpu.roll(a, 64, 1)
        gown[0, f, pl.ds(0, 384)] = r0.astype(BF)
        gown[1, f, pl.ds(0, 384)] = r1.astype(BF)
        gown[0, f, pl.ds(384, 128)] = jnp.where(lo, rq, sw(rk)).astype(BF)
        gown[1, f, pl.ds(384, 128)] = jnp.where(lo, sw(rq), rk).astype(BF)
        gown[0, f, pl.ds(512, 128)] = jnp.where(lo, rv, sw(o[2])).astype(BF)
        gown[1, f, pl.ds(512, 128)] = jnp.where(lo, sw(rv), o[2]).astype(BF)
        gown[0, f, pl.ds(640, 128)] = o[0].astype(BF)
        gown[1, f, pl.ds(640, 128)] = o[1].astype(BF)
    c = pltpu.make_async_copy(gown, gown_hbm, sem); c.start(); c.wait()

def attn_bwd(ga, mixed, xt, qt, kt, vt, lse, idk, idq, wa):
    feats = xt.shape[0]; rows = ga.shape[0]
    V = lambda *s, d=BF: pltpu.VMEM(s, d)
    vm = pl.BlockSpec(memory_space=pltpu.VMEM); an = pl.BlockSpec(memory_space=pl.ANY)
    S = jax.ShapeDtypeStruct
    return pl.pallas_call(attn_bwd_kernel,
        out_shape=(S((rows, feats), F32), S((3, 8, 384), F32), S(wa.shape, BF)),
        in_specs=[vm] * 9 + [an], out_specs=(vm, vm, an),
        scratch_shapes=[V(*wa.shape), V(3, feats, 384), V(feats, 384), V(feats, rows), V(3, rows, 128), V(3, rows, 384), V(rows, 128, d=F32), V(rows, 128, d=F32),
            V(128, rows, d=F32), V(128, rows), V(8, rows, d=F32), V(8, 128), V(*wa.shape), pltpu.SemaphoreType.DMA],
        compiler_params=pltpu.CompilerParams(vmem_limit_bytes=63*2**20))(ga, mixed, xt, qt, kt, vt, lse, idk, idq, wa)
MESH = pl.DeviceIdType.MESH

class Move:
    def __init__(self, net, src, dst, dev, index):
        self.net, self.src, self.dst, self.dev, self.index = net, src, dst, dev, index
    def make(self):
        return pltpu.make_async_remote_copy(src_ref=self.src(), dst_ref=self.dst(), send_sem=self.net.ss.at[self.index],
                                            recv_sem=self.net.rs.at[self.index], device_id=self.dev, device_id_type=MESH)
    def start(self):
        self.make().start()
    def wait_recv(self):
        self.make().wait_recv()
    def wait_send(self):
        self.make().wait_send()

class Copy:
    def __init__(self, net, src, dst, index):
        self.net, self.src, self.dst, self.index = net, src, dst, index
    def make(self):
        return pltpu.make_async_copy(self.src(), self.dst(), self.net.ls.at[self.index])
    def start(self):
        self.make().start()
    def wait(self):
        self.make().wait()

class Net:
    def __init__(self, send_sems, recv_sems, local_sems):
        self.ss, self.rs, self.ls = send_sems, recv_sems, local_sems
        self.count, self.locals, self.moves, self.copies = 0, 0, [], []
        self.d, self.z, self.c = (lax.axis_index(a) for a in ("dp", "row", "col"))
        self.nd, self.nz = lax.axis_size("dp"), lax.axis_size("row")
        self.y, self.k = self.c // 2, self.c % 2
        self.x = self.d % 2
        self.oc = lax.rem(self.c + 2, 4)
        self.xp = (self.d + 1 - 2 * self.x, self.z, self.c)
        self.yp = (self.d, self.z, self.oc)
        self.kp = (self.d, self.z, self.c + 1 - 2 * self.k)
        self.ykp = (self.d, self.z, 3 - self.c)
        self.zs = [lax.rem(self.z + i, self.nz) for i in range(self.nz)]
        self.zp = [(self.d, zz, self.c) for zz in self.zs]
        self.others = [(lax.rem(self.d + 2 * i, self.nd), self.z, self.c) for i in range(1, self.nd // 2)]
    def from_row(self, i):
        return self.zs[(self.nz - i) % self.nz]
    def hello(self, peers):
        b = pltpu.get_barrier_semaphore()
        for p in peers:
            pl.semaphore_signal(b, inc=1, device_id=p, device_id_type=MESH)
    def await_hello(self, peers):
        pl.semaphore_wait(pltpu.get_barrier_semaphore(), len(peers))
    def barrier(self, peers):
        self.hello(peers)
        self.await_hello(peers)
    def move(self, src, dst, dev):
        m = Move(self, src, dst, dev, self.count)
        self.count += 1
        self.moves.append(m)
        return m
    def send(self, src, dst, dev):
        m = self.move(src, dst, dev)
        m.start()
        return m
    def copy(self, src, dst):
        m = Copy(self, src, dst, self.locals)
        self.locals += 1
        self.copies.append(m)
        return m
    def local(self, src, dst):
        m = self.copy(src, dst)
        m.start()
        return m
    def finish(self):
        for m in self.moves:
            m.wait_send()

def at(i, table):
    for j, events in table.items():
        if events:
            @pl.when(i == j)
            def _(events=events):
                for e in events:
                    e()

def spread_events(events, steps):
    table = {}
    for n, e in enumerate(events):
        table.setdefault(n * steps // len(events), []).append(e)
    return table

def join192(t, dst):
    lo = lax.broadcasted_iota(jnp.int32, t[0][0].shape, 1) < 64
    sw = lambda a: pltpu.roll(a, 64, 1)
    for h in range(2):
        a, b = t[2 * h], t[2 * h + 1]
        dst[:, pl.ds(384 * h, 128)] = a[0]
        dst[:, pl.ds(384 * h + 128, 128)] = jnp.where(lo, a[1], sw(b[0]))
        dst[:, pl.ds(384 * h + 256, 128)] = jnp.where(lo, sw(b[0]), sw(b[1]))

def row_ids(ids, y, half, idk, idq):
    length = ids.shape[1]
    idq[:, pl.ds(0, length)] = ids[pl.ds(y, 1), :].astype(F32)
    i = lax.broadcasted_iota(jnp.int32, (1, 128), 1)
    idq[:, pl.ds(length, 128)] = jnp.where(i < half, -1.0, jnp.where(i < 2 * half, 1.0 * length, 2.0 * length))
    for j in range(length // 128 + 1):
        idk[pl.ds(128 * j, 128), :] = jnp.broadcast_to(idq[:, pl.ds(128 * j, 128)], (128, 128)).T

def pack_inputs(w3, wo, la, vecs, bias_up, bias_qv, scale, ls, memory, mtmp, mem):
    b = w3.shape[1]
    f = lambda r: r.astype(F32)
    lo = lax.broadcasted_iota(jnp.int32, (b, 128), 1) < 64
    t0, t1 = f(w3[0, :, pl.ds(0, 128)]), f(w3[1, :, pl.ds(0, 128)])
    la[:, pl.ds(0, 128)] = jnp.where(lo, t0, pltpu.roll(t1, 64, 1)).astype(BF)
    la[:, pl.ds(128, 128)] = jnp.where(lo, pltpu.roll(t0, 64, 1), t1).astype(BF)
    v = [f(w3[j, :, pl.ds(128, 64)]) for j in range(3)]
    la[:, pl.ds(256, 128)] = jnp.concatenate([v[0], v[1]], axis=1).astype(BF)
    la[:, pl.ds(384, 128)] = w3[2, :, pl.ds(0, 128)]
    wot = f(wo[...]).T
    la[:, pl.ds(512, 128)] = jnp.concatenate([v[2], wot[:, 128:]], axis=1).astype(BF)
    la[:, pl.ds(640, 128)] = wot[:, :128].astype(BF)
    ls[...] = jnp.zeros_like(ls)
    for j, r in enumerate(vecs):
        ls[pl.ds(j, 1), pl.ds(0, b)] = r[...]
    ls[pl.ds(6, 1), :] = scale
    for j in range(3):
        ls[pl.ds(8 + j, 1), :] = bias_up[:, pl.ds(256 * j, 256)]
    ls[pl.ds(11, 1), pl.ds(0, 128)] = bias_qv[0:1, :]
    ls[pl.ds(11, 1), pl.ds(128, 128)] = bias_qv[1:2, :]
    ls[pl.ds(12, 1), pl.ds(0, 128)] = bias_qv[2:3, :]
    mtmp[...] = jnp.zeros_like(mtmp)
    for s in range(2):
        mtmp[pl.ds(0, memory.shape[1]), :] = f(memory[s])
        mem[s] = mtmp[...].T.astype(BF)

def forward_kernel(valid_ref, tok, memory, tch, w3, wo, lu, ld, v0, v1, v2, v3, v4, v5, bias_up, bias_qv, ids,
                   xt_o, q_o, k_o, v_o, mixed_o, wa_o, ga_o, hu_o, hd_o, lse, g_one, vgrad, bupgrad, out4,
                   xt, x, wa, wu, wd, sm, tt, tr, wp, qt, kt, vt, vtt, ot, mixed, mrows, bias, vec, wt,
                   h1, h2, rs1, low, lowt, br, brt, hid, dgl, gdz, guz, hu, hd, ru, rd, ga, o4, la, ls, mem, mtmp, idk, idq, ss, rs, lsem, zsem, zrem):
    n = Net(ss, rs, lsem)
    peers = n.zp[1:] + [n.yp, n.ykp, n.kp, n.xp]
    n.hello(peers)
    total = lax.fori_loop(0, valid_ref.shape[0], lambda i, t: t + valid_ref[i], jnp.int32(0))
    count = valid_ref[(n.d * n.nz + n.z) * 2 + n.y]
    scale_row = (valid_ref.shape[0] * tok.shape[2]) / jnp.full((1, 256), total, jnp.int32).astype(F32)
    pack_inputs(w3, wo, la, (v0, v1, v2, v3, v4, v5), bias_up, bias_qv, scale_row, ls, memory, mtmp, mem)
    n.await_hello(peers)
    nz, y, k, c, z, oc = n.nz, n.y, n.k, n.c, n.z, n.oc
    b = la.shape[0]; hb = b // 2
    feats = x.shape[1]; rows = x.shape[0]; length = tok.shape[2]; main = length // 2
    own_rows = main + 16
    row = lambda cc, off=0, num=b: pl.ds(pl.multiple_of(cc * b + off, 16), num)
    blk = lambda w, zz, cc: (lambda: w.at[zz, row(cc)])
    hlf = lambda w, zz, cc, h: (lambda: w.at[zz, row(cc, h * hb, hb)])
    mine, theirs = n.x, 1 - n.x
    part = lambda w: (lambda: w.at[pl.ds(pl.multiple_of(n.x * hb, 16), hb)])
    all_of = lambda r: (lambda: r)
    tail = pl.ds(length, 128); body = pl.ds(0, length)
    fz = n.from_row
    R = range(1, nz)
    e1 = z + 1 - 2 * lax.rem(z, 2)
    e2 = lax.rem(z + 2, nz)
    e3 = lax.rem(e1 + 2, nz)
    dev1, dev2 = (n.d, e1, c), (n.d, e2, c)
    order = [z, e2, e1, e3]
    s_blk = lambda zz, cc: (lambda: sm.at[zz, cc])
    fwd = lambda u, dev: n.move(u, u, dev)
    local = [n.local(lambda: tok.at[y], lambda: xt.at[row(c), body]), n.local(lambda: mem.at[y], lambda: xt.at[row(c), tail])]
    au = lambda zz, cc: hlf(wa, zz, cc, mine)
    a2 = n.send(part(la), au(z, c), dev2)
    a1 = n.send(part(la), au(z, c), dev1)
    a_y = [n.send(part(la), au(z, c), n.yp)]
    a_k = [n.send(all_of(la), blk(wa, z, c), n.kp)]
    s_z = [n.send(all_of(ls), s_blk(z, c), n.zp[i]) for i in R]
    s_y = [n.send(all_of(ls), s_blk(z, c), n.yp)]
    s_k = [n.send(all_of(ls), s_blk(z, c), n.kp)]
    t_k = [n.send(lambda: tok.at[y], lambda: xt.at[row(c), body], n.kp), n.send(lambda: mem.at[y], lambda: xt.at[row(c), tail], n.kp)]
    for w, l in ((wa, la), (wu, lu), (wd, ld)):
        local.append(n.local(all_of(l), blk(w, z, c)))
    local.append(n.local(all_of(ls), s_blk(z, c)))
    a_x, a_xu = [], []
    def pass_on(u, lists):
        for lst, dev in lists:
            lst.append(fwd(u, dev)); lst[-1].start()
    def a_own(zz):
        a_xu.append((zz, c))
        pass_on(au(zz, c), ((a_x, n.xp), (a_y, n.yp), (a_k, n.kp)))
    def a_far(i):
        a_y[i].wait_recv()
        a_xu.append((order[i], oc))
        pass_on(au(order[i], oc), ((a_x, n.xp), (a_k, n.kp)))
    def a_home(i):
        a_x[i].wait_recv()
        pass_on(hlf(wa, *a_xu[i], theirs), ((a_k, n.kp),))
    first, second = pl.ds(0, main), pl.ds(main, main)
    t_y = [n.send(lambda: tok.at[1 - y, :, first], lambda: xt.at[row(c), first], n.yp), n.send(lambda: mem.at[1 - y], lambda: xt.at[row(c), tail], n.yp)]
    def t_pass(i, w_):
        t_y[i].wait_recv()
        t_k.append(fwd(lambda: xt.at[row(oc), w_], n.kp)); t_k[-1].start()
    a_far(0)
    a2.wait_recv()
    a3 = fwd(au(e2, c), dev1); a3.start()
    a_own(e2)
    a1.wait_recv()
    a_own(e1)
    a_far(1)
    for i in R:
        s_z[i - 1].wait_recv()
        pass_on(s_blk(fz(i), c), ((s_y, n.yp), (s_k, n.kp)))
    a3.wait_recv()
    a_own(e3)
    t_y.append(n.send(lambda: tok.at[1 - y, :, second], lambda: xt.at[row(c), second], n.yp))
    t_pass(0, first)
    t_pass(1, tail)
    uu = lambda zz, cc: blk(wu, zz, cc)
    du = lambda zz, cc: hlf(wd, zz, cc, mine)
    u2 = n.send(all_of(lu), uu(z, c), dev2)
    u1 = n.send(all_of(lu), uu(z, c), dev1)
    d_y = n.send(part(ld), du(z, c), n.yp)
    u_y = [n.send(all_of(lu), uu(z, c), n.yp)]
    u_k = {0: n.send(all_of(lu), uu(z, c), n.kp)}
    d_k = [n.send(all_of(ld), blk(wd, z, c), n.kp)]
    tsl = lambda s, kk: (lambda: tch.at[s, :, pl.ds(pl.multiple_of(kk * main, 128), main)])
    th = lambda: tt.at[row(c)]
    h_y = [n.send(tsl(y, 1 - k), th, n.kp)]
    local.append(n.local(tsl(y, k), th))
    a_far(2)
    a_far(3)
    row_ids(ids, y, memory.shape[1] // 2, idk, idq)
    for i in range(3):
        a_home(i)
    for i in range(nz):
        s_y[i].wait_recv()
        pass_on(s_blk(fz(i), oc), ((s_k, n.kp),))
    local[0].wait(); local[1].wait()
    a_home(3)
    t_pass(2, second)
    a_home(4)
    for m in t_k:
        m.wait_recv()
    def turn(i, _):
        f = pl.ds(pl.multiple_of(128 * i, 128), 128)
        x[f, :] = xt[:, f].T
        return 0
    lax.fori_loop(0, length // 128, turn, 0)
    x[pl.ds(length, rows - length), :] = xt[:, tail].T[: rows - length, :]
    o_x = n.local(all_of(xt), all_of(xt_o))
    u2.wait_recv()
    u3 = fwd(uu(e2, c), dev1); u3.start()
    d2 = n.send(part(ld), du(z, c), dev2)
    d1 = n.send(part(ld), du(z, c), dev1)
    def u_put(i, cc, y_too=True):
        m = fwd(uu(order[i], cc), n.kp)
        u_k[(i, cc is oc)] = m
        if y_too:
            u_y.append(fwd(uu(order[i], cc), n.yp))
            u_y[-1].start()
        m.start()
    u_put(1, c)
    d_x, d_xu = [], []
    def d_put(zz, cc):
        d_xu.append((zz, cc))
        d_x.append(fwd(du(zz, cc), n.xp)); d_k.append(fwd(du(zz, cc), n.kp))
        return [d_x[-1], d_k[-1]]
    d_own = d_put(z, oc)
    for i in range(5, 7):
        a_home(i)
    def step(wait, moves):
        def run():
            wait.wait_recv()
            for m in moves:
                m.start()
        return run
    def u_step(wait, i):
        u_y.append(fwd(uu(order[i], c), n.yp))
        u_w.append(fwd(uu(order[i], c), n.kp))
        return step(wait, [u_y[-1], u_w[-1]])
    u_w = list(u_k.values())
    def u_far(i):
        u_w.append(fwd(uu(order[i], oc), n.kp))
        return step(u_y[i], [u_w[-1]])
    E_dy = step(d_y, d_own)
    d3, d2o, d1o, d3o = fwd(du(e2, c), dev1), fwd(du(z, oc), dev2), fwd(du(z, oc), dev1), fwd(du(e2, oc), dev1)
    E_u1 = u_step(u1, 2)
    E_u3 = u_step(u3, 3)
    h_m = [n.move(tsl(1 - y, k), th, n.yp), n.move(tsl(1 - y, 1 - k), th, n.ykp)]
    def E_h():
        for m in h_m:
            m.start()
    h_y += h_m
    E_uy = [u_far(i) for i in range(4)]
    E_d2 = step(d2, [d3] + d_put(e2, c))
    def E_do():
        d2o.start(); d1o.start()
    E_d1 = step(d1, d_put(e1, c))
    E_d3 = step(d3, d_put(e3, c))
    E_d2o = step(d2o, [d3o] + d_put(e2, oc))
    E_d1o = step(d1o, d_put(e1, oc))
    E_d3o = step(d3o, d_put(e3, oc))
    E_dx = []
    for m, (zz, cc) in zip(d_x, d_xu):
        d_k.append(fwd(hlf(wd, zz, cc, theirs), n.kp))
        E_dx.append(step(m, [d_k[-1]]))
    proj_events = {0: [E_dy], 1: [E_u1]}
    head_events = {2: [E_do, E_dx[0]], 4: [E_uy[0], E_u3, E_h], 6: [E_d2], 8: [E_d1], 10: [E_uy[1]], 14: [E_d3, E_d2o], 15: [E_uy[2], E_dx[1], E_dx[2]], 17: [E_d1o]}
    out_events = [E_d3o, E_dx[3]]
    gate_events = {0: [], 3: [], 6: [E_dx[4], E_dx[5]], 9: [E_dx[6]]}
    for m in s_k:
        m.wait_recv()
    for m in local[2:6]:
        m.wait()
    join192([[sm[0, cc, pl.ds(0, 8), pl.ds(0, 128)], sm[0, cc, pl.ds(0, 8), pl.ds(128, 128)]] for cc in range(4)], vec)
    lo1 = lax.broadcasted_iota(jnp.int32, (1, 128), 1) < 64
    sw = lambda a: pltpu.roll(a, 64, 1)
    bias[...] = jnp.zeros_like(bias)
    hv = [[sm[2 * k + j, 0, 11:12, pl.ds(0, 128)], sm[2 * k + j, 0, 11:12, pl.ds(128, 128)], sm[2 * k + j, 0, 12:13, pl.ds(0, 128)]] for j in range(2)]
    for p, (ea, eb) in enumerate(((hv[0][0], hv[0][1]), (hv[1][0], hv[1][1]), (hv[0][2], hv[1][2]))):
        w8 = lambda a: jnp.broadcast_to(a, (8, 128))
        lo8 = lax.broadcasted_iota(jnp.int32, (8, 128), 1) < 64
        bias[p, :, pl.ds(0, 128)] = jnp.where(lo8, w8(ea), sw(w8(eb)))
        bias[p, :, pl.ds(256, 128)] = jnp.where(lo8, sw(w8(ea)), w8(eb))
    for m in a_k:
        m.wait_recv()
    own = pl.ds(2 * k, 2)
    o_w = n.local(lambda: wa.at[own], all_of(wa_o))
    w = wa.at[own]
    assemble_pairs(w, wp, feats)
    rc = rows // 3

    def project(i, _):
        p = i // 3
        r = pl.ds(pl.multiple_of((i % 3) * rc, 16), rc)
        v = nn(x[r, :], wp[p]) + bias[p, 0:1, :]
        qt[p, r, :] = (v[:, :128].astype(BF).astype(F32) * 0.125).astype(BF)
        kt[p, r, :] = v[:, 128:256].astype(BF)
        vt[p, r, :] = v[:, 256:].astype(BF)
        at(i, proj_events)
        return 0
    lax.fori_loop(0, 9, project, 0)
    o_q = [n.local(all_of(a), all_of(o)) for a, o in ((qt, q_o), (kt, k_o), (vt, v_o))]
    m_k = [(n.move((lambda p=p: mixed.at[p, pl.ds(pl.multiple_of((1 - k) * main, 16), main)]), (lambda p=p: mrows.at[k * 3 + p, pl.ds(0, main)]), n.kp),
            n.move((lambda p=p: mixed.at[p, pl.ds(pl.multiple_of(length + (1 - k) * 16, 16), 16)]), (lambda p=p: mrows.at[k * 3 + p, pl.ds(main, 16)]), n.kp)) for p in range(3)]
    m_l = [(n.copy((lambda p=p: mixed.at[p, pl.ds(pl.multiple_of(k * main, 16), main)]), (lambda p=p: mrows.at[k * 3 + p, pl.ds(0, main)])),
            n.copy((lambda p=p: mixed.at[p, pl.ds(pl.multiple_of(length + k * 16, 16), 16)]), (lambda p=p: mrows.at[k * 3 + p, pl.ds(main, 16)]))) for p in range(3)]
    cuts = {1: 0, 3: 1, 4: 2}

    def head(i, _):
        p = i // 2
        e = i % 2
        he = pl.ds(pl.multiple_of(64 * e, 64), 64)

        @pl.when(e == 0)
        def _():
            vtt[...] = vt[p].T
        lanes = (lax.broadcasted_iota(jnp.int32, (1, 128), 1) // 64) == e
        for t_, (q0, qn, spans) in enumerate(tiles(rows, length)):
            q = qt[p, pl.ds(q0, qn), :]
            qm = jnp.where(lanes, q, jnp.zeros_like(q))
            sc = scores_of(kt, qm, idk, idq[0:1, pl.ds(q0, qn)], p, spans)
            m = jnp.max(sc[0], axis=0, keepdims=True)
            for s in sc[1:]:
                m = jnp.maximum(m, jnp.max(s, axis=0, keepdims=True))
            tot, acc = None, None
            for s, (k0, kn, _) in zip(sc, spans):
                ex = jnp.exp(s - m)
                t = jnp.sum(ex, axis=0, keepdims=True)
                o = nn(vtt[he, pl.ds(k0, kn)], ex.astype(BF))
                tot = t if tot is None else tot + t
                acc = o if acc is None else acc + o
            ot[he, pl.ds(q0, qn)] = acc / tot
            lse[i, :, pl.ds(q0, qn)] = m + jnp.log(tot)
            if t_ in cuts:
                at(3 * i + cuts[t_], head_events)

        @pl.when(e == 1)
        def _():
            mixed[p] = ot[...].T.astype(BF)
        at(i, {2 * p + 1: [m.start for m in m_k[p] + m_l[p]] for p in range(3)})
        return 0
    lax.fori_loop(0, 6, head, 0)
    o_m = n.local(all_of(mixed), all_of(mixed_o))
    lo = lax.broadcasted_iota(jnp.int32, (feats, 128), 1) < 64
    for kk in range(2):
        z0, z1 = 2 * kk, 2 * kk + 1
        wt[:, pl.ds(384 * kk, 128)] = wa[z0, :, pl.ds(640, 128)]
        wt[:, pl.ds(384 * kk + 128, 128)] = wa[z1, :, pl.ds(640, 128)]
        t0 = pltpu.roll(wa[z0, :, pl.ds(512, 128)].astype(F32), 64, 1)
        wt[:, pl.ds(384 * kk + 256, 128)] = jnp.where(lo, t0, wa[z1, :, pl.ds(512, 128)].astype(F32)).astype(BF)
    for pair_ in m_k:
        for m in pair_:
            m.wait_recv()
    for pair_ in m_l:
        for m in pair_:
            m.wait()
    nb = feats // 256
    CHS = own_rows // CH

    def own_slice(i, num):
        start = jnp.where(i < main, k * main + i, length + k * 16)
        return pl.ds(pl.multiple_of(start, 16), num)

    for f0 in range(0, feats, 256):
        f = pl.ds(f0, 256)
        acc = nt(mrows[0], wt[f, pl.ds(0, 128)])
        for j in range(1, 6):
            acc = acc + nt(mrows[j], wt[f, pl.ds(128 * j, 128)])
        h1[:, f] = acc + vec[0:1, f]
    for e in out_events:
        e()
    inv = 1.0 / feats
    vgrad[...] = jnp.zeros_like(vgrad)
    bupgrad[...] = jnp.zeros_like(bupgrad)

    def norm1(i, _):
        r = pl.ds(pl.multiple_of(i * 16, 16), 16)
        h = h1[r, :] + x[own_slice(i * 16, 16), :].astype(F32)
        m = jnp.sum(h, axis=1, keepdims=True) * inv
        s = jnp.sum(h * h, axis=1, keepdims=True) * inv
        rstd = lax.rsqrt(s - m * m + EPSILON)
        xhat = (h - m) * rstd
        h1[r, :] = xhat
        rs1[r, :] = jnp.broadcast_to(rstd, (16, 128))
        low[r, :] = (xhat * vec[1:2, :] + vec[2:3, :]).astype(BF)
        return 0
    lax.fori_loop(0, own_rows // 16, norm1, 0, unroll=3)
    lowt[...] = low[...].T
    E_uy[3]()
    for m in u_w:
        m.wait_recv()

    def gate(i, _):
        at(i, gate_events)
        zz = i // nb
        j = i % nb
        f = pl.ds(pl.multiple_of(j * 256, 256), 256)
        v = nn(low[...], wu[zz, :, f]) + sm[zz, 0, pl.ds(8 + j, 1), :]
        a, g = gelu_pair(v)
        hid[zz, :, f] = a.astype(BF)
        dgl[zz, :, f] = g.astype(BF)
        return 0
    lax.fori_loop(0, nz * nb, gate, 0)
    for m in h_y:
        m.wait_recv()
    local[6].wait()
    def turn_t(i, _):
        f = pl.ds(pl.multiple_of(128 * i, 128), 128)
        tr[f, :] = tt[:, f].T
        return 0
    lax.fori_loop(0, main // 128, turn_t, 0)
    tr[pl.ds(main, 16), :] = jnp.zeros((16, feats), BF)
    for m in d_k:
        m.wait_recv()

    def down(j, _):
        f = pl.ds(pl.multiple_of(j * 256, 256), 256)
        acc = nt(hid[0], wd[0, f, :])
        for zz in range(1, nz):
            acc = acc + nt(hid[zz], wd[zz, f, :])
        h2[:, f] = acc
        return 0
    lax.fori_loop(0, nb, down, 0)
    scale = vec[6:7, 0:1]
    o4[:, :, pl.ds(b, o4.shape[2] - b)] = jnp.zeros((4, own_rows, o4.shape[2] - b), BF)

    def norm2(i, _):
        r = pl.ds(pl.multiple_of(i * CH, 16), CH)
        h = h2[r, :] + (h1[r, :] * vec[1:2, :] + vec[2:3, :]) + vec[3:4, :]
        m = jnp.sum(h, axis=1, keepdims=True) * inv
        s = jnp.sum(h * h, axis=1, keepdims=True) * inv
        rstd = lax.rsqrt(s - m * m + EPSILON)
        xhat = (h - m) * rstd
        o = xhat * vec[4:5, :] + vec[5:6, :]
        for cc in range(4):
            o4[cc, r, pl.ds(0, b)] = o[:, cc * b:(cc + 1) * b].astype(BF)
        place = lax.broadcasted_iota(jnp.int32, (CH, 1), 0) + i * CH
        place = jnp.where(place < main, place + k * main, count)
        go = jnp.where(place < count, scale * (o - tr[r, :].astype(F32)), 0.0)
        a = go * vec[4:5, :]
        m1 = jnp.sum(a, axis=1, keepdims=True) * inv
        m2 = jnp.sum(a * xhat, axis=1, keepdims=True) * inv
        g2 = rstd * (a - m1 - xhat * m2)
        h2[r, :] = g2
        g2b = g2.astype(BF)
        br[r, :] = g2b
        vgrad[0] += group_sum(go * xhat)
        vgrad[1] += group_sum(go)
        vgrad[2] += group_sum(g2b.astype(F32))
        return 0
    lax.fori_loop(0, CHS, norm2, 0)
    o_dst = lambda: out4.at[y, k]
    o_s = [n.send(lambda: o4.at[oc], o_dst, n.yp), n.send(lambda: o4.at[3 - c], o_dst, n.ykp), n.send(lambda: o4.at[c + 1 - 2 * k], o_dst, n.kp)]
    o_l = n.local(lambda: o4.at[c], o_dst)
    brt[...] = br[...].T
    def gmove(which, src, dst, zz, slot, yy):
        return pltpu.make_async_remote_copy(src_ref=src.at[slot, 2 * yy + 1 - k], dst_ref=dst.at[yy, zz], send_sem=zsem.at[which, yy, zz],
                                            recv_sem=zrem.at[which, yy, zz], device_id=n.kp, device_id_type=MESH)
    def each(fn, zz, slot):
        for which, src, dst in ((0, gdz, rd), (1, guz, ru)):
            for yy in range(2):
                fn(gmove(which, src, dst, zz, slot, yy))
    def fold(zz):
        each(lambda m: m.wait_recv(), zz, 0)
        for yy in range(2):
            add_to(hd.at[yy, zz], rd.at[yy, zz])
            add_to(hu.at[yy, zz], ru.at[yy, zz])

    def back(zz, _):
        slot = zz % 2

        @pl.when(zz >= 2)
        def _():
            each(lambda m: m.wait_send(), zz - 2, slot)

        def chunk(j, _):
            f = pl.ds(pl.multiple_of(j * 256, 256), 256)
            gh = nn(br[...], wd[zz, :, f])
            g = (gh * dgl[zz, :, f].astype(F32)).astype(BF)
            bupgrad[zz, :, f] += group_sum(g.astype(F32))
            gdc = nn(brt[...], hid[zz, :, f])
            guc = nn(lowt[...], g)
            hid[zz, :, f] = g
            for cc in range(4):
                gdz[slot, cc, :, f] = gdc[cc * b:(cc + 1) * b, :].astype(BF)
                guz[slot, cc, :, f] = guc[cc * b:(cc + 1) * b, :].astype(BF)
            return 0
        lax.fori_loop(0, nb, chunk, 0)
        each(lambda m: m.start(), zz, slot)
        for yy in range(2):
            hd[yy, zz] = gdz[slot, 2 * yy + k]
            hu[yy, zz] = guz[slot, 2 * yy + k]

        @pl.when(zz >= 1)
        def _():
            fold(zz - 1)
        return 0
    lax.fori_loop(0, nz, back, 0)

    def first_grad(j, _):
        f = pl.ds(pl.multiple_of(j * 256, 256), 256)
        acc = h2[:, f]
        for zz in range(nz):
            acc = acc + nt(hid[zz], wu[zz, f, :])
        h2[:, f] = acc
        return 0
    lax.fori_loop(0, nb, first_grad, 0)
    fold(nz - 1)
    o_h = [n.local(all_of(hd), all_of(hd_o)), n.local(all_of(hu), all_of(hu_o))]

    def norm1_back(i, _):
        r = pl.ds(pl.multiple_of(i * 16, 16), 16)
        g = h2[r, :]
        xhat = h1[r, :]
        a = g * vec[1:2, :]
        m1 = jnp.sum(a, axis=1, keepdims=True) * inv
        m2 = jnp.sum(a * xhat, axis=1, keepdims=True) * inv
        g1 = rs1[r, 0:1] * (a - m1 - xhat * m2)
        g_one[r, :] = g1
        gb = g1.astype(BF)
        ga[own_slice(i * 16, 16), :] = gb
        vgrad[3] += group_sum(g * xhat)
        vgrad[4] += group_sum(g)
        vgrad[5] += group_sum(gb.astype(F32))
        return 0
    early = main // 16 // 6 * 3
    g_rows = lambda start, num: (lambda: ga.at[pl.ds(pl.multiple_of(k * main + start, 16), num)])
    g_tail = lambda: ga.at[pl.ds(pl.multiple_of(length + k * 16, 16), 16)]
    g_first, g_rest = g_rows(0, early * 16), g_rows(early * 16, main - early * 16)
    lax.fori_loop(0, early, norm1_back, 0, unroll=3)
    g_k = [n.send(g_first, g_first, n.kp)]
    lax.fori_loop(early, own_rows // 16, norm1_back, 0, unroll=3)
    g_k += [n.send(g_rest, g_rest, n.kp), n.send(g_tail, g_tail, n.kp)]
    for m in g_k:
        m.wait_recv()
    o_g = n.local(all_of(ga), all_of(ga_o))
    for m in o_s:
        m.wait_recv()
    for m in [o_x, o_w, o_m, o_l, o_g] + o_q + o_h:
        m.wait()
    for zz in range(nz - 2, nz):
        each(lambda m: m.wait_send(), zz, zz % 2)
    n.finish()

def add_to(dst, src):
    dst[...] = (dst[...].astype(F32) + src[...].astype(F32)).astype(BF)

def forward(valid, tok, memory, tch, w3, wo, lu, ld, vecs, bias_up, bias_qv, ids, nz):
    b, width = lu.shape
    feats = 4 * b; length = tok.shape[2]; rows = length + 32; main = length // 2; own = main + 16
    V = lambda *s, d=BF: pltpu.VMEM(s, d)
    vm = pl.BlockSpec(memory_space=pltpu.VMEM); sm = pl.BlockSpec(memory_space=pltpu.SMEM); an = pl.BlockSpec(memory_space=pl.ANY)
    S = jax.ShapeDtypeStruct
    t3 = S((3, rows, 128), BF); h = S((2, nz, b, width), BF)
    outs = [(S((feats, length + 128), BF), an), (t3, an), (t3, an), (t3, an), (t3, an), (S((2, feats, width), BF), an), (S((rows, feats), BF), an), (h, an), (h, an),
            (S((6, 1, rows), F32), vm), (S((own, feats), F32), vm), (S((6, 8, feats), F32), vm), (S((nz, 8, width), F32), vm), (S((2, 2, own, 256), BF), vm)]
    w = V(nz, feats, width)
    scratch = [V(feats, length + 128), V(rows, feats), w, w, w, V(nz, 4, 16, 256, d=F32), V(feats, main), V(own, feats), V(3, feats, 384),
               V(3, rows, 128), V(3, rows, 128), V(3, rows, 128), V(128, rows), V(128, rows, d=F32), V(3, rows, 128), V(6, own, 128), V(3, 8, 384, d=F32), V(8, feats, d=F32), V(feats, feats),
               V(own, feats, d=F32), V(own, feats, d=F32), V(own, 128, d=F32), V(own, feats), V(feats, own), V(own, feats), V(feats, own),
               V(nz, own, width), V(nz, own, width), V(2, 4, b, width), V(2, 4, b, width)] + [V(2, nz, b, width)] * 4 + [V(rows, feats), V(4, own, 256), V(b, width), V(16, 256, d=F32), V(2, b, 128), V(128, b, d=F32), V(length + 128, 128, d=F32), V(1, length + 128, d=F32),
               pltpu.SemaphoreType.DMA((136,)), pltpu.SemaphoreType.DMA((136,)), pltpu.SemaphoreType.DMA((32,)),
               pltpu.SemaphoreType.DMA((2, 2, nz)), pltpu.SemaphoreType.DMA((2, 2, nz))]
    return pl.pallas_call(forward_kernel, out_shape=[o for o, _ in outs], out_specs=[s for _, s in outs],
        in_specs=[sm, an, vm, an, vm, vm, an, an] + [vm] * 9, scratch_shapes=scratch,
        compiler_params=pltpu.CompilerParams(collective_id=1, has_side_effects=True, vmem_limit_bytes=67043328))(valid, tok, memory, tch, w3, wo, lu, ld, *vecs, bias_up, bias_qv, ids)
def total_of(refs):
    acc = refs[0][...].astype(F32)
    for r in refs[1:]:
        acc = acc + r[...].astype(F32)
    return acc

class Piece:
    def __init__(self, n, env, col0, num, js, x_first):
        self.n, self.x_first = n, x_first
        gown, ha, ax, ay, ayf, axf, mine, theirs, order = env
        C = pl.ds(col0, num); y, k = n.y, n.k
        self.core = [n.move((lambda j=j, yy=yy: gown.at[j, 2 * yy + 1 - k, :, C]), (lambda j=j, yy=yy: ha.at[yy, 2 * k + j, :, C]), n.kp) for j in js for yy in range(2)]
        self.keep = [n.copy((lambda j=j, yy=yy: gown.at[j, 2 * yy + k, :, C]), (lambda j=j, yy=yy: ha.at[yy, 2 * k + j, :, C])) for j in js for yy in range(2)]
        zz = order if len(js) == 2 else [js[0], js[0] + 2]
        self.first, self.second, self.add1, self.add2 = [], [], [], []
        for q in zz:
            if x_first:
                self.first.append(n.move((lambda q=q: ha.at[:, q, theirs, C]), (lambda q=q: ax.at[:, q, :, C]), n.xp))
                self.add1.append(lambda q=q: [add_to(ha.at[yy, q, mine, C], ax.at[yy, q, :, C]) for yy in range(2)])
                self.second.append(n.move((lambda q=q: ha.at[1 - y, q, mine, C]), (lambda q=q: ay.at[q, :, C]), n.yp))
                self.add2.append(lambda q=q: add_to(ha.at[y, q, mine, C], ay.at[q, :, C]))
            else:
                self.first.append(n.move((lambda q=q: ha.at[1 - y, q, :, C]), (lambda q=q: ayf.at[q, :, C]), n.yp))
                self.add1.append(lambda q=q: add_to(ha.at[y, q, :, C], ayf.at[q, :, C]))
                self.second.append(n.move((lambda q=q: ha.at[y, q, theirs, C]), (lambda q=q: axf.at[q, :, C]), n.xp))
                self.add2.append(lambda q=q: add_to(ha.at[y, q, mine, C], axf.at[q, :, C]))
    def start(self):
        for m in self.core + self.keep:
            m.start()
    def ev1(self):
        for m in self.core:
            m.wait_recv()
        for m in self.keep:
            m.wait()
        for m in self.first:
            m.start()
    def ev2(self):
        for m, f, s in zip(self.first, self.add1, self.second):
            m.wait_recv(); f(); s.start()
    def ev3(self):
        for m, f in zip(self.second, self.add2):
            m.wait_recv(); f()

class Rows:
    def __init__(self, n, here, z1, z2, e, dev1, dev2, add):
        e1, e2, e3 = e
        self.a = n.move((lambda: here(e3)), (lambda: z1(1)), dev1)
        self.b = n.move((lambda: here(e1)), (lambda: z1(0)), dev1)
        self.c = n.move((lambda: here(e2)), z2, dev2)
        self.mid = lambda: add(here(e2), z1(1))
    def start(self):
        self.a.start(); self.b.start()
    def middle(self):
        self.a.wait_recv(); self.mid(); self.c.start()
    def end(self):
        self.b.wait_recv(); self.c.wait_recv()

def backward_kernel(hu_h, hd_h, ga_h, mixed_h, xt_h, q_h, k_h, v_h, w_h, o4_h, g1_h, lse, vgrad, bupgrad, ids,
                    grad4, lout, gmem, g3, gwo, fu, fd, fvec, bup, bqv,
                    hu, hd, ux, uz1, uz2, ut, uy, fub, pu, dy, dz1, dz2, df, dx, pd,
                    ha, ax, ay, ayf, axf, az1, az2, fa, pa, gown,
                    ga, mixed, xt, qt, kt, vt, w, o4, g1, wp, wt, gat, gm, gp, dv, dk, dqt, ktt, dd, g4, gs, gr, lo32,
                    sv, svk, svt, svy, svo, svx, ps, svz, idk, idq, ss, rs, lsem):
    n = Net(ss, rs, lsem)
    nz, y, k, c, z, x, d, nd = n.nz, n.y, n.k, n.c, n.z, n.x, n.d, n.nd
    b = fu.shape[0]; hb = b // 2
    rows, feats = ga.shape
    fb = pl.ds(0, b)
    own_rows = g1.shape[0]; main = own_rows - 16; length = 2 * main
    mine = pl.ds(pl.multiple_of(x * hb, 16), hb)
    theirs = pl.ds(pl.multiple_of((1 - x) * hb, 16), hb)
    all_of = lambda r: (lambda: r)
    l_w, l_ga, l_m = [n.local(all_of(s), all_of(t)) for s, t in ((w_h, w), (ga_h, ga), (mixed_h, mixed))]
    l_q = [n.local(all_of(s), all_of(t)) for s, t in ((k_h, kt), (q_h, qt), (v_h, vt))]
    l_x = n.local(all_of(xt_h), all_of(xt))
    l_d = n.local(lambda: hd_h.at[y], lambda: hd)
    l_u = n.local(lambda: hu_h.at[:, :, mine], lambda: hu)
    l_o = [n.local(all_of(o4_h), all_of(o4)), n.local(all_of(g1_h), all_of(g1))]
    n.barrier(n.zp[1:] + [n.yp, n.ykp, n.kp, n.xp] + n.others)
    e1 = z + 1 - 2 * lax.rem(z, 2)
    e2 = lax.rem(z + 2, nz)
    e3 = lax.rem(e1 + 2, nz)
    e = (e1, e2, e3)
    order = [e3, e2, e1, z]
    dev1, dev2 = (d, e1, c), (d, e2, c)
    d_y = [n.send((lambda q=q: hd_h.at[1 - y, q]), (lambda q=q: dy.at[q]), n.yp) for q in order]
    u_x = [n.send((lambda q=q: hu_h.at[:, q, theirs]), (lambda q=q: ux.at[:, q]), n.xp) for q in order]

    def add2(a, s):
        for yy in range(2):
            add_to(a.at[yy], s.at[yy])
    dz = Rows(n, lambda q: hd.at[q], lambda s: dz1.at[s], lambda: dz2, e, dev1, dev2, add_to)
    uz = Rows(n, lambda q: hu.at[:, q], lambda s: uz1.at[s], lambda: uz2, e, dev1, dev2, add2)
    d_x = n.move(all_of(df), all_of(dx), n.xp)
    u_y = n.move(lambda: ut.at[1 - y], all_of(uy), n.yp)
    u_f = n.move(lambda: fub.at[mine], lambda: fub.at[mine], n.xp)

    mypair = d // 2

    def pairs_sum(value, slots, view):
        if nd == 2:
            return value
        view(slots, mypair)[...] = value.astype(slots.dtype)
        ms = [n.send((lambda: view(slots, mypair)), (lambda: view(slots, mypair)), o) for o in n.others]
        for m in ms:
            m.wait_recv()
        return total_of([view(slots, i) for i in range(nd // 2)])

    def ev_dy(j):
        def run():
            d_y[j].wait_recv()
            if j == 0:
                l_d.wait()
            add_to(hd.at[order[j]], dy.at[order[j]])
            if j == 0:
                dz.a.start()
        return run
    def ev_ux(j):
        def run():
            u_x[j].wait_recv()
            if j == 0:
                l_u.wait()
            add2(hu.at[:, order[j]], ux.at[:, order[j]])
            if j == 0:
                uz.a.start()
        return run
    def ev_df():
        dz.end()
        df[...] = total_of([hd.at[z], dz1.at[0], dz2]).astype(BF)
        d_x.start()
    def ev_ut():
        uz.end()
        for yy in range(2):
            ut[yy] = total_of([hu.at[yy, z], uz1.at[0, yy], uz2.at[yy]]).astype(BF)
        u_y.start()
    def ev_uf():
        u_y.wait_recv()
        fub[mine, :] = pairs_sum(total_of([ut.at[y], uy]), pu, lambda s, i: s.at[i]).astype(BF)
        u_f.start()
    env = (gown, ha, ax, ay, ayf, axf, mine, theirs, order)
    PO = Piece(n, env, 640, 128, (0, 1), True)
    P0 = Piece(n, env, 0, 384, (0,), True)
    P1 = Piece(n, env, 0, 384, (1,), False)
    P2 = Piece(n, env, 384, 128, (0, 1), True)
    P3 = Piece(n, env, 512, 128, (0, 1), False)
    class Cols:
        def __init__(self, col0, num):
            C = pl.ds(col0, num)
            self.C = C
            self.z = Rows(n, lambda q: ha.at[y, q, mine, C], lambda s: az1.at[s, :, C], lambda: az2.at[:, C], e, dev1, dev2, add_to)
            self.f = n.move(lambda: fa.at[mine, C], lambda: fa.at[mine, C], n.xp)
        def end(self):
            self.z.end()
            C = self.C
            fa[mine, C] = pairs_sum(total_of([ha.at[y, z, mine, C], az1.at[0, :, C], az2.at[:, C]]), pa, lambda s, i: s.at[i, :, C]).astype(BF)
            self.f.start()
    ZO, Z01, Z2, Z3 = Cols(640, 128), Cols(0, 384), Cols(384, 128), Cols(512, 128)
    row_ids(ids, y, gmem.shape[1] // 2, idk, idq)
    l_w.wait(); l_ga.wait()
    gat[...] = ga[...].T
    assemble_pairs(w, wp, feats)
    wt[:, pl.ds(0, 128)] = w[0, :, pl.ds(640, 128)]
    wt[:, pl.ds(128, 128)] = w[1, :, pl.ds(640, 128)]
    lo = lax.broadcasted_iota(jnp.int32, (feats, 128), 1) < 64
    wt[:, pl.ds(256, 128)] = jnp.where(lo, pltpu.roll(w[0, :, pl.ds(512, 128)].astype(F32), 64, 1), w[1, :, pl.ds(512, 128)].astype(F32)).astype(BF)
    r3 = rows // 3

    def mixed_grad(i, _):
        r = pl.ds(pl.multiple_of(i * r3, 16), r3)
        v = nn(ga[r, :], wt[...])
        for p in range(3):
            gm[p, r, :] = v[:, 128 * p:128 * p + 128].astype(BF)
        return 0
    lax.fori_loop(0, 3, mixed_grad, 0)
    l_m.wait()
    for cc in range(4):
        af = gat[pl.ds(b * cc, b), :]
        for j in range(2):
            gown[j, cc, :, pl.ds(640, 128)] = nn(af, mixed[j]).astype(BF)
    PO.start()
    for m in l_q:
        m.wait()
    l_x.wait()
    def ev_b():
        dz.b.start(); uz.b.start()
    table = {0: [ev_dy(0), ev_ux(0)], 1: [PO.ev1], 4: [ev_dy(1), ev_ux(1)], 6: [dz.middle], 7: [ev_dy(2), ev_ux(2), P0.ev1], 9: [uz.middle], 10: [ev_b],
             11: [ev_dy(3), ev_ux(3)], 13: [PO.ev2], 15: [P1.ev1], 16: [PO.ev3, ZO.z.start, P0.ev2]}
    cuts = {1: 0, 3: 1, 4: 2}

    def head(i, _):
        p = i // 2
        h = i % 2
        he = pl.ds(pl.multiple_of(64 * h, 64), 64)

        @pl.when(h == 0)
        def _():
            ktt[...] = kt[p].T
            prod = (gm[p].astype(F32) * mixed[p].astype(F32)).T
            dd[0] = jnp.sum(prod[:64, :], axis=0, keepdims=True)
            dd[1] = jnp.sum(prod[64:, :], axis=0, keepdims=True)
            dv[...] = jnp.zeros_like(dv)
            dk[...] = jnp.zeros_like(dk)
        lanes = (lax.broadcasted_iota(jnp.int32, (1, 128), 1) // 64) == h
        for t, (q0, qn, spans) in enumerate(tiles(rows, length)):
            q = qt[p, pl.ds(q0, qn), :]
            qm = jnp.where(lanes, q, jnp.zeros_like(q))
            g = gm[p, pl.ds(q0, qn), :]
            gmm = jnp.where(lanes, g, jnp.zeros_like(g))
            sc = scores_of(kt, qm, idk, idq[0:1, pl.ds(q0, qn)], p, spans)
            l = lse[i, :, pl.ds(q0, qn)]
            dl = dd[h, :, pl.ds(q0, qn)]
            acc = None
            for s, (k0, kn, _) in zip(sc, spans):
                pr = jnp.exp(s - l)
                dp = nt(vt[p, pl.ds(k0, kn), :], gmm)
                ds = (pr * (dp - dl)).astype(BF)
                dv[pl.ds(k0, kn), :] += nn(pr.astype(BF), gmm)
                dk[pl.ds(k0, kn), :] += nn(ds, qm)
                o = nn(ktt[he, pl.ds(k0, kn)], ds)
                acc = o if acc is None else acc + o
            dqt[he, pl.ds(q0, qn)] = acc * 0.125
            if t in cuts:
                at(3 * i + cuts[t], table)

        @pl.when(h == 1)
        def _():
            gp[p, :, pl.ds(0, 128)] = dqt[...].T.astype(BF)
            gp[p, :, pl.ds(128, 128)] = dk[...].astype(BF)
            gp[p, :, pl.ds(256, 128)] = dv[...].astype(BF)

        @pl.when(jnp.logical_and(h == 1, p < 2))
        def _():
            def part(cc, _):
                f = pl.ds(pl.multiple_of(b * cc, 16), b)
                gown[p, cc, :, pl.ds(0, 384)] = nn(xt[f, pl.ds(0, rows)], gp[p]).astype(BF)
                return 0
            lax.fori_loop(0, 4, part, 0)
        at(i, {1: [P0.start], 3: [P1.start]})
        return 0
    lax.fori_loop(0, 6, head, 0)
    sv[...] = jnp.zeros_like(sv)
    for i in range(6):
        sv[pl.ds(i, 1), :] = jnp.sum(vgrad[i], axis=0, keepdims=True)
    for i in range(nz):
        sv[pl.ds(6 + i, 1), :] = jnp.sum(bupgrad[i], axis=0, keepdims=True)
    for p in range(3):
        t = jnp.sum(group_sum(gp[p].astype(F32)), axis=0, keepdims=True)
        sv[pl.ds(6 + nz + p, 1), pl.ds(0, 384)] = jnp.where(k == 0, t, 0.0)
        sv[pl.ds(6 + nz + p, 1), pl.ds(384, 384)] = jnp.where(k == 1, t, 0.0)
    s_k = n.send(all_of(sv), all_of(svk), n.kp)
    sw = lambda a: pltpu.roll(a, 64, 1)

    def last(cc, _):
        f = pl.ds(pl.multiple_of(b * cc, 16), b)
        r2 = nn(xt[f, pl.ds(0, rows)], gp[2])
        o2 = nn(gat[f, :], mixed[2])
        lo = lax.broadcasted_iota(jnp.int32, (b, 128), 1) < 64
        rq, rk, rv = r2[:, :128], r2[:, 128:256], r2[:, 256:]
        gown[0, cc, :, pl.ds(384, 128)] = jnp.where(lo, rq, sw(rk)).astype(BF)
        gown[1, cc, :, pl.ds(384, 128)] = jnp.where(lo, sw(rq), rk).astype(BF)
        gown[0, cc, :, pl.ds(512, 128)] = jnp.where(lo, rv, sw(o2)).astype(BF)
        gown[1, cc, :, pl.ds(512, 128)] = jnp.where(lo, sw(rv), o2).astype(BF)
        return 0
    lax.fori_loop(0, 4, last, 0)
    P2.start(); P3.start()
    def rowsgrad(r):
        return nt(gp[0, r, :], wp[0]) + nt(gp[1, r, :], wp[1]) + nt(gp[2, r, :], wp[2])

    def half_rows(kk, put):
        def chunk(i, _):
            put(pl.ds(pl.multiple_of(i * 256, 16), 256), rowsgrad(pl.ds(pl.multiple_of(kk * main + i * 256, 16), 256)))
            return 0
        lax.fori_loop(0, main // 256, chunk, 0)
        put(pl.ds(main, 16), rowsgrad(pl.ds(pl.multiple_of(length + kk * 16, 16), 16)))
    def put_other(r, v):
        gs[r, :] = v.astype(BF)
    half_rows(1 - k, put_other)
    g_k = n.send(all_of(gs), all_of(gr), n.kp)
    s_k.wait_recv()
    svt[...] = sv[...] + svk[...]
    s_y = n.send(all_of(svt), all_of(svy), n.yp)
    P1.ev2()
    P2.ev1(); P3.ev1()
    for m in l_o:
        m.wait()
    g4[:, :, pl.ds(b, g4.shape[2] - b)] = jnp.zeros((4, own_rows, g4.shape[2] - b), BF)
    def put_own(r, v):
        g1[r, :] = g1[r, :] + v
    half_rows(k, put_own)
    s_y.wait_recv()
    svo[...] = svt[...] + svy[...]
    s_x = n.send(all_of(svo), all_of(svx), n.xp)
    ev_ut()
    P0.ev3()
    ev_df()
    P1.ev3(); Z01.z.start(); ZO.z.middle()
    P2.ev2()
    g_k.wait_recv()

    def own(i, _):
        r = pl.ds(pl.multiple_of(i * 48, 16), 48)
        v = g1[r, :] + gr[r, :].astype(F32)
        for cc in range(4):
            g4[cc, r, fb] = v[:, cc * b:(cc + 1) * b].astype(BF)
        return 0
    lax.fori_loop(0, own_rows // 48, own, 0)
    g_l = n.local(lambda: g4.at[c], lambda: grad4.at[y, k])
    dst = lambda: grad4.at[y, k]
    g_s = [n.send(lambda: g4.at[n.oc], dst, n.yp), n.send(lambda: g4.at[3 - c], dst, n.ykp), n.send(lambda: g4.at[c + 1 - 2 * k], dst, n.kp)]
    P3.ev2()
    s_x.wait_recv()
    svz[z] = pairs_sum(svo[...] + svx[...], ps, lambda s, i: s.at[i])
    s_z = [n.send(lambda: svz.at[z], lambda: svz.at[z], n.zp[i]) for i in range(1, nz)]
    P2.ev3(); Z2.z.start()
    ev_uf()
    Z01.z.middle(); ZO.end()
    P3.ev3(); Z3.z.start()
    half = (lout.shape[1] - length) // 2
    for s in range(2):
        lo32[pl.ds(0, half), :] = o4[s, 0, pl.ds(main, 16), fb].astype(F32)[:half]
        lo32[pl.ds(half, main), :] = o4[s, 0, pl.ds(0, main), fb].astype(F32)
        lo32[pl.ds(half + main, main), :] = o4[s, 1, pl.ds(0, main), fb].astype(F32)
        lo32[pl.ds(half + length, 16 - half), :] = o4[s, 0, pl.ds(main, 16), fb].astype(F32)[half:]
        lo32[pl.ds(length + 16, 2 * half - 16), :] = o4[s, 1, pl.ds(main, 16), fb].astype(F32)[:2 * half - 16]
        lout[s] = lo32[pl.ds(0, length + 2 * half), :].astype(BF)
    Z2.z.middle(); Z01.end(); Z3.z.middle()
    d_x.wait_recv()
    fd[...] = pairs_sum(total_of([df, dx]), pd, lambda s, i: s.at[i])
    u_f.wait_recv()
    fu[...] = fub[...].astype(F32)
    Z2.end(); Z3.end()
    for m in s_z:
        m.wait_recv()
    acc = svz[0]
    for i in range(1, nz):
        acc = acc + svz[i]
    pick = jnp.where(c == 0, acc[:8, 0:b], 0.0)
    for cc in range(1, 4):
        pick = pick + jnp.where(c == cc, acc[:8, cc * b:(cc + 1) * b], 0.0)
    fvec[...] = pick
    t = jnp.where(z == 0, acc[6:7], 0.0)
    for i in range(1, nz):
        t = t + jnp.where(z == i, acc[6 + i:7 + i], 0.0)
    bup[...] = t
    hbias = acc[6 + nz:9 + nz]
    hbias = jnp.where(z // 2 == 0, hbias[:, :384], hbias[:, 384:])
    odd = z % 2 == 1
    two = jnp.where(odd, hbias[1:2], hbias[0:1])
    lo1 = lax.broadcasted_iota(jnp.int32, (8, 128), 1) < 64
    w8 = lambda a: jnp.broadcast_to(a, (8, 128))
    left = lambda a, v: jnp.where(lo1, w8(a), sw(w8(v)))[0:1]
    right = lambda a, v: jnp.where(lo1, sw(w8(a)), w8(v))[0:1]
    lq, lv = hbias[2:3, :128], hbias[2:3, 256:]
    bqv[pl.ds(0, 1), :] = left(two[:, :128], two[:, 256:])
    bqv[pl.ds(1, 1), :] = right(two[:, :128], two[:, 256:])
    bqv[pl.ds(2, 1), :] = jnp.where(odd, right(lq, lv), left(lq, lv))
    for m in (ZO, Z01, Z2, Z3):
        m.f.wait_recv()
    lob = lax.broadcasted_iota(jnp.int32, (b, 128), 1) < 64
    tile = lambda i: fa[:, pl.ds(128 * i, 128)].astype(F32)
    t0, t1, t2, t3, t4, t5 = [tile(i) for i in range(6)]
    g3[0, :, pl.ds(0, 128)] = jnp.where(lob, t0, sw(t1))
    g3[0, :, pl.ds(128, 64)] = t2[:, :64]
    g3[1, :, pl.ds(0, 128)] = jnp.where(lob, sw(t0), t1)
    g3[1, :, pl.ds(128, 64)] = sw(t2)[:, :64]
    g3[2, :, pl.ds(0, 128)] = t3
    g3[2, :, pl.ds(128, 64)] = t4[:, :64]
    gwo[pl.ds(0, 128), :] = t5.T
    gwo[pl.ds(128, 64), :] = sw(t4).T[:64]
    for m in g_s:
        m.wait_recv()
    g_l.wait()
    for s in range(2):
        gmem[s, pl.ds(0, 16), :] = grad4[s, 0, pl.ds(main, 16), fb].astype(F32)
        gmem[s, pl.ds(16, 2 * half - 16), :] = grad4[s, 1, pl.ds(main, 16), fb].astype(F32)[:2 * half - 16]
    n.finish()

def backward(hu, hd, ga, mixed, xt, qt, kt, vt, w, o4, g1, lse, vgrad, bupgrad, ids, half, nz, nd):
    b, width = hu.shape[2:]
    feats = 4 * b; hb = b // 2; rows = ga.shape[0]; own = g1.shape[0]; length = 2 * (own - 16)
    V = lambda *s, d=BF: pltpu.VMEM(s, d)
    vm = pl.BlockSpec(memory_space=pltpu.VMEM); an = pl.BlockSpec(memory_space=pl.ANY)
    S = jax.ShapeDtypeStruct
    np_ = max(1, nd // 2) if nd > 2 else 1
    pw = (hb, width) if nd > 2 else (16, 128)
    t3 = V(3, rows, 128); f3 = lambda *s: V(*s, d=F32)
    sm = f3(16, feats)
    outs = (S((2, 2, own, 256), BF), S((2, length + 2 * half, b), BF), S((2, 2 * half, b), F32), S((3, b, b), F32), S((b, b), F32), S((b, width), F32), S((b, width), F32), S((8, b), F32), S((1, feats), F32), S((3, 128), F32))
    scratch = [V(2, nz, hb, width), V(nz, b, width), V(2, nz, hb, width), V(2, 2, hb, width), V(2, hb, width), V(2, hb, width), V(hb, width), V(b, width), V(np_, *pw),
               V(nz, b, width), V(2, b, width), V(b, width), V(b, width), V(b, width), V(np_, b, width) if nd > 2 else V(1, 16, 128),
               V(2, nz, b, width), V(2, nz, hb, width), V(nz, hb, width), V(nz, b, width), V(nz, hb, width), V(2, hb, width), V(hb, width), V(b, width), V(np_, *pw), V(2, 4, b, width),
               V(rows, feats), t3, V(*xt.shape), t3, t3, t3, V(*w.shape), V(*o4.shape), f3(*g1.shape), V(3, feats, 384), V(feats, 384), V(feats, rows), t3, V(3, rows, 384),
               f3(rows, 128), f3(rows, 128), f3(128, rows), V(128, rows), f3(2, 1, rows), V(4, own, 256), V(own, feats), V(own, feats), f3(rows, b),
               sm, sm, sm, sm, sm, sm, f3(np_, 16, feats), f3(nz, 16, feats), f3(length + 128, 128), f3(1, length + 128),
               pltpu.SemaphoreType.DMA((128 + 5 * nd,)), pltpu.SemaphoreType.DMA((128 + 5 * nd,)), pltpu.SemaphoreType.DMA((40,))]
    return pl.pallas_call(backward_kernel, out_shape=outs, in_specs=[an] * 11 + [vm] * 4, out_specs=(vm,) * len(outs), scratch_shapes=scratch,
        compiler_params=pltpu.CompilerParams(collective_id=2, has_side_effects=True, vmem_limit_bytes=67043328))(hu, hd, ga, mixed, xt, qt, kt, vt, w, o4, g1, lse, vgrad, bupgrad, ids)

def per_device(tokens, memory, block_ids, valid, teacher, w_qkv, bias_qv, w_out, bias_out, ln1_gain, ln1_bias, w_up, bias_up, w_down, bias_down, ln2_gain, ln2_bias):
    _, b, length = tokens.shape
    nd, nz = lax.axis_size("dp"), lax.axis_size("row")
    d, z, c = (lax.axis_index(a) for a in ("dp", "row", "col"))
    y, k = c // 2, c % 2
    feats = 4 * b
    half = memory.shape[1] // 2
    main = length // 2
    rows = length + 32
    one = lambda a: a.reshape(1, -1)
    xt, qt, kt, vt, mixed, wown, ga, hu, hd, lse, g_one, vgrad, bupgrad, out4 = forward(valid, tokens, memory, teacher, w_qkv.reshape(3, b, 192), w_out, w_up, w_down, [one(a) for a in (bias_out, ln1_gain, ln1_bias, bias_down, ln2_gain, ln2_bias)], one(bias_up), bias_qv, block_ids, nz)
    grad4, lout, gmem, g3, gwo, fu, fd, fvec, bup, bqv = backward(hu, hd, ga, mixed, xt, qt, kt, vt, wown, out4, g_one, lse, vgrad, bupgrad, block_ids, half, nz, nd)
    grad_tokens = grad4[:, :, :main, :b].reshape(2, length, b).astype(F32)
    return (lout, grad_tokens, gmem, g3.reshape(3, b * b), bqv, gwo, fvec[5], fvec[3], fvec[4], fu, bup[0], fd, fvec[2], fvec[0], fvec[1])

def solution(mesh):
    rows, feat = ("dp", "row"), "col"
    in_specs = (P(rows, feat, None), P(rows, None, feat), P(rows, None), P(), P(rows, feat, None), P("row", feat), P("row", None), P("row", feat), P(feat), P(feat), P(feat), P(feat, "row"), P("row"), P(feat, "row"), P(feat), P(feat), P(feat))
    out_specs = (P(rows, None, feat), P(rows, None, feat), P(rows, None, feat), P("row", feat), P("row", None), P("row", feat), P(feat), P(feat), P(feat), P(feat, "row"), P("row"), P(feat, "row"), P(feat), P(feat), P(feat))
    return jax.shard_map(per_device, mesh=mesh, in_specs=in_specs, out_specs=out_specs, check_vma=False)
```
